128 devices in a mesh: dp: 32 (over x, z, core), mp: 4 (over y).
Axes of the slice: x: 4, y: 4, z: 4, core: 2. Of those that a mesh axis runs over, the one named last changes fastest.
Arguments:
- tokens: bfloat16 [32, 768, 1536], P('dp'), may hold values from -6 to 6
- lengths: int32 [32], P('dp'), may hold values from 1 to 768, as said below
- buckets: int32 [32], P('dp'), may hold values from 0 to 3, as said below
- out_cotangent: bfloat16 [32, 768, 1536], P('dp'), may hold values from -6 to 6
- gain_attn: bfloat16 [1536], replicated, may hold values from 0.5 to 1.5
- w_query: bfloat16 [1536, 1536], P(None, 'mp'), may hold values from -0.15625 to 0.15625
- w_key: bfloat16 [1536, 1536], P(None, 'mp'), may hold values from -0.15625 to 0.15625
- w_value: bfloat16 [1536, 1536], P(None, 'mp'), may hold values from -0.15625 to 0.15625
- w_outgate: bfloat16 [1536, 1536], P(None, 'mp'), may hold values from -0.15625 to 0.15625
- w_forget: bfloat16 [1536, 24], P(None, 'mp'), may hold values from -0.15625 to 0.15625
- b_forget: bfloat16 [24], P('mp'), may hold values from 1 to 7
- w_out: bfloat16 [1536, 1536], P('mp'), may hold values from -1.5 to 1.5
- gain_mlp: bfloat16 [1536], replicated, may hold values from 0.5 to 1.5
- w_gate: bfloat16 [1536, 4096], P(None, 'mp'), may hold values from -0.15625 to 0.15625
- w_up: bfloat16 [1536, 4096], P(None, 'mp'), may hold values from -0.15625 to 0.15625
- w_down: bfloat16 [4096, 1536], P('mp'), may hold values from -0.09375 to 0.09375
Outputs:
- output: bfloat16 [32, 768, 1536], P('dp')
- input_grad: float32 [32, 768, 1536], P('dp')
- grad_gain_attn: float32 [1536], P('dp')
- grad_query: float32 [1536, 1536], P('dp', 'mp')
- grad_key: float32 [1536, 1536], P('dp', 'mp')
- grad_value: float32 [1536, 1536], P('dp', 'mp')
- grad_outgate: float32 [1536, 1536], P('dp', 'mp')
- grad_forget: float32 [1536, 24], P('dp', 'mp')
- grad_bias: float32 [24], P('mp')
- grad_out: float32 [1536, 1536], P('mp', 'dp')
- grad_gain_mlp: float32 [1536], P('dp')
- grad_gate: float32 [1536, 4096], P('dp', 'mp')
- grad_up: float32 [1536, 4096], P('dp', 'mp')
- grad_down: float32 [4096, 1536], P('mp', 'dp')
- rms: float32 [3, 4], replicated
The draws below stay inside these ranges and needn't reach their ends.
Inputs may be any that keep to these rules, and one draw needn't show every extreme that they name: `lengths`: A sequence with bucket id b has a length between b * 192 + 1 and (b + 1) * 192; some sequence has length 768. `buckets`: every bucket id occurs in every draw.
All inputs are finite; a program needn't handle non-finite values.
Results may differ from the reference program's by a relative error of at most 0.014.
Values sent between devices are 32-bit elements; how exact they have to be, the bound alone decides.
A program may use at most 256 MiB of HBM per device.

```python
import jax
import jax.numpy as jnp
from jax import lax

D = 1536
H = 24
HD = 64
FF = 4096
SEQ_LEN = 768
NBUCKET = 4
SEQS = 32


def bucket_plan(key):
    base_key = jax.random.fold_in(key, 11)
    first_key, rest_key, inner_key, spot_key = jax.random.split(base_key, 4)
    ordering = jax.random.permutation(first_key, NBUCKET).astype(jnp.int32)
    chosen = jax.random.randint(rest_key, (SEQS,), 0, NBUCKET).astype(jnp.int32)
    chosen = chosen.at[:NBUCKET].set(ordering)
    shuffle = jax.random.permutation(spot_key, SEQS)
    chosen = chosen[shuffle]
    bucket_span = SEQ_LEN // NBUCKET
    inside = jax.random.randint(inner_key, (SEQS,), 1, bucket_span + 1).astype(jnp.int32)
    seq_lengths = chosen * bucket_span + inside
    longest = jnp.argmax((chosen == NBUCKET - 1).astype(jnp.int32))
    seq_lengths = jnp.where(jnp.arange(SEQS) == longest, SEQ_LEN, seq_lengths).astype(jnp.int32)
    return (chosen, seq_lengths)


def draw_lengths(key, part):
    return bucket_plan(key)[1]


def draw_buckets(key, part):
    return bucket_plan(key)[0]


def steps_of(rng, shape, pieces, low, largest):
    def one(position, parts):
        draws = jax.random.uniform(jax.random.fold_in(jax.random.fold_in(rng, 6), position), (parts,), jnp.float32, low / len(pieces), largest / len(pieces))
        return jnp.repeat(jnp.exp(draws), shape[position] // parts).reshape((-1,) + (1,) * (len(shape) - position - 1))

    loudness = one(*pieces[0])
    for cut in pieces[1:]:
        loudness = loudness * one(*cut)
    return loudness


def centred(own_key, dims, width, bound, shards=(), held_as=jnp.bfloat16):
    values = width * jax.random.normal(own_key, dims, jnp.float32)
    if shards:
        values = values * steps_of(own_key, dims, shards, -0.22, 0.18)
    return jnp.clip(values, -bound, bound).astype(held_as)


def setup_inputs(seed: int = 0) -> dict:
    splits = jax.random.split(jax.random.key(seed), 17)
    tokens = centred(splits[0], (SEQS, SEQ_LEN, D), 1.0, 6.0, ((0, 32),))
    lengths = draw_lengths(jax.random.fold_in(splits[16], 71), 0)
    buckets = draw_buckets(jax.random.fold_in(splits[16], 71), 0)
    out_cotangent = centred(splits[3], (SEQS, SEQ_LEN, D), 1.0, 6.0, ((0, 32),))
    gain_attn = jnp.clip(1.0 + 0.1 * jax.random.normal(splits[4], (D,), jnp.float32), 0.5, 1.5).astype(jnp.bfloat16)
    w_query = centred(splits[5], (D, H * HD), D ** -0.5, 0.15625, ((1, 4),))
    w_key = centred(splits[6], (D, H * HD), D ** -0.5, 0.15625, ((1, 4),))
    w_value = centred(splits[7], (D, H * HD), D ** -0.5, 0.15625, ((1, 4),))
    w_outgate = centred(splits[8], (D, H * HD), D ** -0.5, 0.15625, ((1, 4),))
    w_forget = centred(splits[9], (D, H), D ** -0.5, 0.15625, ((1, 4),))
    b_forget = jnp.clip(1.0 + 6.0 * jax.random.uniform(splits[10], (H,), jnp.float32) ** steps_of(splits[10], (H,), ((0, 4),), -0.2, 0.2), 1.0, 7.0).astype(jnp.bfloat16)
    w_out = centred(splits[11], (H * HD, D), (H * HD // 96) ** -0.5, 1.5, ((0, 4),))
    gain_mlp = jnp.clip(1.0 + 0.1 * jax.random.normal(splits[12], (D,), jnp.float32), 0.5, 1.5).astype(jnp.bfloat16)
    w_gate = centred(splits[13], (D, FF), D ** -0.5, 0.15625, ((1, 4),))
    w_up = centred(splits[14], (D, FF), D ** -0.5, 0.15625, ((1, 4),))
    w_down = centred(splits[15], (FF, D), FF ** -0.5, 0.09375, ((0, 4),))
    return dict(tokens=tokens, lengths=lengths, buckets=buckets, out_cotangent=out_cotangent, gain_attn=gain_attn, w_query=w_query, w_key=w_key, w_value=w_value, w_outgate=w_outgate, w_forget=w_forget, b_forget=b_forget, w_out=w_out, gain_mlp=gain_mlp, w_gate=w_gate, w_up=w_up, w_down=w_down)


EPSILON = 1e-06
PRECISE = lax.Precision.HIGHEST

@jax.custom_vjp
def low(v):
    return lax.optimization_barrier(v.astype(jnp.bfloat16)).astype(jnp.float32)

@jax.custom_vjp
def low_back(v):
    return v

def low_keep(v):
    return (low(v), None)

def low_pass(kept, grad):
    return (grad,)

def back_keep(v):
    return (v, None)

def back_low(kept, grad):
    return (low(grad),)
low.defvjp(low_keep, low_pass)
low_back.defvjp(back_keep, back_low)

def high_dot(left, right):
    return jnp.dot(left, right, precision=PRECISE, preferred_element_type=jnp.float32)

def norm_rows(values):
    return values * lax.rsqrt(lax.optimization_barrier(jnp.mean(values * values, axis=-1, keepdims=True)) + EPSILON)

def sequence_layer(params, inputs, length):
    gain_attn, w_query, w_key, w_value, w_outgate, w_forget, b_forget, w_out, gain_mlp, w_gate, w_up, w_down = params
    seq_len = inputs.shape[0]
    normed_attn = low(norm_rows(inputs) * gain_attn)
    queries = low_back(high_dot(normed_attn, w_query))
    key_rows = low_back(high_dot(normed_attn, w_key))
    value_rows = low_back(high_dot(normed_attn, w_value))
    outgate = low_back(high_dot(normed_attn, w_outgate))
    forget_pre = low_back(high_dot(normed_attn, w_forget) + b_forget)
    query_norm = low(norm_rows(queries.reshape(seq_len, H, HD)))
    key_norm = low(norm_rows(key_rows.reshape(seq_len, H, HD)))
    value_low = low(value_rows).reshape(seq_len, H, HD)
    log_decay = jnp.cumsum(jax.nn.log_sigmoid(forget_pre), axis=0).T
    raw = jnp.einsum('ihd,jhd->hij', query_norm, key_norm, precision=PRECISE) * HD ** (-0.5)
    raw = raw + log_decay[:, :, None] - log_decay[:, None, :]
    scores = low_back(raw)
    positions = jnp.arange(seq_len)
    allowed = (positions[None, :] <= positions[:, None]) & (positions[None, :] < length)
    scores = jnp.where(allowed[None], scores, -1e+30)
    attn_probs = jax.nn.softmax(scores, axis=-1)
    attended = jnp.einsum('hij,jhd->ihd', low(attn_probs), value_low, precision=PRECISE).reshape(seq_len, H * HD)
    attended = low_back(attended)
    gated = low(attended * jax.nn.sigmoid(outgate))
    branch_attn = low_back(high_dot(gated, w_out))
    middle = inputs + branch_attn
    normed_mlp = low(norm_rows(middle) * gain_mlp)
    gate_pre = low_back(high_dot(normed_mlp, w_gate))
    up_pre = low_back(high_dot(normed_mlp, w_up))
    hidden = low(jax.nn.silu(gate_pre) * up_pre)
    branch_mlp = low_back(high_dot(hidden, w_down))
    return (middle + branch_mlp, branch_attn, branch_mlp)

def reference(tokens, lengths, buckets, out_cotangent, gain_attn, w_query, w_key, w_value, w_outgate, w_forget, b_forget, w_out, gain_mlp, w_gate, w_up, w_down):
    params = tuple((w.astype(jnp.float32) for w in (gain_attn, w_query, w_key, w_value, w_outgate, w_forget, b_forget, w_out, gain_mlp, w_gate, w_up, w_down)))
    inputs = tokens.astype(jnp.float32)

    def whole_layer(params_in, inputs_in):

        def one_sequence(seq_pair):
            return jax.checkpoint(sequence_layer)(params_in, seq_pair[0], seq_pair[1])
        return lax.map(one_sequence, (inputs_in, lengths))
    (result, branch_attn, branch_mlp), pullback = jax.vjp(whole_layer, params, inputs)
    positions = jnp.arange(SEQ_LEN)
    valid_rows = (positions[None, :] < lengths[:, None]).astype(jnp.float32)[:, :, None]
    grad_rows = out_cotangent.astype(jnp.float32) * valid_rows
    param_grads, input_grad = pullback((grad_rows, jnp.zeros_like(branch_attn), jnp.zeros_like(branch_mlp)))
    bucket_hot = (buckets[:, None] == jnp.arange(NBUCKET)[None, :]).astype(jnp.float32)
    per_sequence = jnp.stack([lax.optimization_barrier(jnp.sum(valid_rows * inputs * inputs, axis=(1, 2))), lax.optimization_barrier(jnp.sum(valid_rows * branch_attn * branch_attn, axis=(1, 2))), lax.optimization_barrier(jnp.sum(valid_rows * branch_mlp * branch_mlp, axis=(1, 2)))])
    totals = high_dot(per_sequence, bucket_hot)
    counts = lax.optimization_barrier(jnp.sum(lengths.astype(jnp.float32)[:, None] * bucket_hot, axis=0))
    rms = jnp.sqrt(totals / (counts[None, :] * D))
    return (result.astype(jnp.bfloat16), input_grad, param_grads[0], param_grads[1], param_grads[2], param_grads[3], param_grads[4], param_grads[5], param_grads[6], param_grads[7], param_grads[8], param_grads[9], param_grads[10], param_grads[11], rms)
```

```python
import functools

import jax
import jax.numpy as jnp
from jax import lax
from jax.experimental import pallas as pl
from jax.experimental.pallas import tpu as pltpu
from jax.sharding import PartitionSpec as P

NBUCKET = 4


EPSILON = 1e-06


def sent_to_all(array, axis):
    devices = lax.axis_size(axis)
    return lax.all_to_all(
        jnp.broadcast_to(array[None], (devices, *array.shape)), axis, 0, 0, tiled=True
    )


def over_copies(array, axis):
    return sent_to_all(array, axis).sum(axis=0)


def in_one(arrays, axis):
    ends = [0]
    for a in arrays:
        ends.append(ends[-1] + a.size)
    subtotal = over_copies(jnp.concatenate([a.ravel() for a in arrays]), axis)
    return tuple((subtotal[b:e].reshape(a.shape) for a, b, e in zip(arrays, ends, ends[1:])))


def norm_rows(values):
    return values * lax.rsqrt(jnp.mean(values * values, axis=-1, keepdims=True) + EPSILON)


def gain_norm(values, gain_row):
    return norm_rows(values) * gain_row


def swiglu(gate_pre, up_pre):
    return jax.nn.silu(gate_pre) * up_pre


def low_dot(left, right):
    return jnp.dot(left, right, preferred_element_type=jnp.float32)


def back_dot(left, right):
    return lax.dot_general(
        left, right, (((0,), (0,)), ((), ())), preferred_element_type=jnp.float32
    )


def trans_dot(left, right):
    return lax.dot_general(
        left, right, (((1,), (1,)), ((), ())), preferred_element_type=jnp.float32
    )

MESH = pl.DeviceIdType.MESH
F32 = jnp.float32
Y = 4
STEPS = ("oR", "oL", "iR", "iL", "dR", "dL", "gRa", "gRb", "gLa", "gLb", "fR", "fL")


def rows_of(ref, start, count):
    return ref.at[pl.ds(pl.multiple_of(start, 8), count)]


class YReduce:
    def __init__(self, in_ref, out_ref, opp, nbr, held, ssem, rsem):
        self.refs = (in_ref, out_ref, opp, nbr, held)
        self.sems = (ssem, rsem)
        self.dp, self.me = lax.axis_index("dp"), lax.axis_index("mp")
        self.right, self.left = lax.rem(self.me + 1, Y), lax.rem(self.me + 3, Y)
        self.far = lax.rem(self.me + 2, Y)
        self.quarter = in_ref.shape[0] // Y
        self.half = self.quarter // 2
        self.sent = {}

    def neighbours(self):
        return [(self.dp, self.right), (self.dp, self.left)]

    def send(self, name, src, dst, to):
        k = STEPS.index(name)
        copy = pltpu.make_async_remote_copy(
            src_ref=src,
            dst_ref=dst,
            send_sem=self.sems[0].at[k],
            recv_sem=self.sems[1].at[k],
            device_id=(self.dp, to),
            device_id_type=MESH,
        )
        copy.start()
        self.sent[name] = copy

    def start(self):
        x, _, opp, nbr, _ = self.refs
        q, h = self.quarter, self.half
        self.send("oR", rows_of(x, self.far * q, h), opp.at[0], self.right)
        self.send("oL", rows_of(x, self.far * q + h, h), opp.at[1], self.left)
        self.send("iR", rows_of(x, self.right * q + h, h), nbr.at[0, h:q], self.right)
        self.send("iL", rows_of(x, self.left * q, h), nbr.at[1, 0:h], self.left)

    def relay(self):
        x, _, opp, nbr, held = self.refs
        q, h = self.quarter, self.half
        self.sent["oR"].wait_recv()
        held[0] = rows_of(x, self.right * q, h)[...] + opp[0]
        self.send("dR", held.at[0], nbr.at[0, 0:h], self.right)
        self.sent["oL"].wait_recv()
        held[1] = rows_of(x, self.left * q + h, h)[...] + opp[1]
        self.send("dL", held.at[1], nbr.at[1, h:q], self.left)

    def spread(self):
        x, out, _, nbr, _ = self.refs
        q, h = self.quarter, self.half
        for part, names, tag in ((0, ("dR", "iL"), "a"), (1, ("iR", "dL"), "b")):
            for name in names:
                self.sent[name].wait_recv()
            at = self.me * q + part * h
            own = rows_of(out, at, h)
            own[...] = (
                rows_of(x, at, h)[...]
                + nbr[0, part * h : part * h + h]
                + nbr[1, part * h : part * h + h]
            )
            self.send("gR" + tag, own, own, self.right)
            self.send("gL" + tag, own, own, self.left)

    def forward(self):
        _, out, _, _, _ = self.refs
        q, h = self.quarter, self.half
        self.sent["gRa"].wait_recv()
        block = rows_of(out, self.left * q, h)
        self.send("fR", block, block, self.right)
        self.sent["gLb"].wait_recv()
        block = rows_of(out, self.right * q + h, h)
        self.send("fL", block, block, self.left)

    def finish(self):
        for name in ("gRb", "gLa", "fR", "fL"):
            self.sent[name].wait_recv()
        for name in STEPS:
            self.sent[name].wait_send()


def y_scratch(rows, columns):
    quarter = rows // Y
    return [
        pltpu.VMEM((2, quarter // 2, columns), F32),
        pltpu.VMEM((2, quarter, columns), F32),
        pltpu.VMEM((2, quarter // 2, columns), F32),
        pltpu.SemaphoreType.DMA((12,)),
        pltpu.SemaphoreType.DMA((12,)),
    ]


def y_reduce_kernel(in_ref, out_ref, *scratch):
    ring = YReduce(in_ref, out_ref, *scratch)
    meet(ring.neighbours())
    ring.start()
    ring.relay()
    ring.spread()
    ring.forward()
    ring.finish()


def meet(devices):
    barrier = pltpu.get_barrier_semaphore()
    for device in devices:
        pl.semaphore_signal(barrier, inc=1, device_id=device, device_id_type=MESH)
    pl.semaphore_wait(barrier, len(devices))


def y_reduce(array, call_id):
    return pl.pallas_call(
        y_reduce_kernel,
        out_shape=jax.ShapeDtypeStruct(array.shape, F32),
        in_specs=[pl.BlockSpec(memory_space=pltpu.VMEM)],
        out_specs=pl.BlockSpec(memory_space=pltpu.VMEM),
        scratch_shapes=y_scratch(*array.shape),
        compiler_params=pltpu.CompilerParams(
            collective_id=call_id, has_side_effects=True, vmem_limit_bytes=20 << 20
        ),
    )(array)


class ScatterSum:
    def __init__(self, ins, pieces, own, other, near, last, psem, lsem, ssem, rsem):
        self.ins, self.pieces = ins, pieces
        self.own, self.other, self.near, self.last = own, other, near, last
        self.psem, self.lsem, self.ssem, self.rsem = psem, lsem, ssem, rsem
        dp, self.my = lax.axis_index("dp"), lax.axis_index("mp")
        c, z, x = lax.rem(dp, 2), lax.rem(dp // 2, 4), dp // 8
        self.c, self.sib = c, dp + 1 - 2 * c
        self.st1, self.st2 = 4 - 3 * c, 1 + 3 * c
        self.p1, self.p2 = x + c * (z - x), z + c * (x - z)
        step = lambda p, by: lax.rem(p + by, 4)
        self.r1, self.l1, self.o1 = (step(self.p1, by) for by in (1, 3, 2))
        self.r2, self.l2, self.o2 = (step(self.p2, by) for by in (1, 3, 2))
        device = lambda a, b: (a * self.st1 + b * self.st2) * 2 + c
        self.to = (
            (device(self.r1, self.p2), device(self.l1, self.p2)),
            (device(self.p1, self.r2), device(self.p1, self.l2)),
        )
        self.sent = {}

    def neighbours(self):
        return [(n, self.my) for n in (self.sib, *self.to[0], *self.to[1])]

    def send(self, name, k, stage, src, dst):
        at = (k * 2 + stage) * 6 + STEPS.index(name)
        copy = pltpu.make_async_remote_copy(
            src_ref=src,
            dst_ref=dst,
            send_sem=self.ssem.at[at],
            recv_sem=self.rsem.at[at],
            device_id=(self.to[stage][0 if name[1] == "R" else 1], self.my),
            device_id_type=MESH,
        )
        copy.start()
        self.sent[name, k, stage] = copy

    def source(self, k, block):
        which, start, width = self.pieces[k]
        rows = pl.ds(pl.multiple_of(block * 48, 16), 48)
        return self.ins[which].at[rows, pl.ds(start, width)]

    def whole(self, k):
        return pltpu.make_async_remote_copy(
            src_ref=self.own[k],
            dst_ref=self.other[k],
            send_sem=self.psem.at[0, k],
            recv_sem=self.psem.at[1, k],
            device_id=(self.sib, self.my),
            device_id_type=MESH,
        )

    def exchange(self, k):
        def cross(i, carry):
            a, b = i // 4, lax.rem(i, 4)
            pltpu.make_async_remote_copy(
                src_ref=self.source(k, (a * self.st2 + b * self.st1) * 2 + 1 - self.c),
                dst_ref=self.other[k].at[a, b],
                send_sem=self.psem.at[0, k],
                recv_sem=self.psem.at[1, k],
                device_id=(self.sib, self.my),
                device_id_type=MESH,
            ).start()
            return carry

        def load(i, carry):
            a, b = i // 4, lax.rem(i, 4)
            pltpu.make_async_copy(
                self.source(k, (a * self.st1 + b * self.st2) * 2 + self.c),
                self.own[k].at[a, b],
                self.lsem.at[k],
            ).start()
            return carry

        lax.fori_loop(0, 16, cross, 0)
        lax.fori_loop(0, 16, load, 0)

    def first(self, k):
        own, other, near = self.own[k], self.other[k], self.near[k]
        pltpu.make_async_copy(own, own, self.lsem.at[k]).wait()
        self.whole(k).wait_recv()

        def add(p):
            def body(b, carry):
                own[p, b] = own[p, b] + other[p, b]
                return carry

            lax.fori_loop(0, 4, body, 0)

        add(self.o1)
        self.send("oR", k, 0, own.at[self.o1, 0:2], near.at[0])
        self.send("oL", k, 0, own.at[self.o1, 2:4], near.at[1])
        add(self.r1)
        self.send("iR", k, 0, own.at[self.r1, 2:4], near.at[3])
        add(self.l1)
        self.send("iL", k, 0, own.at[self.l1, 0:2], near.at[4])
        add(self.p1)

    def first_relay(self, k):
        own, near = self.own[k], self.near[k]

        def add(p, at, slot):
            def body(b, carry):
                own[p, at + b] = own[p, at + b] + near[slot, b]
                return carry

            lax.fori_loop(0, 2, body, 0)

        self.sent["oR", k, 0].wait_recv()
        add(self.r1, 0, 0)
        self.send("dR", k, 0, own.at[self.r1, 0:2], near.at[2])
        self.sent["oL", k, 0].wait_recv()
        add(self.l1, 2, 1)
        self.send("dL", k, 0, own.at[self.l1, 2:4], near.at[5])

    def second(self, k):
        own, near, last = self.own[k], self.near[k], self.last[k]
        for name in ("iR", "dR", "iL", "dL"):
            self.sent[name, k, 0].wait_recv()

        def add(p):
            h, b = p // 2, lax.rem(p, 2)
            own[self.p1, p] = own[self.p1, p] + near[2 + h, b] + near[4 + h, b]

        mine = own.at[self.p1]
        add(self.o2)
        self.send("oR", k, 1, mine.at[self.o2, 0:24], last.at[0])
        self.send("oL", k, 1, mine.at[self.o2, 24:48], last.at[1])
        add(self.r2)
        self.send("iR", k, 1, mine.at[self.r2, 24:48], last.at[3])
        add(self.l2)
        self.send("iL", k, 1, mine.at[self.l2, 0:24], last.at[4])
        add(self.p2)

    def second_relay(self, k):
        own, last = self.own[k], self.last[k]
        self.sent["oR", k, 1].wait_recv()
        own[self.p1, self.r2, 0:24] = own[self.p1, self.r2, 0:24] + last[0]
        self.send("dR", k, 1, own.at[self.p1, self.r2, 0:24], last.at[2])
        self.sent["oL", k, 1].wait_recv()
        own[self.p1, self.l2, 24:48] = own[self.p1, self.l2, 24:48] + last[1]
        self.send("dL", k, 1, own.at[self.p1, self.l2, 24:48], last.at[5])

    def result(self, k, outs):
        own, last = self.own[k], self.last[k]
        which, start, width = self.pieces[k]
        for name in ("iR", "dR", "iL", "dL"):
            self.sent[name, k, 1].wait_recv()
        columns = pl.ds(start, width)
        outs[which][0:24, columns] = own[self.p1, self.p2, 0:24] + last[2] + last[4]
        outs[which][24:48, columns] = own[self.p1, self.p2, 24:48] + last[3] + last[5]

    def finish(self):
        for k in range(len(self.pieces)):
            self.whole(k).wait_send()
            for stage in (0, 1):
                for name in STEPS[:6]:
                    self.sent[name, k, stage].wait_send()


def both_kernel(pieces, count, x_ref, *refs):
    ins, out_ref, outs = refs[:count], refs[count], refs[count + 1 : 2 * count + 1]
    scratch, n = refs[2 * count + 1 :], len(pieces)
    ring = YReduce(x_ref, out_ref, *scratch[:5])
    rest = scratch[5:]
    total = ScatterSum(
        ins, pieces, *(rest[j * n : j * n + n] for j in range(4)), *rest[4 * n :]
    )
    meet(ring.neighbours() + total.neighbours())
    ring.start()
    for k in range(n):
        total.exchange(k)
    early = (n + 1) // 2
    for k in range(n):
        if k == early:
            ring.relay()
        total.first(k)
    for k in range(n):
        total.first_relay(k)
    ring.spread()
    for k in range(n):
        total.second(k)
    for k in range(n):
        total.second_relay(k)
    for k in range(n):
        total.result(k, outs)
    ring.forward()
    ring.finish()
    total.finish()


def reduce_both(partial, grads, step, call_id, limit):
    pieces = []
    for which, g in enumerate(grads):
        for start in range(0, g.shape[1], step):
            pieces.append((which, start, min(step, g.shape[1] - start)))
    n, count = len(pieces), len(grads)
    hbm, vmem = pl.BlockSpec(memory_space=pl.ANY), pl.BlockSpec(memory_space=pltpu.VMEM)
    widths = [w for _, _, w in pieces]
    return pl.pallas_call(
        functools.partial(both_kernel, pieces, count),
        out_shape=[jax.ShapeDtypeStruct(partial.shape, F32)]
        + [jax.ShapeDtypeStruct((48, g.shape[1]), F32) for g in grads],
        in_specs=[vmem] + [hbm] * count,
        out_specs=[vmem] * (count + 1),
        scratch_shapes=y_scratch(*partial.shape)
        + [pltpu.VMEM((4, 4, 48, w), F32) for w in widths] * 2
        + [pltpu.VMEM((6, 2, 48, w), F32) for w in widths]
        + [pltpu.VMEM((6, 24, w), F32) for w in widths]
        + [
            pltpu.SemaphoreType.DMA((2, n)),
            pltpu.SemaphoreType.DMA((n,)),
            pltpu.SemaphoreType.DMA((12 * n,)),
            pltpu.SemaphoreType.DMA((12 * n,)),
        ],
        compiler_params=pltpu.CompilerParams(
            collective_id=call_id, has_side_effects=True, vmem_limit_bytes=limit << 20
        ),
    )(partial, *grads)


def per_device(
    tokens,
    lengths,
    buckets,
    out_cotangent,
    gain_attn,
    w_query,
    w_key,
    w_value,
    w_outgate,
    w_forget,
    b_forget,
    w_out,
    gain_mlp,
    w_gate,
    w_up,
    w_down,
):
    inputs = tokens[0].astype(jnp.float32)
    seq_len, model_width = inputs.shape
    head_count = w_forget.shape[1]
    head_dim = w_query.shape[1] // head_count
    score_scale = head_dim ** (-0.5)
    valid_len = lengths[0]
    positions = jnp.arange(seq_len)
    valid_rows = (positions < valid_len).astype(jnp.float32)[:, None]
    allowed = (positions[None, :] <= positions[:, None]) & (positions[None, :] < valid_len)
    normed_in, norm_back_in = jax.vjp(gain_norm, inputs, gain_attn.astype(jnp.float32))
    in_low = normed_in.astype(jnp.bfloat16)
    query_pre = low_dot(in_low, w_query)
    key_pre = low_dot(in_low, w_key)
    value_pre = low_dot(in_low, w_value)
    outgate_pre = low_dot(in_low, w_outgate)
    forget_pre = low_dot(in_low, w_forget) + b_forget.astype(jnp.float32)
    query_norm, query_back = jax.vjp(norm_rows, query_pre.reshape(seq_len, head_count, head_dim))
    key_norm, key_back = jax.vjp(norm_rows, key_pre.reshape(seq_len, head_count, head_dim))
    query_low = query_norm.astype(jnp.bfloat16)
    key_low = key_norm.astype(jnp.bfloat16)
    value_low = value_pre.astype(jnp.bfloat16).reshape(seq_len, head_count, head_dim)
    log_decay = jnp.cumsum(jax.nn.log_sigmoid(forget_pre), axis=0).T

    def masked_scores():
        base_scores = (
            jnp.einsum("ihd,jhd->hij", query_low, key_low, preferred_element_type=jnp.float32)
            * score_scale
        )
        base_scores = base_scores + log_decay[:, :, None] - log_decay[:, None, :]
        return jnp.where(allowed[None], base_scores, -1e30)

    masked = masked_scores()
    row_top = jnp.max(masked, axis=-1, keepdims=True)
    exponent = jnp.exp(masked - row_top)
    row_total = jnp.sum(exponent, axis=-1, keepdims=True)
    attn_probs = exponent / row_total
    log_total = row_top + jnp.log(row_total)
    attended = jnp.einsum(
        "hij,jhd->ihd",
        attn_probs.astype(jnp.bfloat16),
        value_low,
        preferred_element_type=jnp.float32,
    ).reshape(seq_len, head_count * head_dim)
    gate_sig = jax.nn.sigmoid(outgate_pre)
    gated_low = (attended * gate_sig).astype(jnp.bfloat16)
    branch_attn = y_reduce(low_dot(gated_low, w_out), 0)
    middle = inputs + branch_attn
    normed_mid, norm_back_mid = jax.vjp(gain_norm, middle, gain_mlp.astype(jnp.float32))
    mid_low = normed_mid.astype(jnp.bfloat16)
    gate_pre = low_dot(mid_low, w_gate)
    up_pre = low_dot(mid_low, w_up)
    hidden_f, swiglu_back = jax.vjp(swiglu, gate_pre, up_pre)
    hidden_low = hidden_f.astype(jnp.bfloat16)
    branch_mlp = lax.psum(low_dot(hidden_low, w_down), "mp")
    layer_out = (middle + branch_mlp).astype(jnp.bfloat16)
    bucket_hot = (buckets[0] == jnp.arange(NBUCKET)).astype(jnp.float32)
    square_sums = jnp.stack(
        [
            jnp.sum(valid_rows * inputs * inputs),
            jnp.sum(valid_rows * branch_attn * branch_attn),
            jnp.sum(valid_rows * branch_mlp * branch_mlp),
        ]
    )
    bucket_sums = square_sums[:, None] * bucket_hot[None, :]
    bucket_count = valid_len.astype(jnp.float32) * bucket_hot
    grad_rows = out_cotangent[0].astype(jnp.float32) * valid_rows
    grad_rows_low = grad_rows.astype(jnp.bfloat16)
    grad_w_down = back_dot(grad_rows_low, hidden_low)
    grad_hidden = trans_dot(grad_rows_low, w_down)
    grad_gate_f, grad_up_f = swiglu_back(grad_hidden)
    gate_grad_low = grad_gate_f.astype(jnp.bfloat16)
    up_grad_low = grad_up_f.astype(jnp.bfloat16)
    grad_w_gate = back_dot(mid_low, gate_grad_low)
    grad_w_up = back_dot(mid_low, up_grad_low)
    grad_mid_local = trans_dot(gate_grad_low, w_gate) + trans_dot(up_grad_low, w_up)
    grad_mid_norm, down_share, gate_share, up_share = reduce_both(
        grad_mid_local, [grad_w_down, grad_w_gate, grad_w_up], 512, 1, 48
    )
    grad_middle_part, grad_gain_mlp = norm_back_mid(grad_mid_norm)
    grad_middle = grad_rows + grad_middle_part
    middle_low = grad_middle.astype(jnp.bfloat16)
    grad_w_out = back_dot(middle_low, gated_low)
    grad_gated = trans_dot(middle_low, w_out)
    attended_grad_low = (grad_gated * gate_sig).astype(jnp.bfloat16)
    outgate_grad_low = (grad_gated * attended * gate_sig * (1.0 - gate_sig)).astype(jnp.bfloat16)
    attended_heads = attended_grad_low.reshape(seq_len, head_count, head_dim)
    again_probs = jnp.exp(masked_scores() - log_total)
    grad_probs = jnp.einsum(
        "ihd,jhd->hij", attended_heads, value_low, preferred_element_type=jnp.float32
    )
    row_delta = jnp.sum(again_probs * grad_probs, axis=-1, keepdims=True)
    scores_grad_low = (again_probs * (grad_probs - row_delta)).astype(jnp.bfloat16)
    value_grad_low = (
        jnp.einsum(
            "hij,ihd->jhd",
            again_probs.astype(jnp.bfloat16),
            attended_heads,
            preferred_element_type=jnp.float32,
        )
        .reshape(seq_len, head_count * head_dim)
        .astype(jnp.bfloat16)
    )
    grad_query_norm = (
        jnp.einsum("hij,jhd->ihd", scores_grad_low, key_low, preferred_element_type=jnp.float32)
        * score_scale
    )
    grad_key_norm = (
        jnp.einsum("hij,ihd->jhd", scores_grad_low, query_low, preferred_element_type=jnp.float32)
        * score_scale
    )
    score_grad = scores_grad_low.astype(jnp.float32)
    grad_decay = jnp.sum(score_grad, axis=2) - jnp.sum(score_grad, axis=1)
    grad_log_forget = jnp.flip(jnp.cumsum(jnp.flip(grad_decay, 1), axis=1), 1).T
    forget_grad_low = (grad_log_forget * jax.nn.sigmoid(-forget_pre)).astype(jnp.bfloat16)
    query_grad_low = (
        query_back(grad_query_norm)[0].reshape(seq_len, head_count * head_dim).astype(jnp.bfloat16)
    )
    key_grad_low = (
        key_back(grad_key_norm)[0].reshape(seq_len, head_count * head_dim).astype(jnp.bfloat16)
    )
    grad_w_query = back_dot(in_low, query_grad_low)
    grad_w_key = back_dot(in_low, key_grad_low)
    grad_w_value = back_dot(in_low, value_grad_low)
    grad_w_outgate = back_dot(in_low, outgate_grad_low)
    grad_w_forget = back_dot(in_low, forget_grad_low)
    grad_b_forget = jnp.sum(forget_grad_low.astype(jnp.float32), axis=0)
    grad_in_local = (
        trans_dot(query_grad_low, w_query)
        + trans_dot(key_grad_low, w_key)
        + trans_dot(value_grad_low, w_value)
    )
    grad_in_local = (
        grad_in_local
        + trans_dot(outgate_grad_low, w_outgate)
        + trans_dot(forget_grad_low, w_forget)
    )
    rms_in = norm_rows(inputs)
    gain_local = jnp.sum(grad_in_local * rms_in, axis=0)
    small = jnp.concatenate(
        [
            grad_w_forget,
            grad_gain_mlp[:, None] * (1.0 / Y),
            gain_local[:, None],
            jnp.zeros((model_width, 120), F32),
        ],
        axis=1,
    )
    grad_in_norm, query_share, key_share, value_share, outgate_share, out_share, small_share = (
        reduce_both(
            grad_in_local,
            [grad_w_query, grad_w_key, grad_w_value, grad_w_outgate, grad_w_out, small],
            512,
            2,
            40,
        )
    )
    gains = lax.psum(small_share[:, 6:8], "mp")
    grad_in_part, _ = norm_back_in(grad_in_norm)
    input_grad = grad_middle + grad_in_part
    bucket_total, bucket_rows, bias_sum = in_one((bucket_sums, bucket_count, grad_b_forget), "dp")
    rms = jnp.sqrt(bucket_total / (bucket_rows[None, :] * model_width))
    return (
        layer_out[None],
        input_grad[None],
        gains[:, 1],
        query_share,
        key_share,
        value_share,
        outgate_share,
        small_share[:, :6],
        bias_sum,
        out_share.T,
        gains[:, 0],
        gate_share,
        up_share,
        down_share.T,
        rms,
    )


def solution(mesh):
    placed = (
        P("dp", None, None),
        P("dp"),
        P("dp"),
        P("dp", None, None),
        P(),
        P(None, "mp"),
        P(None, "mp"),
        P(None, "mp"),
        P(None, "mp"),
        P(None, "mp"),
        P("mp"),
        P("mp", None),
        P(),
        P(None, "mp"),
        P(None, "mp"),
        P("mp", None),
    )
    return jax.shard_map(
        per_device,
        mesh=mesh,
        in_specs=placed,
        out_specs=(
            P("dp", None, None),
            P("dp", None, None),
            P("dp"),
            P("dp", "mp"),
            P("dp", "mp"),
            P("dp", "mp"),
            P("dp", "mp"),
            P("dp", "mp"),
            P("mp"),
            P("mp", "dp"),
            P("dp"),
            P("dp", "mp"),
            P("dp", "mp"),
            P("mp", "dp"),
            P(),
        ),
        check_vma=False,
    )
```

```python
import functools

import jax
import jax.numpy as jnp
from jax import lax
from jax.experimental import pallas as pl
from jax.experimental.pallas import tpu as pltpu
from jax.sharding import PartitionSpec as P

NBUCKET = 4


EPSILON = 1e-06


def sent_to_all(array, axis):
    devices = lax.axis_size(axis)
    return lax.all_to_all(
        jnp.broadcast_to(array[None], (devices, *array.shape)), axis, 0, 0, tiled=True
    )


def over_copies(array, axis):
    return sent_to_all(array, axis).sum(axis=0)


def in_one(arrays, axis):
    ends = [0]
    for a in arrays:
        ends.append(ends[-1] + a.size)
    subtotal = over_copies(jnp.concatenate([a.ravel() for a in arrays]), axis)
    return tuple((subtotal[b:e].reshape(a.shape) for a, b, e in zip(arrays, ends, ends[1:])))


def low_dot(left, right):
    return jnp.dot(left, right, preferred_element_type=jnp.float32)


MESH = pl.DeviceIdType.MESH
F32 = jnp.float32
Y = 4
STEPS = ("oR", "oL", "iR", "iL", "dR", "dL", "gRa", "gRb", "gLa", "gLb", "fR", "fL")


def rows_of(ref, start, count):
    return ref.at[pl.ds(pl.multiple_of(start, 8), count)]


class YReduce:
    def __init__(self, in_ref, out_ref, opp, nbr, held, ssem, rsem):
        self.refs = (in_ref, out_ref, opp, nbr, held)
        self.sems = (ssem, rsem)
        self.dp, self.me = lax.axis_index("dp"), lax.axis_index("mp")
        self.right, self.left = lax.rem(self.me + 1, Y), lax.rem(self.me + 3, Y)
        self.far = lax.rem(self.me + 2, Y)
        self.quarter = in_ref.shape[0] // Y
        self.half = self.quarter // 2
        self.sent = {}

    def neighbours(self):
        return [(self.dp, self.right), (self.dp, self.left)]

    def send(self, name, src, dst, to):
        k = STEPS.index(name)
        copy = pltpu.make_async_remote_copy(
            src_ref=src,
            dst_ref=dst,
            send_sem=self.sems[0].at[k],
            recv_sem=self.sems[1].at[k],
            device_id=(self.dp, to),
            device_id_type=MESH,
        )
        copy.start()
        self.sent[name] = copy

    def start(self):
        x, _, opp, nbr, _ = self.refs
        q, h = self.quarter, self.half
        self.send("oR", rows_of(x, self.far * q, h), opp.at[0], self.right)
        self.send("oL", rows_of(x, self.far * q + h, h), opp.at[1], self.left)
        self.send("iR", rows_of(x, self.right * q + h, h), nbr.at[0, h:q], self.right)
        self.send("iL", rows_of(x, self.left * q, h), nbr.at[1, 0:h], self.left)

    def relay(self):
        x, _, opp, nbr, held = self.refs
        q, h = self.quarter, self.half
        self.sent["oR"].wait_recv()
        held[0] = rows_of(x, self.right * q, h)[...] + opp[0]
        self.send("dR", held.at[0], nbr.at[0, 0:h], self.right)
        self.sent["oL"].wait_recv()
        held[1] = rows_of(x, self.left * q + h, h)[...] + opp[1]
        self.send("dL", held.at[1], nbr.at[1, h:q], self.left)

    def spread(self, change=lambda value, part: value):
        x, out, _, nbr, _ = self.refs
        q, h = self.quarter, self.half
        for part, names, tag in ((0, ("dR", "iL"), "a"), (1, ("iR", "dL"), "b")):
            for name in names:
                self.sent[name].wait_recv()
            at = self.me * q + part * h
            own = rows_of(out, at, h)
            own[...] = change(
                rows_of(x, at, h)[...]
                + nbr[0, part * h : part * h + h]
                + nbr[1, part * h : part * h + h],
                part,
            )
            self.send("gR" + tag, own, own, self.right)
            self.send("gL" + tag, own, own, self.left)

    def forward(self):
        _, out, _, _, _ = self.refs
        q, h = self.quarter, self.half
        self.sent["gRa"].wait_recv()
        block = rows_of(out, self.left * q, h)
        self.send("fR", block, block, self.right)
        self.sent["gLb"].wait_recv()
        block = rows_of(out, self.right * q + h, h)
        self.send("fL", block, block, self.left)

    def finish(self):
        for name in ("gRb", "gLa", "fR", "fL"):
            self.sent[name].wait_recv()
        for name in STEPS:
            self.sent[name].wait_send()


def y_scratch(rows, columns):
    quarter = rows // Y
    return [
        pltpu.VMEM((2, quarter // 2, columns), F32),
        pltpu.VMEM((2, quarter, columns), F32),
        pltpu.VMEM((2, quarter // 2, columns), F32),
        pltpu.SemaphoreType.DMA((12,)),
        pltpu.SemaphoreType.DMA((12,)),
    ]


def y_reduce_kernel(in_ref, out_ref, *scratch):
    ring = YReduce(in_ref, out_ref, *scratch)
    meet(ring.neighbours())
    ring.start()
    ring.relay()
    ring.spread()
    ring.forward()
    ring.finish()


def meet(devices):
    barrier = pltpu.get_barrier_semaphore()
    for device in devices:
        pl.semaphore_signal(barrier, inc=1, device_id=device, device_id_type=MESH)
    pl.semaphore_wait(barrier, len(devices))


def y_reduce(array, call_id):
    return pl.pallas_call(
        y_reduce_kernel,
        out_shape=jax.ShapeDtypeStruct(array.shape, F32),
        in_specs=[pl.BlockSpec(memory_space=pltpu.VMEM)],
        out_specs=pl.BlockSpec(memory_space=pltpu.VMEM),
        scratch_shapes=y_scratch(*array.shape),
        compiler_params=pltpu.CompilerParams(
            collective_id=call_id, has_side_effects=True, vmem_limit_bytes=20 << 20
        ),
    )(array)


class ScatterSum:
    def __init__(self, ins, pieces, own, other, near, last, psem, lsem, ssem, rsem):
        self.ins, self.pieces = ins, pieces
        self.own, self.other, self.near, self.last = own, other, near, last
        self.psem, self.lsem, self.ssem, self.rsem = psem, lsem, ssem, rsem
        dp, self.my = lax.axis_index("dp"), lax.axis_index("mp")
        c, z, x = lax.rem(dp, 2), lax.rem(dp // 2, 4), dp // 8
        self.c, self.sib = c, dp + 1 - 2 * c
        self.st1, self.st2 = 4 - 3 * c, 1 + 3 * c
        self.p1, self.p2 = x + c * (z - x), z + c * (x - z)
        step = lambda p, by: lax.rem(p + by, 4)
        self.r1, self.l1, self.o1 = (step(self.p1, by) for by in (1, 3, 2))
        self.r2, self.l2, self.o2 = (step(self.p2, by) for by in (1, 3, 2))
        device = lambda a, b: (a * self.st1 + b * self.st2) * 2 + c
        self.to = (
            (device(self.r1, self.p2), device(self.l1, self.p2)),
            (device(self.p1, self.r2), device(self.p1, self.l2)),
        )
        self.sent = {}

    def neighbours(self):
        return [(n, self.my) for n in (self.sib, *self.to[0], *self.to[1])]

    def send(self, name, k, stage, src, dst):
        at = (k * 2 + stage) * 6 + STEPS.index(name)
        copy = pltpu.make_async_remote_copy(
            src_ref=src,
            dst_ref=dst,
            send_sem=self.ssem.at[at],
            recv_sem=self.rsem.at[at],
            device_id=(self.to[stage][0 if name[1] == "R" else 1], self.my),
            device_id_type=MESH,
        )
        copy.start()
        self.sent[name, k, stage] = copy

    def source(self, k, block):
        which, start, width = self.pieces[k]
        rows = pl.ds(pl.multiple_of(block * 48, 16), 48)
        return self.ins[which].at[rows, pl.ds(start, width)]

    def whole(self, k):
        return pltpu.make_async_remote_copy(
            src_ref=self.own[k],
            dst_ref=self.other[k],
            send_sem=self.psem.at[0, k],
            recv_sem=self.psem.at[1, k],
            device_id=(self.sib, self.my),
            device_id_type=MESH,
        )

    def exchange(self, k):
        def cross(i, carry):
            a, b = i // 4, lax.rem(i, 4)
            pltpu.make_async_remote_copy(
                src_ref=self.source(k, (a * self.st2 + b * self.st1) * 2 + 1 - self.c),
                dst_ref=self.other[k].at[a, b],
                send_sem=self.psem.at[0, k],
                recv_sem=self.psem.at[1, k],
                device_id=(self.sib, self.my),
                device_id_type=MESH,
            ).start()
            return carry

        def load(i, carry):
            a, b = i // 4, lax.rem(i, 4)
            pltpu.make_async_copy(
                self.source(k, (a * self.st1 + b * self.st2) * 2 + self.c),
                self.own[k].at[a, b],
                self.lsem.at[k],
            ).start()
            return carry

        lax.fori_loop(0, 16, cross, 0)
        lax.fori_loop(0, 16, load, 0)

    def first(self, k):
        own, other, near = self.own[k], self.other[k], self.near[k]
        pltpu.make_async_copy(own, own, self.lsem.at[k]).wait()
        self.whole(k).wait_recv()

        def add(p):
            def body(b, carry):
                own[p, b] = own[p, b] + other[p, b]
                return carry

            lax.fori_loop(0, 4, body, 0)

        add(self.o1)
        self.send("oR", k, 0, own.at[self.o1, 0:2], near.at[0])
        self.send("oL", k, 0, own.at[self.o1, 2:4], near.at[1])
        add(self.r1)
        self.send("iR", k, 0, own.at[self.r1, 2:4], near.at[3])
        add(self.l1)
        self.send("iL", k, 0, own.at[self.l1, 0:2], near.at[4])
        add(self.p1)

    def first_relay(self, k):
        own, near = self.own[k], self.near[k]

        def add(p, at, slot):
            def body(b, carry):
                own[p, at + b] = own[p, at + b] + near[slot, b]
                return carry

            lax.fori_loop(0, 2, body, 0)

        self.sent["oR", k, 0].wait_recv()
        add(self.r1, 0, 0)
        self.send("dR", k, 0, own.at[self.r1, 0:2], near.at[2])
        self.sent["oL", k, 0].wait_recv()
        add(self.l1, 2, 1)
        self.send("dL", k, 0, own.at[self.l1, 2:4], near.at[5])

    def second(self, k):
        own, near, last = self.own[k], self.near[k], self.last[k]
        for name in ("iR", "dR", "iL", "dL"):
            self.sent[name, k, 0].wait_recv()

        def add(p):
            h, b = p // 2, lax.rem(p, 2)
            own[self.p1, p] = own[self.p1, p] + near[2 + h, b] + near[4 + h, b]

        mine = own.at[self.p1]
        add(self.o2)
        self.send("oR", k, 1, mine.at[self.o2, 0:24], last.at[0])
        self.send("oL", k, 1, mine.at[self.o2, 24:48], last.at[1])
        add(self.r2)
        self.send("iR", k, 1, mine.at[self.r2, 24:48], last.at[3])
        add(self.l2)
        self.send("iL", k, 1, mine.at[self.l2, 0:24], last.at[4])
        add(self.p2)

    def second_relay(self, k):
        own, last = self.own[k], self.last[k]
        self.sent["oR", k, 1].wait_recv()
        own[self.p1, self.r2, 0:24] = own[self.p1, self.r2, 0:24] + last[0]
        self.send("dR", k, 1, own.at[self.p1, self.r2, 0:24], last.at[2])
        self.sent["oL", k, 1].wait_recv()
        own[self.p1, self.l2, 24:48] = own[self.p1, self.l2, 24:48] + last[1]
        self.send("dL", k, 1, own.at[self.p1, self.l2, 24:48], last.at[5])

    def result(self, k, out):
        own, last = self.own[k], self.last[k]
        width = self.pieces[k][2]
        start = sum(piece[2] for piece in self.pieces[:k])
        for name in ("iR", "dR", "iL", "dL"):
            self.sent[name, k, 1].wait_recv()
        columns = pl.ds(start, width)
        out[0:24, columns] = own[self.p1, self.p2, 0:24] + last[2] + last[4]
        out[24:48, columns] = own[self.p1, self.p2, 24:48] + last[3] + last[5]

    def finish(self):
        for k in range(len(self.pieces)):
            self.whole(k).wait_send()
            for stage in (0, 1):
                for name in STEPS[:6]:
                    self.sent[name, k, stage].wait_send()


class SmallSum:
    def __init__(self, total, ring, bufs, landed, ssem, rsem):
        self.bufs, self.landed, self.ssem, self.rsem = bufs, landed, ssem, rsem
        dp, my = lax.axis_index("dp"), lax.axis_index("mp")
        device = lambda a, b: ((a * total.st1 + b * total.st2) * 2 + total.c, my)
        turn = lambda p, by: lax.rem(p + by, 4)
        self.stages = [
            [(total.sib, my)],
            [device(turn(total.p1, by), total.p2) for by in (1, 2, 3)],
            [device(total.p1, turn(total.p2, by)) for by in (1, 2, 3)],
            [(dp, turn(my, by)) for by in (1, 2, 3)],
        ]
        self.far = [self.stages[1][1], self.stages[2][1], self.stages[3][1]]
        self.sent = []

    def slot(self, stage, j):
        return 3 * stage - 2 + j if stage else 0

    def send(self, stage):
        for j, to in enumerate(self.stages[stage]):
            at = self.slot(stage, j)
            copy = pltpu.make_async_remote_copy(
                src_ref=self.bufs.at[stage],
                dst_ref=self.landed.at[at],
                send_sem=self.ssem.at[at],
                recv_sem=self.rsem.at[at],
                device_id=to,
                device_id_type=MESH,
            )
            copy.start()
            self.sent.append(copy)

    def take(self, stage):
        value = self.bufs[stage]
        for j in range(len(self.stages[stage])):
            at = self.slot(stage, j)
            self.sent[at].wait_recv()
            value = value + self.landed[at]
        self.bufs[stage + 1] = value

    def finish(self):
        for copy in self.sent:
            copy.wait_send()


def both_kernel(pieces, count, small, x_ref, source_ref, base_ref, gain_ref, *refs):
    if small:
        other_ref, refs = refs[0], refs[1:]
    ins, out_ref, share_ref, sums_ref = refs[:count], *refs[count : count + 3]
    scratch, n = refs[count + 3 :], len(pieces)
    source_s, base_s, csem = scratch[:3]
    ring = YReduce(x_ref, out_ref, *scratch[3:8])
    rest = scratch[8:]
    total = ScatterSum(
        ins, pieces, *(rest[j * n : j * n + n] for j in range(4)), *rest[4 * n : 4 * n + 4]
    )
    peers = ring.neighbours() + total.neighbours()
    if small:
        tiny = SmallSum(total, ring, *rest[4 * n + 4 :])
        peers = peers + tiny.far
    meet(peers)
    ring.start()
    loads = []
    for j, (ref, scr) in enumerate(((source_ref, source_s), (base_ref, base_s))):
        copy = pltpu.make_async_copy(rows_of(ref, ring.me * ring.quarter, ring.quarter), scr, csem.at[j])
        copy.start()
        loads.append(copy)
    for k in range(n):
        total.exchange(k)
    early = (n + 1) // 2
    for k in range(n):
        if k == early:
            ring.relay()
        total.first(k)
    for k in range(n):
        total.first_relay(k)
    for copy in loads:
        copy.wait()
    parts = []

    def change(value, part):
        at = slice(part * ring.half, part * ring.half + ring.half)
        source = source_s[at, :].astype(F32)
        r = lax.rsqrt(jnp.mean(source * source, axis=1, keepdims=True) + EPSILON)
        n = source * r
        e = value * gain_ref[...]
        parts.append(jnp.sum(value * n, axis=0, keepdims=True))
        inner = jnp.mean(e * n, axis=1, keepdims=True)
        return base_s[at, :].astype(F32) + r * (e - n * inner)

    ring.spread(change)
    if small:
        tiny.bufs[0, 0:1, :] = parts[0] + parts[1]
        tiny.bufs[0, 1:2, :] = other_ref[...]
        tiny.bufs[0, 2:8, :] = jnp.zeros_like(tiny.bufs[0, 2:8, :])
        tiny.send(0)
    else:
        sums_ref[...] = parts[0] + parts[1]
    for k in range(n):
        total.second(k)
    if small:
        tiny.take(0)
        tiny.send(1)
    for k in range(n):
        total.second_relay(k)
    if small:
        tiny.take(1)
        tiny.send(2)
    for k in range(n):
        total.result(k, share_ref)
    if small:
        tiny.take(2)
        tiny.send(3)
    ring.forward()
    if small:
        tiny.take(3)
        sums_ref[...] = tiny.bufs[4]
        tiny.finish()
    ring.finish()
    total.finish()


def reduce_both(partial, source, base, gain, grads, step, call_id, limit, other=None):
    pieces = []
    for which, g in enumerate(grads):
        for start in range(0, g.shape[1], step):
            pieces.append((which, start, min(step, g.shape[1] - start)))
    n, count = len(pieces), len(grads)
    small = other is not None
    hbm, vmem = pl.BlockSpec(memory_space=pl.ANY), pl.BlockSpec(memory_space=pltpu.VMEM)
    widths = [w for _, _, w in pieces]
    rows, columns = partial.shape
    quarter = (rows // Y, columns)
    sums = (8, columns) if small else (1, columns)
    extra = [
        pltpu.VMEM((5, 8, columns), F32),
        pltpu.VMEM((10, 8, columns), F32),
        pltpu.SemaphoreType.DMA((10,)),
        pltpu.SemaphoreType.DMA((10,)),
    ]
    return pl.pallas_call(
        functools.partial(both_kernel, pieces, count, small),
        out_shape=[
            jax.ShapeDtypeStruct(partial.shape, F32),
            jax.ShapeDtypeStruct((48, sum(widths)), F32),
            jax.ShapeDtypeStruct(sums, F32),
        ],
        in_specs=[vmem, hbm, hbm, vmem] + [vmem] * small + [hbm] * count,
        out_specs=[vmem] * 3,
        scratch_shapes=[
            pltpu.VMEM(quarter, source.dtype),
            pltpu.VMEM(quarter, base.dtype),
            pltpu.SemaphoreType.DMA((2,)),
        ]
        + y_scratch(*partial.shape)
        + [pltpu.VMEM((4, 4, 48, w), F32) for w in widths] * 2
        + [pltpu.VMEM((6, 2, 48, w), F32) for w in widths]
        + [pltpu.VMEM((6, 24, w), F32) for w in widths]
        + [
            pltpu.SemaphoreType.DMA((2, n)),
            pltpu.SemaphoreType.DMA((n,)),
            pltpu.SemaphoreType.DMA((12 * n,)),
            pltpu.SemaphoreType.DMA((12 * n,)),
        ]
        + extra * small,
        compiler_params=pltpu.CompilerParams(
            collective_id=call_id, has_side_effects=True, vmem_limit_bytes=limit << 20
        ),
    )(partial, source, base, gain, *([other] * small), *grads)


HEAD = 64
PAIR = 128
NEG = -1e30


def rows_at(i, size):
    return pl.ds(pl.multiple_of(i * size, size), size)


def lane_is(shape, index):
    return lax.broadcasted_iota(jnp.int32, shape, len(shape) - 1) == index


def first_head(shape):
    return lax.broadcasted_iota(jnp.int32, shape, len(shape) - 1) < HEAD


def halves_mean(values):
    first = first_head(values.shape)
    low = jnp.sum(jnp.where(first, values, 0.0), axis=1, keepdims=True) * (1.0 / HEAD)
    high = jnp.sum(jnp.where(first, 0.0, values), axis=1, keepdims=True) * (1.0 / HEAD)
    return low, high


def one_row(ref, index):
    rows = ref[...]
    picked = lax.broadcasted_iota(jnp.int32, rows.shape, 0) == index
    return jnp.sum(jnp.where(picked, rows, 0.0), axis=0, keepdims=True)


def running_sum(values, backward=False):
    count = values.shape[0]
    row = lax.broadcasted_iota(jnp.int32, values.shape, 0)
    shift = 1
    while shift < count:
        if backward:
            moved = jnp.where(row < count - shift, pltpu.roll(values, count - shift, 0), 0.0)
        else:
            moved = jnp.where(row >= shift, pltpu.roll(values, shift, 0), 0.0)
        values = values + moved
        shift *= 2
    return values


def forward_kernel(
    length_ref, x_ref, gain_ref, wq_ref, wk_ref, wv_ref, wo_ref, wf_ref, bf_ref,
    low_ref, qn_ref, kn_ref, v_ref, sig_ref, att_ref, gated_ref, stat_ref, decay_ref,
    top_s, row_s, q_s, k_s, v_s,
):
    step = pl.program_id(0)
    seq = x_ref.shape[0]
    length = length_ref[0]

    @pl.when(step == 0)
    def _():
        def norm(i, carry):
            at = rows_at(i, 128)
            x = x_ref[at, :].astype(F32)
            r = lax.rsqrt(jnp.mean(x * x, axis=1, keepdims=True) + EPSILON)
            low_ref[at, :] = (x * r * gain_ref[...]).astype(jnp.bfloat16)
            return carry

        lax.fori_loop(0, seq // 128, norm, 0)
        pre = jnp.dot(low_ref[...], wf_ref[...], preferred_element_type=F32) + bf_ref[...]
        fall = jnp.minimum(pre, 0.0) - jnp.log1p(jnp.exp(-jnp.abs(pre)))
        decay = running_sum(fall)
        row = lax.broadcasted_iota(jnp.int32, decay.shape, 0)
        final = jnp.sum(jnp.where(row == length - 1, decay, 0.0), axis=0, keepdims=True)
        decay_ref[0] = decay
        decay_ref[1] = jax.nn.sigmoid(-pre)
        top_s[...] = jnp.where(row < length, decay, final)
        row_s[...] = jnp.where(row < length, decay, -NEG).T[0:8]

    def project(i, carry):
        at = rows_at(i, 256)
        low = low_ref[at, :]
        for w, n_ref, s, col in ((wq_ref, qn_ref, q_s, 0), (wk_ref, kn_ref, k_s, 2)):
            pre = jnp.dot(low, w[...], preferred_element_type=F32)
            a, b = halves_mean(pre * pre)
            a, b = lax.rsqrt(a + EPSILON), lax.rsqrt(b + EPSILON)
            n = pre * jnp.where(first_head(pre.shape), a, b)
            n_ref[at, :] = n
            s[at, :] = n.astype(jnp.bfloat16)
            here = jnp.where(lane_is(pre.shape, col), a, jnp.where(lane_is(pre.shape, col + 1), b, 0.0))
            stat_ref[at, :] = here if col == 0 else stat_ref[at, :] + here
        value = jnp.dot(low, wv_ref[...], preferred_element_type=F32).astype(jnp.bfloat16)
        v_s[at, :] = value
        v_ref[at, :] = value
        sig_ref[at, :] = jax.nn.sigmoid(jnp.dot(low, wo_ref[...], preferred_element_type=F32))
        return carry

    lax.fori_loop(0, seq // 256, project, 0)
    lines = [one_row(row_s, 2 * step + head) for head in (0, 1)]
    first = first_head((128, PAIR))
    zero = jnp.zeros((128, PAIR), jnp.bfloat16)
    upper = lax.broadcasted_iota(jnp.int32, (128, 128), 1) > lax.broadcasted_iota(
        jnp.int32, (128, 128), 0
    )
    for i in range(seq // 128):
        at, n = slice(i * 128, i * 128 + 128), i * 128 + 128
        q = q_s[at, :]
        both = []
        for head in (0, 1):
            own = jnp.where(first, q, zero) if head == 0 else jnp.where(first, zero, q)
            s = lax.dot_general(
                own, k_s[0:n, :], (((1,), (1,)), ((), ())), preferred_element_type=F32
            )
            column = jnp.sum(
                jnp.where(lane_is((128, PAIR), 2 * step + head), top_s[at, :], 0.0), axis=1, keepdims=True
            )
            line = lines[head][:, 0:n]
            s = s * (HEAD ** (-0.5)) + (column - line)
            diagonal = jnp.where(upper, NEG, s[:, n - 128 :])
            s = diagonal if i == 0 else jnp.concatenate([s[:, : n - 128], diagonal], axis=1)
            p = jnp.exp(s)
            p = p * (1.0 / jnp.sum(p, axis=1, keepdims=True))
            both.append(
                jnp.dot(p.astype(jnp.bfloat16), v_s[0:n, :], preferred_element_type=F32)
            )
        out = jnp.where(first, both[0], both[1])
        att_ref[at, :] = out
        gated_ref[at, :] = (out * sig_ref[at, :]).astype(jnp.bfloat16)


def whole(shape):
    return pl.BlockSpec(shape, lambda *_: (0,) * len(shape), pipeline_mode=pl.Buffered(1))


def forward_attention(tokens, length, gain, wq, wk, wv, wo, wf, bf):
    seq, width = tokens.shape
    heads = wq.shape[1]
    weights = pl.BlockSpec((width, PAIR), lambda i, _: (0, i))
    lanes = pl.BlockSpec((seq, PAIR), lambda i, _: (0, i))
    shape = lambda *s, t=F32: jax.ShapeDtypeStruct(s, t)
    low = jnp.bfloat16
    return pl.pallas_call(
        forward_kernel,
        grid_spec=pltpu.PrefetchScalarGridSpec(
            num_scalar_prefetch=1,
            grid=(heads // PAIR,),
            in_specs=[whole((seq, width)), whole((1, width))]
            + [weights] * 4
            + [whole((width, PAIR)), whole((1, PAIR))],
            out_specs=[whole((seq, width))] + [lanes] * 7 + [whole((2, seq, PAIR))],
            scratch_shapes=[
                pltpu.VMEM((seq, PAIR), F32),
                pltpu.VMEM((8, seq), F32),
                pltpu.VMEM((seq, PAIR), low),
                pltpu.VMEM((seq, PAIR), low),
                pltpu.VMEM((seq, PAIR), low),
            ],
        ),
        out_shape=[
            shape(seq, width, t=low), shape(seq, heads), shape(seq, heads), shape(seq, heads, t=low),
            shape(seq, heads), shape(seq, heads), shape(seq, heads, t=low), shape(seq, heads),
            shape(2, seq, PAIR),
        ],
        compiler_params=pltpu.CompilerParams(vmem_limit_bytes=40 << 20),
        cost_estimate=pl.CostEstimate(flops=6 * 10**9, bytes_accessed=20 * 10**6, transcendentals=4 * 10**6),
    )(length, tokens, gain, wq, wk, wv, wo, wf, bf)


def mlp_kernel(
    length_ref, x_ref, branch_ref, cot_ref, gain_ref, wg_ref, wu_ref, wd_ref,
    mid_ref, grad_ref, out_ref, back_ref, gd_ref, gg_ref, gu_ref, sums_ref,
    low_s, low_t, grad_t, hid_s, pair_s,
):
    step = pl.program_id(0)
    seq, width = x_ref.shape
    length = length_ref[0]
    tile = wg_ref.shape[1]

    @pl.when(step == 0)
    def _():
        def norm(i, carry):
            at = rows_at(i, 128)
            x, branch = x_ref[at, :].astype(F32), branch_ref[at, :]
            mid = x + branch
            r = lax.rsqrt(jnp.mean(mid * mid, axis=1, keepdims=True) + EPSILON)
            low = (mid * r * gain_ref[...]).astype(jnp.bfloat16)
            mid_ref[at, :] = mid
            low_s[at, :] = low
            low_t[:, at] = low.T
            valid = lax.broadcasted_iota(jnp.int32, (128, 1), 0) + i * 128 < length
            grad = jnp.where(valid, cot_ref[at, :].astype(F32), 0.0).astype(jnp.bfloat16)
            grad_ref[at, :] = grad
            grad_t[:, at] = grad.T
            kept = jnp.where(valid, 1.0, 0.0)
            a = jnp.sum(kept * (x * x), axis=0, keepdims=True)
            b = jnp.sum(kept * (branch * branch), axis=0, keepdims=True)
            return carry[0] + a, carry[1] + b

        zero = jnp.zeros((1, width), F32)
        a, b = lax.fori_loop(0, seq // 128, norm, (zero, zero))
        sums_ref[0:1, :] = a
        sums_ref[1:2, :] = b

    def hidden(i, carry):
        at = rows_at(i, 256)
        gate = jnp.dot(low_s[at, :], wg_ref[...], preferred_element_type=F32)
        up = jnp.dot(low_s[at, :], wu_ref[...], preferred_element_type=F32)
        grad = lax.dot_general(
            grad_ref[at, :], wd_ref[...], (((1,), (1,)), ((), ())), preferred_element_type=F32
        )
        sig = jax.nn.sigmoid(gate)
        silu = gate * sig
        hid_s[at, :] = (silu * up).astype(jnp.bfloat16)
        pair_s[at, 0:tile] = (grad * up * (sig * (1.0 + gate * (1.0 - sig)))).astype(jnp.bfloat16)
        pair_s[at, tile : 2 * tile] = (grad * silu).astype(jnp.bfloat16)
        return carry

    lax.fori_loop(0, seq // 256, hidden, 0)
    both = jnp.concatenate([wg_ref[...], wu_ref[...]], axis=1)

    def rows(i, carry):
        at = rows_at(i, 256)
        out = jnp.dot(hid_s[at, :], wd_ref[...], preferred_element_type=F32)
        back = lax.dot_general(
            pair_s[at, :], both, (((1,), (1,)), ((), ())), preferred_element_type=F32
        )

        @pl.when(step == 0)
        def _():
            out_ref[at, :] = out
            back_ref[at, :] = back

        @pl.when(step > 0)
        def _():
            out_ref[at, :] = out_ref[at, :] + out
            back_ref[at, :] = back_ref[at, :] + back

        return carry

    lax.fori_loop(0, seq // 256, rows, 0)

    def grads(i, carry):
        at = rows_at(i, 512)
        gd_ref[at, :] = jnp.dot(grad_t[at, :], hid_s[...], preferred_element_type=F32)
        two = jnp.dot(low_t[at, :], pair_s[...], preferred_element_type=F32)
        gg_ref[at, :] = two[:, 0:tile]
        gu_ref[at, :] = two[:, tile:]
        return carry

    lax.fori_loop(0, width // 512, grads, 0)


def mlp(tokens, length, branch, cotangent, gain, wg, wu, wd):
    seq, width = tokens.shape
    units, tile = wg.shape[1], 256
    columns = pl.BlockSpec((width, tile), lambda i, _: (0, i))
    full = whole((seq, width))
    shape = lambda *s, t=F32: jax.ShapeDtypeStruct(s, t)
    low = jnp.bfloat16
    return pl.pallas_call(
        mlp_kernel,
        grid_spec=pltpu.PrefetchScalarGridSpec(
            num_scalar_prefetch=1,
            grid=(units // tile,),
            in_specs=[full, full, full, whole((1, width)), columns, columns]
            + [pl.BlockSpec((tile, width), lambda i, _: (i, 0))],
            out_specs=[full] * 4 + [columns] * 3 + [whole((2, width))],
            scratch_shapes=[
                pltpu.VMEM((seq, width), low),
                pltpu.VMEM((width, seq), low),
                pltpu.VMEM((width, seq), low),
                pltpu.VMEM((seq, tile), low),
                pltpu.VMEM((seq, 2 * tile), low),
            ],
        ),
        out_shape=[
            shape(seq, width), shape(seq, width, t=low), shape(seq, width), shape(seq, width),
            shape(width, units), shape(width, units), shape(width, units), shape(2, width),
        ],
        compiler_params=pltpu.CompilerParams(vmem_limit_bytes=56 << 20),
        cost_estimate=pl.CostEstimate(flops=20 * 10**9, bytes_accessed=60 * 10**6, transcendentals=10**6),
    )(length, tokens, branch, cotangent, gain, wg, wu, wd)


def backward_kernel(
    length_ref, grad_ref, low_ref, qn_ref, kn_ref, v_ref, sig_ref, att_ref, gated_ref, stat_ref,
    decay_ref, wq_ref, wk_ref, wv_ref, wo_ref, wf_ref, wout_ref,
    back_ref, gq_ref, gk_ref, gv_ref, go_ref, gout_ref, gf_ref, bias_ref,
    low_t, grad_s, grad_t, k_s, do_s, line_s, dq_s, dk_s, dv_s, all_s, fall_s,
):
    step = pl.program_id(0)
    seq, width = low_ref.shape
    length = length_ref[0]
    low16 = jnp.bfloat16

    @pl.when(step == 0)
    def _():
        def turn(i, carry):
            at = rows_at(i, 128)
            grad = grad_ref[at, :].astype(low16)
            grad_s[at, :] = grad
            grad_t[:, at] = grad.T
            low_t[:, at] = low_ref[at, :].T
            return carry

        lax.fori_loop(0, seq // 128, turn, 0)
        decay = decay_ref[0]
        row = lax.broadcasted_iota(jnp.int32, decay.shape, 0)
        final = jnp.sum(jnp.where(row == length - 1, decay, 0.0), axis=0, keepdims=True)
        line_s[...] = jnp.where(row < length, decay, final).T[0:8]
        fall_s[...] = jnp.zeros_like(fall_s)

    first = first_head((seq, PAIR))
    gg = lax.dot_general(
        grad_s[...], wout_ref[...], (((1,), (1,)), ((), ())), preferred_element_type=F32
    )
    sig = sig_ref[...]
    do_s[...] = (gg * sig).astype(low16)
    all_s[:, 3 * PAIR : 4 * PAIR] = (gg * att_ref[...] * sig * (1.0 - sig)).astype(low16)
    k_s[...] = kn_ref[...].astype(low16)
    dk_s[...] = jnp.zeros_like(dk_s)
    dv_s[...] = jnp.zeros_like(dv_s)
    row = lax.broadcasted_iota(jnp.int32, (seq, PAIR), 0)
    columns, lines = [], [one_row(line_s, 2 * step + head) for head in (0, 1)]
    for head in (0, 1):
        column = jnp.sum(
            jnp.where(lane_is((seq, PAIR), 2 * step + head), decay_ref[0], 0.0), axis=1, keepdims=True
        )
        columns.append(jnp.where(row[:, 0:1] < length, column, -NEG))
    block = first_head((128, PAIR))
    zero = jnp.zeros((128, PAIR), low16)
    lower = lax.broadcasted_iota(jnp.int32, (128, 128), 0) > lax.broadcasted_iota(
        jnp.int32, (128, 128), 1
    )
    for i in range(seq // 128):
        at, n = slice(i * 128, i * 128 + 128), i * 128 + 128
        q = qn_ref[at, :].astype(low16)
        do = do_s[at, :]
        pieces = []
        for head in (0, 1):
            pick = (lambda t: jnp.where(block, t, zero)) if head == 0 else (lambda t: jnp.where(block, zero, t))
            own_q, own_do = pick(q), pick(do)
            one = jnp.where(lane_is((128, PAIR), 2 * step + head), 1.0, 0.0).astype(low16)
            s = lax.dot_general(
                k_s[0:n, :], own_q, (((1,), (1,)), ((), ())), preferred_element_type=F32
            )
            s = s * (HEAD ** (-0.5)) + (lines[head][:, at] - columns[head][0:n])
            diagonal = jnp.where(lower, NEG, s[n - 128 :, :])
            s = diagonal if i == 0 else jnp.concatenate([s[: n - 128, :], diagonal], axis=0)
            p = jnp.exp(s)
            p = p * (1.0 / jnp.sum(p, axis=0, keepdims=True))
            dp = lax.dot_general(
                v_ref[0:n, :], own_do, (((1,), (1,)), ((), ())), preferred_element_type=F32
            )
            ds = (p * (dp - jnp.sum(p * dp, axis=0, keepdims=True))).astype(low16)
            dv_s[0:n, :] = dv_s[0:n, :] + jnp.dot(
                p.astype(low16), own_do, preferred_element_type=F32
            )
            dk_s[0:n, :] = dk_s[0:n, :] + jnp.dot(
                ds, jnp.concatenate([own_q, one], axis=1), preferred_element_type=F32
            )
            keys = k_s[0:n, :]
            mark = jnp.where(lane_is((n, PAIR), 2 * step + head), 1.0, 0.0).astype(low16)
            pieces.append(
                lax.dot_general(
                    ds, jnp.concatenate([keys, mark], axis=1), (((0,), (0,)), ((), ())),
                    preferred_element_type=F32,
                )
            )
        dq_s[at, :] = jnp.where(block, pieces[0][:, 0:PAIR], pieces[1][:, 0:PAIR])
        fall_s[at, :] = fall_s[at, :] + pieces[0][:, PAIR:] + pieces[1][:, PAIR:]
    fall_s[...] = fall_s[...] - dk_s[:, PAIR:]
    stat = stat_ref[...]
    for e, n_ref, col, to in ((dq_s, qn_ref, 0, 0), (dk_s, kn_ref, 2, PAIR)):
        e = e[:, 0:PAIR] * (HEAD ** (-0.5))
        n = n_ref[...]
        a, b = halves_mean(e * n)
        r = jnp.where(first, stat[:, col : col + 1], stat[:, col + 1 : col + 2])
        all_s[:, to : to + PAIR] = (r * (e - n * jnp.where(first, a, b))).astype(low16)
    all_s[:, 2 * PAIR : 3 * PAIR] = dv_s[...].astype(low16)
    weights = jnp.concatenate([wq_ref[...], wk_ref[...], wv_ref[...], wo_ref[...]], axis=1)

    def rows(i, carry):
        at = rows_at(i, 256)
        back = lax.dot_general(
            all_s[at, :], weights, (((1,), (1,)), ((), ())), preferred_element_type=F32
        )

        @pl.when(step == 0)
        def _():
            back_ref[at, :] = back

        @pl.when(step > 0)
        def _():
            back_ref[at, :] = back_ref[at, :] + back

        return carry

    lax.fori_loop(0, seq // 256, rows, 0)

    def grads(i, carry):
        at = rows_at(i, 512)
        four = jnp.dot(low_t[at, :], all_s[...], preferred_element_type=F32)
        for j, ref in enumerate((gq_ref, gk_ref, gv_ref, go_ref)):
            ref[at, :] = four[:, j * PAIR : j * PAIR + PAIR]
        gout_ref[at, :] = jnp.dot(grad_t[at, :], gated_ref[...], preferred_element_type=F32)
        return carry

    lax.fori_loop(0, width // 512, grads, 0)

    @pl.when(step == pl.num_programs(0) - 1)
    def _():
        back = running_sum(fall_s[...], backward=True) * decay_ref[1]
        back = back.astype(low16)
        bias_ref[...] = jnp.sum(back.astype(F32), axis=0, keepdims=True)
        gf_ref[...] = jnp.dot(low_t[...], back, preferred_element_type=F32)
        back_ref[...] = back_ref[...] + lax.dot_general(
            back, wf_ref[...], (((1,), (1,)), ((), ())), preferred_element_type=F32
        )


def backward_attention(length, grad, low, qn, kn, v, sig, att, gated, stat, decay, wq, wk, wv, wo, wf, wout):
    seq, width = low.shape
    heads = wq.shape[1]
    weights = pl.BlockSpec((width, PAIR), lambda i, _: (0, i))
    lanes = pl.BlockSpec((seq, PAIR), lambda i, _: (0, i))
    full = whole((seq, width))
    shape = lambda *s: jax.ShapeDtypeStruct(s, F32)
    low16 = jnp.bfloat16
    return pl.pallas_call(
        backward_kernel,
        grid_spec=pltpu.PrefetchScalarGridSpec(
            num_scalar_prefetch=1,
            grid=(heads // PAIR,),
            in_specs=[full, full] + [lanes] * 7 + [whole((2, seq, PAIR))] + [weights] * 4
            + [whole((width, PAIR)), pl.BlockSpec((PAIR, width), lambda i, _: (i, 0))],
            out_specs=[full] + [weights] * 5 + [whole((width, PAIR)), whole((1, PAIR))],
            scratch_shapes=[
                pltpu.VMEM((width, seq), low16),
                pltpu.VMEM((seq, width), low16),
                pltpu.VMEM((width, seq), low16),
                pltpu.VMEM((seq, PAIR), low16),
                pltpu.VMEM((seq, PAIR), low16),
                pltpu.VMEM((8, seq), F32),
                pltpu.VMEM((seq, PAIR), F32),
                pltpu.VMEM((seq, 2 * PAIR), F32),
                pltpu.VMEM((seq, PAIR), F32),
                pltpu.VMEM((seq, 4 * PAIR), low16),
                pltpu.VMEM((seq, PAIR), F32),
            ],
        ),
        out_shape=[shape(seq, width)] + [shape(width, heads)] * 5 + [shape(width, PAIR), shape(1, PAIR)],
        compiler_params=pltpu.CompilerParams(vmem_limit_bytes=56 << 20),
        cost_estimate=pl.CostEstimate(flops=14 * 10**9, bytes_accessed=50 * 10**6, transcendentals=4 * 10**6),
    )(length, grad, low, qn, kn, v, sig, att, gated, stat, decay, wq, wk, wv, wo, wf, wout)


def per_device(
    tokens, lengths, buckets, out_cotangent, gain_attn, w_query, w_key, w_value, w_outgate,
    w_forget, b_forget, w_out, gain_mlp, w_gate, w_up, w_down,
):
    x, cotangent = tokens[0], out_cotangent[0]
    model_width = x.shape[1]
    heads = w_forget.shape[1]
    gain_in = gain_attn.astype(F32)[None]
    gain_mid = gain_mlp.astype(F32)[None]
    w_fall = jnp.pad(w_forget, ((0, 0), (0, PAIR - heads)))
    b_fall = jnp.pad(b_forget.astype(F32), (0, PAIR - heads))[None]
    weights = (w_query, w_key, w_value, w_outgate, w_fall)
    low, *saved = forward_attention(x, lengths, gain_in, *weights, b_fall)
    branch_attn = y_reduce(low_dot(saved[5], w_out), 0)
    middle, grad_rows, mlp_local, mid_local, g_down, g_gate, g_up, squares = mlp(
        x, lengths, branch_attn, cotangent, gain_mid, w_gate, w_up, w_down
    )
    grad_middle, mlp_share, mlp_gain = reduce_both(
        mid_local, middle, grad_rows, gain_mid, [g_down, g_gate, g_up], 512, 1, 52
    )
    mlp_local, grad_middle = lax.optimization_barrier((mlp_local, grad_middle))
    branch_mlp = lax.psum(mlp_local, "mp")
    in_local, g_query, g_key, g_value, g_outgate, g_out, g_fall, bias = backward_attention(
        lengths, grad_middle, low, *saved, *weights, w_out
    )
    input_grad, share, gains = reduce_both(
        in_local, x, grad_middle, gain_in,
        [g_query, g_key, g_value, g_outgate, g_out, g_fall], 512, 2, 48, mlp_gain,
    )
    layer_out = (middle + branch_mlp).astype(jnp.bfloat16)
    valid = (jnp.arange(x.shape[0]) < lengths[0]).astype(F32)[:, None]
    bucket_hot = (buckets[0] == jnp.arange(NBUCKET)).astype(F32)
    square_sums = jnp.concatenate(
        [jnp.sum(squares, axis=1), jnp.sum(valid * branch_mlp * branch_mlp)[None]]
    )
    bucket_sums = square_sums[:, None] * bucket_hot[None, :]
    bucket_count = lengths[0].astype(F32) * bucket_hot
    bucket_total, bucket_rows, bias_sum = in_one(
        (bucket_sums, bucket_count, bias[0, :heads]), "dp"
    )
    rms = jnp.sqrt(bucket_total / (bucket_rows[None, :] * model_width))
    rows = model_width // lax.axis_size("dp")
    mine = lax.dynamic_slice_in_dim(gains, lax.axis_index("dp") * rows, rows, axis=1)
    units, inner = w_gate.shape[1], w_query.shape[1]
    part = lambda i: share[:, i * inner : i * inner + inner]
    return (
        layer_out[None],
        input_grad[None],
        mine[0],
        part(0),
        part(1),
        part(2),
        part(3),
        share[:, 5 * inner : 5 * inner + heads],
        bias_sum,
        part(4).T,
        mine[1],
        mlp_share[:, units : 2 * units],
        mlp_share[:, 2 * units :],
        mlp_share[:, :units].T,
        rms,
    )


def solution(mesh):
    placed = (
        P("dp", None, None),
        P("dp"),
        P("dp"),
        P("dp", None, None),
        P(),
        P(None, "mp"),
        P(None, "mp"),
        P(None, "mp"),
        P(None, "mp"),
        P(None, "mp"),
        P("mp"),
        P("mp", None),
        P(),
        P(None, "mp"),
        P(None, "mp"),
        P("mp", None),
    )
    return jax.shard_map(
        per_device,
        mesh=mesh,
        in_specs=placed,
        out_specs=(
            P("dp", None, None),
            P("dp", None, None),
            P("dp"),
            P("dp", "mp"),
            P("dp", "mp"),
            P("dp", "mp"),
            P("dp", "mp"),
            P("dp", "mp"),
            P("mp"),
            P("mp", "dp"),
            P("dp"),
            P("dp", "mp"),
            P("dp", "mp"),
            P("mp", "dp"),
            P(),
        ),
        check_vma=False,
    )
```

```python
import functools

import jax
import jax.numpy as jnp
from jax import lax
from jax.experimental import pallas as pl
from jax.experimental.pallas import tpu as pltpu
from jax.sharding import PartitionSpec as P

NBUCKET = 4


EPSILON = 1e-06


MESH = pl.DeviceIdType.MESH
F32 = jnp.float32
Y = 4
STEP = 512
STEPS = ("oR", "oL", "iR", "iL", "dR", "dL", "gRa", "gRb", "gLa", "gLb", "fR", "fL")


def rows_of(ref, start, count):
    return ref.at[pl.ds(pl.multiple_of(start, 8), count)]


def meet(devices):
    barrier = pltpu.get_barrier_semaphore()
    for device in devices:
        pl.semaphore_signal(barrier, inc=1, device_id=device, device_id_type=MESH)
    pl.semaphore_wait(barrier, len(devices))


def link(src, dst, ssem, rsem, at, device):
    return pltpu.make_async_remote_copy(
        src_ref=src,
        dst_ref=dst,
        send_sem=ssem.at[at],
        recv_sem=rsem.at[at],
        device_id=device,
        device_id_type=MESH,
    )


def push(*args):
    copy = link(*args)
    copy.start()
    return copy


class YRing:
    def __init__(self, rows, ssem, rsem):
        self.sems = (ssem, rsem)
        self.dp, self.me = lax.axis_index("dp"), lax.axis_index("mp")
        self.right, self.left = lax.rem(self.me + 1, Y), lax.rem(self.me + 3, Y)
        self.far = lax.rem(self.me + 2, Y)
        self.quarter, self.half = rows // Y, rows // Y // 2
        self.sent = {}

    def neighbours(self):
        return [(self.dp, self.right), (self.dp, self.left)]

    def send(self, name, src, dst, to):
        self.sent[name] = push(src, dst, *self.sems, STEPS.index(name), (self.dp, to))

    def start(self, x, opp, nbr):
        q, h = self.quarter, self.half
        self.send("oR", rows_of(x, self.far * q, h), opp.at[0], self.right)
        self.send("oL", rows_of(x, self.far * q + h, h), opp.at[1], self.left)
        self.send("iR", rows_of(x, self.right * q + h, h), nbr.at[0, h:q], self.right)
        self.send("iL", rows_of(x, self.left * q, h), nbr.at[1, 0:h], self.left)

    def relay(self, x, opp, nbr, held):
        q, h = self.quarter, self.half
        self.sent["oR"].wait_recv()
        held[0] = rows_of(x, self.right * q, h)[...] + opp[0]
        self.send("dR", held.at[0], nbr.at[0, 0:h], self.right)
        self.sent["oL"].wait_recv()
        held[1] = rows_of(x, self.left * q + h, h)[...] + opp[1]
        self.send("dL", held.at[1], nbr.at[1, h:q], self.left)

    def collect(self, x, nbr, part):
        h = self.half
        for name in (("dR", "iL"), ("iR", "dL"))[part]:
            self.sent[name].wait_recv()
        at = slice(part * h, part * h + h)
        return rows_of(x, self.me * self.quarter + part * h, h)[...] + nbr[0, at] + nbr[1, at]

    def spread(self, part, block):
        own, tag = block(self.me, part), "ab"[part]
        self.send("gR" + tag, own, own, self.right)
        self.send("gL" + tag, own, own, self.left)

    def forward(self, block):
        self.sent["gRa"].wait_recv()
        self.send("fR", block(self.left, 0), block(self.left, 0), self.right)
        self.sent["gLb"].wait_recv()
        self.send("fL", block(self.right, 1), block(self.right, 1), self.left)

    def arrive(self):
        for name in ("gRb", "gLa", "fR", "fL"):
            self.sent[name].wait_recv()

    def finish(self):
        for copy in self.sent.values():
            copy.wait_send()


def ring_scratch(quarter, columns):
    return [
        pltpu.VMEM((2, quarter // 2, columns), F32),
        pltpu.VMEM((2, quarter, columns), F32),
        pltpu.VMEM((2, quarter // 2, columns), F32),
    ]


def sems(*counts):
    return [pltpu.SemaphoreType.DMA((n,)) for n in counts for _ in (0, 1)]


class Place:
    def __init__(self):
        self.dp, self.my = lax.axis_index("dp"), lax.axis_index("mp")
        c, z, x = lax.rem(self.dp, 2), lax.rem(self.dp // 2, 4), self.dp // 8
        self.c, self.sib, self.chip = c, self.dp + 1 - 2 * c, x * 4 + z
        self.st1, self.st2 = 4 - 3 * c, 1 + 3 * c
        self.p1, self.p2 = x + c * (z - x), z + c * (x - z)
        step = lambda p, by: lax.rem(p + by, 4)
        self.r1, self.l1, self.o1 = (step(self.p1, by) for by in (1, 3, 2))
        self.r2, self.l2, self.o2 = (step(self.p2, by) for by in (1, 3, 2))

    def device(self, a, b):
        return ((a * self.st1 + b * self.st2) * 2 + self.c, self.my)

    def peers(self):
        return [
            (self.sib, self.my),
            self.device(self.r1, self.p2),
            self.device(self.l1, self.p2),
            self.device(self.p1, self.r2),
            self.device(self.p1, self.l2),
        ]


class ScatterSum:
    def __init__(self, here, sources, own, other, near, last, asem, bsem, lsem, ssem, rsem):
        self.here, self.sources = here, sources
        self.own, self.other, self.near, self.last = own, other, near, last
        self.asem, self.bsem, self.lsem, self.ssem, self.rsem = asem, bsem, lsem, ssem, rsem
        self.n = own.shape[0]
        self.sibling, *to = here.peers()
        self.to = (to[0:2], to[2:4])

    def message(self, name, k, stage):
        at = (k * 2 + stage) * 6 + STEPS.index(name)
        device = self.to[stage][0 if name[1] == "R" else 1]
        here, own = self.here, self.own.at[k]
        if stage:
            own, into, cut = own.at[here.p1], self.last.at[k], (slice(0, 24), slice(24, 48))
            far, right, left = here.o2, here.r2, here.l2
        else:
            into, cut = self.near.at[k], (slice(0, 2), slice(2, 4))
            far, right, left = here.o1, here.r1, here.l1
        row, part, slot = {
            "oR": (far, 0, 0),
            "oL": (far, 1, 1),
            "iR": (right, 1, 3),
            "iL": (left, 0, 4),
            "dR": (right, 0, 2),
            "dL": (left, 1, 5),
        }[name]
        return link(own.at[row, cut[part]], into.at[slot], self.ssem, self.rsem, at, device)

    def whole(self, k):
        own, other = self.own.at[k], self.other.at[k]
        return link(own, other, self.asem, self.bsem, k, self.sibling)

    def exchange(self, k):
        here = self.here
        ref, start, width = self.sources[k]

        def source(block):
            return ref.at[pl.ds(pl.multiple_of(block * 48, 16), 48), pl.ds(start, width)]

        def cross(i, carry):
            a, b = i // 4, lax.rem(i, 4)
            block = source((a * here.st2 + b * here.st1) * 2 + 1 - here.c)
            push(block, self.other.at[k, a, b], self.asem, self.bsem, k, self.sibling)
            return carry

        def fetch(i, carry):
            a, b = i // 4, lax.rem(i, 4)
            block = source((a * here.st1 + b * here.st2) * 2 + here.c)
            pltpu.make_async_copy(block, self.own.at[k, a, b], self.lsem.at[k]).start()
            return carry

        lax.fori_loop(0, 16, cross, 0)
        lax.fori_loop(0, 16, fetch, 0)

    def first(self, k):
        here, own, other = self.here, self.own, self.other
        pltpu.make_async_copy(own.at[k], own.at[k], self.lsem.at[k]).wait()
        self.whole(k).wait_recv()

        def add(p):
            def body(b, carry):
                own[k, p, b] = own[k, p, b] + other[k, p, b]
                return carry

            lax.fori_loop(0, 4, body, 0)

        add(here.o1)
        self.message("oR", k, 0).start()
        self.message("oL", k, 0).start()
        add(here.r1)
        self.message("iR", k, 0).start()
        add(here.l1)
        self.message("iL", k, 0).start()
        add(here.p1)

    def first_relay(self, k):
        here, own, near = self.here, self.own, self.near

        def add(p, at, slot):
            def body(b, carry):
                own[k, p, at + b] = own[k, p, at + b] + near[k, slot, b]
                return carry

            lax.fori_loop(0, 2, body, 0)

        self.message("oR", k, 0).wait_recv()
        add(here.r1, 0, 0)
        self.message("dR", k, 0).start()
        self.message("oL", k, 0).wait_recv()
        add(here.l1, 2, 1)
        self.message("dL", k, 0).start()

    def second(self, k):
        here, own, near = self.here, self.own, self.near
        for name in ("iR", "dR", "iL", "dL"):
            self.message(name, k, 0).wait_recv()

        def add(p):
            h, b = p // 2, lax.rem(p, 2)
            own[k, here.p1, p] = own[k, here.p1, p] + near[k, 2 + h, b] + near[k, 4 + h, b]

        add(here.o2)
        self.message("oR", k, 1).start()
        self.message("oL", k, 1).start()
        add(here.r2)
        self.message("iR", k, 1).start()
        add(here.l2)
        self.message("iL", k, 1).start()
        add(here.p2)

    def second_relay(self, k):
        here, own, last = self.here, self.own, self.last
        self.message("oR", k, 1).wait_recv()
        own[k, here.p1, here.r2, 0:24] = own[k, here.p1, here.r2, 0:24] + last[k, 0]
        self.message("dR", k, 1).start()
        self.message("oL", k, 1).wait_recv()
        own[k, here.p1, here.l2, 24:48] = own[k, here.p1, here.l2, 24:48] + last[k, 1]
        self.message("dL", k, 1).start()

    def result(self, k, out, at):
        here, own, last = self.here, self.own, self.last
        width = own.shape[4]
        for name in ("iR", "dR", "iL", "dL"):
            self.message(name, k, 1).wait_recv()
        columns = pl.ds(pl.multiple_of(at * width, 128), width)
        out[0:24, columns] = own[k, here.p1, here.p2, 0:24] + last[k, 2] + last[k, 4]
        out[24:48, columns] = own[k, here.p1, here.p2, 24:48] + last[k, 3] + last[k, 5]

    def sent(self, k):
        self.whole(k).wait_send()
        for stage in (0, 1):
            for name in STEPS[:6]:
                self.message(name, k, stage).wait_send()


def each(low, high, step):
    def body(k, carry):
        step(k)
        return carry

    lax.fori_loop(low, high, body, 0)


class SmallSum:
    def __init__(self, here, bufs, landed, ssem, rsem):
        self.bufs, self.landed, self.ssem, self.rsem = bufs, landed, ssem, rsem
        turn = lambda p, by: lax.rem(p + by, 4)
        self.stages = [
            [(here.sib, here.my)],
            [here.device(turn(here.p1, by), here.p2) for by in (1, 2, 3)],
            [here.device(here.p1, turn(here.p2, by)) for by in (1, 2, 3)],
            [(here.dp, turn(here.my, by)) for by in (1, 2, 3)],
        ]
        self.far = [self.stages[1][1], self.stages[2][1], self.stages[3][1]]
        self.sent = []

    def send(self, stage):
        for to in self.stages[stage]:
            at = len(self.sent)
            copy = push(self.bufs.at[stage], self.landed.at[at], self.ssem, self.rsem, at, to)
            self.sent.append(copy)

    def take(self, stage):
        value, count = self.bufs[stage], len(self.stages[stage])
        for at in range(len(self.sent) - count, len(self.sent)):
            self.sent[at].wait_recv()
            value = value + self.landed[at]
        self.bufs[stage + 1] = value

    def finish(self):
        for copy in self.sent:
            copy.wait_send()


def scatter_scratch(n, w):
    return [
        pltpu.VMEM((n, 4, 4, 48, w), F32),
        pltpu.VMEM((n, 4, 4, 48, w), F32),
        pltpu.VMEM((n, 6, 2, 48, w), F32),
        pltpu.VMEM((n, 6, 24, w), F32),
        pltpu.SemaphoreType.DMA((n,)),
        pltpu.SemaphoreType.DMA((n,)),
        pltpu.SemaphoreType.DMA((n,)),
        pltpu.SemaphoreType.DMA((12 * n,)),
        pltpu.SemaphoreType.DMA((12 * n,)),
    ]


def scatter_sources(refs, step):
    return [(ref, start, step) for ref in refs for start in range(0, ref.shape[1], step)]


def norm_back(value, source, base, gain):
    source = source.astype(F32)
    r = lax.rsqrt(jnp.mean(source * source, axis=1, keepdims=True) + EPSILON)
    n = source * r
    e = value * gain.astype(F32)
    inner = jnp.mean(e * n, axis=1, keepdims=True)
    return base.astype(F32) + r * (e - n * inner), jnp.sum(value * n, axis=0, keepdims=True)


def load(ref, scratch, sem):
    copy = pltpu.make_async_copy(ref, scratch, sem)
    copy.start()
    return copy


def middle_kernel(count, x_ref, source_ref, base_ref, gain_ref, w_ref, *refs):
    ins, refs = refs[:count], refs[count:]
    grad_ref, gg_ref, share_ref, sums_ref = refs[:4]
    source_s, base_s, w_s, opp, nbr, held, blocks, csem, *sem = refs[4:16]
    here, ring = Place(), YRing(x_ref.shape[0], *sem[0:2])
    total = ScatterSum(here, scatter_sources(ins, STEP), *refs[16:])
    n = total.n
    far = (ring.dp, ring.far)
    meet(ring.neighbours() + [far] + here.peers())
    ring.start(x_ref, opp, nbr)
    q, h = ring.quarter, ring.half
    loads = [
        load(rows_of(source_ref, ring.me * q, q), source_s, csem.at[0]),
        load(rows_of(base_ref, ring.me * q, q), base_s, csem.at[1]),
        load(w_ref, w_s, csem.at[2]),
    ]
    for k in range(n):
        total.exchange(k)
    each(0, n // 2, total.first)
    ring.relay(x_ref, opp, nbr, held)
    each(n // 2, n, total.first)
    each(0, n - 2, total.first_relay)
    for copy in loads:
        copy.wait()
    sums = 0.0
    for part in (0, 1):
        at = slice(part * h, part * h + h)
        value, more = norm_back(
            ring.collect(x_ref, nbr, part), source_s[at, :], base_s[at, :], gain_ref[...]
        )
        grad_ref[at, :] = value
        sums = sums + more
    sums_ref[...] = sums
    low = grad_ref[...].astype(jnp.bfloat16)
    inner = gg_ref.shape[1]
    swaps = []
    for j, by in enumerate((2, 1, 3, 0)):
        to = lax.rem(ring.me + by, Y)
        block = lax.dot_general(
            low, rows_of(w_s, to * inner, inner)[...], (((1,), (1,)), ((), ())),
            preferred_element_type=F32,
        )
        place = rows_of(gg_ref, ring.me * q, q)
        if by:
            blocks[j] = block
            swaps.append(push(blocks.at[j], place, *sem[2:4], j, (ring.dp, to)))
        else:
            place[...] = block
    each(n - 2, n, total.first_relay)
    each(0, n, total.second)
    each(0, n, total.second_relay)
    each(0, n, lambda k: total.result(k, share_ref, k))
    for copy in swaps:
        copy.wait_recv()
    for copy in swaps:
        copy.wait_send()
    ring.finish()
    each(0, n, total.sent)


def reduce_middle(partial, source, base, gain, w_full, grads, call_id):
    n = sum(g.shape[1] for g in grads) // STEP
    hbm, vmem = pl.BlockSpec(memory_space=pl.ANY), pl.BlockSpec(memory_space=pltpu.VMEM)
    rows, columns = partial.shape
    quarter, inner = rows // Y, w_full.shape[0] // Y
    return pl.pallas_call(
        functools.partial(middle_kernel, len(grads)),
        out_shape=[
            jax.ShapeDtypeStruct((quarter, columns), F32),
            jax.ShapeDtypeStruct((rows, inner), F32),
            jax.ShapeDtypeStruct((48, n * STEP), F32),
            jax.ShapeDtypeStruct((1, columns), F32),
        ],
        in_specs=[vmem, hbm, hbm, vmem, hbm] + [hbm] * len(grads),
        out_specs=[vmem] * 4,
        scratch_shapes=[
            pltpu.VMEM((quarter, columns), source.dtype),
            pltpu.VMEM((quarter, columns), base.dtype),
            pltpu.VMEM(w_full.shape, w_full.dtype),
        ]
        + ring_scratch(quarter, columns)
        + [pltpu.VMEM((3, quarter, inner), F32), pltpu.SemaphoreType.DMA((3,))]
        + sems(12, 3)
        + scatter_scratch(n, STEP),
        compiler_params=pltpu.CompilerParams(
            collective_id=call_id, has_side_effects=True, vmem_limit_bytes=56 << 20
        ),
    )(partial, source, base, gain, w_full, *grads)


def input_kernel(count, x_ref, source_ref, base_ref, gain_ref, other_ref, fall_ref, misc_ref, bias_ref, *refs):
    ins, refs = refs[:count], refs[count:]
    out_ref, out_share_ref, share_ref, sums_ref = refs[:4]
    source_s, opp, nbr, held, wide_s, landed, csem, *sem = refs[4:15]
    bufs, arrived, asem, bsem = refs[15:19]
    here, ring = Place(), YRing(x_ref.shape[0], *sem[0:2])
    total = ScatterSum(here, scatter_sources(ins, STEP), *refs[19:])
    tiny = SmallSum(here, bufs, arrived, asem, bsem)
    n, first = total.n, ins[0].shape[1] // STEP
    meet(ring.neighbours() + here.peers() + tiny.far)
    ring.start(x_ref, opp, nbr)
    q, h = ring.quarter, ring.half
    copy = load(rows_of(source_ref, ring.me * q, q), source_s, csem.at[0])
    for k in range(n):
        total.exchange(k)
    each(0, n // 2, total.first)
    ring.relay(x_ref, opp, nbr, held)
    each(n // 2, n, total.first)
    each(0, n - 2, total.first_relay)
    copy.wait()
    block = lambda owner, part: rows_of(out_ref, owner * q + part * h, h)
    sums = 0.0
    for part in (0, 1):
        at = slice(part * h, part * h + h)
        value, more = norm_back(
            ring.collect(x_ref, nbr, part), source_s[at, :], base_ref[at, :], gain_ref[...]
        )
        block(ring.me, part)[...] = value
        ring.spread(part, block)
        sums = sums + more
    bufs[0, 0:1, :] = sums
    bufs[0, 1:2, :] = other_ref[...]
    bufs[0, 8:16, :] = jnp.zeros_like(bufs[0, 8:16, :])
    bufs[0, 2:3, :] = jnp.zeros((1, sums_ref.shape[1]), F32)
    bufs[0, 2:3, 0:PAIR] = misc_ref[1:2, :]
    bufs[0, 3:9, :] = fall_ref[0:6, :]
    bufs[0, 9:10, 0:PAIR] = misc_ref[0:1, :]
    bufs[0, 10:11, 0:PAIR] = bias_ref[...]
    tiny.send(0)
    each(n - 2, n, total.first_relay)
    each(0, n, total.second)
    tiny.take(0)
    tiny.send(1)
    each(0, n, total.second_relay)
    tiny.take(1)
    tiny.send(2)
    each(0, first, lambda k: total.result(k, wide_s, k))
    inner = landed.shape[2]
    swaps = []
    for j, by in enumerate((2, 1, 3)):
        to = lax.rem(ring.me + by, Y)
        columns = pl.ds(pl.multiple_of(to * inner, 128), inner)
        swaps.append(push(wide_s.at[:, columns], landed.at[j], *sem[2:4], j, (ring.dp, to)))
    each(first, n, lambda k: total.result(k, share_ref, k - first))
    ring.forward(block)
    tiny.take(2)
    tiny.send(3)
    own = wide_s[:, pl.ds(pl.multiple_of(ring.me * inner, 128), inner)]
    for j, copy in enumerate(swaps):
        copy.wait_recv()
        own = own + landed[j]
    out_share_ref[...] = own
    tiny.take(3)
    rows = lax.broadcasted_iota(jnp.int32, sums_ref.shape, 0)
    sums_ref[...] = jnp.where(rows < 3, bufs[4], bufs[3])
    ring.arrive()
    for copy in swaps:
        copy.wait_send()
    tiny.finish()
    ring.finish()
    each(0, n, total.sent)


def reduce_input(partial, source, base, gain, small, grads, call_id):
    n = sum(g.shape[1] for g in grads) // STEP
    hbm, vmem = pl.BlockSpec(memory_space=pl.ANY), pl.BlockSpec(memory_space=pltpu.VMEM)
    rows, columns = partial.shape
    quarter, inner = rows // Y, grads[0].shape[1] // Y
    wide = grads[0].shape[1]
    shares = sum(g.shape[1] for g in grads[1:])
    return pl.pallas_call(
        functools.partial(input_kernel, len(grads)),
        out_shape=[
            jax.ShapeDtypeStruct(partial.shape, F32),
            jax.ShapeDtypeStruct((48, inner), F32),
            jax.ShapeDtypeStruct((48, shares), F32),
            jax.ShapeDtypeStruct((16, columns), F32),
        ],
        in_specs=[vmem, hbm, vmem, vmem] + [vmem] * 4 + [hbm] * len(grads),
        out_specs=[vmem] * 4,
        scratch_shapes=[pltpu.VMEM((quarter, columns), source.dtype)]
        + ring_scratch(quarter, columns)
        + [
            pltpu.VMEM((48, wide), F32),
            pltpu.VMEM((3, 48, inner), F32),
            pltpu.SemaphoreType.DMA((1,)),
        ]
        + sems(12, 3)
        + [pltpu.VMEM((5, 16, columns), F32), pltpu.VMEM((10, 16, columns), F32)]
        + sems(10)
        + scatter_scratch(n, STEP),
        compiler_params=pltpu.CompilerParams(
            collective_id=call_id, has_side_effects=True, vmem_limit_bytes=56 << 20
        ),
    )(partial, source, base, gain, *small, *grads)


HEAD = 64
PAIR = 128
NEG = -1e30


def rows_at(i, size):
    return pl.ds(pl.multiple_of(i * size, size), size)


def lane_is(shape, index):
    return lax.broadcasted_iota(jnp.int32, shape, len(shape) - 1) == index


def first_head(shape):
    return lax.broadcasted_iota(jnp.int32, shape, len(shape) - 1) < HEAD


def halves_mean(values):
    first = first_head(values.shape)
    low = jnp.sum(jnp.where(first, values, 0.0), axis=1, keepdims=True) * (1.0 / HEAD)
    high = jnp.sum(jnp.where(first, 0.0, values), axis=1, keepdims=True) * (1.0 / HEAD)
    return low, high


def one_row(ref, index):
    rows = ref[...]
    picked = lax.broadcasted_iota(jnp.int32, rows.shape, 0) == index
    return jnp.sum(jnp.where(picked, rows, 0.0), axis=0, keepdims=True)


def running_sum(values, backward=False):
    count = values.shape[0]
    row = lax.broadcasted_iota(jnp.int32, values.shape, 0)
    shift = 1
    while shift < count:
        if backward:
            moved = jnp.where(row < count - shift, pltpu.roll(values, count - shift, 0), 0.0)
        else:
            moved = jnp.where(row >= shift, pltpu.roll(values, shift, 0), 0.0)
        values = values + moved
        shift *= 2
    return values


def mm(left, right):
    return jnp.dot(left, right, preferred_element_type=F32)


def mm_t(left, right):
    return lax.dot_general(left, right, (((1,), (1,)), ((), ())), preferred_element_type=F32)


def t_mm(left, right):
    return lax.dot_general(left, right, (((0,), (0,)), ((), ())), preferred_element_type=F32)


def whole(shape):
    return pl.BlockSpec(shape, lambda *_: (0,) * len(shape), pipeline_mode=pl.Buffered(1))


def struct(*shape, t=F32):
    return jax.ShapeDtypeStruct(shape, t)


def local_call(kernel, grid, in_specs, out_specs, out_shape, scratch, limit, flops, moved, call_id=None):
    return pl.pallas_call(
        kernel,
        grid_spec=pltpu.PrefetchScalarGridSpec(
            num_scalar_prefetch=1,
            grid=(grid,),
            in_specs=in_specs,
            out_specs=out_specs,
            scratch_shapes=scratch,
        ),
        out_shape=out_shape,
        compiler_params=pltpu.CompilerParams(
            vmem_limit_bytes=limit << 20,
            collective_id=call_id,
            has_side_effects=call_id is not None,
        ),
        cost_estimate=pl.CostEstimate(
            flops=flops * 10**9, bytes_accessed=moved * 10**6, transcendentals=4 * 10**6
        ),
    )


def forward_kernel(
    length_ref, x_ref, gain_ref, wq_ref, wk_ref, wv_ref, wo_ref, wf_ref, bf_ref, w_ref,
    low_ref, qn_ref, kn_ref, v_ref, sig_ref, att_ref, stat_ref, decay_ref, gated_ref, full_ref,
    top_s, row_s, q_s, k_s, w_s, pre_s, gs, ws, wf_s, bf_s, *sem,
):
    step = pl.program_id(0)
    seq = x_ref.shape[0]
    length = length_ref[0]
    here = Place()
    me, right, left, far = (lax.rem(here.my + by, Y) for by in (0, 1, 3, 2))
    sibling, right1, left1, right2, left2 = here.peers()
    c, p1, p2, half = here.c, here.p1, here.p2, seq // 2
    mine = ws.at[c, p2, p1, me]
    cross_order = (p2, here.l2, here.r2, here.o2)

    def plane(j):
        return link(mine, mine, *sem[2:4], j, (here.dp, (right, far, left)[j]))

    def torus(stage, j):
        if stage == 0:
            at, spots, to = (lambda p: ws.at[c, p2, p]), (p1, here.l1, here.r1), (right1, left1)
        else:
            at, spots, to = (lambda p: ws.at[c, p]), (p2, here.l2, here.r2), (right2, left2)
        spot, part, side = ((0, 0, 0), (0, 1, 0), (0, 0, 1), (0, 1, 1), (1, 0, 0), (2, 1, 1))[j]
        piece = at(spots[spot]).at[2 * part : 2 * part + 2]
        return link(piece, piece, *sem[4 + 2 * stage : 6 + 2 * stage], j, to[side])

    def cross(j):
        piece = ws.at[c, cross_order[j]]
        return link(piece, piece, *sem[8:10], j, sibling)

    def gate(pair, j):
        owner, part, to = (
            (me, 0, right), (me, 1, right), (me, 0, left), (me, 1, left), (left, 0, right), (right, 1, left)
        )[j]
        piece = gs.at[pair, owner, part * half : part * half + half]
        return link(piece, piece, *sem[0:2], pair * 6 + j, (here.dp, to))

    def pass_on(make):
        make(0).wait_recv()
        make(4).start()
        make(3).wait_recv()
        make(5).start()

    def arrived(make):
        for j in (1, 2, 4, 5):
            make(j).wait_recv()

    @pl.when(step == 0)
    def _():
        tall, wide = ws.shape[4], ws.shape[5]
        two = w_ref[
            pl.ds(pl.multiple_of(here.chip // 2 * (2 * tall), 16), 2 * tall),
            pl.ds(pl.multiple_of(c * wide, 128), wide),
        ].astype(F32)
        mine[...] = jnp.where(lax.rem(here.chip, 2) == 0, two[0:tall], two[tall:])
        meet([(here.dp, right), (here.dp, left), (here.dp, far)] + here.peers())
        for j in range(3):
            plane(j).start()

    @pl.when(step == 0)
    def _():
        def norm(i, carry):
            at = rows_at(i, 128)
            x = x_ref[at, :].astype(F32)
            r = lax.rsqrt(jnp.mean(x * x, axis=1, keepdims=True) + EPSILON)
            low_ref[at, :] = (x * r * gain_ref[...].astype(F32)).astype(jnp.bfloat16)
            return carry

        lax.fori_loop(0, seq // 128, norm, 0)
        heads = wf_ref.shape[1]
        wf_s[...] = jnp.zeros_like(wf_s)
        wf_s[:, 0:heads] = wf_ref[...]
        bf_s[...] = jnp.zeros_like(bf_s)
        bf_s[0:1, 0:heads] = bf_ref[...].astype(F32)
        pre = mm(low_ref[...], wf_s[...]) + bf_s[0:1, :]
        fall = jnp.minimum(pre, 0.0) - jnp.log1p(jnp.exp(-jnp.abs(pre)))
        decay = running_sum(fall)
        row = lax.broadcasted_iota(jnp.int32, decay.shape, 0)
        final = jnp.sum(jnp.where(row == length - 1, decay, 0.0), axis=0, keepdims=True)
        decay_ref[0] = decay
        decay_ref[1] = jax.nn.sigmoid(-pre)
        top_s[...] = jnp.where(row < length, decay, final)
        row_s[...] = jnp.where(row < length, decay, -NEG).T[0:8]

    for j, ref in enumerate((wq_ref, wk_ref, wv_ref, wo_ref)):
        w_s[:, j * PAIR : j * PAIR + PAIR] = ref[...]
    pre_s[...] = mm(low_ref[...], w_s[...])

    def norms(i, carry):
        at = rows_at(i, 128)
        for j, n_ref, s, col in ((0, qn_ref, q_s, 0), (1, kn_ref, k_s, 2)):
            pre = pre_s[at, j * PAIR : j * PAIR + PAIR]
            a, b = halves_mean(pre * pre)
            a, b = lax.rsqrt(a + EPSILON), lax.rsqrt(b + EPSILON)
            n = pre * jnp.where(first_head(pre.shape), a, b)
            n_ref[at, :] = n
            s[at, :] = n.astype(jnp.bfloat16)
            here = jnp.where(lane_is(pre.shape, col), a, jnp.where(lane_is(pre.shape, col + 1), b, 0.0))
            stat_ref[at, :] = here if col == 0 else stat_ref[at, :] + here
        v_ref[at, :] = pre_s[at, 2 * PAIR : 3 * PAIR].astype(jnp.bfloat16)
        sig_ref[at, :] = jax.nn.sigmoid(pre_s[at, 3 * PAIR : 4 * PAIR])
        return carry

    lax.fori_loop(0, seq // 128, norms, 0)

    @pl.when(step == 0)
    def _():
        for j in range(3):
            plane(j).wait_recv()
        for j in range(4):
            torus(0, j).start()

    @pl.when(step == 1)
    def _():
        arrived(lambda j: torus(0, j))
        for j in range(4):
            torus(1, j).start()
        cross(0).start()

    @pl.when(step == 2)
    def _():
        pass_on(lambda j: torus(1, j))

    lines = [one_row(row_s, 2 * step + head) for head in (0, 1)]
    first = first_head((128, PAIR))
    zero = jnp.zeros((128, PAIR), jnp.bfloat16)
    upper = lax.broadcasted_iota(jnp.int32, (128, 128), 1) > lax.broadcasted_iota(
        jnp.int32, (128, 128), 0
    )
    for i in range(seq // 128):
        at, n = slice(i * 128, i * 128 + 128), i * 128 + 128
        q = q_s[at, :]
        both = []
        for head in (0, 1):
            own = jnp.where(first, q, zero) if head == 0 else jnp.where(first, zero, q)
            s = mm_t(own, k_s[0:n, :])
            column = jnp.sum(
                jnp.where(lane_is((128, PAIR), 2 * step + head), top_s[at, :], 0.0), axis=1, keepdims=True
            )
            s = s * (HEAD ** (-0.5)) + (column - lines[head][:, 0:n])
            diagonal = jnp.where(upper, NEG, s[:, n - 128 :])
            s = diagonal if i == 0 else jnp.concatenate([s[:, : n - 128], diagonal], axis=1)
            p = jnp.exp(s)
            p = p * (1.0 / jnp.sum(p, axis=1, keepdims=True))
            both.append(mm(p.astype(jnp.bfloat16), v_ref[0:n, :]))
        out = jnp.where(first, both[0], both[1])
        att_ref[at, :] = out
        gs[step, me, at, :] = (out * sig_ref[at, :]).astype(jnp.bfloat16).astype(F32)
    for j in range(4):
        gate(step, j).start()

    @pl.when(step == 0)
    def _():
        pass_on(lambda j: torus(0, j))

    @pl.when(step > 0)
    def _():
        pass_on(lambda j: gate(step - 1, j))

    @pl.when(step == pl.num_programs(0) - 1)
    def _():
        torus(1, 1).wait_recv()
        cross(1).start()
        torus(1, 2).wait_recv()
        cross(2).start()
        torus(1, 4).wait_recv()
        torus(1, 5).wait_recv()
        cross(3).start()
        pass_on(lambda j: gate(step, j))
        for j in range(4):
            cross(j).wait_recv()
        tall, wide, shard = ws.shape[4], ws.shape[5], w_ref.shape[0]

        def turn(k, carry):
            y, m = k // 8, lax.rem(k, 8)
            x, z = m // 2, lax.rem(m, 2) * 2
            rows = pl.ds(pl.multiple_of(y * shard + m * 2 * tall, 16), 2 * tall)
            for h, one, two in (
                (0, ws[0, z, x, y], ws[0, z + 1, x, y]),
                (1, ws[1, x, z, y], ws[1, x, z + 1, y]),
            ):
                both = jnp.concatenate([one, two], axis=0).astype(jnp.bfloat16)
                full_ref[rows, h * wide : h * wide + wide] = both
            return carry

        lax.fori_loop(0, 8 * Y, turn, 0)
        pairs = gs.shape[0]
        for pair in range(pairs):
            arrived(lambda j: gate(pair, j))
            for y in range(Y):
                lane = (y * pairs + pair) * PAIR
                gated_ref[:, lane : lane + PAIR] = gs[pair, y].astype(jnp.bfloat16)
        for j in range(3):
            plane(j).wait_send()
        for stage in (0, 1):
            for j in range(6):
                torus(stage, j).wait_send()
        for j in range(4):
            cross(j).wait_send()
        for pair in range(pairs):
            for j in range(6):
                gate(pair, j).wait_send()


def forward_attention(tokens, length, gain, wq, wk, wv, wo, wf, bf, w_out, call_id):
    seq, width = tokens.shape
    heads = wq.shape[1]
    weights = pl.BlockSpec((width, PAIR), lambda i, _: (0, i))
    lanes = pl.BlockSpec((seq, PAIR), lambda i, _: (0, i))
    low = jnp.bfloat16
    return local_call(
        forward_kernel,
        heads // PAIR,
        [whole((seq, width)), whole((1, width))] + [weights] * 4 + [whole(wf.shape), whole(bf.shape), whole(w_out.shape)],
        [whole((seq, width))] + [lanes] * 6 + [whole((2, seq, PAIR)), whole((seq, width)), whole((width, width))],
        [
            struct(seq, width, t=low), struct(seq, heads), struct(seq, heads), struct(seq, heads, t=low),
            struct(seq, heads), struct(seq, heads), struct(seq, heads),
            struct(2, seq, PAIR), struct(seq, heads * Y, t=low), struct(heads * Y, width, t=low),
        ],
        [
            pltpu.VMEM((seq, PAIR), F32),
            pltpu.VMEM((8, seq), F32),
            pltpu.VMEM((seq, PAIR), low),
            pltpu.VMEM((seq, PAIR), low),
            pltpu.VMEM((width, 4 * PAIR), low),
            pltpu.VMEM((seq, 4 * PAIR), F32),
            pltpu.VMEM((heads // PAIR, Y, seq, PAIR), F32),
            pltpu.VMEM((2, 4, 4, Y, heads // 16, width // 2), F32),
            pltpu.VMEM((width, PAIR), low),
            pltpu.VMEM((8, PAIR), F32),
        ]
        + sems(6 * (heads // PAIR), 3, 6, 6, 4),
        56, 6, 20, call_id,
    )(length, tokens, gain, wq, wk, wv, wo, wf, bf, w_out)


def mlp_forward_kernel(
    length_ref, x_ref, cot_ref, gated_ref, gain_ref, wo_ref, wg_ref, wu_ref, wd_ref,
    mid_ref, low_ref, grad_ref, gate_ref, up_ref, hid_ref, out_ref, sums_ref,
    all_s,
):
    step = pl.program_id(0)
    seq = x_ref.shape[0]
    length = length_ref[0]
    tile, units = wo_ref.shape[1], wg_ref.shape[1]

    @pl.when(step < 2)
    def _():
        at = pl.ds(pl.multiple_of(step * tile, tile), tile)
        branch = mm(gated_ref[...], wo_ref[...])
        x = x_ref[:, at].astype(F32)
        mid_ref[:, at] = x + branch
        kept = lax.broadcasted_iota(jnp.int32, (seq, 1), 0) < length
        grad_ref[:, at] = jnp.where(kept, cot_ref[:, at].astype(F32), 0.0).astype(jnp.bfloat16)
        sums_ref[0:1, at] = jnp.sum(jnp.where(kept, x * x, 0.0), axis=0, keepdims=True)
        sums_ref[1:2, at] = jnp.sum(jnp.where(kept, branch * branch, 0.0), axis=0, keepdims=True)

    @pl.when(step == 2)
    def _():
        def norm(i, carry):
            at = rows_at(i, 128)
            mid = mid_ref[at, :]
            r = lax.rsqrt(jnp.mean(mid * mid, axis=1, keepdims=True) + EPSILON)
            low_ref[at, :] = (mid * r * gain_ref[...].astype(F32)).astype(jnp.bfloat16)
            return carry

        lax.fori_loop(0, seq // 128, norm, 0)

    @pl.when((step == 2) | (step == 3))
    def _():
        at = pl.ds(pl.multiple_of((step - 2) * units, units), units)
        gate_ref[...] = mm(low_ref[...], wg_ref[...])
        up_ref[...] = mm(low_ref[...], wu_ref[...])
        gate = gate_ref[...]
        hid = (gate * jax.nn.sigmoid(gate) * up_ref[...]).astype(jnp.bfloat16)
        hid_ref[...] = hid
        all_s[:, at] = hid

    @pl.when(step > 3)
    def _():
        out_ref[...] = mm(all_s[...], wd_ref[...])


def mlp_forward(tokens, cotangent, length, gated, gain, wo, wg, wu, wd):
    seq, width = tokens.shape
    hidden = wg.shape[1]
    tile, units = width // 2, hidden // 2
    low = jnp.bfloat16
    stage = lambda first: (lambda i, _: (0, jnp.clip(i - first, 0, 1)))
    columns = pl.BlockSpec((width, units), stage(2))
    values = pl.BlockSpec((seq, units), stage(2))
    full = whole((seq, width))
    return local_call(
        mlp_forward_kernel,
        6,
        [full, full, full, whole((1, width)), pl.BlockSpec((width, tile), stage(0)), columns, columns]
        + [pl.BlockSpec((hidden, tile), stage(4))],
        [full, full, full, values, values, values, pl.BlockSpec((seq, tile), stage(4)), whole((2, width))],
        [
            struct(seq, width), struct(seq, width, t=low), struct(seq, width, t=low),
            struct(seq, hidden), struct(seq, hidden),
            struct(seq, hidden, t=low), struct(seq, width), struct(2, width),
        ],
        [pltpu.VMEM((seq, hidden), low)],
        56, 11, 40,
    )(length, tokens, cotangent, gated, gain, wo, wg, wu, wd)


def reduce_links(rows, x, opp, nbr, held, sem):
    dp, me = lax.axis_index("dp"), lax.axis_index("mp")
    right, left, far = lax.rem(me + 1, Y), lax.rem(me + 3, Y), lax.rem(me + 2, Y)
    q, h = rows // Y, rows // Y // 2

    def message(name):
        src, dst, to = {
            "oR": (lambda: rows_of(x, far * q, h), lambda: opp.at[0], right),
            "oL": (lambda: rows_of(x, far * q + h, h), lambda: opp.at[1], left),
            "iR": (lambda: rows_of(x, right * q + h, h), lambda: nbr.at[0, h:q], right),
            "iL": (lambda: rows_of(x, left * q, h), lambda: nbr.at[1, 0:h], left),
            "dR": (lambda: held.at[0], lambda: nbr.at[0, 0:h], right),
            "dL": (lambda: held.at[1], lambda: nbr.at[1, h:q], left),
        }[name]
        return link(src(), dst(), *sem, STEPS.index(name), (dp, to))

    return message, me, right, left, [(dp, right), (dp, left)]


def mlp_backward_kernel(
    length_ref, grad_ref, low_ref, gate_ref, up_ref, hid_ref, wd_ref, wg_ref, wu_ref, x_ref, mid_ref,
    back_ref, gd_ref, gg_ref, gu_ref, layer_ref, square_ref,
    dg_s, du_s, opp, nbr, held, own_s, mid_s, csem, *sem,
):
    step = pl.program_id(0)
    seq = grad_ref.shape[0]
    units = wd_ref.shape[0]
    low16 = jnp.bfloat16
    message, me, right, left, peers = reduce_links(seq, x_ref, opp, nbr, held, sem)
    q = seq // Y
    h = q // 2

    def fetch(j):
        src, dst = (
            (rows_of(x_ref, right * q, h), held.at[0]),
            (rows_of(x_ref, left * q + h, h), held.at[1]),
            (rows_of(x_ref, me * q, q), own_s),
            (rows_of(mid_ref, me * q, q), mid_s),
        )[j]
        return pltpu.make_async_copy(src, dst, csem.at[j])

    @pl.when(step == 0)
    def _():
        meet(peers)
        for name in STEPS[:4]:
            message(name).start()
        for j in range(4):
            fetch(j).start()

    @pl.when(step == 2)
    def _():
        for j, (come, go) in enumerate((("oR", "dR"), ("oL", "dL"))):
            message(come).wait_recv()
            fetch(j).wait()
            held[j] = held[j] + opp[j]
            message(go).start()

    @pl.when(step < 2)
    def _():
        at = pl.ds(pl.multiple_of(step * units, units), units)
        grad = mm_t(grad_ref[...], wd_ref[...])
        gate = gate_ref[...]
        sig = jax.nn.sigmoid(gate)
        dg_s[:, at] = (grad * up_ref[...] * (sig * (1.0 + gate * (1.0 - sig)))).astype(low16)
        du_s[:, at] = (grad * (gate * sig)).astype(low16)

        def grads(k, carry):
            rows = rows_at(k, 768)
            gd_ref[rows, :] = t_mm(grad_ref[:, rows], hid_ref[...])
            gg_ref[rows, :] = t_mm(low_ref[:, rows], dg_s[:, at])
            gu_ref[rows, :] = t_mm(low_ref[:, rows], du_s[:, at])
            return carry

        lax.fori_loop(0, gd_ref.shape[0] // 768, grads, 0)

    @pl.when(step >= 2)
    def _():
        back_ref[...] = mm_t(dg_s[...], wg_ref[...])
        back_ref[...] = back_ref[...] + mm_t(du_s[...], wu_ref[...])

    @pl.when(step == 3)
    def _():
        fetch(2).wait()
        fetch(3).wait()
        sums = 0.0
        for part, names in enumerate((("dR", "iL"), ("iR", "dL"))):
            for name in names:
                message(name).wait_recv()
            at = slice(part * h, part * h + h)
            branch = own_s[at, :] + nbr[0, at] + nbr[1, at]
            layer_ref[at, :] = (mid_s[at, :] + branch).astype(low16).astype(F32)
            row = lax.broadcasted_iota(jnp.int32, (h, 1), 0) + (me * q + part * h)
            kept = jnp.where(row < length_ref[0], branch * branch, 0.0)
            sums = sums + jnp.sum(kept, axis=0, keepdims=True)
        square_ref[...] = sums
        for name in STEPS[:6]:
            message(name).wait_send()


def mlp_backward(length, grad, low, gate, up, hid, wg, wu, wd, branch, mid, call_id):
    seq, width = low.shape
    hidden = wg.shape[1]
    tile, units, quarter = width // 2, hidden // 2, seq // Y
    stage = lambda first: (lambda i, _: (0, jnp.clip(i - first, 0, 1)))
    down = lambda first: (lambda i, _: (jnp.clip(i - first, 0, 1), 0))
    values = pl.BlockSpec((seq, units), stage(0))
    grads = pl.BlockSpec((width, units), stage(0))
    weights = pl.BlockSpec((tile, hidden), down(2))
    full, hbm = whole((seq, width)), pl.BlockSpec(memory_space=pl.ANY)
    return local_call(
        mlp_backward_kernel,
        4,
        [full, full, values, values, values, pl.BlockSpec((units, width), down(0)), weights, weights, hbm, hbm],
        [pl.BlockSpec((seq, tile), stage(2)), grads, grads, grads, whole((quarter, width)), whole((1, width))],
        [struct(seq, width)] + [struct(width, hidden)] * 3 + [struct(quarter, width), struct(1, width)],
        [pltpu.VMEM((seq, hidden), jnp.bfloat16)] * 2
        + ring_scratch(quarter, width)
        + [pltpu.VMEM((quarter, width), F32)] * 2
        + [pltpu.SemaphoreType.DMA((4,))]
        + sems(6),
        62, 13, 60, call_id,
    )(length, grad, low, gate, up, hid, wd, wg, wu, branch, mid)


def backward_kernel(
    length_ref, gg_ref, low_ref, qn_ref, kn_ref, v_ref, sig_ref, att_ref, stat_ref,
    decay_ref, wq_ref, wk_ref, wv_ref, wo_ref, wf_ref, own_ref, gated_ref, layer_ref,
    back_ref, four_ref, gout_ref, gf_ref, bias_ref, out_ref,
    k_s, do_s, line_s, dq_s, dk_s, dv_s, all_s, fall_s, w_s, wf_s, lay_s, *sem,
):
    step = pl.program_id(0)
    seq, width = low_ref.shape
    length = length_ref[0]
    low16 = jnp.bfloat16
    wide = 4 * PAIR
    dp, me = lax.axis_index("dp"), lax.axis_index("mp")
    right, left = lax.rem(me + 1, Y), lax.rem(me + 3, Y)
    q, h = seq // Y, seq // Y // 2

    def spread(j):
        owner, part, to = (
            (me, 0, right), (me, 1, right), (me, 0, left), (me, 1, left), (left, 0, right), (right, 1, left)
        )[j]
        piece = rows_of(lay_s, owner * q + part * h, h)
        return link(piece, piece, *sem, j, (dp, to))

    @pl.when(step == 0)
    def _():
        rows_of(lay_s, me * q, q)[...] = layer_ref[...]
        meet([(dp, right), (dp, left)])
        for j in range(4):
            spread(j).start()

    @pl.when(step == 1)
    def _():
        spread(0).wait_recv()
        spread(4).start()
        spread(3).wait_recv()
        spread(5).start()

    @pl.when(step == 0)
    def _():
        heads = wf_ref.shape[1]
        wf_s[...] = jnp.zeros_like(wf_s)
        wf_s[:, 0:heads] = wf_ref[...]
        decay = decay_ref[0]
        row = lax.broadcasted_iota(jnp.int32, decay.shape, 0)
        final = jnp.sum(jnp.where(row == length - 1, decay, 0.0), axis=0, keepdims=True)
        line_s[...] = jnp.where(row < length, decay, final).T[0:8]
        fall_s[...] = jnp.zeros_like(fall_s)

    base = pl.multiple_of(step * wide, wide)
    part = lambda j: pl.ds(pl.multiple_of(base + j * PAIR, PAIR), PAIR)
    for j, w_ref in enumerate((wq_ref, wk_ref, wv_ref, wo_ref)):
        w_s[:, part(j)] = w_ref[...]
    first = first_head((seq, PAIR))
    gg, sig = gg_ref[...], sig_ref[...]
    do_s[...] = (gg * sig).astype(low16)
    all_s[:, part(3)] = (gg * att_ref[...] * sig * (1.0 - sig)).astype(low16)
    k_s[...] = kn_ref[...].astype(low16)
    dk_s[...] = jnp.zeros_like(dk_s)
    dv_s[...] = jnp.zeros_like(dv_s)
    row = lax.broadcasted_iota(jnp.int32, (seq, PAIR), 0)
    columns, lines = [], [one_row(line_s, 2 * step + head) for head in (0, 1)]
    for head in (0, 1):
        column = jnp.sum(
            jnp.where(lane_is((seq, PAIR), 2 * step + head), decay_ref[0], 0.0), axis=1, keepdims=True
        )
        columns.append(jnp.where(row[:, 0:1] < length, column, -NEG))
    block = first_head((128, PAIR))
    zero = jnp.zeros((128, PAIR), low16)
    lower = lax.broadcasted_iota(jnp.int32, (128, 128), 0) > lax.broadcasted_iota(
        jnp.int32, (128, 128), 1
    )
    for i in range(seq // 128):
        at, n = slice(i * 128, i * 128 + 128), i * 128 + 128
        query = qn_ref[at, :].astype(low16)
        do = do_s[at, :]
        pieces = []
        for head in (0, 1):
            pick = (lambda t: jnp.where(block, t, zero)) if head == 0 else (lambda t: jnp.where(block, zero, t))
            own_q, own_do = pick(query), pick(do)
            one = jnp.where(lane_is((128, PAIR), 2 * step + head), 1.0, 0.0).astype(low16)
            s = mm_t(k_s[0:n, :], own_q)
            s = s * (HEAD ** (-0.5)) + (lines[head][:, at] - columns[head][0:n])
            diagonal = jnp.where(lower, NEG, s[n - 128 :, :])
            s = diagonal if i == 0 else jnp.concatenate([s[: n - 128, :], diagonal], axis=0)
            p = jnp.exp(s)
            p = p * (1.0 / jnp.sum(p, axis=0, keepdims=True))
            gp = mm_t(v_ref[0:n, :], own_do)
            ds = (p * (gp - jnp.sum(p * gp, axis=0, keepdims=True))).astype(low16)
            dv_s[0:n, :] = dv_s[0:n, :] + mm(p.astype(low16), own_do)
            dk_s[0:n, :] = dk_s[0:n, :] + mm(ds, jnp.concatenate([own_q, one], axis=1))
            mark = jnp.where(lane_is((n, PAIR), 2 * step + head), 1.0, 0.0).astype(low16)
            pieces.append(t_mm(ds, jnp.concatenate([k_s[0:n, :], mark], axis=1)))
        dq_s[at, :] = jnp.where(block, pieces[0][:, 0:PAIR], pieces[1][:, 0:PAIR])
        fall_s[at, :] = fall_s[at, :] + pieces[0][:, PAIR:] + pieces[1][:, PAIR:]
    fall_s[...] = fall_s[...] - dk_s[:, PAIR:]
    stat = stat_ref[...]
    for e, n_ref, col, to in ((dq_s, qn_ref, 0, 0), (dk_s, kn_ref, 2, 1)):
        e = e[:, 0:PAIR] * (HEAD ** (-0.5))
        n = n_ref[...]
        a, b = halves_mean(e * n)
        r = jnp.where(first, stat[:, col : col + 1], stat[:, col + 1 : col + 2])
        all_s[:, part(to)] = (r * (e - n * jnp.where(first, a, b))).astype(low16)
    all_s[:, part(2)] = dv_s[...].astype(low16)

    def grads(k, carry):
        rows = rows_at(k, 768)
        four_ref[rows, :] = t_mm(low_ref[:, rows], all_s[:, pl.ds(base, wide)])
        gout_ref[rows, :] = t_mm(own_ref[:, rows].astype(low16), gated_ref[...])
        return carry

    lax.fori_loop(0, width // 768, grads, 0)

    @pl.when(step == pl.num_programs(0) - 1)
    def _():
        fall = running_sum(fall_s[...], backward=True) * decay_ref[1]
        fall = fall.astype(low16)
        bias_ref[...] = jnp.sum(fall.astype(F32), axis=0, keepdims=True)
        gf_ref[...] = t_mm(fall, low_ref[...])[0:8]

        def tail(k, carry):
            rows = rows_at(k, 768)
            back_ref[:, rows] = mm_t(all_s[...], w_s[rows, :])
            back_ref[:, rows] = back_ref[:, rows] + mm_t(fall, wf_s[rows, :])
            return carry

        lax.fori_loop(0, width // 768, tail, 0)
        for j in (1, 2, 4, 5):
            spread(j).wait_recv()
        out_ref[...] = lay_s[...].astype(low16)
        for j in range(6):
            spread(j).wait_send()


def backward_attention(place, gg, low, qn, kn, v, sig, att, stat, decay, wq, wk, wv, wo, wf, own, gated, layer, call_id):
    seq, width = low.shape
    heads = wq.shape[1]
    weights = pl.BlockSpec((width, PAIR), lambda i, _: (0, i))
    lanes = pl.BlockSpec((seq, PAIR), lambda i, _: (0, i))
    wide = pl.BlockSpec((width, 4 * PAIR), lambda i, _: (0, i))
    full = whole((seq, width))
    low16 = jnp.bfloat16
    return local_call(
        backward_kernel,
        heads // PAIR,
        [lanes, full] + [lanes] * 6 + [whole((2, seq, PAIR))] + [weights] * 4
        + [whole(wf.shape), whole(own.shape)]
        + [pl.BlockSpec((own.shape[0], 4 * PAIR), lambda i, _: (lax.axis_index("mp"), i)), whole(layer.shape)],
        [full, wide, wide, whole((8, width)), whole((1, PAIR)), full],
        [
            struct(seq, width), struct(width, 4 * heads), struct(width, width), struct(8, width),
            struct(1, PAIR), struct(seq, width, t=low16),
        ],
        [
            pltpu.VMEM((seq, PAIR), low16),
            pltpu.VMEM((seq, PAIR), low16),
            pltpu.VMEM((8, seq), F32),
            pltpu.VMEM((seq, PAIR), F32),
            pltpu.VMEM((seq, 2 * PAIR), F32),
            pltpu.VMEM((seq, PAIR), F32),
            pltpu.VMEM((seq, 4 * heads), low16),
            pltpu.VMEM((seq, PAIR), F32),
            pltpu.VMEM((width, 4 * heads), low16),
            pltpu.VMEM((width, PAIR), low16),
            pltpu.VMEM((seq, width), F32),
        ]
        + sems(6),
        60, 14, 50, call_id,
    )(place, gg, low, qn, kn, v, sig, att, stat, decay, wq, wk, wv, wo, wf, own, gated, layer)


def finish_kernel(
    grad_in, layer_in, wout_in, four_in, mlp_in,
    grad_ref, layer_ref, wout_ref, q_ref, k_ref, v_ref, o_ref, gate_ref, up_ref, down_ref,
    sem,
):
    rows = grad_in.shape[0] // 4
    copies = []
    for j in range(4):
        for src, dst, at in ((grad_in, grad_ref, j), (layer_in, layer_ref, 4 + j)):
            part = slice(j * rows, j * rows + rows)
            copies.append(load(src.at[part], dst.at[part], sem.at[at]))
    wout_ref[...] = wout_in[...].T
    for j, ref in enumerate((q_ref, k_ref, v_ref, o_ref)):
        for pair in range(q_ref.shape[1] // PAIR):
            lane = (pair * 4 + j) * PAIR
            ref[:, pair * PAIR : pair * PAIR + PAIR] = four_in[:, lane : lane + PAIR]
    units = gate_ref.shape[1]
    down_ref[...] = mlp_in[:, 0:units].T
    gate_ref[...] = mlp_in[:, units : 2 * units]
    up_ref[...] = mlp_in[:, 2 * units : 3 * units]
    for copy in copies:
        copy.wait()


def finish(grad, layer, out_share, share, mlp_share):
    rows, inner = out_share.shape
    units = mlp_share.shape[1] // 3
    hbm, vmem = pl.BlockSpec(memory_space=pl.ANY), pl.BlockSpec(memory_space=pltpu.VMEM)
    return pl.pallas_call(
        finish_kernel,
        out_shape=[
            struct(*grad.shape), struct(*layer.shape, t=layer.dtype), struct(inner, rows),
            *[struct(rows, inner)] * 4, struct(rows, units), struct(rows, units), struct(units, rows),
        ],
        in_specs=[hbm, hbm, vmem, vmem, vmem],
        out_specs=[hbm, hbm] + [vmem] * 8,
        scratch_shapes=[pltpu.SemaphoreType.DMA((8,))],
        compiler_params=pltpu.CompilerParams(vmem_limit_bytes=16 << 20),
    )(grad, layer, out_share, share, mlp_share)


def per_device(
    tokens, lengths, buckets, out_cotangent, gain_attn, w_query, w_key, w_value, w_outgate,
    w_forget, b_forget, w_out, gain_mlp, w_gate, w_up, w_down,
):
    x, cotangent = tokens[0], out_cotangent[0]
    model_width = x.shape[1]
    heads = w_forget.shape[1]
    gain_in, gain_mid = gain_attn[None], gain_mlp[None]
    weights = (w_query, w_key, w_value, w_outgate, w_forget)
    low, qn, kn, value, sig, attended, stat, decay, gated, w_full = forward_attention(
        x, lengths, gain_in, *weights, b_forget[None], w_out, 0
    )
    middle, mid_low, grad_rows, gate, up, hidden, mlp_local, squares = mlp_forward(
        x, cotangent, lengths, gated, gain_mid, w_full, w_gate, w_up, w_down
    )
    mid_local, g_down, g_gate, g_up, layer_own, mlp_square = mlp_backward(
        lengths, grad_rows, mid_low, gate, up, hidden, w_gate, w_up, w_down, mlp_local, middle, 1
    )
    grad_own, gg, mlp_share, mlp_gain = reduce_middle(
        mid_local, middle, grad_rows, gain_mid, w_full, [g_down, g_gate, g_up], 2
    )
    in_local, g_four, g_out, g_fall, bias, layer_out = backward_attention(
        lengths, gg, low, qn, kn, value, sig, attended, stat, decay, *weights, grad_own, gated,
        layer_own, 3,
    )
    bucket_hot = (buckets[0] == jnp.arange(NBUCKET)).astype(F32)
    square_sums = jnp.concatenate([squares, mlp_square]).sum(axis=1)
    misc = jnp.stack([square_sums[0], square_sums[1], lengths[0].astype(F32), square_sums[2]])
    misc = misc[:, None] * bucket_hot[None, :]
    misc = jnp.stack([misc[:3].reshape(-1), jnp.pad(misc[3], (0, 2 * NBUCKET))])
    misc = jnp.pad(misc, ((0, 0), (0, PAIR - 3 * NBUCKET)))
    input_grad, out_share, share, sums = reduce_input(
        in_local, x, grad_own, gain_in, (mlp_gain, g_fall, misc, bias), [g_out, g_four], 4
    )
    input_grad, layer_out, g_out, g_query, g_key, g_value, g_outgate, g_gate, g_up, g_down = finish(
        input_grad, layer_out, out_share, share, mlp_share
    )
    totals = jnp.stack([sums[9, :NBUCKET], sums[9, NBUCKET : 2 * NBUCKET], sums[2, :NBUCKET]])
    rms = jnp.sqrt(totals / (sums[9, 2 * NBUCKET : 3 * NBUCKET] * model_width)[None, :])
    rows = model_width // lax.axis_size("dp")
    mine = lax.dynamic_slice_in_dim(sums[:9], lax.axis_index("dp") * rows, rows, axis=1)
    return (
        layer_out[None],
        input_grad[None],
        mine[0],
        g_query,
        g_key,
        g_value,
        g_outgate,
        mine[3 : 3 + heads].T,
        sums[10, :heads],
        g_out,
        mine[1],
        g_gate,
        g_up,
        g_down,
        rms,
    )


def solution(mesh):
    placed = (
        P("dp", None, None),
        P("dp"),
        P("dp"),
        P("dp", None, None),
        P(),
        P(None, "mp"),
        P(None, "mp"),
        P(None, "mp"),
        P(None, "mp"),
        P(None, "mp"),
        P("mp"),
        P("mp", None),
        P(),
        P(None, "mp"),
        P(None, "mp"),
        P("mp", None),
    )
    return jax.shard_map(
        per_device,
        mesh=mesh,
        in_specs=placed,
        out_specs=(
            P("dp", None, None),
            P("dp", None, None),
            P("dp"),
            P("dp", "mp"),
            P("dp", "mp"),
            P("dp", "mp"),
            P("dp", "mp"),
            P("dp", "mp"),
            P("mp"),
            P("mp", "dp"),
            P("dp"),
            P("dp", "mp"),
            P("dp", "mp"),
            P("mp", "dp"),
            P(),
        ),
        check_vma=False,
    )
```

```python
import functools

import jax
import jax.numpy as jnp
from jax import lax
from jax.experimental import pallas as pl
from jax.experimental.pallas import tpu as pltpu
from jax.sharding import PartitionSpec as P

NBUCKET = 4


EPSILON = 1e-06


MESH = pl.DeviceIdType.MESH
F32 = jnp.float32
Y = 4
STEP = 512
HBM = pl.BlockSpec(memory_space=pl.ANY)
VMEM = pl.BlockSpec(memory_space=pltpu.VMEM)
STEPS = ("oR", "oL", "iR", "iL", "dR", "dL", "gRa", "gRb", "gLa", "gLb", "fR", "fL")


def rows_of(ref, start, count):
    return ref.at[pl.ds(pl.multiple_of(start, 8), count)]


def meet(devices):
    barrier = pltpu.get_barrier_semaphore()
    for device in devices:
        pl.semaphore_signal(barrier, inc=1, device_id=device, device_id_type=MESH)
    pl.semaphore_wait(barrier, len(devices))


def link(src, dst, ssem, rsem, at, device):
    return pltpu.make_async_remote_copy(
        src_ref=src,
        dst_ref=dst,
        send_sem=ssem.at[at],
        recv_sem=rsem.at[at],
        device_id=device,
        device_id_type=MESH,
    )


def push(*args):
    copy = link(*args)
    copy.start()
    return copy


class YRing:
    def __init__(self, rows, ssem, rsem):
        self.sems = (ssem, rsem)
        self.dp, self.me = lax.axis_index("dp"), lax.axis_index("mp")
        self.right, self.left = lax.rem(self.me + 1, Y), lax.rem(self.me + 3, Y)
        self.far = lax.rem(self.me + 2, Y)
        self.quarter, self.half = rows // Y, rows // Y // 2
        self.sent = {}

    def neighbours(self):
        return [(self.dp, self.right), (self.dp, self.left)]

    def send(self, name, src, dst, to):
        self.sent[name] = push(src, dst, *self.sems, STEPS.index(name), (self.dp, to))

    def start(self, x, opp, nbr):
        q, h = self.quarter, self.half
        self.send("oR", rows_of(x, self.far * q, h), opp.at[0], self.right)
        self.send("oL", rows_of(x, self.far * q + h, h), opp.at[1], self.left)
        self.send("iR", rows_of(x, self.right * q + h, h), nbr.at[0, h:q], self.right)
        self.send("iL", rows_of(x, self.left * q, h), nbr.at[1, 0:h], self.left)

    def relay(self, x, opp, nbr, held):
        q, h = self.quarter, self.half
        self.sent["oR"].wait_recv()
        held[0] = rows_of(x, self.right * q, h)[...] + opp[0]
        self.send("dR", held.at[0], nbr.at[0, 0:h], self.right)
        self.sent["oL"].wait_recv()
        held[1] = rows_of(x, self.left * q + h, h)[...] + opp[1]
        self.send("dL", held.at[1], nbr.at[1, h:q], self.left)

    def collect(self, x, nbr, part):
        h = self.half
        for name in (("dR", "iL"), ("iR", "dL"))[part]:
            self.sent[name].wait_recv()
        at = slice(part * h, part * h + h)
        return rows_of(x, self.me * self.quarter + part * h, h)[...] + nbr[0, at] + nbr[1, at]

    def spread(self, part, block):
        own, tag = block(self.me, part), "ab"[part]
        self.send("gR" + tag, own, own, self.right)
        self.send("gL" + tag, own, own, self.left)

    def forward(self, block):
        self.sent["gRa"].wait_recv()
        self.send("fR", block(self.left, 0), block(self.left, 0), self.right)
        self.sent["gLb"].wait_recv()
        self.send("fL", block(self.right, 1), block(self.right, 1), self.left)

    def arrive(self):
        for name in ("gRb", "gLa", "fR", "fL"):
            self.sent[name].wait_recv()

    def finish(self):
        for copy in self.sent.values():
            copy.wait_send()


def ring_scratch(quarter, columns):
    return [
        pltpu.VMEM((2, quarter // 2, columns), F32),
        pltpu.VMEM((2, quarter, columns), F32),
        pltpu.VMEM((2, quarter // 2, columns), F32),
    ]


def sems(*counts):
    return [pltpu.SemaphoreType.DMA((n,)) for n in counts for _ in (0, 1)]


class Place:
    def __init__(self):
        self.dp, self.my = lax.axis_index("dp"), lax.axis_index("mp")
        c, z, x = lax.rem(self.dp, 2), lax.rem(self.dp // 2, 4), self.dp // 8
        self.c, self.sib, self.chip = c, self.dp + 1 - 2 * c, x * 4 + z
        self.st1, self.st2 = 4 - 3 * c, 1 + 3 * c
        self.p1, self.p2 = x + c * (z - x), z + c * (x - z)
        step = lambda p, by: lax.rem(p + by, 4)
        self.r1, self.l1, self.o1 = (step(self.p1, by) for by in (1, 3, 2))
        self.r2, self.l2, self.o2 = (step(self.p2, by) for by in (1, 3, 2))

    def device(self, a, b):
        return ((a * self.st1 + b * self.st2) * 2 + self.c, self.my)

    def peers(self):
        return [
            (self.sib, self.my),
            self.device(self.r1, self.p2),
            self.device(self.l1, self.p2),
            self.device(self.p1, self.r2),
            self.device(self.p1, self.l2),
        ]


class ScatterSum:
    def __init__(self, here, sources, own, other, near, last, asem, bsem, lsem, ssem, rsem):
        self.here, self.sources = here, sources
        self.own, self.other, self.near, self.last = own, other, near, last
        self.asem, self.bsem, self.lsem, self.ssem, self.rsem = asem, bsem, lsem, ssem, rsem
        self.n = own.shape[0]
        self.sibling, *to = here.peers()
        self.to = (to[0:2], to[2:4])

    def message(self, name, k, stage):
        at = (k * 2 + stage) * 6 + STEPS.index(name)
        device = self.to[stage][0 if name[1] == "R" else 1]
        here, own = self.here, self.own.at[k]
        if stage:
            own, into, cut = own.at[here.p1], self.last.at[k], (slice(0, 24), slice(24, 48))
            far, right, left = here.o2, here.r2, here.l2
        else:
            into, cut = self.near.at[k], (slice(0, 2), slice(2, 4))
            far, right, left = here.o1, here.r1, here.l1
        row, part, slot = {
            "oR": (far, 0, 0),
            "oL": (far, 1, 1),
            "iR": (right, 1, 3),
            "iL": (left, 0, 4),
            "dR": (right, 0, 2),
            "dL": (left, 1, 5),
        }[name]
        return link(own.at[row, cut[part]], into.at[slot], self.ssem, self.rsem, at, device)

    def whole(self, k):
        own, other = self.own.at[k], self.other.at[k]
        return link(own, other, self.asem, self.bsem, k, self.sibling)

    def exchange(self, k):
        here = self.here
        ref, start, width = self.sources[k]

        def source(block):
            return ref.at[pl.ds(pl.multiple_of(block * 48, 16), 48), pl.ds(start, width)]

        def cross(i, carry):
            a, b = i // 4, lax.rem(i, 4)
            block = source((a * here.st2 + b * here.st1) * 2 + 1 - here.c)
            push(block, self.other.at[k, a, b], self.asem, self.bsem, k, self.sibling)
            return carry

        def fetch(i, carry):
            a, b = i // 4, lax.rem(i, 4)
            block = source((a * here.st1 + b * here.st2) * 2 + here.c)
            pltpu.make_async_copy(block, self.own.at[k, a, b], self.lsem.at[k]).start()
            return carry

        lax.fori_loop(0, 16, cross, 0)
        lax.fori_loop(0, 16, fetch, 0)

    def first(self, k):
        here, own, other = self.here, self.own, self.other
        pltpu.make_async_copy(own.at[k], own.at[k], self.lsem.at[k]).wait()
        self.whole(k).wait_recv()

        def add(p):
            def body(b, carry):
                own[k, p, b] = own[k, p, b] + other[k, p, b]
                return carry

            lax.fori_loop(0, 4, body, 0)

        add(here.o1)
        self.message("oR", k, 0).start()
        self.message("oL", k, 0).start()
        add(here.r1)
        self.message("iR", k, 0).start()
        add(here.l1)
        self.message("iL", k, 0).start()
        add(here.p1)

    def first_relay(self, k):
        here, own, near = self.here, self.own, self.near

        def add(p, at, slot):
            def body(b, carry):
                own[k, p, at + b] = own[k, p, at + b] + near[k, slot, b]
                return carry

            lax.fori_loop(0, 2, body, 0)

        self.message("oR", k, 0).wait_recv()
        add(here.r1, 0, 0)
        self.message("dR", k, 0).start()
        self.message("oL", k, 0).wait_recv()
        add(here.l1, 2, 1)
        self.message("dL", k, 0).start()

    def second(self, k):
        here, own, near = self.here, self.own, self.near
        for name in ("iR", "dR", "iL", "dL"):
            self.message(name, k, 0).wait_recv()

        def add(p):
            h, b = p // 2, lax.rem(p, 2)
            own[k, here.p1, p] = own[k, here.p1, p] + near[k, 2 + h, b] + near[k, 4 + h, b]

        add(here.o2)
        self.message("oR", k, 1).start()
        self.message("oL", k, 1).start()
        add(here.r2)
        self.message("iR", k, 1).start()
        add(here.l2)
        self.message("iL", k, 1).start()
        add(here.p2)

    def second_relay(self, k):
        here, own, last = self.here, self.own, self.last
        self.message("oR", k, 1).wait_recv()
        own[k, here.p1, here.r2, 0:24] = own[k, here.p1, here.r2, 0:24] + last[k, 0]
        self.message("dR", k, 1).start()
        self.message("oL", k, 1).wait_recv()
        own[k, here.p1, here.l2, 24:48] = own[k, here.p1, here.l2, 24:48] + last[k, 1]
        self.message("dL", k, 1).start()

    def result(self, k, out, at):
        here, own, last = self.here, self.own, self.last
        width = own.shape[4]
        for name in ("iR", "dR", "iL", "dL"):
            self.message(name, k, 1).wait_recv()
        columns = pl.ds(pl.multiple_of(at * width, 128), width)
        out[0:24, columns] = own[k, here.p1, here.p2, 0:24] + last[k, 2] + last[k, 4]
        out[24:48, columns] = own[k, here.p1, here.p2, 24:48] + last[k, 3] + last[k, 5]

    def sent(self, k):
        self.whole(k).wait_send()
        for stage in (0, 1):
            for name in STEPS[:6]:
                self.message(name, k, stage).wait_send()


def each(low, high, step):
    def body(k, carry):
        step(k)
        return carry

    lax.fori_loop(low, high, body, 0)


class SmallSum:
    def __init__(self, here, bufs, landed, ssem, rsem):
        self.bufs, self.landed, self.ssem, self.rsem = bufs, landed, ssem, rsem
        turn = lambda p, by: lax.rem(p + by, 4)
        self.stages = [
            [(here.sib, here.my)],
            [here.device(turn(here.p1, by), here.p2) for by in (1, 2, 3)],
            [here.device(here.p1, turn(here.p2, by)) for by in (1, 2, 3)],
            [(here.dp, turn(here.my, by)) for by in (1, 2, 3)],
        ]
        self.far = [self.stages[1][1], self.stages[2][1], self.stages[3][1]]
        self.sent = []

    def send(self, stage):
        for to in self.stages[stage]:
            at = len(self.sent)
            copy = push(self.bufs.at[stage], self.landed.at[at], self.ssem, self.rsem, at, to)
            self.sent.append(copy)

    def take(self, stage):
        value, count = self.bufs[stage], len(self.stages[stage])
        for at in range(len(self.sent) - count, len(self.sent)):
            self.sent[at].wait_recv()
            value = value + self.landed[at]
        self.bufs[stage + 1] = value

    def finish(self):
        for copy in self.sent:
            copy.wait_send()


def scatter_scratch(n, w):
    return [
        pltpu.VMEM((n, 4, 4, 48, w), F32),
        pltpu.VMEM((n, 4, 4, 48, w), F32),
        pltpu.VMEM((n, 6, 2, 48, w), F32),
        pltpu.VMEM((n, 6, 24, w), F32),
        pltpu.SemaphoreType.DMA((n,)),
        pltpu.SemaphoreType.DMA((n,)),
        pltpu.SemaphoreType.DMA((n,)),
        pltpu.SemaphoreType.DMA((12 * n,)),
        pltpu.SemaphoreType.DMA((12 * n,)),
    ]


def scatter_sources(refs, pieces):
    return [(refs[which], at * STEP, STEP) for which, at in pieces]


def norm_back(value, source, base, gain):
    source = source.astype(F32)
    r = lax.rsqrt(jnp.mean(source * source, axis=1, keepdims=True) + EPSILON)
    n = source * r
    e = value * gain.astype(F32)
    inner = jnp.mean(e * n, axis=1, keepdims=True)
    return base.astype(F32) + r * (e - n * inner), jnp.sum(value * n, axis=0, keepdims=True)


def load(ref, scratch, sem):
    copy = pltpu.make_async_copy(ref, scratch, sem)
    copy.start()
    return copy


def middle_kernel(pieces, count, x_ref, source_ref, base_ref, gain_ref, w_ref, *refs):
    ins, refs = refs[:count], refs[count:]
    grad_ref, gg_ref, share_ref, sums_ref = refs[:4]
    source_s, base_s, w_s, opp, nbr, held, blocks, csem, *sem = refs[4:16]
    here, ring = Place(), YRing(x_ref.shape[0], *sem[0:2])
    total = ScatterSum(here, scatter_sources(ins, pieces), *refs[16:])
    n = total.n
    far = (ring.dp, ring.far)
    meet(ring.neighbours() + [far] + here.peers())
    ring.start(x_ref, opp, nbr)
    q, h = ring.quarter, ring.half
    loads = [
        load(rows_of(source_ref, ring.me * q, q), source_s, csem.at[0]),
        load(rows_of(base_ref, ring.me * q, q), base_s, csem.at[1]),
        load(w_ref, w_s, csem.at[2]),
    ]
    for k in range(n):
        total.exchange(k)
    each(0, n // 2, total.first)
    ring.relay(x_ref, opp, nbr, held)
    each(n // 2, n, total.first)
    each(0, n - 2, total.first_relay)
    for copy in loads:
        copy.wait()
    sums = 0.0
    for part in (0, 1):
        at = slice(part * h, part * h + h)
        value, more = norm_back(
            ring.collect(x_ref, nbr, part), source_s[at, :], base_s[at, :], gain_ref[...]
        )
        grad_ref[at, :] = value
        sums = sums + more
    sums_ref[...] = sums
    low = grad_ref[...].astype(jnp.bfloat16)
    inner = gg_ref.shape[1]
    swaps = []
    for j, by in enumerate((2, 1, 3, 0)):
        to = lax.rem(ring.me + by, Y)
        block = lax.dot_general(
            low, rows_of(w_s, to * inner, inner)[...], (((1,), (1,)), ((), ())),
            preferred_element_type=F32,
        )
        place = rows_of(gg_ref, ring.me * q, q)
        if by:
            blocks[j] = block
            swaps.append(push(blocks.at[j], place, *sem[2:4], j, (ring.dp, to)))
        else:
            place[...] = block
    each(n - 2, n, total.first_relay)
    each(0, n, total.second)
    each(0, n, total.second_relay)
    each(0, n, lambda k: total.result(k, share_ref, k))
    for copy in swaps:
        copy.wait_recv()
    for copy in swaps:
        copy.wait_send()
    ring.finish()
    each(0, n, total.sent)


def reduce_middle(partial, source, base, gain, w_full, grads, pieces, call_id):
    n = len(pieces)
    hbm, vmem = pl.BlockSpec(memory_space=pl.ANY), pl.BlockSpec(memory_space=pltpu.VMEM)
    rows, columns = partial.shape
    quarter, inner = rows // Y, w_full.shape[0] // Y
    return pl.pallas_call(
        functools.partial(middle_kernel, pieces, len(grads)),
        out_shape=[
            jax.ShapeDtypeStruct((quarter, columns), F32),
            jax.ShapeDtypeStruct((rows, inner), F32),
            jax.ShapeDtypeStruct((48, n * STEP), F32),
            jax.ShapeDtypeStruct((1, columns), F32),
        ],
        in_specs=[vmem, hbm, hbm, vmem, hbm] + [hbm] * len(grads),
        out_specs=[vmem] * 4,
        scratch_shapes=[
            pltpu.VMEM((quarter, columns), source.dtype),
            pltpu.VMEM((quarter, columns), base.dtype),
            pltpu.VMEM(w_full.shape, w_full.dtype),
        ]
        + ring_scratch(quarter, columns)
        + [pltpu.VMEM((3, quarter, inner), F32), pltpu.SemaphoreType.DMA((3,))]
        + sems(12, 3)
        + scatter_scratch(n, STEP),
        compiler_params=pltpu.CompilerParams(
            collective_id=call_id, has_side_effects=True, vmem_limit_bytes=56 << 20
        ),
    )(partial, source, base, gain, w_full, *grads)


def input_kernel(
    pieces, count, x_ref, source_ref, base_ref, gain_ref, other_ref, fall_ref, square_ref, more_ref,
    bias_ref, length_ref, bucket_ref, *refs
):
    ins, refs = refs[:count], refs[count:]
    out_ref, out_share_ref, share_ref, sums_ref = refs[:4]
    source_s, opp, nbr, held, wide_s, landed, csem, *sem = refs[4:15]
    bufs, arrived, asem, bsem = refs[15:19]
    here, ring = Place(), YRing(x_ref.shape[0], *sem[0:2])
    total = ScatterSum(here, scatter_sources(ins, pieces), *refs[19:])
    tiny = SmallSum(here, bufs, arrived, asem, bsem)
    n, first = total.n, wide_s.shape[1] // STEP
    meet(ring.neighbours() + here.peers() + tiny.far)
    ring.start(x_ref, opp, nbr)
    q, h = ring.quarter, ring.half
    copy = load(rows_of(source_ref, ring.me * q, q), source_s, csem.at[0])
    for k in range(n):
        total.exchange(k)
    each(0, n // 2, total.first)
    ring.relay(x_ref, opp, nbr, held)
    each(n // 2, n, total.first)
    each(0, n - 2, total.first_relay)
    copy.wait()
    block = lambda owner, part: rows_of(out_ref, owner * q + part * h, h)
    sums = 0.0
    for part in (0, 1):
        at = slice(part * h, part * h + h)
        value, more = norm_back(
            ring.collect(x_ref, nbr, part), source_s[at, :], base_ref[at, :], gain_ref[...]
        )
        block(ring.me, part)[...] = value
        ring.spread(part, block)
        sums = sums + more
    bufs[0, 0:1, :] = sums
    bufs[0, 1:2, :] = other_ref[...]
    bufs[0, 8:16, :] = jnp.zeros_like(bufs[0, 8:16, :])
    bufs[0, 2:3, :] = jnp.zeros((1, sums_ref.shape[1]), F32)
    bufs[0, 3:9, :] = fall_ref[0:6, :]
    lane = lax.broadcasted_iota(jnp.int32, (1, PAIR), 1)
    both = jnp.sum(square_ref[...], axis=1, keepdims=True)
    total_of = lambda at, value: jnp.where(lane == bucket_ref[0] + at * NBUCKET, value, 0.0)
    bufs[0, 2:3, 0:PAIR] = total_of(0, jnp.sum(more_ref[...], axis=1, keepdims=True))
    bufs[0, 9:10, 0:PAIR] = (
        total_of(0, both[0:1]) + total_of(1, both[1:2]) + total_of(2, length_ref[0].astype(F32))
    )
    bufs[0, 10:11, 0:PAIR] = bias_ref[...]
    tiny.send(0)
    each(n - 2, n, total.first_relay)
    each(0, n, total.second)
    ring.forward(block)
    tiny.take(0)
    tiny.send(1)
    each(0, n, total.second_relay)
    tiny.take(1)
    tiny.send(2)
    each(0, first, lambda k: total.result(k, wide_s, k))
    inner = landed.shape[2]
    swaps = []
    for j, by in enumerate((2, 1, 3)):
        to = lax.rem(ring.me + by, Y)
        columns = pl.ds(pl.multiple_of(to * inner, 128), inner)
        swaps.append(push(wide_s.at[:, columns], landed.at[j], *sem[2:4], j, (ring.dp, to)))
    each(first, n, lambda k: total.result(k, share_ref, k - first))
    tiny.take(2)
    tiny.send(3)
    own = wide_s[:, pl.ds(pl.multiple_of(ring.me * inner, 128), inner)]
    for j, copy in enumerate(swaps):
        copy.wait_recv()
        own = own + landed[j]
    out_share_ref[...] = own
    tiny.take(3)
    rows = lax.broadcasted_iota(jnp.int32, sums_ref.shape, 0)
    sums_ref[...] = jnp.where(rows < 3, bufs[4], bufs[3])
    ring.arrive()
    for copy in swaps:
        copy.wait_send()
    tiny.finish()
    ring.finish()
    each(0, n, total.sent)


def reduce_input(partial, source, base, gain, small, grads, pieces, call_id):
    n = len(pieces)
    smem = pl.BlockSpec(memory_space=pltpu.SMEM)
    hbm, vmem = pl.BlockSpec(memory_space=pl.ANY), pl.BlockSpec(memory_space=pltpu.VMEM)
    rows, columns = partial.shape
    quarter, inner = rows // Y, grads[0].shape[1] // Y
    wide = grads[0].shape[1]
    shares = n * STEP - wide
    return pl.pallas_call(
        functools.partial(input_kernel, pieces, len(grads)),
        out_shape=[
            jax.ShapeDtypeStruct(partial.shape, F32),
            jax.ShapeDtypeStruct((48, inner), F32),
            jax.ShapeDtypeStruct((48, shares), F32),
            jax.ShapeDtypeStruct((16, columns), F32),
        ],
        in_specs=[vmem, hbm, vmem, vmem] + [vmem] * 5 + [smem] * 2 + [hbm] * len(grads),
        out_specs=[vmem] * 4,
        scratch_shapes=[pltpu.VMEM((quarter, columns), source.dtype)]
        + ring_scratch(quarter, columns)
        + [
            pltpu.VMEM((48, wide), F32),
            pltpu.VMEM((3, 48, inner), F32),
            pltpu.SemaphoreType.DMA((1,)),
        ]
        + sems(12, 3)
        + [pltpu.VMEM((5, 16, columns), F32), pltpu.VMEM((10, 16, columns), F32)]
        + sems(10)
        + scatter_scratch(n, STEP),
        compiler_params=pltpu.CompilerParams(
            collective_id=call_id, has_side_effects=True, vmem_limit_bytes=56 << 20
        ),
    )(partial, source, base, gain, *small, *grads)


HEAD = 64
PAIR = 128
NEG = -1e30


def rows_at(i, size):
    return pl.ds(pl.multiple_of(i * size, size), size)


def lane_is(shape, index):
    return lax.broadcasted_iota(jnp.int32, shape, len(shape) - 1) == index


def first_head(shape):
    return lax.broadcasted_iota(jnp.int32, shape, len(shape) - 1) < HEAD


def halves_mean(values):
    first = first_head(values.shape)
    low = jnp.sum(jnp.where(first, values, 0.0), axis=1, keepdims=True) * (1.0 / HEAD)
    high = jnp.sum(jnp.where(first, 0.0, values), axis=1, keepdims=True) * (1.0 / HEAD)
    return low, high


def one_row(ref, index):
    rows = ref[...]
    picked = lax.broadcasted_iota(jnp.int32, rows.shape, 0) == index
    return jnp.sum(jnp.where(picked, rows, 0.0), axis=0, keepdims=True)


def running_sum(values, backward=False):
    count = values.shape[0]
    row = lax.broadcasted_iota(jnp.int32, values.shape, 0)
    shift = 1
    while shift < count:
        if backward:
            moved = jnp.where(row < count - shift, pltpu.roll(values, count - shift, 0), 0.0)
        else:
            moved = jnp.where(row >= shift, pltpu.roll(values, shift, 0), 0.0)
        values = values + moved
        shift *= 2
    return values


def mm(left, right):
    return jnp.dot(left, right, preferred_element_type=F32)


def mm_t(left, right):
    return lax.dot_general(left, right, (((1,), (1,)), ((), ())), preferred_element_type=F32)


def t_mm(left, right):
    return lax.dot_general(left, right, (((0,), (0,)), ((), ())), preferred_element_type=F32)


def whole(shape):
    return pl.BlockSpec(shape, lambda *_: (0,) * len(shape), pipeline_mode=pl.Buffered(1))


def struct(*shape, t=F32):
    return jax.ShapeDtypeStruct(shape, t)


def local_call(kernel, grid, in_specs, out_specs, out_shape, scratch, limit, flops, moved, call_id=None):
    return pl.pallas_call(
        kernel,
        grid_spec=pltpu.PrefetchScalarGridSpec(
            num_scalar_prefetch=1,
            grid=(grid,),
            in_specs=in_specs,
            out_specs=out_specs,
            scratch_shapes=scratch,
        ),
        out_shape=out_shape,
        compiler_params=pltpu.CompilerParams(
            vmem_limit_bytes=limit << 20,
            collective_id=call_id,
            has_side_effects=call_id is not None,
        ),
        cost_estimate=pl.CostEstimate(
            flops=flops * 10**9, bytes_accessed=moved * 10**6, transcendentals=4 * 10**6
        ),
    )


def forward_kernel(
    length_ref, x_ref, gain_ref, wq_ref, wk_ref, wv_ref, wo_ref, wf_ref, bf_ref, w_ref,
    low_out, qn_ref, kn_ref, v_ref, sig_ref, att_ref, stat_ref, decay_ref, gated_out, full_out,
    top_s, row_s, q_s, k_s, w_s, pre_s, gs, ws, wf_s, bf_s, low_ref, gated_ref, full_ref, osem, *sem,
):
    step = pl.program_id(0)
    seq = x_ref.shape[0]
    length = length_ref[0]
    here = Place()
    me, right, left, far = (lax.rem(here.my + by, Y) for by in (0, 1, 3, 2))
    sibling, right1, left1, right2, left2 = here.peers()
    c, p1, p2, half = here.c, here.p1, here.p2, seq // 2
    mine = ws.at[c, p2, p1, me]
    cross_order = (p2, here.l2, here.r2, here.o2)

    def plane(j):
        return link(mine, mine, *sem[2:4], j, (here.dp, (right, far, left)[j]))

    def torus(stage, j):
        if stage == 0:
            at, spots, to = (lambda p: ws.at[c, p2, p]), (p1, here.l1, here.r1), (right1, left1)
        else:
            at, spots, to = (lambda p: ws.at[c, p]), (p2, here.l2, here.r2), (right2, left2)
        spot, part, side = ((0, 0, 0), (0, 1, 0), (0, 0, 1), (0, 1, 1), (1, 0, 0), (2, 1, 1))[j]
        piece = at(spots[spot]).at[2 * part : 2 * part + 2]
        return link(piece, piece, *sem[4 + 2 * stage : 6 + 2 * stage], j, to[side])

    def cross(j):
        piece = ws.at[c, cross_order[j]]
        return link(piece, piece, *sem[8:10], j, sibling)

    def gate(pair, j):
        owner, part, to = (
            (me, 0, right), (me, 1, right), (me, 0, left), (me, 1, left), (left, 0, right), (right, 1, left)
        )[j]
        piece = gs.at[pair, owner, part * half : part * half + half]
        return link(piece, piece, *sem[0:2], pair * 6 + j, (here.dp, to))

    def flush(j):
        src, dst = ((low_ref, low_out), (full_ref, full_out), (gated_ref, gated_out))[j]
        return pltpu.make_async_copy(src, dst, osem.at[j])

    def pass_on(make):
        make(0).wait_recv()
        make(4).start()
        make(3).wait_recv()
        make(5).start()

    def arrived(make):
        for j in (1, 2, 4, 5):
            make(j).wait_recv()

    @pl.when(step == 0)
    def _():
        tall, wide = ws.shape[4], ws.shape[5]
        two = w_ref[
            pl.ds(pl.multiple_of(here.chip // 2 * (2 * tall), 16), 2 * tall),
            pl.ds(pl.multiple_of(c * wide, 128), wide),
        ].astype(F32)
        mine[...] = jnp.where(lax.rem(here.chip, 2) == 0, two[0:tall], two[tall:])
        meet([(here.dp, right), (here.dp, left), (here.dp, far)] + here.peers())
        for j in range(3):
            plane(j).start()

    @pl.when(step == 0)
    def _():
        def norm(i, carry):
            at = rows_at(i, 128)
            x = x_ref[at, :].astype(F32)
            r = lax.rsqrt(jnp.mean(x * x, axis=1, keepdims=True) + EPSILON)
            low_ref[at, :] = (x * r * gain_ref[...].astype(F32)).astype(jnp.bfloat16)
            return carry

        lax.fori_loop(0, seq // 128, norm, 0)
        flush(0).start()
        heads = wf_ref.shape[0]
        wf_s[...] = jnp.zeros_like(wf_s)
        wf_s[0:heads, :] = wf_ref[...]
        bf_s[...] = jnp.zeros_like(bf_s)
        bf_s[0:1, 0:heads] = bf_ref[...].astype(F32)
        pre = mm_t(low_ref[...], wf_s[...]) + bf_s[0:1, :]
        fall = jnp.minimum(pre, 0.0) - jnp.log1p(jnp.exp(-jnp.abs(pre)))
        decay = running_sum(fall)
        row = lax.broadcasted_iota(jnp.int32, decay.shape, 0)
        final = jnp.sum(jnp.where(row == length - 1, decay, 0.0), axis=0, keepdims=True)
        decay_ref[0] = decay
        decay_ref[1] = jax.nn.sigmoid(-pre)
        top_s[...] = jnp.where(row < length, decay, final)
        row_s[...] = jnp.where(row < length, decay, -NEG).T[0:8]

    for j, ref in enumerate((wq_ref, wk_ref, wv_ref, wo_ref)):
        w_s[:, j * PAIR : j * PAIR + PAIR] = ref[...]
    pre_s[...] = mm(low_ref[...], w_s[...])

    def norms(i, carry):
        at = rows_at(i, 128)
        for j, n_ref, s, col in ((0, qn_ref, q_s, 0), (1, kn_ref, k_s, 2)):
            pre = pre_s[at, j * PAIR : j * PAIR + PAIR]
            a, b = halves_mean(pre * pre)
            a, b = lax.rsqrt(a + EPSILON), lax.rsqrt(b + EPSILON)
            n = pre * jnp.where(first_head(pre.shape), a, b)
            n_ref[at, :] = n
            s[at, :] = n.astype(jnp.bfloat16)
            here = jnp.where(lane_is(pre.shape, col), a, jnp.where(lane_is(pre.shape, col + 1), b, 0.0))
            stat_ref[at, :] = here if col == 0 else stat_ref[at, :] + here
        v_ref[at, :] = pre_s[at, 2 * PAIR : 3 * PAIR].astype(jnp.bfloat16)
        sig_ref[at, :] = jax.nn.sigmoid(pre_s[at, 3 * PAIR : 4 * PAIR])
        return carry

    lax.fori_loop(0, seq // 128, norms, 0)

    @pl.when(step == 0)
    def _():
        for j in range(3):
            plane(j).wait_recv()
        for j in range(4):
            torus(0, j).start()

    @pl.when(step == 1)
    def _():
        arrived(lambda j: torus(0, j))
        for j in range(4):
            torus(1, j).start()
        cross(0).start()

    @pl.when(step == 2)
    def _():
        pass_on(lambda j: torus(1, j))

    lines = [one_row(row_s, 2 * step + head) for head in (0, 1)]
    first = first_head((128, PAIR))
    zero = jnp.zeros((128, PAIR), jnp.bfloat16)
    upper = lax.broadcasted_iota(jnp.int32, (128, 128), 1) > lax.broadcasted_iota(
        jnp.int32, (128, 128), 0
    )
    for i in range(seq // 128):
        at, n = slice(i * 128, i * 128 + 128), i * 128 + 128
        q = q_s[at, :]
        both = []
        for head in (0, 1):
            own = jnp.where(first, q, zero) if head == 0 else jnp.where(first, zero, q)
            s = mm_t(own, k_s[0:n, :])
            column = jnp.sum(
                jnp.where(lane_is((128, PAIR), 2 * step + head), top_s[at, :], 0.0), axis=1, keepdims=True
            )
            s = s * (HEAD ** (-0.5)) + (column - lines[head][:, 0:n])
            diagonal = jnp.where(upper, NEG, s[:, n - 128 :])
            s = diagonal if i == 0 else jnp.concatenate([s[:, : n - 128], diagonal], axis=1)
            p = jnp.exp(s)
            p = p * (1.0 / jnp.sum(p, axis=1, keepdims=True))
            both.append(mm(p.astype(jnp.bfloat16), v_ref[0:n, :]))
        out = jnp.where(first, both[0], both[1])
        att_ref[at, :] = out
        gs[step, me, at, :] = (out * sig_ref[at, :]).astype(jnp.bfloat16).astype(F32)
    for j in range(4):
        gate(step, j).start()

    @pl.when(step == 0)
    def _():
        pass_on(lambda j: torus(0, j))

    @pl.when(step > 0)
    def _():
        pass_on(lambda j: gate(step - 1, j))

    @pl.when(step == pl.num_programs(0) - 1)
    def _():
        torus(1, 1).wait_recv()
        cross(1).start()
        torus(1, 2).wait_recv()
        cross(2).start()
        torus(1, 4).wait_recv()
        torus(1, 5).wait_recv()
        cross(3).start()
        pass_on(lambda j: gate(step, j))
        for j in range(4):
            cross(j).wait_recv()
        tall, wide, shard = ws.shape[4], ws.shape[5], w_ref.shape[0]

        def turn(k, carry):
            y, m = k // 8, lax.rem(k, 8)
            x, z = m // 2, lax.rem(m, 2) * 2
            rows = pl.ds(pl.multiple_of(y * shard + m * 2 * tall, 16), 2 * tall)
            for h, one, two in (
                (0, ws[0, z, x, y], ws[0, z + 1, x, y]),
                (1, ws[1, x, z, y], ws[1, x, z + 1, y]),
            ):
                both = jnp.concatenate([one, two], axis=0).astype(jnp.bfloat16)
                full_ref[rows, h * wide : h * wide + wide] = both
            return carry

        lax.fori_loop(0, 8 * Y, turn, 0)
        flush(1).start()
        pairs = gs.shape[0]
        for pair in range(pairs):
            arrived(lambda j: gate(pair, j))
            for y in range(Y):
                lane = (y * pairs + pair) * PAIR
                gated_ref[:, lane : lane + PAIR] = gs[pair, y].astype(jnp.bfloat16)
        flush(2).start()
        for j in range(3):
            flush(j).wait()
            plane(j).wait_send()
        for stage in (0, 1):
            for j in range(6):
                torus(stage, j).wait_send()
        for j in range(4):
            cross(j).wait_send()
        for pair in range(pairs):
            for j in range(6):
                gate(pair, j).wait_send()


def forward_attention(tokens, length, gain, wq, wk, wv, wo, wf, bf, w_out, call_id):
    seq, width = tokens.shape
    heads = wq.shape[1]
    weights = pl.BlockSpec((width, PAIR), lambda i, _: (0, i))
    lanes = pl.BlockSpec((seq, PAIR), lambda i, _: (0, i))
    low = jnp.bfloat16
    return local_call(
        forward_kernel,
        heads // PAIR,
        [whole((seq, width)), whole((1, width))] + [weights] * 4 + [whole(wf.shape), whole(bf.shape), whole(w_out.shape)],
        [HBM] + [lanes] * 6 + [whole((2, seq, PAIR)), HBM, HBM],
        [
            struct(seq, width, t=low), struct(seq, heads), struct(seq, heads), struct(seq, heads, t=low),
            struct(seq, heads), struct(seq, heads), struct(seq, heads),
            struct(2, seq, PAIR), struct(seq, heads * Y, t=low), struct(heads * Y, width, t=low),
        ],
        [
            pltpu.VMEM((seq, PAIR), F32),
            pltpu.VMEM((8, seq), F32),
            pltpu.VMEM((seq, PAIR), low),
            pltpu.VMEM((seq, PAIR), low),
            pltpu.VMEM((width, 4 * PAIR), low),
            pltpu.VMEM((seq, 4 * PAIR), F32),
            pltpu.VMEM((heads // PAIR, Y, seq, PAIR), F32),
            pltpu.VMEM((2, 4, 4, Y, heads // 16, width // 2), F32),
            pltpu.VMEM((PAIR, width), low),
            pltpu.VMEM((8, PAIR), F32),
            pltpu.VMEM((seq, width), low),
            pltpu.VMEM((seq, width), low),
            pltpu.VMEM((heads * Y, width), low),
            pltpu.SemaphoreType.DMA((3,)),
        ]
        + sems(6 * (heads // PAIR), 3, 6, 6, 4),
        56, 6, 20, call_id,
    )(length, tokens, gain, wq, wk, wv, wo, wf, bf, w_out)


def copier(sem):
    count = iter(range(sem.shape[0]))

    def copy(src, dst):
        return load(src, dst, sem.at[next(count)])

    return copy


def mlp_forward_kernel(
    length_ref, x_in, cot_in, gated_in, gain_ref, wo_in, wg_in, wu_in, wd_in,
    mid_out, low_out, grad_out, gate_out, up_out, hid_out, out_out, sums_ref,
    x_ref, cot_ref, gated_ref, wo_ref, wg_ref, wu_ref, wd_ref,
    mid_ref, low_ref, grad_ref, gate_ref, up_ref, hid_ref, out_ref, sem,
):
    seq, width = x_ref.shape
    length = length_ref[0]
    tile, units = wo_ref.shape[2], hid_ref.shape[1] // 2
    copy = copier(sem)
    columns = lambda j, size: pl.ds(pl.multiple_of(j * size, size), size)
    outer = lambda j: pltpu.make_async_copy(
        wo_in.at[:, columns(j, tile)], wo_ref.at[j], sem.at[sem.shape[0] - 2 + j]
    )
    need = copy(gated_in, gated_ref)
    outer(0).start()
    need_x = copy(x_in, x_ref)
    need.wait()
    outer(1).start()
    need_cot = copy(cot_in, cot_ref)
    weights = [copy(wg_in, wg_ref), copy(wu_in, wu_ref), copy(wd_in, wd_ref)]
    kept = lax.broadcasted_iota(jnp.int32, (seq, 1), 0) < length
    flushes = []

    def project(j):
        at = columns(j, tile)
        outer(j).wait()
        branch = mm(gated_ref[...], wo_ref[j])
        x = x_ref[:, at].astype(F32)
        mid_ref[:, at] = x + branch
        sums_ref[0:1, at] = jnp.sum(jnp.where(kept, x * x, 0.0), axis=0, keepdims=True)
        sums_ref[1:2, at] = jnp.sum(jnp.where(kept, branch * branch, 0.0), axis=0, keepdims=True)

    need_x.wait()
    each(0, 2, project)
    flushes.append(copy(mid_ref, mid_out))

    def norm(i, carry):
        at = rows_at(i, 128)
        mid = mid_ref[at, :]
        r = lax.rsqrt(jnp.mean(mid * mid, axis=1, keepdims=True) + EPSILON)
        low_ref[at, :] = (mid * r * gain_ref[...].astype(F32)).astype(jnp.bfloat16)
        return carry

    lax.fori_loop(0, seq // 128, norm, 0)
    flushes.append(copy(low_ref, low_out))
    weights[0].wait()
    weights[1].wait()

    def hidden(j):
        at = columns(j, units)
        gate_ref[:, at] = mm(low_ref[...], wg_ref[:, at])
        up_ref[:, at] = mm(low_ref[...], wu_ref[:, at])
        gate = gate_ref[:, at]
        hid_ref[:, at] = (gate * jax.nn.sigmoid(gate) * up_ref[:, at]).astype(jnp.bfloat16)

    each(0, 2, hidden)
    for src, dst in ((gate_ref, gate_out), (up_ref, up_out), (hid_ref, hid_out)):
        flushes.append(copy(src, dst))
    need_cot.wait()
    grad_ref[...] = jnp.where(kept, cot_ref[...].astype(F32), 0.0).astype(jnp.bfloat16)
    flushes.append(copy(grad_ref, grad_out))
    weights[2].wait()
    result = lambda j: pltpu.make_async_copy(
        out_ref.at[:, columns(j, tile)], out_out.at[:, columns(j, tile)], sem.at[sem.shape[0] - 4 + j]
    )

    def project_out(j):
        at = columns(j, tile)
        out_ref[:, at] = mm(hid_ref[...], wd_ref[:, at])
        result(j).start()

    each(0, 2, project_out)
    flushes += [result(0), result(1)]
    for c in flushes:
        c.wait()


def mlp_forward(tokens, cotangent, length, gated, gain, wo, wg, wu, wd):
    seq, width = tokens.shape
    hidden = wg.shape[1]
    low = jnp.bfloat16
    smem = pl.BlockSpec(memory_space=pltpu.SMEM)
    outs = [
        struct(seq, width), struct(seq, width, t=low), struct(seq, width, t=low),
        struct(seq, hidden), struct(seq, hidden), struct(seq, hidden, t=low), struct(seq, width),
    ]
    return pl.pallas_call(
        mlp_forward_kernel,
        in_specs=[smem, HBM, HBM, HBM, VMEM] + [HBM] * 4,
        out_specs=[HBM] * 7 + [VMEM],
        out_shape=outs + [struct(2, width)],
        scratch_shapes=[
            pltpu.VMEM((seq, width), low),
            pltpu.VMEM((seq, width), low),
            pltpu.VMEM((seq, width), low),
            pltpu.VMEM((2, width, width // 2), low),
            pltpu.VMEM((width, hidden), low),
            pltpu.VMEM((width, hidden), low),
            pltpu.VMEM((hidden, width), low),
        ]
        + [pltpu.VMEM(out.shape, out.dtype) for out in outs]
        + [pltpu.SemaphoreType.DMA((18,))],
        compiler_params=pltpu.CompilerParams(vmem_limit_bytes=58 << 20),
    )(length, tokens, cotangent, gated, gain, wo, wg, wu, wd)


def reduce_links(rows, x, opp, nbr, held, sem):
    dp, me = lax.axis_index("dp"), lax.axis_index("mp")
    right, left, far = lax.rem(me + 1, Y), lax.rem(me + 3, Y), lax.rem(me + 2, Y)
    q, h = rows // Y, rows // Y // 2

    def message(name):
        src, dst, to = {
            "oR": (lambda: rows_of(x, far * q, h), lambda: opp.at[0], right),
            "oL": (lambda: rows_of(x, far * q + h, h), lambda: opp.at[1], left),
            "iR": (lambda: rows_of(x, right * q + h, h), lambda: nbr.at[0, h:q], right),
            "iL": (lambda: rows_of(x, left * q, h), lambda: nbr.at[1, 0:h], left),
            "dR": (lambda: held.at[0], lambda: nbr.at[0, 0:h], right),
            "dL": (lambda: held.at[1], lambda: nbr.at[1, h:q], left),
        }[name]
        return link(src(), dst(), *sem, STEPS.index(name), (dp, to))

    return message, me, right, left, [(dp, right), (dp, left)]


def mlp_backward_kernel(
    length_ref, grad_in, low_in, gate_in, up_in, hid_in, wd_in, wg_in, wu_in, x_ref, mid_ref,
    back_out, gd_out, gg_out, gu_out, layer_ref, square_ref,
    grad_ref, low_ref, gate_ref, up_ref, hid_ref, wd_ref, wg_ref, wu_ref,
    dg_s, du_s, back_s, bufs, opp, nbr, held, own_s, mid_s, csem, *sem,
):
    seq, width = grad_ref.shape
    units = wd_ref.shape[0] // 2
    low16 = jnp.bfloat16
    message, me, right, left, peers = reduce_links(seq, x_ref, opp, nbr, held, sem)
    q, h = seq // Y, seq // Y // 2
    copy = copier(csem)
    need = [
        copy(grad_in, grad_ref),
        copy(wd_in.at[0:units], wd_ref.at[0:units]),
        copy(gate_in.at[:, 0:units], gate_ref.at[:, 0:units]),
        copy(up_in.at[:, 0:units], up_ref.at[:, 0:units]),
    ]
    meet(peers)
    for name in STEPS[:4]:
        message(name).start()
    for c in need[0:2]:
        c.wait()
    next_low, next_hid = copy(low_in, low_ref), copy(hid_in, hid_ref)
    more = [
        copy(wd_in.at[units:], wd_ref.at[units:]),
        copy(gate_in.at[:, units:], gate_ref.at[:, units:]),
        copy(up_in.at[:, units:], up_ref.at[:, units:]),
    ]
    weights = [copy(wg_in, wg_ref), copy(wu_in, wu_ref)]
    adds = [
        copy(rows_of(x_ref, right * q, h), held.at[0]),
        copy(rows_of(x_ref, left * q + h, h), held.at[1]),
        copy(rows_of(x_ref, me * q, q), own_s),
        copy(rows_of(mid_ref, me * q, q), mid_s),
    ]
    spots = (gd_out, gg_out, gu_out)
    columns = lambda j: pl.ds(pl.multiple_of(j * units, units), units)
    flush = lambda j, which: pltpu.make_async_copy(
        bufs.at[which, j], spots[which].at[:, columns(j)], csem.at[csem.shape[0] - 6 + which * 2 + j]
    )

    def write(which, left_of, right_of, j):
        slot, at = bufs.at[which, j], columns(j)

        def rows(i, carry):
            part = rows_at(i, 768)
            slot[part, :] = t_mm(left_of[:, part], right_of[:, at])
            return carry

        lax.fori_loop(0, width // 768, rows, 0)
        flush(j, which).start()

    def tile(j):
        at = columns(j)

        @pl.when(j == 1)
        def _():
            for c in more:
                c.wait()

        grad = mm_t(grad_ref[...], wd_ref[at, :])

        @pl.when(j == 0)
        def _():
            for c in need[2:4]:
                c.wait()

        gate = gate_ref[:, at]
        sig = jax.nn.sigmoid(gate)
        dg_s[:, at] = (grad * up_ref[:, at] * (sig * (1.0 + gate * (1.0 - sig)))).astype(low16)
        du_s[:, at] = (grad * (gate * sig)).astype(low16)

        @pl.when(j == 0)
        def _():
            next_low.wait()
            next_hid.wait()

        write(0, grad_ref, hid_ref, j)
        write(1, low_ref, dg_s, j)

        @pl.when(j == 1)
        def _():
            for part, (come, go) in enumerate((("oR", "dR"), ("oL", "dL"))):
                message(come).wait_recv()
                adds[part].wait()
                held[part] = held[part] + opp[part]
                message(go).start()

        write(2, low_ref, du_s, j)

    each(0, 2, tile)
    for c in weights:
        c.wait()

    def back(i, carry):
        rows = rows_at(i, 768)
        back_s[:, rows] = mm_t(dg_s[...], wg_ref[rows, :])
        back_s[:, rows] = back_s[:, rows] + mm_t(du_s[...], wu_ref[rows, :])
        return carry

    lax.fori_loop(0, width // 768, back, 0)
    last = copy(back_s, back_out)
    adds[2].wait()
    adds[3].wait()
    sums = 0.0
    for part, names in enumerate((("dR", "iL"), ("iR", "dL"))):
        for name in names:
            message(name).wait_recv()
        at = slice(part * h, part * h + h)
        branch = own_s[at, :] + nbr[0, at] + nbr[1, at]
        layer_ref[at, :] = (mid_s[at, :] + branch).astype(low16).astype(F32)
        row = lax.broadcasted_iota(jnp.int32, (h, 1), 0) + (me * q + part * h)
        kept = jnp.where(row < length_ref[0], branch * branch, 0.0)
        sums = sums + jnp.sum(kept, axis=0, keepdims=True)
    square_ref[...] = sums
    last.wait()
    for j in (0, 1):
        for which in range(3):
            flush(j, which).wait()
    for name in STEPS[:6]:
        message(name).wait_send()


def mlp_backward(length, grad, low, gate, up, hid, wg, wu, wd, branch, mid, call_id):
    seq, width = low.shape
    hidden = wg.shape[1]
    quarter = seq // Y
    low16 = jnp.bfloat16
    smem = pl.BlockSpec(memory_space=pltpu.SMEM)
    inputs = (grad, low, gate, up, hid, wd, wg, wu)
    return pl.pallas_call(
        mlp_backward_kernel,
        in_specs=[smem] + [HBM] * 10,
        out_specs=[HBM] * 4 + [VMEM] * 2,
        out_shape=[struct(seq, width)] + [struct(width, hidden)] * 3
        + [struct(quarter, width), struct(1, width)],
        scratch_shapes=[pltpu.VMEM(a.shape, a.dtype) for a in inputs]
        + [pltpu.VMEM((seq, hidden), low16)] * 2
        + [pltpu.VMEM((seq, width), F32), pltpu.VMEM((3, 2, width, hidden // 2), F32)]
        + ring_scratch(quarter, width)
        + [pltpu.VMEM((quarter, width), F32)] * 2
        + [pltpu.SemaphoreType.DMA((22,))]
        + sems(6),
        compiler_params=pltpu.CompilerParams(
            vmem_limit_bytes=62 << 20, collective_id=call_id, has_side_effects=True
        ),
    )(length, *inputs, branch, mid)


def backward_kernel(
    length_ref, gg_ref, low_ref, qn_ref, kn_ref, v_ref, sig_ref, att_ref, stat_ref,
    decay_ref, wq_ref, wk_ref, wv_ref, wo_ref, wf_ref, own_ref, gated_ref, layer_ref,
    back_out, four_out, gout_out, gf_ref, bias_ref, out_ref,
    k_s, do_s, line_s, dq_s, dk_s, dv_s, all_s, fall_s, w_s, wf_s, lay_s, back_ref, wide_s, osem, *sem,
):
    step = pl.program_id(0)
    seq, width = low_ref.shape
    length = length_ref[0]
    low16 = jnp.bfloat16
    wide = 4 * PAIR
    dp, me = lax.axis_index("dp"), lax.axis_index("mp")
    right, left = lax.rem(me + 1, Y), lax.rem(me + 3, Y)
    q, h = seq // Y, seq // Y // 2

    def spread(j):
        owner, part, to = (
            (me, 0, right), (me, 1, right), (me, 0, left), (me, 1, left), (left, 0, right), (right, 1, left)
        )[j]
        piece = rows_of(lay_s, owner * q + part * h, h)
        return link(piece, piece, *sem, j, (dp, to))

    @pl.when(step == 0)
    def _():
        rows_of(lay_s, me * q, q)[...] = layer_ref[...]
        meet([(dp, right), (dp, left)])
        for j in range(4):
            spread(j).start()

    @pl.when(step == 1)
    def _():
        spread(0).wait_recv()
        spread(4).start()
        spread(3).wait_recv()
        spread(5).start()

    @pl.when(step == 0)
    def _():
        heads = wf_ref.shape[0]
        wf_s[...] = jnp.zeros_like(wf_s)
        wf_s[0:heads, :] = wf_ref[...]
        decay = decay_ref[0]
        row = lax.broadcasted_iota(jnp.int32, decay.shape, 0)
        final = jnp.sum(jnp.where(row == length - 1, decay, 0.0), axis=0, keepdims=True)
        line_s[...] = jnp.where(row < length, decay, final).T[0:8]
        fall_s[...] = jnp.zeros_like(fall_s)

    base = pl.multiple_of(step * wide, wide)
    part = lambda j: pl.ds(pl.multiple_of(base + j * PAIR, PAIR), PAIR)
    for j, w_ref in enumerate((wq_ref, wk_ref, wv_ref, wo_ref)):
        w_s[:, part(j)] = w_ref[...]
    first = first_head((seq, PAIR))
    gg, sig = gg_ref[...], sig_ref[...]
    do_s[...] = (gg * sig).astype(low16)
    all_s[:, part(3)] = (gg * att_ref[...] * sig * (1.0 - sig)).astype(low16)
    k_s[...] = kn_ref[...].astype(low16)
    dk_s[...] = jnp.zeros_like(dk_s)
    dv_s[...] = jnp.zeros_like(dv_s)
    row = lax.broadcasted_iota(jnp.int32, (seq, PAIR), 0)
    columns, lines = [], [one_row(line_s, 2 * step + head) for head in (0, 1)]
    for head in (0, 1):
        column = jnp.sum(
            jnp.where(lane_is((seq, PAIR), 2 * step + head), decay_ref[0], 0.0), axis=1, keepdims=True
        )
        columns.append(jnp.where(row[:, 0:1] < length, column, -NEG))
    block = first_head((128, PAIR))
    zero = jnp.zeros((128, PAIR), low16)
    lower = lax.broadcasted_iota(jnp.int32, (128, 128), 0) > lax.broadcasted_iota(
        jnp.int32, (128, 128), 1
    )
    for i in range(seq // 128):
        at, n = slice(i * 128, i * 128 + 128), i * 128 + 128
        query = qn_ref[at, :].astype(low16)
        do = do_s[at, :]
        pieces = []
        for head in (0, 1):
            pick = (lambda t: jnp.where(block, t, zero)) if head == 0 else (lambda t: jnp.where(block, zero, t))
            own_q, own_do = pick(query), pick(do)
            one = jnp.where(lane_is((128, PAIR), 2 * step + head), 1.0, 0.0).astype(low16)
            s = mm_t(k_s[0:n, :], own_q)
            s = s * (HEAD ** (-0.5)) + (lines[head][:, at] - columns[head][0:n])
            diagonal = jnp.where(lower, NEG, s[n - 128 :, :])
            s = diagonal if i == 0 else jnp.concatenate([s[: n - 128, :], diagonal], axis=0)
            p = jnp.exp(s)
            p = p * (1.0 / jnp.sum(p, axis=0, keepdims=True))
            gp = mm_t(v_ref[0:n, :], own_do)
            ds = (p * (gp - jnp.sum(p * gp, axis=0, keepdims=True))).astype(low16)
            dv_s[0:n, :] = dv_s[0:n, :] + mm(p.astype(low16), own_do)
            dk_s[0:n, :] = dk_s[0:n, :] + mm(ds, jnp.concatenate([own_q, one], axis=1))
            mark = jnp.where(lane_is((n, PAIR), 2 * step + head), 1.0, 0.0).astype(low16)
            pieces.append(t_mm(ds, jnp.concatenate([k_s[0:n, :], mark], axis=1)))
        dq_s[at, :] = jnp.where(block, pieces[0][:, 0:PAIR], pieces[1][:, 0:PAIR])
        fall_s[at, :] = fall_s[at, :] + pieces[0][:, PAIR:] + pieces[1][:, PAIR:]
    fall_s[...] = fall_s[...] - dk_s[:, PAIR:]
    stat = stat_ref[...]
    for e, n_ref, col, to in ((dq_s, qn_ref, 0, 0), (dk_s, kn_ref, 2, 1)):
        e = e[:, 0:PAIR] * (HEAD ** (-0.5))
        n = n_ref[...]
        a, b = halves_mean(e * n)
        r = jnp.where(first, stat[:, col : col + 1], stat[:, col + 1 : col + 2])
        all_s[:, part(to)] = (r * (e - n * jnp.where(first, a, b))).astype(low16)
    all_s[:, part(2)] = dv_s[...].astype(low16)
    slot = lax.rem(step, 2)

    def flush(j, at, step):
        columns = pl.ds(pl.multiple_of(step * wide, wide), wide)
        out = (four_out, gout_out)[j].at[:, columns]
        return pltpu.make_async_copy(wide_s.at[at, j], out, osem.at[at * 2 + j])

    @pl.when(step == 2)
    def _():
        for j in (0, 1):
            flush(j, 0, 0).wait()

    def grads(k, carry):
        rows = rows_at(k, 768)
        wide_s[slot, 0, rows, :] = t_mm(low_ref[:, rows], all_s[:, pl.ds(base, wide)])
        wide_s[slot, 1, rows, :] = t_mm(own_ref[:, rows].astype(low16), gated_ref[...])
        return carry

    lax.fori_loop(0, width // 768, grads, 0)
    for j in (0, 1):
        flush(j, slot, step).start()

    @pl.when(step == pl.num_programs(0) - 1)
    def _():
        fall = running_sum(fall_s[...], backward=True) * decay_ref[1]
        fall = fall.astype(low16)
        bias_ref[...] = jnp.sum(fall.astype(F32), axis=0, keepdims=True)
        gf_ref[...] = t_mm(fall, low_ref[...])[0:8]

        def tail(k, carry):
            rows = rows_at(k, 768)
            back_ref[:, rows] = mm_t(all_s[...], w_s[rows, :])
            back_ref[:, rows] = back_ref[:, rows] + mm(fall, wf_s[:, rows])
            return carry

        lax.fori_loop(0, width // 768, tail, 0)
        last = load(back_ref, back_out, osem.at[4])
        for j in (1, 2, 4, 5):
            spread(j).wait_recv()
        out_ref[...] = lay_s[...].astype(low16)
        for at, done in ((1, 1), (0, 2)):
            for j in (0, 1):
                flush(j, at, done).wait()
        last.wait()
        for j in range(6):
            spread(j).wait_send()


def backward_attention(place, gg, low, qn, kn, v, sig, att, stat, decay, wq, wk, wv, wo, wf, own, gated, layer, call_id):
    seq, width = low.shape
    heads = wq.shape[1]
    weights = pl.BlockSpec((width, PAIR), lambda i, _: (0, i))
    lanes = pl.BlockSpec((seq, PAIR), lambda i, _: (0, i))
    full = whole((seq, width))
    low16 = jnp.bfloat16
    return local_call(
        backward_kernel,
        heads // PAIR,
        [lanes, full] + [lanes] * 6 + [whole((2, seq, PAIR))] + [weights] * 4
        + [whole(wf.shape), whole(own.shape)]
        + [pl.BlockSpec((own.shape[0], 4 * PAIR), lambda i, _: (lax.axis_index("mp"), i)), whole(layer.shape)],
        [HBM, HBM, HBM, whole((8, width)), whole((1, PAIR)), full],
        [
            struct(seq, width), struct(width, 4 * heads), struct(width, width), struct(8, width),
            struct(1, PAIR), struct(seq, width, t=low16),
        ],
        [
            pltpu.VMEM((seq, PAIR), low16),
            pltpu.VMEM((seq, PAIR), low16),
            pltpu.VMEM((8, seq), F32),
            pltpu.VMEM((seq, PAIR), F32),
            pltpu.VMEM((seq, 2 * PAIR), F32),
            pltpu.VMEM((seq, PAIR), F32),
            pltpu.VMEM((seq, 4 * heads), low16),
            pltpu.VMEM((seq, PAIR), F32),
            pltpu.VMEM((width, 4 * heads), low16),
            pltpu.VMEM((PAIR, width), low16),
            pltpu.VMEM((seq, width), F32),
            pltpu.VMEM((seq, width), F32),
            pltpu.VMEM((2, 2, width, 4 * PAIR), F32),
            pltpu.SemaphoreType.DMA((5,)),
        ]
        + sems(6),
        62, 14, 50, call_id,
    )(place, gg, low, qn, kn, v, sig, att, stat, decay, wq, wk, wv, wo, wf, own, gated, layer)


def finish_kernel(
    grad_in, layer_in, wout_in, four_in, mlp_in, sums_in,
    grad_ref, layer_ref, wout_ref, q_ref, k_ref, v_ref, o_ref, gate_ref, up_ref, down_ref,
    gain_ref, gain2_ref, fall_ref,
    sem,
):
    rows = grad_in.shape[0] // 4
    copies = []
    for j in range(4):
        for src, dst, at in ((grad_in, grad_ref, j), (layer_in, layer_ref, 4 + j)):
            part = slice(j * rows, j * rows + rows)
            copies.append(load(src.at[part], dst.at[part], sem.at[at]))
    wout_ref[...] = wout_in[...].T
    inner = q_ref.shape[1]
    for j, ref in enumerate((q_ref, k_ref, v_ref, o_ref)):
        for pair in range(inner // PAIR):
            lane = (pair * 4 + j) * PAIR
            ref[:, pair * PAIR : pair * PAIR + PAIR] = four_in[:, lane : lane + PAIR]
    units = gate_ref.shape[1]
    down_ref[...] = mlp_in[:, 0:units].T
    gate_ref[...] = mlp_in[:, units : 2 * units]
    up_ref[:, 0:STEP] = mlp_in[:, 2 * units : 2 * units + STEP]
    up_ref[:, STEP:] = four_in[:, 4 * inner : 4 * inner + STEP]
    share, width = gain_ref.shape[1], sums_in.shape[1]
    row = lax.broadcasted_iota(jnp.int32, (width, share), 0)
    lane = lax.broadcasted_iota(jnp.int32, (width, share), 1)
    pick = jnp.where(row == lane + lax.axis_index("dp") * share, 1.0, 0.0)
    own = jnp.dot(
        sums_in[...], pick, precision=lax.Precision.HIGHEST, preferred_element_type=F32
    )
    gain_ref[...] = own[0:1]
    gain2_ref[...] = own[1:2]
    fall_ref[...] = own[3 : 3 + fall_ref.shape[1]].T
    for copy in copies:
        copy.wait()


def finish(grad, layer, out_share, share, mlp_share, sums, heads):
    rows, inner = out_share.shape
    units = mlp_share.shape[1] * 2 // 5
    return pl.pallas_call(
        finish_kernel,
        out_shape=[
            struct(*grad.shape), struct(*layer.shape, t=layer.dtype), struct(inner, rows),
            *[struct(rows, inner)] * 4, struct(rows, units), struct(rows, units), struct(units, rows),
            struct(1, rows), struct(1, rows), struct(rows, heads),
        ],
        in_specs=[HBM, HBM] + [VMEM] * 4,
        out_specs=[HBM, HBM] + [VMEM] * 11,
        scratch_shapes=[pltpu.SemaphoreType.DMA((8,))],
        compiler_params=pltpu.CompilerParams(vmem_limit_bytes=16 << 20),
    )(grad, layer, out_share, share, mlp_share, sums)


def per_device(
    tokens, lengths, buckets, out_cotangent, gain_attn, w_query, w_key, w_value, w_outgate,
    w_forget, b_forget, w_out, gain_mlp, w_gate, w_up, w_down,
):
    x, cotangent = tokens[0], out_cotangent[0]
    model_width = x.shape[1]
    heads = w_forget.shape[1]
    gain_in, gain_mid = gain_attn[None], gain_mlp[None]
    weights = (w_query, w_key, w_value, w_outgate, w_forget.T)
    low, qn, kn, value, sig, attended, stat, decay, gated, w_full = forward_attention(
        x, lengths, gain_in, *weights, b_forget[None], w_out, 0
    )
    middle, mid_low, grad_rows, gate, up, hidden, mlp_local, squares = mlp_forward(
        x, cotangent, lengths, gated, gain_mid, w_full, w_gate, w_up, w_down
    )
    mid_local, g_down, g_gate, g_up, layer_own, mlp_square = mlp_backward(
        lengths, grad_rows, mid_low, gate, up, hidden, w_gate, w_up, w_down, mlp_local, middle, 1
    )
    grad_own, gg, mlp_share, mlp_gain = reduce_middle(
        mid_local, middle, grad_rows, gain_mid, w_full, [g_down, g_gate, g_up],
        ((0, 0), (0, 1), (1, 0), (1, 1), (2, 0)), 2,
    )
    in_local, g_four, g_out, g_fall, bias, layer_out = backward_attention(
        lengths, gg, low, qn, kn, value, sig, attended, stat, decay, *weights, grad_own, gated,
        layer_own, 3,
    )
    small = (mlp_gain, g_fall, squares, mlp_square, bias, lengths, buckets)
    input_grad, out_share, share, sums = reduce_input(
        in_local, x, grad_own, gain_in, small, [g_out, g_four, g_up],
        ((0, 0), (0, 1), (0, 2), (1, 0), (1, 1), (1, 2), (2, 1)), 4,
    )
    (
        input_grad, layer_out, g_out, g_query, g_key, g_value, g_outgate, g_gate, g_up, g_down,
        g_gain, g_gain_mid, g_fall,
    ) = finish(input_grad, layer_out, out_share, share, mlp_share, sums, heads)
    totals = jnp.stack([sums[9, :NBUCKET], sums[9, NBUCKET : 2 * NBUCKET], sums[2, :NBUCKET]])
    rms = jnp.sqrt(totals / (sums[9, 2 * NBUCKET : 3 * NBUCKET] * model_width)[None, :])
    return (
        layer_out[None],
        input_grad[None],
        g_gain[0],
        g_query,
        g_key,
        g_value,
        g_outgate,
        g_fall,
        sums[10, :heads],
        g_out,
        g_gain_mid[0],
        g_gate,
        g_up,
        g_down,
        rms,
    )


def solution(mesh):
    placed = (
        P("dp", None, None),
        P("dp"),
        P("dp"),
        P("dp", None, None),
        P(),
        P(None, "mp"),
        P(None, "mp"),
        P(None, "mp"),
        P(None, "mp"),
        P(None, "mp"),
        P("mp"),
        P("mp", None),
        P(),
        P(None, "mp"),
        P(None, "mp"),
        P("mp", None),
    )
    return jax.shard_map(
        per_device,
        mesh=mesh,
        in_specs=placed,
        out_specs=(
            P("dp", None, None),
            P("dp", None, None),
            P("dp"),
            P("dp", "mp"),
            P("dp", "mp"),
            P("dp", "mp"),
            P("dp", "mp"),
            P("dp", "mp"),
            P("mp"),
            P("mp", "dp"),
            P("dp"),
            P("dp", "mp"),
            P("dp", "mp"),
            P("mp", "dp"),
            P(),
        ),
        check_vma=False,
    )
```

```python
import functools

import jax
import jax.numpy as jnp
from jax import lax
from jax.experimental import pallas as pl
from jax.experimental.pallas import tpu as pltpu
from jax.sharding import PartitionSpec as P

NBUCKET = 4


EPSILON = 1e-06


MESH = pl.DeviceIdType.MESH
F32 = jnp.float32
Y = 4
STEP = 512
HBM = pl.BlockSpec(memory_space=pl.ANY)
VMEM = pl.BlockSpec(memory_space=pltpu.VMEM)
STEPS = ("oR", "oL", "iR", "iL", "dR", "dL", "gRa", "gRb", "gLa", "gLb", "fR", "fL")


def rows_of(ref, start, count):
    return ref.at[pl.ds(pl.multiple_of(start, 8), count)]


def meet(devices):
    barrier = pltpu.get_barrier_semaphore()
    for device in devices:
        pl.semaphore_signal(barrier, inc=1, device_id=device, device_id_type=MESH)
    pl.semaphore_wait(barrier, len(devices))


def link(src, dst, ssem, rsem, at, device):
    return pltpu.make_async_remote_copy(
        src_ref=src,
        dst_ref=dst,
        send_sem=ssem.at[at],
        recv_sem=rsem.at[at],
        device_id=device,
        device_id_type=MESH,
    )


def push(*args):
    copy = link(*args)
    copy.start()
    return copy


class YRing:
    def __init__(self, rows, waves, ssem, rsem):
        self.sems = (ssem, rsem)
        self.dp, self.me = lax.axis_index("dp"), lax.axis_index("mp")
        self.right, self.left = lax.rem(self.me + 1, Y), lax.rem(self.me + 3, Y)
        self.far = lax.rem(self.me + 2, Y)
        self.quarter, self.half = rows // Y, rows // Y // 2
        self.tall = self.half // waves
        self.sent = {}

    def neighbours(self):
        return [(self.dp, self.right), (self.dp, self.left)]

    def send(self, name, wave, src, dst, to):
        at = wave * 6 + STEPS.index(name)
        self.sent[name, wave] = push(src, dst, *self.sems, at, (self.dp, to))

    def rows(self, x, owner, part, wave):
        return rows_of(x, owner * self.quarter + part * self.half + wave * self.tall, self.tall)

    def fetch(self, x, held, own, sem):
        self.loads = [
            load(rows_of(x, self.right * self.quarter, self.half), held.at[0], sem.at[0]),
            load(rows_of(x, self.left * self.quarter + self.half, self.half), held.at[1], sem.at[1]),
            load(rows_of(x, self.me * self.quarter, self.quarter), own, sem.at[2]),
        ]

    def start(self, x, opp, nbr, wave):
        w = slice(wave * self.tall, wave * self.tall + self.tall)
        low = slice(self.half + wave * self.tall, self.half + wave * self.tall + self.tall)
        self.send("oR", wave, self.rows(x, self.far, 0, wave), opp.at[0, w], self.right)
        self.send("oL", wave, self.rows(x, self.far, 1, wave), opp.at[1, w], self.left)
        self.send("iR", wave, self.rows(x, self.right, 1, wave), nbr.at[0, low], self.right)
        self.send("iL", wave, self.rows(x, self.left, 0, wave), nbr.at[1, w], self.left)

    def relay(self, opp, nbr, held, wave):
        w = slice(wave * self.tall, wave * self.tall + self.tall)
        low = slice(self.half + wave * self.tall, self.half + wave * self.tall + self.tall)
        for part, (come, go, into, to) in enumerate(
            (("oR", "dR", nbr.at[0, w], self.right), ("oL", "dL", nbr.at[1, low], self.left))
        ):
            self.sent[come, wave].wait_recv()
            if wave == 0:
                self.loads[part].wait()
            held[part, w] = held[part, w] + opp[part, w]
            self.send(go, wave, held.at[part, w], into, to)

    def collect(self, own, nbr, part, wave):
        if part == 0 and wave == 0:
            self.loads[2].wait()
        for name in (("dR", "iL"), ("iR", "dL"))[part]:
            self.sent[name, wave].wait_recv()
        start = part * self.half + wave * self.tall
        at = slice(start, start + self.tall)
        return at, own[at, :] + nbr[0, at] + nbr[1, at]

    def spread(self, part, own, block):
        into, tag = block(self.me, part), "ab"[part]
        mine = own.at[part * self.half : part * self.half + self.half]
        self.send("gR" + tag, 0, mine, into, self.right)
        self.send("gL" + tag, 0, mine, into, self.left)

    def forward(self, block):
        self.sent["gRa", 0].wait_recv()
        self.send("fR", 0, block(self.left, 0), block(self.left, 0), self.right)
        self.sent["gLb", 0].wait_recv()
        self.send("fL", 0, block(self.right, 1), block(self.right, 1), self.left)

    def arrive(self):
        for name in ("gRb", "gLa", "fR", "fL"):
            self.sent[name, 0].wait_recv()

    def finish(self):
        for copy in self.sent.values():
            copy.wait_send()


def ring_scratch(quarter, columns):
    return [
        pltpu.VMEM((2, quarter // 2, columns), F32),
        pltpu.VMEM((2, quarter, columns), F32),
        pltpu.VMEM((2, quarter // 2, columns), F32),
    ]


def sems(*counts):
    return [pltpu.SemaphoreType.DMA((n,)) for n in counts for _ in (0, 1)]


class Place:
    def __init__(self):
        self.dp, self.my = lax.axis_index("dp"), lax.axis_index("mp")
        c, z, x = lax.rem(self.dp, 2), lax.rem(self.dp // 2, 4), self.dp // 8
        self.c, self.sib, self.chip = c, self.dp + 1 - 2 * c, x * 4 + z
        self.st1, self.st2 = 4 - 3 * c, 1 + 3 * c
        self.p1, self.p2 = x + c * (z - x), z + c * (x - z)
        step = lambda p, by: lax.rem(p + by, 4)
        self.r1, self.l1, self.o1 = (step(self.p1, by) for by in (1, 3, 2))
        self.r2, self.l2, self.o2 = (step(self.p2, by) for by in (1, 3, 2))

    def device(self, a, b):
        return ((a * self.st1 + b * self.st2) * 2 + self.c, self.my)

    def peers(self):
        return [
            (self.sib, self.my),
            self.device(self.r1, self.p2),
            self.device(self.l1, self.p2),
            self.device(self.p1, self.r2),
            self.device(self.p1, self.l2),
        ]


class ScatterSum:
    def __init__(self, here, sources, own, other, near, last, asem, bsem, lsem, ssem, rsem):
        self.here, self.sources = here, sources
        self.own, self.other, self.near, self.last = own, other, near, last
        self.asem, self.bsem, self.lsem, self.ssem, self.rsem = asem, bsem, lsem, ssem, rsem
        self.n = own.shape[0]
        self.sibling, *to = here.peers()
        self.to = (to[0:2], to[2:4])

    def message(self, name, k, stage):
        at = (k * 2 + stage) * 6 + STEPS.index(name)
        device = self.to[stage][0 if name[1] == "R" else 1]
        here, own = self.here, self.own.at[k]
        if stage:
            own, into, cut = own.at[here.p1], self.last.at[k], (slice(0, 24), slice(24, 48))
            far, right, left = here.o2, here.r2, here.l2
        else:
            into, cut = self.near.at[k], (slice(0, 2), slice(2, 4))
            far, right, left = here.o1, here.r1, here.l1
        row, part, slot = {
            "oR": (far, 0, 0),
            "oL": (far, 1, 1),
            "iR": (right, 1, 3),
            "iL": (left, 0, 4),
            "dR": (right, 0, 2),
            "dL": (left, 1, 5),
        }[name]
        return link(own.at[row, cut[part]], into.at[slot], self.ssem, self.rsem, at, device)

    def whole(self, k):
        own, other = self.own.at[k], self.other.at[k]
        return link(own, other, self.asem, self.bsem, k, self.sibling)

    def exchange(self, k):
        here = self.here
        ref, start, width = self.sources[k]

        def source(block):
            return ref.at[pl.ds(pl.multiple_of(block * 48, 16), 48), pl.ds(start, width)]

        def cross(i, carry):
            a, b = i // 4, lax.rem(i, 4)
            block = source((a * here.st2 + b * here.st1) * 2 + 1 - here.c)
            push(block, self.other.at[k, a, b], self.asem, self.bsem, k, self.sibling)
            return carry

        def fetch(i, carry):
            a, b = i // 4, lax.rem(i, 4)
            block = source((a * here.st1 + b * here.st2) * 2 + here.c)
            pltpu.make_async_copy(block, self.own.at[k, a, b], self.lsem.at[k]).start()
            return carry

        lax.fori_loop(0, 16, cross, 0)
        lax.fori_loop(0, 16, fetch, 0)

    def first(self, k):
        here, own, other = self.here, self.own, self.other
        pltpu.make_async_copy(own.at[k], own.at[k], self.lsem.at[k]).wait()
        self.whole(k).wait_recv()

        def add(p):
            def body(b, carry):
                own[k, p, b] = own[k, p, b] + other[k, p, b]
                return carry

            lax.fori_loop(0, 4, body, 0)

        add(here.o1)
        self.message("oR", k, 0).start()
        self.message("oL", k, 0).start()
        add(here.r1)
        self.message("iR", k, 0).start()
        add(here.l1)
        self.message("iL", k, 0).start()
        add(here.p1)

    def first_relay(self, k):
        here, own, near = self.here, self.own, self.near

        def add(p, at, slot):
            def body(b, carry):
                own[k, p, at + b] = own[k, p, at + b] + near[k, slot, b]
                return carry

            lax.fori_loop(0, 2, body, 0)

        self.message("oR", k, 0).wait_recv()
        add(here.r1, 0, 0)
        self.message("dR", k, 0).start()
        self.message("oL", k, 0).wait_recv()
        add(here.l1, 2, 1)
        self.message("dL", k, 0).start()

    def second(self, k):
        here, own, near = self.here, self.own, self.near
        for name in ("iR", "dR", "iL", "dL"):
            self.message(name, k, 0).wait_recv()

        def add(p):
            h, b = p // 2, lax.rem(p, 2)
            own[k, here.p1, p] = own[k, here.p1, p] + near[k, 2 + h, b] + near[k, 4 + h, b]

        add(here.o2)
        self.message("oR", k, 1).start()
        self.message("oL", k, 1).start()
        add(here.r2)
        self.message("iR", k, 1).start()
        add(here.l2)
        self.message("iL", k, 1).start()
        add(here.p2)

    def second_relay(self, k):
        here, own, last = self.here, self.own, self.last
        self.message("oR", k, 1).wait_recv()
        own[k, here.p1, here.r2, 0:24] = own[k, here.p1, here.r2, 0:24] + last[k, 0]
        self.message("dR", k, 1).start()
        self.message("oL", k, 1).wait_recv()
        own[k, here.p1, here.l2, 24:48] = own[k, here.p1, here.l2, 24:48] + last[k, 1]
        self.message("dL", k, 1).start()

    def result(self, k, out, at):
        here, own, last = self.here, self.own, self.last
        width = own.shape[4]
        for name in ("iR", "dR", "iL", "dL"):
            self.message(name, k, 1).wait_recv()
        columns = pl.ds(pl.multiple_of(at * width, 128), width)
        out[0:24, columns] = own[k, here.p1, here.p2, 0:24] + last[k, 2] + last[k, 4]
        out[24:48, columns] = own[k, here.p1, here.p2, 24:48] + last[k, 3] + last[k, 5]

    def sent(self, k):
        self.whole(k).wait_send()
        for stage in (0, 1):
            for name in STEPS[:6]:
                self.message(name, k, stage).wait_send()


def each(low, high, step):
    def body(k, carry):
        step(k)
        return carry

    lax.fori_loop(low, high, body, 0)


class SmallSum:
    def __init__(self, here, bufs, landed, ssem, rsem):
        self.bufs, self.landed, self.ssem, self.rsem = bufs, landed, ssem, rsem
        turn = lambda p, by: lax.rem(p + by, 4)
        self.stages = [
            [(here.sib, here.my)],
            [here.device(turn(here.p1, by), here.p2) for by in (1, 2, 3)],
            [here.device(here.p1, turn(here.p2, by)) for by in (1, 2, 3)],
            [(here.dp, turn(here.my, by)) for by in (1, 2, 3)],
        ]
        self.far = [self.stages[1][1], self.stages[2][1], self.stages[3][1]]
        self.sent = []

    def send(self, stage):
        for to in self.stages[stage]:
            at = len(self.sent)
            copy = push(self.bufs.at[stage], self.landed.at[at], self.ssem, self.rsem, at, to)
            self.sent.append(copy)

    def take(self, stage):
        value, count = self.bufs[stage], len(self.stages[stage])
        for at in range(len(self.sent) - count, len(self.sent)):
            self.sent[at].wait_recv()
            value = value + self.landed[at]
        self.bufs[stage + 1] = value

    def finish(self):
        for copy in self.sent:
            copy.wait_send()


def scatter_scratch(n, w):
    return [
        pltpu.VMEM((n, 4, 4, 48, w), F32),
        pltpu.VMEM((n, 4, 4, 48, w), F32),
        pltpu.VMEM((n, 6, 2, 48, w), F32),
        pltpu.VMEM((n, 6, 24, w), F32),
        pltpu.SemaphoreType.DMA((n,)),
        pltpu.SemaphoreType.DMA((n,)),
        pltpu.SemaphoreType.DMA((n,)),
        pltpu.SemaphoreType.DMA((12 * n,)),
        pltpu.SemaphoreType.DMA((12 * n,)),
    ]


def scatter_sources(refs, pieces):
    return [(refs[which], at * STEP, STEP) for which, at in pieces]


def norm_back(value, source, base, gain):
    source = source.astype(F32)
    r = lax.rsqrt(jnp.mean(source * source, axis=1, keepdims=True) + EPSILON)
    n = source * r
    e = value * gain.astype(F32)
    inner = jnp.mean(e * n, axis=1, keepdims=True)
    return base.astype(F32) + r * (e - n * inner), jnp.sum(value * n, axis=0, keepdims=True)


def load(ref, scratch, sem):
    copy = pltpu.make_async_copy(ref, scratch, sem)
    copy.start()
    return copy


def middle_kernel(pieces, count, x_ref, source_ref, base_ref, gain_ref, w_ref, *refs):
    ins, refs = refs[:count], refs[count:]
    grad_ref, gg_ref, share_ref, sums_ref = refs[:4]
    source_s, base_s, w_s, opp, nbr, held, own_s, blocks, csem, *sem = refs[4:17]
    here, ring = Place(), YRing(x_ref.shape[0], 2, *sem[0:2])
    total = ScatterSum(here, scatter_sources(ins, pieces), *refs[17:])
    n = total.n
    far = (ring.dp, ring.far)
    meet(ring.neighbours() + [far] + here.peers())
    ring.start(x_ref, opp, nbr, 0)
    q, h = ring.quarter, ring.half
    ring.fetch(x_ref, held, own_s, csem)
    for k in range(n):
        total.exchange(k)
    loads = [
        load(rows_of(source_ref, ring.me * q, q), source_s, csem.at[3]),
        load(rows_of(base_ref, ring.me * q, q), base_s, csem.at[4]),
        load(w_ref, w_s, csem.at[5]),
    ]
    ring.relay(opp, nbr, held, 0)
    ring.start(x_ref, opp, nbr, 1)
    each(0, n, total.first)
    each(0, n - 2, total.first_relay)
    ring.relay(opp, nbr, held, 1)
    for copy in loads:
        copy.wait()
    sums, swaps, keeps = 0.0, [], []
    inner = gg_ref.shape[1]
    for wave in (0, 1):
        for part in (0, 1):
            at, value = ring.collect(own_s, nbr, part, wave)
            value, more = norm_back(value, source_s[at, :], base_s[at, :], gain_ref[...])
            grad_ref[at, :] = value
            sums = sums + more
        tall = ring.tall
        low = jnp.concatenate(
            [grad_ref[part * h + wave * tall : part * h + wave * tall + tall, :] for part in (0, 1)], axis=0
        ).astype(jnp.bfloat16)
        for j, by in enumerate((2, 1, 3, 0)):
            to = lax.rem(ring.me + by, Y)
            blocks[wave, j] = mm_t(low, rows_of(w_s, to * inner, inner)[...])
            for part in (0, 1):
                src = blocks.at[wave, j, part * tall : part * tall + tall]
                into = rows_of(gg_ref, ring.me * q + part * h + wave * tall, tall)
                if by:
                    at = (wave * 3 + j) * 2 + part
                    swaps.append(push(src, into, *sem[2:4], at, (ring.dp, to)))
                else:
                    keeps.append(load(src, into, csem.at[6 + wave * 2 + part]))
        if wave == 0:
            each(n - 2, n, total.first_relay)
    sums_ref[...] = sums
    each(0, n, total.second)
    each(0, n, total.second_relay)
    each(0, n, lambda k: total.result(k, share_ref, k))
    for copy in swaps:
        copy.wait_recv()
    for copy in keeps:
        copy.wait()
    for copy in swaps:
        copy.wait_send()
    ring.finish()
    each(0, n, total.sent)


def reduce_middle(partial, source, base, gain, w_full, grads, pieces, call_id):
    n = len(pieces)
    hbm, vmem = pl.BlockSpec(memory_space=pl.ANY), pl.BlockSpec(memory_space=pltpu.VMEM)
    rows, columns = partial.shape
    quarter, inner = rows // Y, w_full.shape[0] // Y
    return pl.pallas_call(
        functools.partial(middle_kernel, pieces, len(grads)),
        out_shape=[
            jax.ShapeDtypeStruct((quarter, columns), F32),
            jax.ShapeDtypeStruct((rows, inner), F32),
            jax.ShapeDtypeStruct((48, n * STEP), F32),
            jax.ShapeDtypeStruct((1, columns), F32),
        ],
        in_specs=[hbm, hbm, hbm, vmem, hbm] + [hbm] * len(grads),
        out_specs=[vmem, hbm, vmem, vmem],
        scratch_shapes=[
            pltpu.VMEM((quarter, columns), source.dtype),
            pltpu.VMEM((quarter, columns), base.dtype),
            pltpu.VMEM(w_full.shape, w_full.dtype),
        ]
        + ring_scratch(quarter, columns)
        + [
            pltpu.VMEM((quarter, columns), F32),
            pltpu.VMEM((2, 4, quarter // 2, inner), F32),
            pltpu.SemaphoreType.DMA((10,)),
        ]
        + sems(12, 12)
        + scatter_scratch(n, STEP),
        compiler_params=pltpu.CompilerParams(
            collective_id=call_id, has_side_effects=True, vmem_limit_bytes=56 << 20
        ),
    )(partial, source, base, gain, w_full, *grads)


def input_kernel(
    pieces, count, x_ref, source_ref, base_ref, gain_ref, other_ref, fall_ref, square_ref, more_ref,
    bias_ref, length_ref, bucket_ref, *refs
):
    ins, refs = refs[:count], refs[count:]
    out_ref, out_share_ref, share_ref, sums_ref = refs[:4]
    source_s, opp, nbr, held, own_s, mine_s, wide_s, landed, csem, *sem = refs[4:17]
    bufs, arrived, asem, bsem = refs[17:21]
    here, ring = Place(), YRing(x_ref.shape[0], 1, *sem[0:2])
    total = ScatterSum(here, scatter_sources(ins, pieces), *refs[21:])
    tiny = SmallSum(here, bufs, arrived, asem, bsem)
    n, first = total.n, wide_s.shape[1] // STEP
    meet(ring.neighbours() + here.peers() + tiny.far)
    ring.start(x_ref, opp, nbr, 0)
    q, h = ring.quarter, ring.half
    ring.fetch(x_ref, held, own_s, csem)
    copy = load(rows_of(source_ref, ring.me * q, q), source_s, csem.at[3])
    for k in range(n):
        total.exchange(k)
    each(0, n // 2, total.first)
    ring.relay(opp, nbr, held, 0)
    each(n // 2, n, total.first)
    each(0, n - 2, total.first_relay)
    copy.wait()
    block = lambda owner, part: rows_of(out_ref, owner * q + part * h, h)
    sums = 0.0
    for part in (0, 1):
        at, value = ring.collect(own_s, nbr, part, 0)
        value, more = norm_back(value, source_s[at, :], base_ref[at, :], gain_ref[...])
        mine_s[at, :] = value
        ring.spread(part, mine_s, block)
        sums = sums + more
    kept = load(mine_s, rows_of(out_ref, ring.me * q, q), csem.at[4])
    bufs[0, 0:1, :] = sums
    bufs[0, 1:2, :] = other_ref[...]
    bufs[0, 8:16, :] = jnp.zeros_like(bufs[0, 8:16, :])
    bufs[0, 2:3, :] = jnp.zeros((1, sums_ref.shape[1]), F32)
    bufs[0, 3:9, :] = fall_ref[0:6, :]
    lane = lax.broadcasted_iota(jnp.int32, (1, PAIR), 1)
    both = jnp.sum(square_ref[...], axis=1, keepdims=True)
    in_bucket = lambda value: jnp.where(lane == bucket_ref[0], value, 0.0)
    bufs[0, 2:3, 0:PAIR] = in_bucket(jnp.sum(more_ref[...], axis=1, keepdims=True))
    for at, value in enumerate((both[0:1], both[1:2], length_ref[0].astype(F32))):
        bufs[0, 9:10, at * PAIR : at * PAIR + PAIR] = in_bucket(value)
    bufs[0, 10:11, 0:PAIR] = bias_ref[...]
    tiny.send(0)
    each(n - 2, n, total.first_relay)
    each(0, n, total.second)
    ring.forward(block)
    tiny.take(0)
    tiny.send(1)
    each(0, n, total.second_relay)
    tiny.take(1)
    tiny.send(2)
    each(0, first, lambda k: total.result(k, wide_s, k))
    inner = landed.shape[2]
    swaps = []
    for j, by in enumerate((2, 1, 3)):
        to = lax.rem(ring.me + by, Y)
        columns = pl.ds(pl.multiple_of(to * inner, 128), inner)
        swaps.append(push(wide_s.at[:, columns], landed.at[j], *sem[2:4], j, (ring.dp, to)))
    each(first, n, lambda k: total.result(k, share_ref, k - first))
    tiny.take(2)
    tiny.send(3)
    own = wide_s[:, pl.ds(pl.multiple_of(ring.me * inner, 128), inner)]
    for j, copy in enumerate(swaps):
        copy.wait_recv()
        own = own + landed[j]
    out_share_ref[...] = own
    tiny.take(3)
    rows = lax.broadcasted_iota(jnp.int32, sums_ref.shape, 0)
    sums_ref[...] = jnp.where(rows < 3, bufs[4], bufs[3])
    ring.arrive()
    kept.wait()
    for copy in swaps:
        copy.wait_send()
    tiny.finish()
    ring.finish()
    each(0, n, total.sent)


def reduce_input(partial, source, base, gain, small, grads, pieces, call_id):
    n = len(pieces)
    smem = pl.BlockSpec(memory_space=pltpu.SMEM)
    hbm, vmem = pl.BlockSpec(memory_space=pl.ANY), pl.BlockSpec(memory_space=pltpu.VMEM)
    rows, columns = partial.shape
    quarter, inner = rows // Y, grads[0].shape[1] // Y
    wide = grads[0].shape[1]
    shares = n * STEP - wide
    return pl.pallas_call(
        functools.partial(input_kernel, pieces, len(grads)),
        out_shape=[
            jax.ShapeDtypeStruct(partial.shape, F32),
            jax.ShapeDtypeStruct((48, inner), F32),
            jax.ShapeDtypeStruct((48, shares), F32),
            jax.ShapeDtypeStruct((16, columns), F32),
        ],
        in_specs=[hbm, hbm, vmem, vmem] + [vmem] * 5 + [smem] * 2 + [hbm] * len(grads),
        out_specs=[hbm] + [vmem] * 3,
        scratch_shapes=[pltpu.VMEM((quarter, columns), source.dtype)]
        + ring_scratch(quarter, columns)
        + [
            pltpu.VMEM((quarter, columns), F32),
            pltpu.VMEM((quarter, columns), F32),
            pltpu.VMEM((48, wide), F32),
            pltpu.VMEM((3, 48, inner), F32),
            pltpu.SemaphoreType.DMA((5,)),
        ]
        + sems(12, 3)
        + [pltpu.VMEM((5, 16, columns), F32), pltpu.VMEM((10, 16, columns), F32)]
        + sems(10)
        + scatter_scratch(n, STEP),
        compiler_params=pltpu.CompilerParams(
            collective_id=call_id, has_side_effects=True, vmem_limit_bytes=56 << 20
        ),
    )(partial, source, base, gain, *small, *grads)


HEAD = 64
PAIR = 128
NEG = -1e30


def rows_at(i, size):
    return pl.ds(pl.multiple_of(i * size, size), size)


def lane_is(shape, index):
    return lax.broadcasted_iota(jnp.int32, shape, len(shape) - 1) == index


def first_head(shape):
    return lax.broadcasted_iota(jnp.int32, shape, len(shape) - 1) < HEAD


def halves_mean(values):
    first = first_head(values.shape)
    low = jnp.sum(jnp.where(first, values, 0.0), axis=1, keepdims=True) * (1.0 / HEAD)
    high = jnp.sum(jnp.where(first, 0.0, values), axis=1, keepdims=True) * (1.0 / HEAD)
    return low, high


def one_row(ref, index):
    rows = ref[...]
    picked = lax.broadcasted_iota(jnp.int32, rows.shape, 0) == index
    return jnp.sum(jnp.where(picked, rows, 0.0), axis=0, keepdims=True)


def running_sum(values, backward=False):
    count = values.shape[0]
    row = lax.broadcasted_iota(jnp.int32, values.shape, 0)
    shift = 1
    while shift < count:
        if backward:
            moved = jnp.where(row < count - shift, pltpu.roll(values, count - shift, 0), 0.0)
        else:
            moved = jnp.where(row >= shift, pltpu.roll(values, shift, 0), 0.0)
        values = values + moved
        shift *= 2
    return values


def mm(left, right):
    return jnp.dot(left, right, preferred_element_type=F32)


def mm_t(left, right):
    return lax.dot_general(left, right, (((1,), (1,)), ((), ())), preferred_element_type=F32)


def t_mm(left, right):
    return lax.dot_general(left, right, (((0,), (0,)), ((), ())), preferred_element_type=F32)


def whole(shape):
    return pl.BlockSpec(shape, lambda *_: (0,) * len(shape), pipeline_mode=pl.Buffered(1))


def struct(*shape, t=F32):
    return jax.ShapeDtypeStruct(shape, t)


def local_call(kernel, grid, in_specs, out_specs, out_shape, scratch, limit, flops, moved, call_id=None):
    return pl.pallas_call(
        kernel,
        grid_spec=pltpu.PrefetchScalarGridSpec(
            num_scalar_prefetch=1,
            grid=(grid,),
            in_specs=in_specs,
            out_specs=out_specs,
            scratch_shapes=scratch,
        ),
        out_shape=out_shape,
        compiler_params=pltpu.CompilerParams(
            vmem_limit_bytes=limit << 20,
            collective_id=call_id,
            has_side_effects=call_id is not None,
        ),
        cost_estimate=pl.CostEstimate(
            flops=flops * 10**9, bytes_accessed=moved * 10**6, transcendentals=4 * 10**6
        ),
    )


def forward_kernel(
    length_ref, x_ref, gain_ref, wq_ref, wk_ref, wv_ref, wo_ref, wf_ref, bf_ref, w_ref,
    low_out, qn_ref, kn_ref, v_ref, sig_ref, att_ref, stat_ref, decay_ref, gated_out, full_out,
    top_s, row_s, q_s, k_s, w_s, pre_s, gs, ws, wf_s, bf_s, low_ref, gated_ref, full_ref, osem, *sem,
):
    step = pl.program_id(0)
    seq = x_ref.shape[0]
    length = length_ref[0]
    here = Place()
    me, right, left, far = (lax.rem(here.my + by, Y) for by in (0, 1, 3, 2))
    sibling, right1, left1, right2, left2 = here.peers()
    c, p1, p2, half = here.c, here.p1, here.p2, seq // 2
    mine = ws.at[c, p2, p1, me]
    cross_order = (p2, here.l2, here.r2, here.o2)

    def plane(j):
        return link(mine, mine, *sem[2:4], j, (here.dp, (right, far, left)[j]))

    def torus(stage, j):
        if stage == 0:
            at, spots, to = (lambda p: ws.at[c, p2, p]), (p1, here.l1, here.r1), (right1, left1)
        else:
            at, spots, to = (lambda p: ws.at[c, p]), (p2, here.l2, here.r2), (right2, left2)
        spot, part, side = ((0, 0, 0), (0, 1, 0), (0, 0, 1), (0, 1, 1), (1, 0, 0), (2, 1, 1))[j]
        piece = at(spots[spot]).at[2 * part : 2 * part + 2]
        return link(piece, piece, *sem[4 + 2 * stage : 6 + 2 * stage], j, to[side])

    def cross(j):
        piece = ws.at[c, cross_order[j]]
        return link(piece, piece, *sem[8:10], j, sibling)

    def gate(pair, j):
        owner, part, to = (
            (me, 0, right), (me, 1, right), (me, 0, left), (me, 1, left), (left, 0, right), (right, 1, left)
        )[j]
        piece = gs.at[pair, owner, part * half : part * half + half]
        return link(piece, piece, *sem[0:2], pair * 6 + j, (here.dp, to))

    def flush(j):
        src, dst = ((low_ref, low_out), (full_ref, full_out), (gated_ref, gated_out))[j]
        return pltpu.make_async_copy(src, dst, osem.at[j])

    def pass_on(make):
        make(0).wait_recv()
        make(4).start()
        make(3).wait_recv()
        make(5).start()

    def arrived(make):
        for j in (1, 2, 4, 5):
            make(j).wait_recv()

    @pl.when(step == 0)
    def _():
        tall, wide = ws.shape[4], ws.shape[5]
        two = w_ref[
            pl.ds(pl.multiple_of(here.chip // 2 * (2 * tall), 16), 2 * tall),
            pl.ds(pl.multiple_of(c * wide, 128), wide),
        ].astype(F32)
        mine[...] = jnp.where(lax.rem(here.chip, 2) == 0, two[0:tall], two[tall:])
        meet([(here.dp, right), (here.dp, left), (here.dp, far)] + here.peers())
        for j in range(3):
            plane(j).start()

    @pl.when(step == 0)
    def _():
        def norm(i, carry):
            at = rows_at(i, 128)
            x = x_ref[at, :].astype(F32)
            r = lax.rsqrt(jnp.mean(x * x, axis=1, keepdims=True) + EPSILON)
            low_ref[at, :] = (x * r * gain_ref[...].astype(F32)).astype(jnp.bfloat16)
            return carry

        lax.fori_loop(0, seq // 128, norm, 0)
        flush(0).start()
        heads = wf_ref.shape[0]
        wf_s[...] = jnp.zeros_like(wf_s)
        wf_s[0:heads, :] = wf_ref[...]
        bf_s[...] = jnp.zeros_like(bf_s)
        bf_s[0:1, 0:heads] = bf_ref[...].astype(F32)
        pre = mm_t(low_ref[...], wf_s[...]) + bf_s[0:1, :]
        fall = jnp.minimum(pre, 0.0) - jnp.log1p(jnp.exp(-jnp.abs(pre)))
        decay = running_sum(fall)
        row = lax.broadcasted_iota(jnp.int32, decay.shape, 0)
        final = jnp.sum(jnp.where(row == length - 1, decay, 0.0), axis=0, keepdims=True)
        decay_ref[0] = decay
        decay_ref[1] = jax.nn.sigmoid(-pre)
        top_s[...] = jnp.where(row < length, decay, final)
        row_s[...] = jnp.where(row < length, decay, -NEG).T[0:8]

    for j, ref in enumerate((wq_ref, wk_ref, wv_ref, wo_ref)):
        w_s[:, j * PAIR : j * PAIR + PAIR] = ref[...]
    pre_s[...] = mm(low_ref[...], w_s[...])

    def norms(i, carry):
        at = rows_at(i, 128)
        for j, n_ref, s, col in ((0, qn_ref, q_s, 0), (1, kn_ref, k_s, 2)):
            pre = pre_s[at, j * PAIR : j * PAIR + PAIR]
            a, b = halves_mean(pre * pre)
            a, b = lax.rsqrt(a + EPSILON), lax.rsqrt(b + EPSILON)
            n = pre * jnp.where(first_head(pre.shape), a, b)
            n_ref[at, :] = n
            s[at, :] = n.astype(jnp.bfloat16)
            here = jnp.where(lane_is(pre.shape, col), a, jnp.where(lane_is(pre.shape, col + 1), b, 0.0))
            stat_ref[at, :] = here if col == 0 else stat_ref[at, :] + here
        v_ref[at, :] = pre_s[at, 2 * PAIR : 3 * PAIR].astype(jnp.bfloat16)
        sig_ref[at, :] = jax.nn.sigmoid(pre_s[at, 3 * PAIR : 4 * PAIR])
        return carry

    lax.fori_loop(0, seq // 128, norms, 0)

    @pl.when(step == 0)
    def _():
        for j in range(3):
            plane(j).wait_recv()
        for j in range(4):
            torus(0, j).start()

    @pl.when(step == 1)
    def _():
        arrived(lambda j: torus(0, j))
        for j in range(4):
            torus(1, j).start()
        cross(0).start()

    @pl.when(step == 2)
    def _():
        pass_on(lambda j: torus(1, j))

    lines = [one_row(row_s, 2 * step + head) for head in (0, 1)]
    first = first_head((128, PAIR))
    zero = jnp.zeros((128, PAIR), jnp.bfloat16)
    upper = lax.broadcasted_iota(jnp.int32, (128, 128), 1) > lax.broadcasted_iota(
        jnp.int32, (128, 128), 0
    )
    for i in range(seq // 128):
        at, n = slice(i * 128, i * 128 + 128), i * 128 + 128
        q = q_s[at, :]
        both = []
        for head in (0, 1):
            own = jnp.where(first, q, zero) if head == 0 else jnp.where(first, zero, q)
            s = mm_t(own, k_s[0:n, :])
            column = jnp.sum(
                jnp.where(lane_is((128, PAIR), 2 * step + head), top_s[at, :], 0.0), axis=1, keepdims=True
            )
            s = s * (HEAD ** (-0.5)) + (column - lines[head][:, 0:n])
            diagonal = jnp.where(upper, NEG, s[:, n - 128 :])
            s = diagonal if i == 0 else jnp.concatenate([s[:, : n - 128], diagonal], axis=1)
            p = jnp.exp(s)
            p = p * (1.0 / jnp.sum(p, axis=1, keepdims=True))
            both.append(mm(p.astype(jnp.bfloat16), v_ref[0:n, :]))
        out = jnp.where(first, both[0], both[1])
        att_ref[at, :] = out
        gs[step, me, at, :] = (out * sig_ref[at, :]).astype(jnp.bfloat16).astype(F32)
        if n % half == 0:
            gate(step, n // half - 1).start()
            gate(step, n // half + 1).start()

    @pl.when(step == 0)
    def _():
        pass_on(lambda j: torus(0, j))

    @pl.when(step > 0)
    def _():
        pass_on(lambda j: gate(step - 1, j))

    @pl.when(step == pl.num_programs(0) - 1)
    def _():
        torus(1, 1).wait_recv()
        cross(1).start()
        torus(1, 2).wait_recv()
        cross(2).start()
        torus(1, 4).wait_recv()
        torus(1, 5).wait_recv()
        cross(3).start()
        pass_on(lambda j: gate(step, j))
        for j in range(4):
            cross(j).wait_recv()
        tall, wide, shard = ws.shape[4], ws.shape[5], w_ref.shape[0]

        def turn(k, carry):
            y, m = k // 8, lax.rem(k, 8)
            x, z = m // 2, lax.rem(m, 2) * 2
            rows = pl.ds(pl.multiple_of(y * shard + m * 2 * tall, 16), 2 * tall)
            for h, one, two in (
                (0, ws[0, z, x, y], ws[0, z + 1, x, y]),
                (1, ws[1, x, z, y], ws[1, x, z + 1, y]),
            ):
                both = jnp.concatenate([one, two], axis=0).astype(jnp.bfloat16)
                full_ref[rows, h * wide : h * wide + wide] = both
            return carry

        lax.fori_loop(0, 8 * Y, turn, 0)
        flush(1).start()
        pairs = gs.shape[0]
        for pair in range(pairs):
            arrived(lambda j: gate(pair, j))
            for y in range(Y):
                lane = (y * pairs + pair) * PAIR
                gated_ref[:, lane : lane + PAIR] = gs[pair, y].astype(jnp.bfloat16)
        flush(2).start()
        for j in range(3):
            flush(j).wait()
            plane(j).wait_send()
        for stage in (0, 1):
            for j in range(6):
                torus(stage, j).wait_send()
        for j in range(4):
            cross(j).wait_send()
        for pair in range(pairs):
            for j in range(6):
                gate(pair, j).wait_send()


def forward_attention(tokens, length, gain, wq, wk, wv, wo, wf, bf, w_out, call_id):
    seq, width = tokens.shape
    heads = wq.shape[1]
    weights = pl.BlockSpec((width, PAIR), lambda i, _: (0, i))
    lanes = pl.BlockSpec((seq, PAIR), lambda i, _: (0, i))
    low = jnp.bfloat16
    return local_call(
        forward_kernel,
        heads // PAIR,
        [whole((seq, width)), whole((1, width))] + [weights] * 4 + [whole(wf.shape), whole(bf.shape), whole(w_out.shape)],
        [HBM] + [lanes] * 6 + [whole((2, seq, PAIR)), HBM, HBM],
        [
            struct(seq, width, t=low), struct(seq, heads), struct(seq, heads), struct(seq, heads, t=low),
            struct(seq, heads), struct(seq, heads), struct(seq, heads),
            struct(2, seq, PAIR), struct(seq, heads * Y, t=low), struct(heads * Y, width, t=low),
        ],
        [
            pltpu.VMEM((seq, PAIR), F32),
            pltpu.VMEM((8, seq), F32),
            pltpu.VMEM((seq, PAIR), low),
            pltpu.VMEM((seq, PAIR), low),
            pltpu.VMEM((width, 4 * PAIR), low),
            pltpu.VMEM((seq, 4 * PAIR), F32),
            pltpu.VMEM((heads // PAIR, Y, seq, PAIR), F32),
            pltpu.VMEM((2, 4, 4, Y, heads // 16, width // 2), F32),
            pltpu.VMEM((PAIR, width), low),
            pltpu.VMEM((8, PAIR), F32),
            pltpu.VMEM((seq, width), low),
            pltpu.VMEM((seq, width), low),
            pltpu.VMEM((heads * Y, width), low),
            pltpu.SemaphoreType.DMA((3,)),
        ]
        + sems(6 * (heads // PAIR), 3, 6, 6, 4),
        56, 6, 20, call_id,
    )(length, tokens, gain, wq, wk, wv, wo, wf, bf, w_out)


def copier(sem):
    count = iter(range(sem.shape[0]))

    def copy(src, dst):
        return load(src, dst, sem.at[next(count)])

    return copy


def mlp_forward_kernel(
    length_ref, x_in, cot_in, gated_in, gain_ref, wo_in, wg_in, wu_in, wd_in,
    mid_out, low_out, grad_out, gate_out, up_out, hid_out, out_out, sums_ref,
    x_ref, cot_ref, gated_ref, wo_ref, wg_ref, wu_ref, wd_ref,
    mid_ref, low_ref, grad_ref, gate_ref, up_ref, hid_ref, out_ref, sem,
):
    seq, width = x_ref.shape
    length = length_ref[0]
    tile, units = wo_ref.shape[2], hid_ref.shape[1] // 2
    copy = copier(sem)
    columns = lambda j, size: pl.ds(pl.multiple_of(j * size, size), size)
    outer = lambda j: pltpu.make_async_copy(
        wo_in.at[:, columns(j, tile)], wo_ref.at[j], sem.at[sem.shape[0] - 2 + j]
    )
    need = copy(gated_in, gated_ref)
    outer(0).start()
    need_x = copy(x_in, x_ref)
    need.wait()
    outer(1).start()
    need_cot = copy(cot_in, cot_ref)
    weights = [copy(wg_in, wg_ref), copy(wu_in, wu_ref), copy(wd_in, wd_ref)]
    kept = lax.broadcasted_iota(jnp.int32, (seq, 1), 0) < length
    flushes = []

    def project(j):
        at = columns(j, tile)
        outer(j).wait()
        branch = mm(gated_ref[...], wo_ref[j])
        x = x_ref[:, at].astype(F32)
        mid_ref[:, at] = x + branch
        sums_ref[0:1, at] = jnp.sum(jnp.where(kept, x * x, 0.0), axis=0, keepdims=True)
        sums_ref[1:2, at] = jnp.sum(jnp.where(kept, branch * branch, 0.0), axis=0, keepdims=True)

    need_x.wait()
    each(0, 2, project)
    flushes.append(copy(mid_ref, mid_out))

    def norm(i, carry):
        at = rows_at(i, 128)
        mid = mid_ref[at, :]
        r = lax.rsqrt(jnp.mean(mid * mid, axis=1, keepdims=True) + EPSILON)
        low_ref[at, :] = (mid * r * gain_ref[...].astype(F32)).astype(jnp.bfloat16)
        return carry

    lax.fori_loop(0, seq // 128, norm, 0)
    flushes.append(copy(low_ref, low_out))
    weights[0].wait()
    weights[1].wait()

    def hidden(j):
        at = columns(j, units)
        gate_ref[:, at] = mm(low_ref[...], wg_ref[:, at])
        up_ref[:, at] = mm(low_ref[...], wu_ref[:, at])
        gate = gate_ref[:, at]
        hid_ref[:, at] = (gate * jax.nn.sigmoid(gate) * up_ref[:, at]).astype(jnp.bfloat16)

    each(0, 2, hidden)
    for src, dst in ((gate_ref, gate_out), (up_ref, up_out), (hid_ref, hid_out)):
        flushes.append(copy(src, dst))
    need_cot.wait()
    grad_ref[...] = jnp.where(kept, cot_ref[...].astype(F32), 0.0).astype(jnp.bfloat16)
    flushes.append(copy(grad_ref, grad_out))
    weights[2].wait()
    result = lambda j: pltpu.make_async_copy(
        out_ref.at[:, columns(j, tile)], out_out.at[:, columns(j, tile)], sem.at[sem.shape[0] - 4 + j]
    )

    def project_out(j):
        at = columns(j, tile)
        out_ref[:, at] = mm(hid_ref[...], wd_ref[:, at])
        result(j).start()

    each(0, 2, project_out)
    flushes += [result(0), result(1)]
    for c in flushes:
        c.wait()


def mlp_forward(tokens, cotangent, length, gated, gain, wo, wg, wu, wd):
    seq, width = tokens.shape
    hidden = wg.shape[1]
    low = jnp.bfloat16
    smem = pl.BlockSpec(memory_space=pltpu.SMEM)
    outs = [
        struct(seq, width), struct(seq, width, t=low), struct(seq, width, t=low),
        struct(seq, hidden), struct(seq, hidden), struct(seq, hidden, t=low), struct(seq, width),
    ]
    return pl.pallas_call(
        mlp_forward_kernel,
        in_specs=[smem, HBM, HBM, HBM, VMEM] + [HBM] * 4,
        out_specs=[HBM] * 7 + [VMEM],
        out_shape=outs + [struct(2, width)],
        scratch_shapes=[
            pltpu.VMEM((seq, width), low),
            pltpu.VMEM((seq, width), low),
            pltpu.VMEM((seq, width), low),
            pltpu.VMEM((2, width, width // 2), low),
            pltpu.VMEM((width, hidden), low),
            pltpu.VMEM((width, hidden), low),
            pltpu.VMEM((hidden, width), low),
        ]
        + [pltpu.VMEM(out.shape, out.dtype) for out in outs]
        + [pltpu.SemaphoreType.DMA((18,))],
        compiler_params=pltpu.CompilerParams(vmem_limit_bytes=58 << 20),
    )(length, tokens, cotangent, gated, gain, wo, wg, wu, wd)


def reduce_links(rows, x, opp, nbr, held, sem):
    dp, me = lax.axis_index("dp"), lax.axis_index("mp")
    right, left, far = lax.rem(me + 1, Y), lax.rem(me + 3, Y), lax.rem(me + 2, Y)
    q, h = rows // Y, rows // Y // 2

    def message(name):
        src, dst, to = {
            "oR": (lambda: rows_of(x, far * q, h), lambda: opp.at[0], right),
            "oL": (lambda: rows_of(x, far * q + h, h), lambda: opp.at[1], left),
            "iR": (lambda: rows_of(x, right * q + h, h), lambda: nbr.at[0, h:q], right),
            "iL": (lambda: rows_of(x, left * q, h), lambda: nbr.at[1, 0:h], left),
            "dR": (lambda: held.at[0], lambda: nbr.at[0, 0:h], right),
            "dL": (lambda: held.at[1], lambda: nbr.at[1, h:q], left),
        }[name]
        return link(src(), dst(), *sem, STEPS.index(name), (dp, to))

    return message, me, right, left, [(dp, right), (dp, left)]


def mlp_backward_kernel(
    length_ref, grad_in, low_in, gate_in, up_in, hid_in, wd_in, wg_in, wu_in, x_ref, mid_ref,
    back_out, gd_out, gg_out, gu_out, layer_ref, square_ref,
    grad_ref, low_ref, gate_ref, up_ref, hid_ref, wd_ref, wg_ref, wu_ref,
    dg_s, du_s, back_s, bufs, opp, nbr, held, own_s, mid_s, csem, *sem,
):
    seq, width = grad_ref.shape
    units = wd_ref.shape[0] // 2
    low16 = jnp.bfloat16
    message, me, right, left, peers = reduce_links(seq, x_ref, opp, nbr, held, sem)
    q, h = seq // Y, seq // Y // 2
    copy = copier(csem)
    need = [
        copy(grad_in, grad_ref),
        copy(wd_in.at[0:units], wd_ref.at[0:units]),
        copy(gate_in.at[:, 0:units], gate_ref.at[:, 0:units]),
        copy(up_in.at[:, 0:units], up_ref.at[:, 0:units]),
    ]
    meet(peers)
    for name in STEPS[:4]:
        message(name).start()
    for c in need[0:2]:
        c.wait()
    next_low, next_hid = copy(low_in, low_ref), copy(hid_in, hid_ref)
    more = [
        copy(wd_in.at[units:], wd_ref.at[units:]),
        copy(gate_in.at[:, units:], gate_ref.at[:, units:]),
        copy(up_in.at[:, units:], up_ref.at[:, units:]),
    ]
    weights = [copy(wg_in, wg_ref), copy(wu_in, wu_ref)]
    adds = [
        copy(rows_of(x_ref, right * q, h), held.at[0]),
        copy(rows_of(x_ref, left * q + h, h), held.at[1]),
        copy(rows_of(x_ref, me * q, q), own_s),
        copy(rows_of(mid_ref, me * q, q), mid_s),
    ]
    spots = (gd_out, gg_out, gu_out)
    columns = lambda j: pl.ds(pl.multiple_of(j * units, units), units)
    flush = lambda j, which: pltpu.make_async_copy(
        bufs.at[which, j], spots[which].at[:, columns(j)], csem.at[csem.shape[0] - 6 + which * 2 + j]
    )

    def write(which, left_of, right_of, j):
        slot, at = bufs.at[which, j], columns(j)

        def rows(i, carry):
            part = rows_at(i, 768)
            slot[part, :] = t_mm(left_of[:, part], right_of[:, at])
            return carry

        lax.fori_loop(0, width // 768, rows, 0)
        flush(j, which).start()

    def tile(j):
        at = columns(j)

        @pl.when(j == 1)
        def _():
            for c in more:
                c.wait()

        grad = mm_t(grad_ref[...], wd_ref[at, :])

        @pl.when(j == 0)
        def _():
            for c in need[2:4]:
                c.wait()

        gate = gate_ref[:, at]
        sig = jax.nn.sigmoid(gate)
        dg_s[:, at] = (grad * up_ref[:, at] * (sig * (1.0 + gate * (1.0 - sig)))).astype(low16)
        du_s[:, at] = (grad * (gate * sig)).astype(low16)

        @pl.when(j == 0)
        def _():
            next_low.wait()
            next_hid.wait()

        write(0, grad_ref, hid_ref, j)
        write(1, low_ref, dg_s, j)

        @pl.when(j == 1)
        def _():
            for part, (come, go) in enumerate((("oR", "dR"), ("oL", "dL"))):
                message(come).wait_recv()
                adds[part].wait()
                held[part] = held[part] + opp[part]
                message(go).start()

        write(2, low_ref, du_s, j)

    each(0, 2, tile)
    for c in weights:
        c.wait()

    def back(i, carry):
        rows = rows_at(i, 768)
        back_s[:, rows] = mm_t(dg_s[...], wg_ref[rows, :])
        back_s[:, rows] = back_s[:, rows] + mm_t(du_s[...], wu_ref[rows, :])
        return carry

    lax.fori_loop(0, width // 768, back, 0)
    last = copy(back_s, back_out)
    adds[2].wait()
    adds[3].wait()
    sums = 0.0
    for part, names in enumerate((("dR", "iL"), ("iR", "dL"))):
        for name in names:
            message(name).wait_recv()
        at = slice(part * h, part * h + h)
        branch = own_s[at, :] + nbr[0, at] + nbr[1, at]
        layer_ref[at, :] = (mid_s[at, :] + branch).astype(low16).astype(F32)
        row = lax.broadcasted_iota(jnp.int32, (h, 1), 0) + (me * q + part * h)
        kept = jnp.where(row < length_ref[0], branch * branch, 0.0)
        sums = sums + jnp.sum(kept, axis=0, keepdims=True)
    square_ref[...] = sums
    last.wait()
    for j in (0, 1):
        for which in range(3):
            flush(j, which).wait()
    for name in STEPS[:6]:
        message(name).wait_send()


def mlp_backward(length, grad, low, gate, up, hid, wg, wu, wd, branch, mid, call_id):
    seq, width = low.shape
    hidden = wg.shape[1]
    quarter = seq // Y
    low16 = jnp.bfloat16
    smem = pl.BlockSpec(memory_space=pltpu.SMEM)
    inputs = (grad, low, gate, up, hid, wd, wg, wu)
    return pl.pallas_call(
        mlp_backward_kernel,
        in_specs=[smem] + [HBM] * 10,
        out_specs=[HBM] * 4 + [VMEM] * 2,
        out_shape=[struct(seq, width)] + [struct(width, hidden)] * 3
        + [struct(quarter, width), struct(1, width)],
        scratch_shapes=[pltpu.VMEM(a.shape, a.dtype) for a in inputs]
        + [pltpu.VMEM((seq, hidden), low16)] * 2
        + [pltpu.VMEM((seq, width), F32), pltpu.VMEM((3, 2, width, hidden // 2), F32)]
        + ring_scratch(quarter, width)
        + [pltpu.VMEM((quarter, width), F32)] * 2
        + [pltpu.SemaphoreType.DMA((22,))]
        + sems(6),
        compiler_params=pltpu.CompilerParams(
            vmem_limit_bytes=62 << 20, collective_id=call_id, has_side_effects=True
        ),
    )(length, *inputs, branch, mid)


def backward_kernel(
    length_ref, gg_ref, low_in, qn_ref, kn_ref, v_ref, sig_ref, att_ref, stat_ref,
    decay_ref, wq_ref, wk_ref, wv_ref, wo_ref, wf_ref, own_ref, gated_ref, layer_ref,
    back_out, four_out, gout_out, gf_ref, bias_ref, out_ref,
    k_s, do_s, line_s, dq_s, dk_s, dv_s, all_s, fall_s, w_s, wf_s, lay_s, back_ref, wide_s, low_ref, osem,
    *sem,
):
    step = pl.program_id(0)
    seq, width = low_ref.shape
    length = length_ref[0]
    low16 = jnp.bfloat16
    wide = 4 * PAIR
    dp, me = lax.axis_index("dp"), lax.axis_index("mp")
    right, left = lax.rem(me + 1, Y), lax.rem(me + 3, Y)
    q, h = seq // Y, seq // Y // 2

    def spread(j):
        owner, part, to = (
            (me, 0, right), (me, 1, right), (me, 0, left), (me, 1, left), (left, 0, right), (right, 1, left)
        )[j]
        piece = rows_of(lay_s, owner * q + part * h, h)
        source = layer_ref.at[part * h : part * h + h] if j < 4 else piece
        return link(source, piece, *sem, j, (dp, to))

    def fetch(j):
        pair = ((layer_ref, rows_of(lay_s, me * q, q)), (low_in, low_ref))[j]
        return pltpu.make_async_copy(*pair, osem.at[5 + j])

    @pl.when(step == 0)
    def _():
        meet([(dp, right), (dp, left)])
        for j in range(4):
            spread(j).start()
        for j in (0, 1):
            fetch(j).start()

    @pl.when(step == 1)
    def _():
        spread(0).wait_recv()
        spread(4).start()
        spread(3).wait_recv()
        spread(5).start()

    @pl.when(step == 0)
    def _():
        heads = wf_ref.shape[0]
        wf_s[...] = jnp.zeros_like(wf_s)
        wf_s[0:heads, :] = wf_ref[...]
        decay = decay_ref[0]
        row = lax.broadcasted_iota(jnp.int32, decay.shape, 0)
        final = jnp.sum(jnp.where(row == length - 1, decay, 0.0), axis=0, keepdims=True)
        line_s[...] = jnp.where(row < length, decay, final).T[0:8]
        fall_s[...] = jnp.zeros_like(fall_s)

    base = pl.multiple_of(step * wide, wide)
    part = lambda j: pl.ds(pl.multiple_of(base + j * PAIR, PAIR), PAIR)
    for j, w_ref in enumerate((wq_ref, wk_ref, wv_ref, wo_ref)):
        w_s[:, part(j)] = w_ref[...]
    first = first_head((seq, PAIR))
    gg, sig = gg_ref[...], sig_ref[...]
    do_s[...] = (gg * sig).astype(low16)
    all_s[:, part(3)] = (gg * att_ref[...] * sig * (1.0 - sig)).astype(low16)
    k_s[...] = kn_ref[...].astype(low16)
    dk_s[...] = jnp.zeros_like(dk_s)
    dv_s[...] = jnp.zeros_like(dv_s)
    row = lax.broadcasted_iota(jnp.int32, (seq, PAIR), 0)
    columns, lines = [], [one_row(line_s, 2 * step + head) for head in (0, 1)]
    for head in (0, 1):
        column = jnp.sum(
            jnp.where(lane_is((seq, PAIR), 2 * step + head), decay_ref[0], 0.0), axis=1, keepdims=True
        )
        columns.append(jnp.where(row[:, 0:1] < length, column, -NEG))
    block = first_head((128, PAIR))
    zero = jnp.zeros((128, PAIR), low16)
    lower = lax.broadcasted_iota(jnp.int32, (128, 128), 0) > lax.broadcasted_iota(
        jnp.int32, (128, 128), 1
    )
    for i in range(seq // 128):
        at, n = slice(i * 128, i * 128 + 128), i * 128 + 128
        query = qn_ref[at, :].astype(low16)
        do = do_s[at, :]
        pieces = []
        for head in (0, 1):
            pick = (lambda t: jnp.where(block, t, zero)) if head == 0 else (lambda t: jnp.where(block, zero, t))
            own_q, own_do = pick(query), pick(do)
            one = jnp.where(lane_is((128, PAIR), 2 * step + head), 1.0, 0.0).astype(low16)
            s = mm_t(k_s[0:n, :], own_q)
            s = s * (HEAD ** (-0.5)) + (lines[head][:, at] - columns[head][0:n])
            diagonal = jnp.where(lower, NEG, s[n - 128 :, :])
            s = diagonal if i == 0 else jnp.concatenate([s[: n - 128, :], diagonal], axis=0)
            p = jnp.exp(s)
            p = p * (1.0 / jnp.sum(p, axis=0, keepdims=True))
            gp = mm_t(v_ref[0:n, :], own_do)
            ds = (p * (gp - jnp.sum(p * gp, axis=0, keepdims=True))).astype(low16)
            dv_s[0:n, :] = dv_s[0:n, :] + mm(p.astype(low16), own_do)
            dk_s[0:n, :] = dk_s[0:n, :] + mm(ds, jnp.concatenate([own_q, one], axis=1))
            mark = jnp.where(lane_is((n, PAIR), 2 * step + head), 1.0, 0.0).astype(low16)
            pieces.append(t_mm(ds, jnp.concatenate([k_s[0:n, :], mark], axis=1)))
        dq_s[at, :] = jnp.where(block, pieces[0][:, 0:PAIR], pieces[1][:, 0:PAIR])
        fall_s[at, :] = fall_s[at, :] + pieces[0][:, PAIR:] + pieces[1][:, PAIR:]
    fall_s[...] = fall_s[...] - dk_s[:, PAIR:]
    stat = stat_ref[...]
    for e, n_ref, col, to in ((dq_s, qn_ref, 0, 0), (dk_s, kn_ref, 2, 1)):
        e = e[:, 0:PAIR] * (HEAD ** (-0.5))
        n = n_ref[...]
        a, b = halves_mean(e * n)
        r = jnp.where(first, stat[:, col : col + 1], stat[:, col + 1 : col + 2])
        all_s[:, part(to)] = (r * (e - n * jnp.where(first, a, b))).astype(low16)
    all_s[:, part(2)] = dv_s[...].astype(low16)
    slot = lax.rem(step, 2)

    @pl.when(step == 0)
    def _():
        for j in (0, 1):
            fetch(j).wait()

    def flush(j, at, step):
        columns = pl.ds(pl.multiple_of(step * wide, wide), wide)
        out = (four_out, gout_out)[j].at[:, columns]
        return pltpu.make_async_copy(wide_s.at[at, j], out, osem.at[at * 2 + j])

    @pl.when(step == 2)
    def _():
        for j in (0, 1):
            flush(j, 0, 0).wait()

    def grads(k, carry):
        rows = rows_at(k, 768)
        wide_s[slot, 0, rows, :] = t_mm(low_ref[:, rows], all_s[:, pl.ds(base, wide)])
        wide_s[slot, 1, rows, :] = t_mm(own_ref[:, rows].astype(low16), gated_ref[...])
        return carry

    lax.fori_loop(0, width // 768, grads, 0)
    for j in (0, 1):
        flush(j, slot, step).start()

    @pl.when(step == pl.num_programs(0) - 1)
    def _():
        fall = running_sum(fall_s[...], backward=True) * decay_ref[1]
        fall = fall.astype(low16)
        bias_ref[...] = jnp.sum(fall.astype(F32), axis=0, keepdims=True)
        gf_ref[...] = t_mm(fall, low_ref[...])[0:8]

        def tail(k, carry):
            rows = rows_at(k, 768)
            back_ref[:, rows] = mm_t(all_s[...], w_s[rows, :])
            back_ref[:, rows] = back_ref[:, rows] + mm(fall, wf_s[:, rows])
            return carry

        lax.fori_loop(0, width // 768, tail, 0)
        last = load(back_ref, back_out, osem.at[4])
        for j in (1, 2, 4, 5):
            spread(j).wait_recv()
        out_ref[...] = lay_s[...].astype(low16)
        for at, done in ((1, 1), (0, 2)):
            for j in (0, 1):
                flush(j, at, done).wait()
        last.wait()
        for j in range(6):
            spread(j).wait_send()


def backward_attention(place, gg, low, qn, kn, v, sig, att, stat, decay, wq, wk, wv, wo, wf, own, gated, layer, call_id):
    seq, width = low.shape
    heads = wq.shape[1]
    weights = pl.BlockSpec((width, PAIR), lambda i, _: (0, i))
    lanes = pl.BlockSpec((seq, PAIR), lambda i, _: (0, i))
    full = whole((seq, width))
    low16 = jnp.bfloat16
    return local_call(
        backward_kernel,
        heads // PAIR,
        [lanes, HBM] + [lanes] * 6 + [whole((2, seq, PAIR))] + [weights] * 4
        + [whole(wf.shape), whole(own.shape)]
        + [pl.BlockSpec((own.shape[0], 4 * PAIR), lambda i, _: (lax.axis_index("mp"), i)), HBM],
        [HBM, HBM, HBM, whole((8, width)), whole((1, PAIR)), full],
        [
            struct(seq, width), struct(width, 4 * heads), struct(width, width), struct(8, width),
            struct(1, PAIR), struct(seq, width, t=low16),
        ],
        [
            pltpu.VMEM((seq, PAIR), low16),
            pltpu.VMEM((seq, PAIR), low16),
            pltpu.VMEM((8, seq), F32),
            pltpu.VMEM((seq, PAIR), F32),
            pltpu.VMEM((seq, 2 * PAIR), F32),
            pltpu.VMEM((seq, PAIR), F32),
            pltpu.VMEM((seq, 4 * heads), low16),
            pltpu.VMEM((seq, PAIR), F32),
            pltpu.VMEM((width, 4 * heads), low16),
            pltpu.VMEM((PAIR, width), low16),
            pltpu.VMEM((seq, width), F32),
            pltpu.VMEM((seq, width), F32),
            pltpu.VMEM((2, 2, width, 4 * PAIR), F32),
            pltpu.VMEM((seq, width), low16),
            pltpu.SemaphoreType.DMA((7,)),
        ]
        + sems(6),
        62, 14, 50, call_id,
    )(place, gg, low, qn, kn, v, sig, att, stat, decay, wq, wk, wv, wo, wf, own, gated, layer)


def finish_kernel(
    grad_in, layer_in, wout_in, four_in, mlp_in, sums_in,
    grad_ref, layer_ref, wout_ref, q_ref, k_ref, v_ref, o_ref, gate_ref, up_ref, down_ref,
    gain_ref, gain2_ref, fall_ref, rms_ref, bias_ref,
    sem,
):
    rows = grad_in.shape[0] // 4
    copies = []
    for j in range(4):
        for src, dst, at in ((grad_in, grad_ref, j), (layer_in, layer_ref, 4 + j)):
            part = slice(j * rows, j * rows + rows)
            copies.append(load(src.at[part], dst.at[part], sem.at[at]))
    wout_ref[...] = wout_in[...]
    inner = q_ref.shape[1]
    for j, ref in enumerate((q_ref, k_ref, v_ref, o_ref)):
        for pair in range(inner // PAIR):
            lane = (pair * 4 + j) * PAIR
            ref[:, pair * PAIR : pair * PAIR + PAIR] = four_in[:, lane : lane + PAIR]
    units = gate_ref.shape[1]
    down_ref[...] = mlp_in[:, 0:units]
    gate_ref[...] = mlp_in[:, units : 2 * units]
    up_ref[:, 0:STEP] = mlp_in[:, 2 * units : 2 * units + STEP]
    up_ref[:, STEP:] = four_in[:, 4 * inner : 4 * inner + STEP]
    share, width = gain_ref.shape[1], sums_in.shape[1]
    row = lax.broadcasted_iota(jnp.int32, (width, share), 0)
    lane = lax.broadcasted_iota(jnp.int32, (width, share), 1)
    pick = jnp.where(row == lane + lax.axis_index("dp") * share, 1.0, 0.0)
    own = jnp.dot(
        sums_in[...], pick, precision=lax.Precision.HIGHEST, preferred_element_type=F32
    )
    gain_ref[...] = own[0:1]
    gain2_ref[...] = own[1:2]
    fall_ref[...] = own[3 : 3 + fall_ref.shape[0]]
    square = lambda row, at: sums_in[row : row + 1, at * PAIR : at * PAIR + NBUCKET]
    squares = jnp.concatenate([square(9, 0), square(9, 1), square(2, 0)], axis=0)
    rms_ref[...] = jnp.sqrt(squares / (square(9, 2) * width))
    bias_ref[...] = sums_in[10:11, 0 : bias_ref.shape[1]]
    for copy in copies:
        copy.wait()


def finish(grad, layer, out_share, share, mlp_share, sums, heads):
    rows, inner = out_share.shape
    units = mlp_share.shape[1] * 2 // 5
    return pl.pallas_call(
        finish_kernel,
        out_shape=[
            struct(*grad.shape), struct(*layer.shape, t=layer.dtype), *[struct(rows, inner)] * 5,
            *[struct(rows, units)] * 3, struct(1, rows), struct(1, rows), struct(heads, rows),
            struct(3, NBUCKET), struct(1, heads),
        ],
        in_specs=[HBM, HBM] + [VMEM] * 4,
        out_specs=[HBM, HBM] + [VMEM] * 13,
        scratch_shapes=[pltpu.SemaphoreType.DMA((8,))],
        compiler_params=pltpu.CompilerParams(vmem_limit_bytes=60 << 20),
    )(grad, layer, out_share, share, mlp_share, sums)


def per_device(
    tokens, lengths, buckets, out_cotangent, gain_attn, w_query, w_key, w_value, w_outgate,
    w_forget, b_forget, w_out, gain_mlp, w_gate, w_up, w_down,
):
    x, cotangent = tokens[0], out_cotangent[0]
    heads = w_forget.shape[1]
    gain_in, gain_mid = gain_attn[None], gain_mlp[None]
    weights = (w_query, w_key, w_value, w_outgate, w_forget.T)
    low, qn, kn, value, sig, attended, stat, decay, gated, w_full = forward_attention(
        x, lengths, gain_in, *weights, b_forget[None], w_out, 0
    )
    middle, mid_low, grad_rows, gate, up, hidden, mlp_local, squares = mlp_forward(
        x, cotangent, lengths, gated, gain_mid, w_full, w_gate, w_up, w_down
    )
    mid_local, g_down, g_gate, g_up, layer_own, mlp_square = mlp_backward(
        lengths, grad_rows, mid_low, gate, up, hidden, w_gate, w_up, w_down, mlp_local, middle, 1
    )
    grad_own, gg, mlp_share, mlp_gain = reduce_middle(
        mid_local, middle, grad_rows, gain_mid, w_full, [g_down, g_gate, g_up],
        ((0, 0), (0, 1), (1, 0), (1, 1), (2, 0)), 2,
    )
    in_local, g_four, g_out, g_fall, bias, layer_out = backward_attention(
        lengths, gg, low, qn, kn, value, sig, attended, stat, decay, *weights, grad_own, gated,
        layer_own, 3,
    )
    small = (mlp_gain, g_fall, squares, mlp_square, bias, lengths, buckets)
    input_grad, out_share, share, sums = reduce_input(
        in_local, x, grad_own, gain_in, small, [g_out, g_four, g_up],
        ((0, 0), (0, 1), (0, 2), (1, 0), (1, 1), (1, 2), (2, 1)), 4,
    )
    (
        input_grad, layer_out, g_out, g_query, g_key, g_value, g_outgate, g_gate, g_up, g_down,
        g_gain, g_gain_mid, g_fall, rms, bias,
    ) = finish(input_grad, layer_out, out_share, share, mlp_share, sums, heads)
    return (
        layer_out[None],
        input_grad[None],
        g_gain[0],
        g_query,
        g_key,
        g_value,
        g_outgate,
        g_fall.T,
        bias[0],
        g_out.T,
        g_gain_mid[0],
        g_gate,
        g_up,
        g_down.T,
        rms,
    )


def solution(mesh):
    placed = (
        P("dp", None, None),
        P("dp"),
        P("dp"),
        P("dp", None, None),
        P(),
        P(None, "mp"),
        P(None, "mp"),
        P(None, "mp"),
        P(None, "mp"),
        P(None, "mp"),
        P("mp"),
        P("mp", None),
        P(),
        P(None, "mp"),
        P(None, "mp"),
        P("mp", None),
    )
    return jax.shard_map(
        per_device,
        mesh=mesh,
        in_specs=placed,
        out_specs=(
            P("dp", None, None),
            P("dp", None, None),
            P("dp"),
            P("dp", "mp"),
            P("dp", "mp"),
            P("dp", "mp"),
            P("dp", "mp"),
            P("dp", "mp"),
            P("mp"),
            P("mp", "dp"),
            P("dp"),
            P("dp", "mp"),
            P("dp", "mp"),
            P("mp", "dp"),
            P(),
        ),
        check_vma=False,
    )
```

```python
import functools

import jax
import jax.numpy as jnp
from jax import lax
from jax.experimental import pallas as pl
from jax.experimental.pallas import tpu as pltpu
from jax.sharding import PartitionSpec as P

NBUCKET = 4


EPSILON = 1e-06


MESH = pl.DeviceIdType.MESH
F32 = jnp.float32
Y = 4
STEP = 512
HBM = pl.BlockSpec(memory_space=pl.ANY)
VMEM = pl.BlockSpec(memory_space=pltpu.VMEM)
STEPS = ("oR", "oL", "iR", "iL", "dR", "dL", "gRa", "gRb", "gLa", "gLb", "fR", "fL")


def rows_of(ref, start, count):
    return ref.at[pl.ds(pl.multiple_of(start, 8), count)]


def meet(devices):
    barrier = pltpu.get_barrier_semaphore()
    for device in devices:
        pl.semaphore_signal(barrier, inc=1, device_id=device, device_id_type=MESH)
    pl.semaphore_wait(barrier, len(devices))


def link(src, dst, ssem, rsem, at, device):
    return pltpu.make_async_remote_copy(
        src_ref=src,
        dst_ref=dst,
        send_sem=ssem.at[at],
        recv_sem=rsem.at[at],
        device_id=device,
        device_id_type=MESH,
    )


def push(*args):
    copy = link(*args)
    copy.start()
    return copy


class YRing:
    def __init__(self, rows, waves, ssem, rsem):
        self.sems = (ssem, rsem)
        self.dp, self.me = lax.axis_index("dp"), lax.axis_index("mp")
        self.right, self.left = lax.rem(self.me + 1, Y), lax.rem(self.me + 3, Y)
        self.far = lax.rem(self.me + 2, Y)
        self.quarter, self.half = rows // Y, rows // Y // 2
        self.tall = self.half // waves
        self.sent = {}

    def neighbours(self):
        return [(self.dp, self.right), (self.dp, self.left)]

    def send(self, name, wave, src, dst, to):
        at = wave * 6 + STEPS.index(name)
        self.sent[name, wave] = push(src, dst, *self.sems, at, (self.dp, to))

    def rows(self, x, owner, part, wave):
        return rows_of(x, owner * self.quarter + part * self.half + wave * self.tall, self.tall)

    def fetch(self, x, held, own, sem):
        self.loads = [
            load(rows_of(x, self.right * self.quarter, self.half), held.at[0], sem.at[0]),
            load(rows_of(x, self.left * self.quarter + self.half, self.half), held.at[1], sem.at[1]),
            load(rows_of(x, self.me * self.quarter, self.quarter), own, sem.at[2]),
        ]

    def start(self, x, opp, nbr, wave):
        w = slice(wave * self.tall, wave * self.tall + self.tall)
        low = slice(self.half + wave * self.tall, self.half + wave * self.tall + self.tall)
        self.send("oR", wave, self.rows(x, self.far, 0, wave), opp.at[0, w], self.right)
        self.send("oL", wave, self.rows(x, self.far, 1, wave), opp.at[1, w], self.left)
        self.send("iR", wave, self.rows(x, self.right, 1, wave), nbr.at[0, low], self.right)
        self.send("iL", wave, self.rows(x, self.left, 0, wave), nbr.at[1, w], self.left)

    def relay(self, opp, nbr, held, wave):
        w = slice(wave * self.tall, wave * self.tall + self.tall)
        low = slice(self.half + wave * self.tall, self.half + wave * self.tall + self.tall)
        for part, (come, go, into, to) in enumerate(
            (("oR", "dR", nbr.at[0, w], self.right), ("oL", "dL", nbr.at[1, low], self.left))
        ):
            self.sent[come, wave].wait_recv()
            if wave == 0:
                self.loads[part].wait()
            held[part, w] = held[part, w] + opp[part, w]
            self.send(go, wave, held.at[part, w], into, to)

    def collect(self, own, nbr, part, wave):
        if part == 0 and wave == 0:
            self.loads[2].wait()
        for name in (("dR", "iL"), ("iR", "dL"))[part]:
            self.sent[name, wave].wait_recv()
        start = part * self.half + wave * self.tall
        at = slice(start, start + self.tall)
        return at, own[at, :] + nbr[0, at] + nbr[1, at]

    def spread(self, part, own, block):
        into, tag = block(self.me, part), "ab"[part]
        mine = own.at[part * self.half : part * self.half + self.half]
        self.send("gR" + tag, 0, mine, into, self.right)
        self.send("gL" + tag, 0, mine, into, self.left)

    def forward(self, block):
        self.sent["gRa", 0].wait_recv()
        self.send("fR", 0, block(self.left, 0), block(self.left, 0), self.right)
        self.sent["gLb", 0].wait_recv()
        self.send("fL", 0, block(self.right, 1), block(self.right, 1), self.left)

    def arrive(self):
        for name in ("gRb", "gLa", "fR", "fL"):
            self.sent[name, 0].wait_recv()

    def finish(self):
        for copy in self.sent.values():
            copy.wait_send()


def ring_scratch(quarter, columns):
    return [
        pltpu.VMEM((2, quarter // 2, columns), F32),
        pltpu.VMEM((2, quarter, columns), F32),
        pltpu.VMEM((2, quarter // 2, columns), F32),
    ]


def sems(*counts):
    return [pltpu.SemaphoreType.DMA((n,)) for n in counts for _ in (0, 1)]


class Place:
    def __init__(self):
        self.dp, self.my = lax.axis_index("dp"), lax.axis_index("mp")
        c, z, x = lax.rem(self.dp, 2), lax.rem(self.dp // 2, 4), self.dp // 8
        self.c, self.sib, self.chip = c, self.dp + 1 - 2 * c, x * 4 + z
        self.st1, self.st2 = 4 - 3 * c, 1 + 3 * c
        self.p1, self.p2 = x + c * (z - x), z + c * (x - z)
        step = lambda p, by: lax.rem(p + by, 4)
        self.r1, self.l1, self.o1 = (step(self.p1, by) for by in (1, 3, 2))
        self.r2, self.l2, self.o2 = (step(self.p2, by) for by in (1, 3, 2))

    def device(self, a, b):
        return ((a * self.st1 + b * self.st2) * 2 + self.c, self.my)

    def peers(self):
        return [
            (self.sib, self.my),
            self.device(self.r1, self.p2),
            self.device(self.l1, self.p2),
            self.device(self.p1, self.r2),
            self.device(self.p1, self.l2),
        ]


class ScatterSum:
    def __init__(self, here, sources, own, other, near, last, asem, bsem, lsem, ssem, rsem):
        self.here, self.sources = here, sources
        self.own, self.other, self.near, self.last = own, other, near, last
        self.asem, self.bsem, self.lsem, self.ssem, self.rsem = asem, bsem, lsem, ssem, rsem
        self.n = own.shape[0]
        self.sibling, *to = here.peers()
        self.to = (to[0:2], to[2:4])

    def message(self, name, k, stage):
        at = (k * 2 + stage) * 6 + STEPS.index(name)
        device = self.to[stage][0 if name[1] == "R" else 1]
        here, own = self.here, self.own.at[k]
        if stage:
            own, into, cut = own.at[here.p1], self.last.at[k], (slice(0, 24), slice(24, 48))
            far, right, left = here.o2, here.r2, here.l2
        else:
            into, cut = self.near.at[k], (slice(0, 2), slice(2, 4))
            far, right, left = here.o1, here.r1, here.l1
        row, part, slot = {
            "oR": (far, 0, 0),
            "oL": (far, 1, 1),
            "iR": (right, 1, 3),
            "iL": (left, 0, 4),
            "dR": (right, 0, 2),
            "dL": (left, 1, 5),
        }[name]
        return link(own.at[row, cut[part]], into.at[slot], self.ssem, self.rsem, at, device)

    def whole(self, k):
        own, other = self.own.at[k], self.other.at[k]
        return link(own, other, self.asem, self.bsem, k, self.sibling)

    def exchange(self, k):
        here = self.here
        ref, start, width = self.sources[k]

        def source(block):
            return ref.at[pl.ds(pl.multiple_of(block * 48, 16), 48), pl.ds(start, width)]

        def cross(i, carry):
            a, b = i // 4, lax.rem(i, 4)
            block = source((a * here.st2 + b * here.st1) * 2 + 1 - here.c)
            push(block, self.other.at[k, a, b], self.asem, self.bsem, k, self.sibling)
            return carry

        def fetch(i, carry):
            a, b = i // 4, lax.rem(i, 4)
            block = source((a * here.st1 + b * here.st2) * 2 + here.c)
            pltpu.make_async_copy(block, self.own.at[k, a, b], self.lsem.at[k]).start()
            return carry

        lax.fori_loop(0, 16, cross, 0)
        lax.fori_loop(0, 16, fetch, 0)

    def first(self, k):
        here, own, other = self.here, self.own, self.other
        pltpu.make_async_copy(own.at[k], own.at[k], self.lsem.at[k]).wait()
        self.whole(k).wait_recv()

        def add(p):
            def body(b, carry):
                own[k, p, b] = own[k, p, b] + other[k, p, b]
                return carry

            lax.fori_loop(0, 4, body, 0)

        add(here.o1)
        self.message("oR", k, 0).start()
        self.message("oL", k, 0).start()
        add(here.r1)
        self.message("iR", k, 0).start()
        add(here.l1)
        self.message("iL", k, 0).start()
        add(here.p1)

    def first_relay(self, k):
        here, own, near = self.here, self.own, self.near

        def add(p, at, slot):
            def body(b, carry):
                own[k, p, at + b] = own[k, p, at + b] + near[k, slot, b]
                return carry

            lax.fori_loop(0, 2, body, 0)

        self.message("oR", k, 0).wait_recv()
        add(here.r1, 0, 0)
        self.message("dR", k, 0).start()
        self.message("oL", k, 0).wait_recv()
        add(here.l1, 2, 1)
        self.message("dL", k, 0).start()

    def second(self, k):
        here, own, near = self.here, self.own, self.near
        for name in ("iR", "dR", "iL", "dL"):
            self.message(name, k, 0).wait_recv()

        def add(p):
            h, b = p // 2, lax.rem(p, 2)
            own[k, here.p1, p] = own[k, here.p1, p] + near[k, 2 + h, b] + near[k, 4 + h, b]

        add(here.o2)
        self.message("oR", k, 1).start()
        self.message("oL", k, 1).start()
        add(here.r2)
        self.message("iR", k, 1).start()
        add(here.l2)
        self.message("iL", k, 1).start()
        add(here.p2)

    def second_relay(self, k):
        here, own, last = self.here, self.own, self.last
        self.message("oR", k, 1).wait_recv()
        own[k, here.p1, here.r2, 0:24] = own[k, here.p1, here.r2, 0:24] + last[k, 0]
        self.message("dR", k, 1).start()
        self.message("oL", k, 1).wait_recv()
        own[k, here.p1, here.l2, 24:48] = own[k, here.p1, here.l2, 24:48] + last[k, 1]
        self.message("dL", k, 1).start()

    def result(self, k, out, at):
        here, own, last = self.here, self.own, self.last
        width = own.shape[4]
        for name in ("iR", "dR", "iL", "dL"):
            self.message(name, k, 1).wait_recv()
        columns = pl.ds(pl.multiple_of(at * width, 128), width)
        out[0:24, columns] = own[k, here.p1, here.p2, 0:24] + last[k, 2] + last[k, 4]
        out[24:48, columns] = own[k, here.p1, here.p2, 24:48] + last[k, 3] + last[k, 5]

    def sent(self, k):
        self.whole(k).wait_send()
        for stage in (0, 1):
            for name in STEPS[:6]:
                self.message(name, k, stage).wait_send()


def each(low, high, step):
    def body(k, carry):
        step(k)
        return carry

    lax.fori_loop(low, high, body, 0)


class SmallSum:
    def __init__(self, here, bufs, landed, ssem, rsem):
        self.bufs, self.landed, self.ssem, self.rsem = bufs, landed, ssem, rsem
        turn = lambda p, by: lax.rem(p + by, 4)
        self.stages = [
            [(here.sib, here.my)],
            [here.device(turn(here.p1, by), here.p2) for by in (1, 2, 3)],
            [here.device(here.p1, turn(here.p2, by)) for by in (1, 2, 3)],
            [(here.dp, turn(here.my, by)) for by in (1, 2, 3)],
        ]
        self.far = [self.stages[1][1], self.stages[2][1], self.stages[3][1]]
        self.sent = []

    def send(self, stage):
        for to in self.stages[stage]:
            at = len(self.sent)
            copy = push(self.bufs.at[stage], self.landed.at[at], self.ssem, self.rsem, at, to)
            self.sent.append(copy)

    def take(self, stage):
        value, count = self.bufs[stage], len(self.stages[stage])
        for at in range(len(self.sent) - count, len(self.sent)):
            self.sent[at].wait_recv()
            value = value + self.landed[at]
        self.bufs[stage + 1] = value

    def finish(self):
        for copy in self.sent:
            copy.wait_send()


def scatter_scratch(n, w):
    return [
        pltpu.VMEM((n, 4, 4, 48, w), F32),
        pltpu.VMEM((n, 4, 4, 48, w), F32),
        pltpu.VMEM((n, 6, 2, 48, w), F32),
        pltpu.VMEM((n, 6, 24, w), F32),
        pltpu.SemaphoreType.DMA((n,)),
        pltpu.SemaphoreType.DMA((n,)),
        pltpu.SemaphoreType.DMA((n,)),
        pltpu.SemaphoreType.DMA((12 * n,)),
        pltpu.SemaphoreType.DMA((12 * n,)),
    ]


def scatter_sources(refs, pieces):
    return [(refs[which], at * STEP, STEP) for which, at in pieces]


def norm_back(value, source, base, gain):
    source = source.astype(F32)
    r = lax.rsqrt(jnp.mean(source * source, axis=1, keepdims=True) + EPSILON)
    n = source * r
    e = value * gain.astype(F32)
    inner = jnp.mean(e * n, axis=1, keepdims=True)
    return base.astype(F32) + r * (e - n * inner), jnp.sum(value * n, axis=0, keepdims=True)


def load(ref, scratch, sem):
    copy = pltpu.make_async_copy(ref, scratch, sem)
    copy.start()
    return copy


def middle_kernel(pieces, count, x_ref, source_ref, base_ref, gain_ref, w_ref, *refs):
    ins, refs = refs[:count], refs[count:]
    grad_ref, gg_ref, share_ref, sums_ref = refs[:4]
    source_s, base_s, w_s, opp, nbr, held, own_s, blocks, csem, *sem = refs[4:17]
    here, ring = Place(), YRing(x_ref.shape[0], 2, *sem[0:2])
    total = ScatterSum(here, scatter_sources(ins, pieces), *refs[17:])
    n = total.n
    far = (ring.dp, ring.far)
    meet(ring.neighbours() + [far] + here.peers())
    ring.start(x_ref, opp, nbr, 0)
    q, h = ring.quarter, ring.half
    ring.fetch(x_ref, held, own_s, csem)
    for k in range(n):
        total.exchange(k)
    loads = [
        load(rows_of(source_ref, ring.me * q, q), source_s, csem.at[3]),
        load(rows_of(base_ref, ring.me * q, q), base_s, csem.at[4]),
        load(w_ref, w_s, csem.at[5]),
    ]
    ring.relay(opp, nbr, held, 0)
    ring.start(x_ref, opp, nbr, 1)
    each(0, n, total.first)
    each(0, n - 2, total.first_relay)
    ring.relay(opp, nbr, held, 1)
    for copy in loads:
        copy.wait()
    sums, swaps, keeps = 0.0, [], []
    inner = gg_ref.shape[1]
    for wave in (0, 1):
        for part in (0, 1):
            at, value = ring.collect(own_s, nbr, part, wave)
            value, more = norm_back(value, source_s[at, :], base_s[at, :], gain_ref[...])
            grad_ref[at, :] = value
            sums = sums + more
        tall = ring.tall
        low = jnp.concatenate(
            [grad_ref[part * h + wave * tall : part * h + wave * tall + tall, :] for part in (0, 1)], axis=0
        ).astype(jnp.bfloat16)
        for j, by in enumerate((2, 1, 3, 0)):
            to = lax.rem(ring.me + by, Y)
            blocks[wave, j] = mm_t(low, rows_of(w_s, to * inner, inner)[...])
            for part in (0, 1):
                src = blocks.at[wave, j, part * tall : part * tall + tall]
                into = rows_of(gg_ref, ring.me * q + part * h + wave * tall, tall)
                if by:
                    at = (wave * 3 + j) * 2 + part
                    swaps.append(push(src, into, *sem[2:4], at, (ring.dp, to)))
                else:
                    keeps.append(load(src, into, csem.at[6 + wave * 2 + part]))
        if wave == 0:
            each(n - 2, n, total.first_relay)
    sums_ref[...] = sums
    each(0, n, total.second)
    each(0, n, total.second_relay)
    each(0, n, lambda k: total.result(k, share_ref, k))
    for copy in swaps:
        copy.wait_recv()
    for copy in keeps:
        copy.wait()
    for copy in swaps:
        copy.wait_send()
    ring.finish()
    each(0, n, total.sent)


def reduce_middle(partial, source, base, gain, w_full, grads, pieces, call_id):
    n = len(pieces)
    hbm, vmem = pl.BlockSpec(memory_space=pl.ANY), pl.BlockSpec(memory_space=pltpu.VMEM)
    rows, columns = partial.shape
    quarter, inner = rows // Y, w_full.shape[0] // Y
    return pl.pallas_call(
        functools.partial(middle_kernel, pieces, len(grads)),
        out_shape=[
            jax.ShapeDtypeStruct((quarter, columns), F32),
            jax.ShapeDtypeStruct((rows, inner), F32),
            jax.ShapeDtypeStruct((48, n * STEP), F32),
            jax.ShapeDtypeStruct((1, columns), F32),
        ],
        in_specs=[hbm, hbm, hbm, vmem, hbm] + [hbm] * len(grads),
        out_specs=[vmem, hbm, vmem, vmem],
        scratch_shapes=[
            pltpu.VMEM((quarter, columns), source.dtype),
            pltpu.VMEM((quarter, columns), base.dtype),
            pltpu.VMEM(w_full.shape, w_full.dtype),
        ]
        + ring_scratch(quarter, columns)
        + [
            pltpu.VMEM((quarter, columns), F32),
            pltpu.VMEM((2, 4, quarter // 2, inner), F32),
            pltpu.SemaphoreType.DMA((10,)),
        ]
        + sems(12, 12)
        + scatter_scratch(n, STEP),
        compiler_params=pltpu.CompilerParams(
            collective_id=call_id, has_side_effects=True, vmem_limit_bytes=56 << 20
        ),
    )(partial, source, base, gain, w_full, *grads)


def input_kernel(
    pieces, count, x_ref, source_ref, base_ref, gain_ref, other_ref, fall_ref, square_ref, more_ref,
    bias_ref, length_ref, bucket_ref, *refs
):
    ins, refs = refs[:count], refs[count:]
    out_ref, out_share_ref, share_ref, sums_ref = refs[:4]
    source_s, opp, nbr, held, own_s, mine_s, wide_s, landed, csem, *sem = refs[4:17]
    bufs, arrived, asem, bsem = refs[17:21]
    here, ring = Place(), YRing(x_ref.shape[0], 1, *sem[0:2])
    total = ScatterSum(here, scatter_sources(ins, pieces), *refs[21:])
    tiny = SmallSum(here, bufs, arrived, asem, bsem)
    n, first = total.n, wide_s.shape[1] // STEP
    meet(ring.neighbours() + here.peers() + tiny.far)
    ring.start(x_ref, opp, nbr, 0)
    q, h = ring.quarter, ring.half
    ring.fetch(x_ref, held, own_s, csem)
    copy = load(rows_of(source_ref, ring.me * q, q), source_s, csem.at[3])
    for k in range(n):
        total.exchange(k)
    each(0, n // 2, total.first)
    ring.relay(opp, nbr, held, 0)
    each(n // 2, n, total.first)
    each(0, n - 2, total.first_relay)
    copy.wait()
    block = lambda owner, part: rows_of(out_ref, owner * q + part * h, h)
    sums = 0.0
    for part in (0, 1):
        at, value = ring.collect(own_s, nbr, part, 0)
        value, more = norm_back(value, source_s[at, :], base_ref[at, :], gain_ref[...])
        mine_s[at, :] = value
        ring.spread(part, mine_s, block)
        sums = sums + more
    kept = load(mine_s, rows_of(out_ref, ring.me * q, q), csem.at[4])
    bufs[0, 0:1, :] = sums
    bufs[0, 1:2, :] = other_ref[...]
    bufs[0, 8:16, :] = jnp.zeros_like(bufs[0, 8:16, :])
    bufs[0, 2:3, :] = jnp.zeros((1, sums_ref.shape[1]), F32)
    bufs[0, 3:9, :] = fall_ref[0:6, :]
    lane = lax.broadcasted_iota(jnp.int32, (1, PAIR), 1)
    both = jnp.sum(square_ref[...], axis=1, keepdims=True)
    in_bucket = lambda value: jnp.where(lane == bucket_ref[0], value, 0.0)
    bufs[0, 2:3, 0:PAIR] = in_bucket(jnp.sum(more_ref[...], axis=1, keepdims=True))
    for at, value in enumerate((both[0:1], both[1:2], length_ref[0].astype(F32))):
        bufs[0, 9:10, at * PAIR : at * PAIR + PAIR] = in_bucket(value)
    bufs[0, 10:11, 0:PAIR] = bias_ref[...]
    tiny.send(0)
    each(n - 2, n, total.first_relay)
    each(0, n, total.second)
    ring.forward(block)
    tiny.take(0)
    tiny.send(1)
    each(0, n, total.second_relay)
    tiny.take(1)
    tiny.send(2)
    each(0, first, lambda k: total.result(k, wide_s, k))
    inner = landed.shape[2]
    swaps = []
    for j, by in enumerate((2, 1, 3)):
        to = lax.rem(ring.me + by, Y)
        columns = pl.ds(pl.multiple_of(to * inner, 128), inner)
        swaps.append(push(wide_s.at[:, columns], landed.at[j], *sem[2:4], j, (ring.dp, to)))
    each(first, n, lambda k: total.result(k, share_ref, k - first))
    tiny.take(2)
    tiny.send(3)
    own = wide_s[:, pl.ds(pl.multiple_of(ring.me * inner, 128), inner)]
    for j, copy in enumerate(swaps):
        copy.wait_recv()
        own = own + landed[j]
    out_share_ref[...] = own
    tiny.take(3)
    rows = lax.broadcasted_iota(jnp.int32, sums_ref.shape, 0)
    sums_ref[...] = jnp.where(rows < 3, bufs[4], bufs[3])
    ring.arrive()
    kept.wait()
    for copy in swaps:
        copy.wait_send()
    tiny.finish()
    ring.finish()
    each(0, n, total.sent)


def reduce_input(partial, source, base, gain, small, grads, pieces, call_id):
    n = len(pieces)
    smem = pl.BlockSpec(memory_space=pltpu.SMEM)
    hbm, vmem = pl.BlockSpec(memory_space=pl.ANY), pl.BlockSpec(memory_space=pltpu.VMEM)
    rows, columns = partial.shape
    quarter, inner = rows // Y, grads[0].shape[1] // Y
    wide = grads[0].shape[1]
    shares = n * STEP - wide
    return pl.pallas_call(
        functools.partial(input_kernel, pieces, len(grads)),
        out_shape=[
            jax.ShapeDtypeStruct(partial.shape, F32),
            jax.ShapeDtypeStruct((48, inner), F32),
            jax.ShapeDtypeStruct((48, shares), F32),
            jax.ShapeDtypeStruct((16, columns), F32),
        ],
        in_specs=[hbm, hbm, vmem, vmem] + [vmem] * 5 + [smem] * 2 + [hbm] * len(grads),
        out_specs=[hbm] + [vmem] * 3,
        scratch_shapes=[pltpu.VMEM((quarter, columns), source.dtype)]
        + ring_scratch(quarter, columns)
        + [
            pltpu.VMEM((quarter, columns), F32),
            pltpu.VMEM((quarter, columns), F32),
            pltpu.VMEM((48, wide), F32),
            pltpu.VMEM((3, 48, inner), F32),
            pltpu.SemaphoreType.DMA((5,)),
        ]
        + sems(12, 3)
        + [pltpu.VMEM((5, 16, columns), F32), pltpu.VMEM((10, 16, columns), F32)]
        + sems(10)
        + scatter_scratch(n, STEP),
        compiler_params=pltpu.CompilerParams(
            collective_id=call_id, has_side_effects=True, vmem_limit_bytes=56 << 20
        ),
    )(partial, source, base, gain, *small, *grads)


HEAD = 64
PAIR = 128
NEG = -1e30


def rows_at(i, size):
    return pl.ds(pl.multiple_of(i * size, size), size)


def lane_is(shape, index):
    return lax.broadcasted_iota(jnp.int32, shape, len(shape) - 1) == index


def first_head(shape):
    return lax.broadcasted_iota(jnp.int32, shape, len(shape) - 1) < HEAD


def halves_mean(values):
    first = first_head(values.shape)
    low = jnp.sum(jnp.where(first, values, 0.0), axis=1, keepdims=True) * (1.0 / HEAD)
    high = jnp.sum(jnp.where(first, 0.0, values), axis=1, keepdims=True) * (1.0 / HEAD)
    return low, high


def one_row(ref, index):
    rows = ref[...]
    picked = lax.broadcasted_iota(jnp.int32, rows.shape, 0) == index
    return jnp.sum(jnp.where(picked, rows, 0.0), axis=0, keepdims=True)


def running_sum(values, backward=False):
    count = values.shape[0]
    row = lax.broadcasted_iota(jnp.int32, values.shape, 0)
    shift = 1
    while shift < count:
        if backward:
            moved = jnp.where(row < count - shift, pltpu.roll(values, count - shift, 0), 0.0)
        else:
            moved = jnp.where(row >= shift, pltpu.roll(values, shift, 0), 0.0)
        values = values + moved
        shift *= 2
    return values


def mm(left, right):
    return jnp.dot(left, right, preferred_element_type=F32)


def mm_t(left, right):
    return lax.dot_general(left, right, (((1,), (1,)), ((), ())), preferred_element_type=F32)


def t_mm(left, right):
    return lax.dot_general(left, right, (((0,), (0,)), ((), ())), preferred_element_type=F32)


def whole(shape):
    return pl.BlockSpec(shape, lambda *_: (0,) * len(shape), pipeline_mode=pl.Buffered(1))


def struct(*shape, t=F32):
    return jax.ShapeDtypeStruct(shape, t)


def local_call(kernel, grid, in_specs, out_specs, out_shape, scratch, limit, flops, moved, call_id=None):
    return pl.pallas_call(
        kernel,
        grid_spec=pltpu.PrefetchScalarGridSpec(
            num_scalar_prefetch=1,
            grid=(grid,),
            in_specs=in_specs,
            out_specs=out_specs,
            scratch_shapes=scratch,
        ),
        out_shape=out_shape,
        compiler_params=pltpu.CompilerParams(
            vmem_limit_bytes=limit << 20,
            collective_id=call_id,
            has_side_effects=call_id is not None,
        ),
        cost_estimate=pl.CostEstimate(
            flops=flops * 10**9, bytes_accessed=moved * 10**6, transcendentals=4 * 10**6
        ),
    )


def forward_kernel(
    length_ref, x_ref, gain_ref, wq_ref, wk_ref, wv_ref, wo_ref, wf_ref, bf_ref, w_ref,
    low_out, qn_ref, kn_ref, v_ref, sig_ref, att_ref, stat_ref, decay_ref, gated_out, full_out,
    top_s, row_s, q_s, k_s, w_s, pre_s, gs, ws, wf_s, bf_s, low_ref, gated_ref, full_ref, osem, *sem,
):
    step = pl.program_id(0)
    seq = x_ref.shape[0]
    length = length_ref[0]
    here = Place()
    me, right, left, far = (lax.rem(here.my + by, Y) for by in (0, 1, 3, 2))
    sibling, right1, left1, right2, left2 = here.peers()
    c, p1, p2, half = here.c, here.p1, here.p2, seq // 2
    mine = ws.at[c, p2, p1, me]
    cross_order = (p2, here.l2, here.r2, here.o2)

    def plane(j):
        return link(mine, mine, *sem[2:4], j, (here.dp, (right, far, left)[j]))

    def torus(stage, j):
        if stage == 0:
            at, spots, to = (lambda p: ws.at[c, p2, p]), (p1, here.l1, here.r1), (right1, left1)
        else:
            at, spots, to = (lambda p: ws.at[c, p]), (p2, here.l2, here.r2), (right2, left2)
        spot, part, side = ((0, 0, 0), (0, 1, 0), (0, 0, 1), (0, 1, 1), (1, 0, 0), (2, 1, 1))[j]
        piece = at(spots[spot]).at[2 * part : 2 * part + 2]
        return link(piece, piece, *sem[4 + 2 * stage : 6 + 2 * stage], j, to[side])

    def cross(j):
        piece = ws.at[c, cross_order[j]]
        return link(piece, piece, *sem[8:10], j, sibling)

    def gate(pair, j):
        owner, part, to = (
            (me, 0, right), (me, 1, right), (me, 0, left), (me, 1, left), (left, 0, right), (right, 1, left)
        )[j]
        piece = gs.at[pair, owner, part * half : part * half + half]
        return link(piece, piece, *sem[0:2], pair * 6 + j, (here.dp, to))

    def flush(j):
        src, dst = ((low_ref, low_out), (full_ref, full_out), (gated_ref, gated_out))[j]
        return pltpu.make_async_copy(src, dst, osem.at[j])

    def pass_on(make):
        make(0).wait_recv()
        make(4).start()
        make(3).wait_recv()
        make(5).start()

    def arrived(make):
        for j in (1, 2, 4, 5):
            make(j).wait_recv()

    @pl.when(step == 0)
    def _():
        tall, wide = ws.shape[4], ws.shape[5]
        two = w_ref[
            pl.ds(pl.multiple_of(here.chip // 2 * (2 * tall), 16), 2 * tall),
            pl.ds(pl.multiple_of(c * wide, 128), wide),
        ].astype(F32)
        mine[...] = jnp.where(lax.rem(here.chip, 2) == 0, two[0:tall], two[tall:])
        meet([(here.dp, right), (here.dp, left), (here.dp, far)] + here.peers())
        for j in range(3):
            plane(j).start()

    @pl.when(step == 0)
    def _():
        def norm(i, carry):
            at = rows_at(i, 128)
            x = x_ref[at, :].astype(F32)
            r = lax.rsqrt(jnp.mean(x * x, axis=1, keepdims=True) + EPSILON)
            low_ref[at, :] = (x * r * gain_ref[...].astype(F32)).astype(jnp.bfloat16)
            return carry

        lax.fori_loop(0, seq // 128, norm, 0)
        flush(0).start()
        heads = wf_ref.shape[0]
        wf_s[...] = jnp.zeros_like(wf_s)
        wf_s[0:heads, :] = wf_ref[...]
        bf_s[...] = jnp.zeros_like(bf_s)
        bf_s[0:1, 0:heads] = bf_ref[...].astype(F32)
        pre = mm_t(low_ref[...], wf_s[...]) + bf_s[0:1, :]
        fall = jnp.minimum(pre, 0.0) - jnp.log1p(jnp.exp(-jnp.abs(pre)))
        decay = running_sum(fall)
        row = lax.broadcasted_iota(jnp.int32, decay.shape, 0)
        final = jnp.sum(jnp.where(row == length - 1, decay, 0.0), axis=0, keepdims=True)
        decay_ref[0] = decay
        decay_ref[1] = jax.nn.sigmoid(-pre)
        top_s[...] = jnp.where(row < length, decay, final)
        row_s[...] = jnp.where(row < length, decay, -NEG).T[0:8]

    for j, ref in enumerate((wq_ref, wk_ref, wv_ref, wo_ref)):
        w_s[:, j * PAIR : j * PAIR + PAIR] = ref[...]
    pre_s[...] = mm(low_ref[...], w_s[...])

    def norms(i, carry):
        at = rows_at(i, 128)
        for j, n_ref, s, col in ((0, qn_ref, q_s, 0), (1, kn_ref, k_s, 2)):
            pre = pre_s[at, j * PAIR : j * PAIR + PAIR]
            a, b = halves_mean(pre * pre)
            a, b = lax.rsqrt(a + EPSILON), lax.rsqrt(b + EPSILON)
            n = pre * jnp.where(first_head(pre.shape), a, b)
            n_ref[at, :] = n
            s[at, :] = n.astype(jnp.bfloat16)
            here = jnp.where(lane_is(pre.shape, col), a, jnp.where(lane_is(pre.shape, col + 1), b, 0.0))
            stat_ref[at, :] = here if col == 0 else stat_ref[at, :] + here
        v_ref[at, :] = pre_s[at, 2 * PAIR : 3 * PAIR].astype(jnp.bfloat16)
        sig_ref[at, :] = jax.nn.sigmoid(pre_s[at, 3 * PAIR : 4 * PAIR])
        return carry

    lax.fori_loop(0, seq // 128, norms, 0)

    @pl.when(step == 0)
    def _():
        for j in range(3):
            plane(j).wait_recv()
        for j in range(4):
            torus(0, j).start()

    @pl.when(step == 1)
    def _():
        arrived(lambda j: torus(0, j))
        for j in range(4):
            torus(1, j).start()
        cross(0).start()

    @pl.when(step == 2)
    def _():
        pass_on(lambda j: torus(1, j))

    lines = [one_row(row_s, 2 * step + head) for head in (0, 1)]
    first = first_head((128, PAIR))
    zero = jnp.zeros((128, PAIR), jnp.bfloat16)
    upper = lax.broadcasted_iota(jnp.int32, (128, 128), 1) > lax.broadcasted_iota(
        jnp.int32, (128, 128), 0
    )
    for i in range(seq // 128):
        at, n = slice(i * 128, i * 128 + 128), i * 128 + 128
        q = q_s[at, :]
        both = []
        for head in (0, 1):
            own = jnp.where(first, q, zero) if head == 0 else jnp.where(first, zero, q)
            s = mm_t(own, k_s[0:n, :])
            column = jnp.sum(
                jnp.where(lane_is((128, PAIR), 2 * step + head), top_s[at, :], 0.0), axis=1, keepdims=True
            )
            s = s * (HEAD ** (-0.5)) + (column - lines[head][:, 0:n])
            diagonal = jnp.where(upper, NEG, s[:, n - 128 :])
            s = diagonal if i == 0 else jnp.concatenate([s[:, : n - 128], diagonal], axis=1)
            p = jnp.exp(s)
            p = p * (1.0 / jnp.sum(p, axis=1, keepdims=True))
            both.append(mm(p.astype(jnp.bfloat16), v_ref[0:n, :]))
        out = jnp.where(first, both[0], both[1])
        att_ref[at, :] = out
        gs[step, me, at, :] = (out * sig_ref[at, :]).astype(jnp.bfloat16).astype(F32)
        if n % half == 0:
            gate(step, n // half - 1).start()
            gate(step, n // half + 1).start()

    @pl.when(step == 0)
    def _():
        pass_on(lambda j: torus(0, j))

    @pl.when(step > 0)
    def _():
        pass_on(lambda j: gate(step - 1, j))

    @pl.when(step == pl.num_programs(0) - 1)
    def _():
        torus(1, 1).wait_recv()
        cross(1).start()
        torus(1, 2).wait_recv()
        cross(2).start()
        torus(1, 4).wait_recv()
        torus(1, 5).wait_recv()
        cross(3).start()
        pass_on(lambda j: gate(step, j))
        for j in range(4):
            cross(j).wait_recv()
        tall, wide, shard = ws.shape[4], ws.shape[5], w_ref.shape[0]

        def turn(k, carry):
            y, m = k // 8, lax.rem(k, 8)
            x, z = m // 2, lax.rem(m, 2) * 2
            rows = pl.ds(pl.multiple_of(y * shard + m * 2 * tall, 16), 2 * tall)
            for h, one, two in (
                (0, ws[0, z, x, y], ws[0, z + 1, x, y]),
                (1, ws[1, x, z, y], ws[1, x, z + 1, y]),
            ):
                both = jnp.concatenate([one, two], axis=0).astype(jnp.bfloat16)
                full_ref[rows, h * wide : h * wide + wide] = both
            return carry

        lax.fori_loop(0, 8 * Y, turn, 0)
        flush(1).start()
        pairs = gs.shape[0]
        for pair in range(pairs):
            arrived(lambda j: gate(pair, j))
            for y in range(Y):
                lane = (y * pairs + pair) * PAIR
                gated_ref[:, lane : lane + PAIR] = gs[pair, y].astype(jnp.bfloat16)
        flush(2).start()
        for j in range(3):
            flush(j).wait()
            plane(j).wait_send()
        for stage in (0, 1):
            for j in range(6):
                torus(stage, j).wait_send()
        for j in range(4):
            cross(j).wait_send()
        for pair in range(pairs):
            for j in range(6):
                gate(pair, j).wait_send()


def forward_attention(tokens, length, gain, wq, wk, wv, wo, wf, bf, w_out, call_id):
    seq, width = tokens.shape
    heads = wq.shape[1]
    weights = pl.BlockSpec((width, PAIR), lambda i, _: (0, i))
    lanes = pl.BlockSpec((seq, PAIR), lambda i, _: (0, i))
    low = jnp.bfloat16
    return local_call(
        forward_kernel,
        heads // PAIR,
        [whole((seq, width)), whole((1, width))] + [weights] * 4 + [whole(wf.shape), whole(bf.shape), whole(w_out.shape)],
        [HBM] + [lanes] * 6 + [whole((2, seq, PAIR)), HBM, HBM],
        [
            struct(seq, width, t=low), struct(seq, heads), struct(seq, heads), struct(seq, heads, t=low),
            struct(seq, heads), struct(seq, heads), struct(seq, heads),
            struct(2, seq, PAIR), struct(seq, heads * Y, t=low), struct(heads * Y, width, t=low),
        ],
        [
            pltpu.VMEM((seq, PAIR), F32),
            pltpu.VMEM((8, seq), F32),
            pltpu.VMEM((seq, PAIR), low),
            pltpu.VMEM((seq, PAIR), low),
            pltpu.VMEM((width, 4 * PAIR), low),
            pltpu.VMEM((seq, 4 * PAIR), F32),
            pltpu.VMEM((heads // PAIR, Y, seq, PAIR), F32),
            pltpu.VMEM((2, 4, 4, Y, heads // 16, width // 2), F32),
            pltpu.VMEM((PAIR, width), low),
            pltpu.VMEM((8, PAIR), F32),
            pltpu.VMEM((seq, width), low),
            pltpu.VMEM((seq, width), low),
            pltpu.VMEM((heads * Y, width), low),
            pltpu.SemaphoreType.DMA((3,)),
        ]
        + sems(6 * (heads // PAIR), 3, 6, 6, 4),
        56, 6, 20, call_id,
    )(length, tokens, gain, wq, wk, wv, wo, wf, bf, w_out)


def copier(sem):
    count = iter(range(sem.shape[0]))

    def copy(src, dst):
        return load(src, dst, sem.at[next(count)])

    return copy


def mlp_forward_kernel(
    length_ref, x_in, cot_in, gated_in, gain_ref, wo_in, wg_in, wu_in, wd_in,
    mid_out, low_out, grad_out, gate_out, up_out, hid_out, out_out, sums_ref,
    x_ref, cot_ref, gated_ref, wo_ref, wg_ref, wu_ref, wd_ref,
    mid_ref, low_ref, grad_ref, gate_ref, up_ref, hid_ref, out_ref, sem,
):
    seq, width = x_ref.shape
    length = length_ref[0]
    tile, units = wo_ref.shape[2], hid_ref.shape[1] // 2
    copy = copier(sem)
    columns = lambda j, size: pl.ds(pl.multiple_of(j * size, size), size)
    outer = lambda j: pltpu.make_async_copy(
        wo_in.at[:, columns(j, tile)], wo_ref.at[j], sem.at[sem.shape[0] - 2 + j]
    )
    need = copy(gated_in, gated_ref)
    outer(0).start()
    need_x = copy(x_in, x_ref)
    need.wait()
    outer(1).start()
    need_cot = copy(cot_in, cot_ref)
    weights = [copy(wg_in, wg_ref), copy(wu_in, wu_ref), copy(wd_in, wd_ref)]
    kept = lax.broadcasted_iota(jnp.int32, (seq, 1), 0) < length
    flushes = []

    def project(j):
        at = columns(j, tile)
        outer(j).wait()
        branch = mm(gated_ref[...], wo_ref[j])
        x = x_ref[:, at].astype(F32)
        mid_ref[:, at] = x + branch
        sums_ref[0:1, at] = jnp.sum(jnp.where(kept, x * x, 0.0), axis=0, keepdims=True)
        sums_ref[1:2, at] = jnp.sum(jnp.where(kept, branch * branch, 0.0), axis=0, keepdims=True)

    need_x.wait()
    each(0, 2, project)
    flushes.append(copy(mid_ref, mid_out))

    def norm(i, carry):
        at = rows_at(i, 128)
        mid = mid_ref[at, :]
        r = lax.rsqrt(jnp.mean(mid * mid, axis=1, keepdims=True) + EPSILON)
        low_ref[at, :] = (mid * r * gain_ref[...].astype(F32)).astype(jnp.bfloat16)
        return carry

    lax.fori_loop(0, seq // 128, norm, 0)
    flushes.append(copy(low_ref, low_out))
    weights[0].wait()
    weights[1].wait()

    def hidden(j):
        at = columns(j, units)
        gate_ref[:, at] = mm(low_ref[...], wg_ref[:, at])
        up_ref[:, at] = mm(low_ref[...], wu_ref[:, at])
        gate = gate_ref[:, at]
        hid_ref[:, at] = (gate * jax.nn.sigmoid(gate) * up_ref[:, at]).astype(jnp.bfloat16)

    each(0, 2, hidden)
    for src, dst in ((gate_ref, gate_out), (up_ref, up_out), (hid_ref, hid_out)):
        flushes.append(copy(src, dst))
    need_cot.wait()
    grad_ref[...] = jnp.where(kept, cot_ref[...].astype(F32), 0.0).astype(jnp.bfloat16)
    flushes.append(copy(grad_ref, grad_out))
    weights[2].wait()
    result = lambda j: pltpu.make_async_copy(
        out_ref.at[:, columns(j, tile)], out_out.at[:, columns(j, tile)], sem.at[sem.shape[0] - 4 + j]
    )

    def project_out(j):
        at = columns(j, tile)
        out_ref[:, at] = mm(hid_ref[...], wd_ref[:, at])
        result(j).start()

    each(0, 2, project_out)
    flushes += [result(0), result(1)]
    for c in flushes:
        c.wait()


def mlp_forward(tokens, cotangent, length, gated, gain, wo, wg, wu, wd):
    seq, width = tokens.shape
    hidden = wg.shape[1]
    low = jnp.bfloat16
    smem = pl.BlockSpec(memory_space=pltpu.SMEM)
    outs = [
        struct(seq, width), struct(seq, width, t=low), struct(seq, width, t=low),
        struct(seq, hidden), struct(seq, hidden), struct(seq, hidden, t=low), struct(seq, width),
    ]
    return pl.pallas_call(
        mlp_forward_kernel,
        in_specs=[smem, HBM, HBM, HBM, VMEM] + [HBM] * 4,
        out_specs=[HBM] * 7 + [VMEM],
        out_shape=outs + [struct(2, width)],
        scratch_shapes=[
            pltpu.VMEM((seq, width), low),
            pltpu.VMEM((seq, width), low),
            pltpu.VMEM((seq, width), low),
            pltpu.VMEM((2, width, width // 2), low),
            pltpu.VMEM((width, hidden), low),
            pltpu.VMEM((width, hidden), low),
            pltpu.VMEM((hidden, width), low),
        ]
        + [pltpu.VMEM(out.shape, out.dtype) for out in outs]
        + [pltpu.SemaphoreType.DMA((18,))],
        compiler_params=pltpu.CompilerParams(vmem_limit_bytes=58 << 20),
    )(length, tokens, cotangent, gated, gain, wo, wg, wu, wd)


def reduce_links(rows, x, opp, nbr, held, sem):
    dp, me = lax.axis_index("dp"), lax.axis_index("mp")
    right, left, far = lax.rem(me + 1, Y), lax.rem(me + 3, Y), lax.rem(me + 2, Y)
    q, h = rows // Y, rows // Y // 2

    def message(name):
        src, dst, to = {
            "oR": (lambda: rows_of(x, far * q, h), lambda: opp.at[0], right),
            "oL": (lambda: rows_of(x, far * q + h, h), lambda: opp.at[1], left),
            "iR": (lambda: rows_of(x, right * q + h, h), lambda: nbr.at[0, h:q], right),
            "iL": (lambda: rows_of(x, left * q, h), lambda: nbr.at[1, 0:h], left),
            "dR": (lambda: held.at[0], lambda: nbr.at[0, 0:h], right),
            "dL": (lambda: held.at[1], lambda: nbr.at[1, h:q], left),
        }[name]
        return link(src(), dst(), *sem, STEPS.index(name), (dp, to))

    return message, me, right, left, [(dp, right), (dp, left)]


def mlp_backward_kernel(
    length_ref, grad_in, low_in, gate_in, up_in, hid_in, wd_in, wg_in, wu_in, x_ref, mid_ref,
    back_out, gd_out, gg_out, gu_out, layer_ref, square_ref,
    grad_ref, low_ref, gate_ref, up_ref, hid_ref, wd_ref, wg_ref, wu_ref,
    dg_s, du_s, back_s, bufs, opp, nbr, held, own_s, mid_s, csem, *sem,
):
    seq, width = grad_ref.shape
    units = wd_ref.shape[0] // 2
    low16 = jnp.bfloat16
    message, me, right, left, peers = reduce_links(seq, x_ref, opp, nbr, held, sem)
    q, h = seq // Y, seq // Y // 2
    copy = copier(csem)
    need = [
        copy(grad_in, grad_ref),
        copy(wd_in.at[0:units], wd_ref.at[0:units]),
        copy(gate_in.at[:, 0:units], gate_ref.at[:, 0:units]),
        copy(up_in.at[:, 0:units], up_ref.at[:, 0:units]),
    ]
    meet(peers)
    for name in STEPS[:4]:
        message(name).start()
    for c in need[0:2]:
        c.wait()
    next_low, next_hid = copy(low_in, low_ref), copy(hid_in, hid_ref)
    more = [
        copy(wd_in.at[units:], wd_ref.at[units:]),
        copy(gate_in.at[:, units:], gate_ref.at[:, units:]),
        copy(up_in.at[:, units:], up_ref.at[:, units:]),
    ]
    weights = [copy(wg_in, wg_ref), copy(wu_in, wu_ref)]
    adds = [
        copy(rows_of(x_ref, right * q, h), held.at[0]),
        copy(rows_of(x_ref, left * q + h, h), held.at[1]),
        copy(rows_of(x_ref, me * q, q), own_s),
        copy(rows_of(mid_ref, me * q, q), mid_s),
    ]
    spots = (gd_out, gg_out, gu_out)
    columns = lambda j: pl.ds(pl.multiple_of(j * units, units), units)
    flush = lambda j, which: pltpu.make_async_copy(
        bufs.at[which, j], spots[which].at[:, columns(j)], csem.at[csem.shape[0] - 6 + which * 2 + j]
    )

    def write(which, left_of, right_of, j):
        slot, at = bufs.at[which, j], columns(j)

        def rows(i, carry):
            part = rows_at(i, 768)
            slot[part, :] = t_mm(left_of[:, part], right_of[:, at])
            return carry

        lax.fori_loop(0, width // 768, rows, 0)
        flush(j, which).start()

    def tile(j):
        at = columns(j)

        @pl.when(j == 1)
        def _():
            for c in more:
                c.wait()

        grad = mm_t(grad_ref[...], wd_ref[at, :])

        @pl.when(j == 0)
        def _():
            for c in need[2:4]:
                c.wait()

        gate = gate_ref[:, at]
        sig = jax.nn.sigmoid(gate)
        dg_s[:, at] = (grad * up_ref[:, at] * (sig * (1.0 + gate * (1.0 - sig)))).astype(low16)
        du_s[:, at] = (grad * (gate * sig)).astype(low16)

        @pl.when(j == 0)
        def _():
            next_low.wait()
            next_hid.wait()

        write(0, grad_ref, hid_ref, j)
        write(1, low_ref, dg_s, j)

        @pl.when(j == 1)
        def _():
            for part, (come, go) in enumerate((("oR", "dR"), ("oL", "dL"))):
                message(come).wait_recv()
                adds[part].wait()
                held[part] = held[part] + opp[part]
                message(go).start()

        write(2, low_ref, du_s, j)

    each(0, 2, tile)
    for c in weights:
        c.wait()

    def back(i, carry):
        rows = rows_at(i, 768)
        back_s[:, rows] = mm_t(dg_s[...], wg_ref[rows, :])
        back_s[:, rows] = back_s[:, rows] + mm_t(du_s[...], wu_ref[rows, :])
        return carry

    lax.fori_loop(0, width // 768, back, 0)
    last = copy(back_s, back_out)
    adds[2].wait()
    adds[3].wait()
    sums = 0.0
    for part, names in enumerate((("dR", "iL"), ("iR", "dL"))):
        for name in names:
            message(name).wait_recv()
        at = slice(part * h, part * h + h)
        branch = own_s[at, :] + nbr[0, at] + nbr[1, at]
        layer_ref[at, :] = (mid_s[at, :] + branch).astype(low16).astype(F32)
        row = lax.broadcasted_iota(jnp.int32, (h, 1), 0) + (me * q + part * h)
        kept = jnp.where(row < length_ref[0], branch * branch, 0.0)
        sums = sums + jnp.sum(kept, axis=0, keepdims=True)
    square_ref[...] = sums
    last.wait()
    for j in (0, 1):
        for which in range(3):
            flush(j, which).wait()
    for name in STEPS[:6]:
        message(name).wait_send()


def mlp_backward(length, grad, low, gate, up, hid, wg, wu, wd, branch, mid, call_id):
    seq, width = low.shape
    hidden = wg.shape[1]
    quarter = seq // Y
    low16 = jnp.bfloat16
    smem = pl.BlockSpec(memory_space=pltpu.SMEM)
    inputs = (grad, low, gate, up, hid, wd, wg, wu)
    return pl.pallas_call(
        mlp_backward_kernel,
        in_specs=[smem] + [HBM] * 10,
        out_specs=[HBM] * 4 + [VMEM] * 2,
        out_shape=[struct(seq, width)] + [struct(width, hidden)] * 3
        + [struct(quarter, width), struct(1, width)],
        scratch_shapes=[pltpu.VMEM(a.shape, a.dtype) for a in inputs]
        + [pltpu.VMEM((seq, hidden), low16)] * 2
        + [pltpu.VMEM((seq, width), F32), pltpu.VMEM((3, 2, width, hidden // 2), F32)]
        + ring_scratch(quarter, width)
        + [pltpu.VMEM((quarter, width), F32)] * 2
        + [pltpu.SemaphoreType.DMA((22,))]
        + sems(6),
        compiler_params=pltpu.CompilerParams(
            vmem_limit_bytes=62 << 20, collective_id=call_id, has_side_effects=True
        ),
    )(length, *inputs, branch, mid)


def backward_kernel(
    length_ref, gg_ref, low_in, qn_ref, kn_ref, v_ref, sig_ref, att_ref, stat_ref,
    decay_ref, wq_ref, wk_ref, wv_ref, wo_ref, wf_ref, own_ref, gated_ref, layer_ref,
    back_out, four_out, gout_out, gf_ref, bias_ref, out_ref,
    k_s, do_s, line_s, dq_s, dk_s, dv_s, all_s, fall_s, w_s, wf_s, lay_s, back_ref, wide_s, low_ref, osem,
    *sem,
):
    step = pl.program_id(0)
    seq, width = low_ref.shape
    length = length_ref[0]
    low16 = jnp.bfloat16
    wide = 4 * PAIR
    dp, me = lax.axis_index("dp"), lax.axis_index("mp")
    right, left = lax.rem(me + 1, Y), lax.rem(me + 3, Y)
    q, h = seq // Y, seq // Y // 2

    def spread(j):
        owner, part, to = (
            (me, 0, right), (me, 1, right), (me, 0, left), (me, 1, left), (left, 0, right), (right, 1, left)
        )[j]
        piece = rows_of(lay_s, owner * q + part * h, h)
        source = layer_ref.at[part * h : part * h + h] if j < 4 else piece
        return link(source, piece, *sem, j, (dp, to))

    def fetch(j):
        pair = ((layer_ref, rows_of(lay_s, me * q, q)), (low_in, low_ref))[j]
        return pltpu.make_async_copy(*pair, osem.at[5 + j])

    @pl.when(step == 0)
    def _():
        meet([(dp, right), (dp, left)])
        for j in range(4):
            spread(j).start()
        for j in (0, 1):
            fetch(j).start()

    @pl.when(step == 1)
    def _():
        spread(0).wait_recv()
        spread(4).start()
        spread(3).wait_recv()
        spread(5).start()

    @pl.when(step == 0)
    def _():
        heads = wf_ref.shape[0]
        wf_s[...] = jnp.zeros_like(wf_s)
        wf_s[0:heads, :] = wf_ref[...]
        decay = decay_ref[0]
        row = lax.broadcasted_iota(jnp.int32, decay.shape, 0)
        final = jnp.sum(jnp.where(row == length - 1, decay, 0.0), axis=0, keepdims=True)
        line_s[...] = jnp.where(row < length, decay, final).T[0:8]
        fall_s[...] = jnp.zeros_like(fall_s)

    base = pl.multiple_of(step * wide, wide)
    part = lambda j: pl.ds(pl.multiple_of(base + j * PAIR, PAIR), PAIR)
    for j, w_ref in enumerate((wq_ref, wk_ref, wv_ref, wo_ref)):
        w_s[:, part(j)] = w_ref[...]
    first = first_head((seq, PAIR))
    gg, sig = gg_ref[...], sig_ref[...]
    do_s[...] = (gg * sig).astype(low16)
    all_s[:, part(3)] = (gg * att_ref[...] * sig * (1.0 - sig)).astype(low16)
    k_s[...] = kn_ref[...].astype(low16)
    dk_s[...] = jnp.zeros_like(dk_s)
    dv_s[...] = jnp.zeros_like(dv_s)
    row = lax.broadcasted_iota(jnp.int32, (seq, PAIR), 0)
    columns, lines = [], [one_row(line_s, 2 * step + head) for head in (0, 1)]
    for head in (0, 1):
        column = jnp.sum(
            jnp.where(lane_is((seq, PAIR), 2 * step + head), decay_ref[0], 0.0), axis=1, keepdims=True
        )
        columns.append(jnp.where(row[:, 0:1] < length, column, -NEG))
    block = first_head((128, PAIR))
    zero = jnp.zeros((128, PAIR), low16)
    lower = lax.broadcasted_iota(jnp.int32, (128, 128), 0) > lax.broadcasted_iota(
        jnp.int32, (128, 128), 1
    )
    for i in range(seq // 128):
        at, n = slice(i * 128, i * 128 + 128), i * 128 + 128
        query = qn_ref[at, :].astype(low16)
        do = do_s[at, :]
        pieces = []
        for head in (0, 1):
            pick = (lambda t: jnp.where(block, t, zero)) if head == 0 else (lambda t: jnp.where(block, zero, t))
            own_q, own_do = pick(query), pick(do)
            one = jnp.where(lane_is((128, PAIR), 2 * step + head), 1.0, 0.0).astype(low16)
            s = mm_t(k_s[0:n, :], own_q)
            s = s * (HEAD ** (-0.5)) + (lines[head][:, at] - columns[head][0:n])
            diagonal = jnp.where(lower, NEG, s[n - 128 :, :])
            s = diagonal if i == 0 else jnp.concatenate([s[: n - 128, :], diagonal], axis=0)
            p = jnp.exp(s)
            p = p * (1.0 / jnp.sum(p, axis=0, keepdims=True))
            gp = mm_t(v_ref[0:n, :], own_do)
            ds = (p * (gp - jnp.sum(p * gp, axis=0, keepdims=True))).astype(low16)
            dv_s[0:n, :] = dv_s[0:n, :] + mm(p.astype(low16), own_do)
            dk_s[0:n, :] = dk_s[0:n, :] + mm(ds, jnp.concatenate([own_q, one], axis=1))
            mark = jnp.where(lane_is((n, PAIR), 2 * step + head), 1.0, 0.0).astype(low16)
            pieces.append(t_mm(ds, jnp.concatenate([k_s[0:n, :], mark], axis=1)))
        dq_s[at, :] = jnp.where(block, pieces[0][:, 0:PAIR], pieces[1][:, 0:PAIR])
        fall_s[at, :] = fall_s[at, :] + pieces[0][:, PAIR:] + pieces[1][:, PAIR:]
    fall_s[...] = fall_s[...] - dk_s[:, PAIR:]
    stat = stat_ref[...]
    for e, n_ref, col, to in ((dq_s, qn_ref, 0, 0), (dk_s, kn_ref, 2, 1)):
        e = e[:, 0:PAIR] * (HEAD ** (-0.5))
        n = n_ref[...]
        a, b = halves_mean(e * n)
        r = jnp.where(first, stat[:, col : col + 1], stat[:, col + 1 : col + 2])
        all_s[:, part(to)] = (r * (e - n * jnp.where(first, a, b))).astype(low16)
    all_s[:, part(2)] = dv_s[...].astype(low16)
    slot = lax.rem(step, 2)

    @pl.when(step == 0)
    def _():
        for j in (0, 1):
            fetch(j).wait()

    def flush(j, at, step):
        columns = pl.ds(pl.multiple_of(step * wide, wide), wide)
        out = (four_out, gout_out)[j].at[:, columns]
        return pltpu.make_async_copy(wide_s.at[at, j], out, osem.at[at * 2 + j])

    @pl.when(step == 2)
    def _():
        for j in (0, 1):
            flush(j, 0, 0).wait()

    def grads(k, carry):
        rows = rows_at(k, 768)
        wide_s[slot, 0, rows, :] = t_mm(low_ref[:, rows], all_s[:, pl.ds(base, wide)])
        wide_s[slot, 1, rows, :] = t_mm(own_ref[:, rows].astype(low16), gated_ref[...])
        return carry

    lax.fori_loop(0, width // 768, grads, 0)
    for j in (0, 1):
        flush(j, slot, step).start()

    @pl.when(step == pl.num_programs(0) - 1)
    def _():
        fall = running_sum(fall_s[...], backward=True) * decay_ref[1]
        fall = fall.astype(low16)
        bias_ref[...] = jnp.sum(fall.astype(F32), axis=0, keepdims=True)
        gf_ref[...] = t_mm(fall, low_ref[...])[0:8]

        def tail(k, carry):
            rows = rows_at(k, 768)
            back_ref[:, rows] = mm_t(all_s[...], w_s[rows, :])
            back_ref[:, rows] = back_ref[:, rows] + mm(fall, wf_s[:, rows])
            return carry

        lax.fori_loop(0, width // 768, tail, 0)
        last = load(back_ref, back_out, osem.at[4])
        for j in (1, 2, 4, 5):
            spread(j).wait_recv()
        out_ref[...] = lay_s[...].astype(low16)
        for at, done in ((1, 1), (0, 2)):
            for j in (0, 1):
                flush(j, at, done).wait()
        last.wait()
        for j in range(6):
            spread(j).wait_send()


def backward_attention(place, gg, low, qn, kn, v, sig, att, stat, decay, wq, wk, wv, wo, wf, own, gated, layer, call_id):
    seq, width = low.shape
    heads = wq.shape[1]
    weights = pl.BlockSpec((width, PAIR), lambda i, _: (0, i))
    lanes = pl.BlockSpec((seq, PAIR), lambda i, _: (0, i))
    full = whole((seq, width))
    low16 = jnp.bfloat16
    return local_call(
        backward_kernel,
        heads // PAIR,
        [lanes, HBM] + [lanes] * 6 + [whole((2, seq, PAIR))] + [weights] * 4
        + [whole(wf.shape), whole(own.shape)]
        + [pl.BlockSpec((own.shape[0], 4 * PAIR), lambda i, _: (lax.axis_index("mp"), i)), HBM],
        [HBM, HBM, HBM, whole((8, width)), whole((1, PAIR)), full],
        [
            struct(seq, width), struct(width, 4 * heads), struct(width, width), struct(8, width),
            struct(1, PAIR), struct(seq, width, t=low16),
        ],
        [
            pltpu.VMEM((seq, PAIR), low16),
            pltpu.VMEM((seq, PAIR), low16),
            pltpu.VMEM((8, seq), F32),
            pltpu.VMEM((seq, PAIR), F32),
            pltpu.VMEM((seq, 2 * PAIR), F32),
            pltpu.VMEM((seq, PAIR), F32),
            pltpu.VMEM((seq, 4 * heads), low16),
            pltpu.VMEM((seq, PAIR), F32),
            pltpu.VMEM((width, 4 * heads), low16),
            pltpu.VMEM((PAIR, width), low16),
            pltpu.VMEM((seq, width), F32),
            pltpu.VMEM((seq, width), F32),
            pltpu.VMEM((2, 2, width, 4 * PAIR), F32),
            pltpu.VMEM((seq, width), low16),
            pltpu.SemaphoreType.DMA((7,)),
        ]
        + sems(6),
        62, 14, 50, call_id,
    )(place, gg, low, qn, kn, v, sig, att, stat, decay, wq, wk, wv, wo, wf, own, gated, layer)


def finish_kernel(
    grad_in, layer_in, wout_in, four_in, mlp_in, sums_in,
    grad_ref, layer_ref, wout_ref, q_ref, k_ref, v_ref, o_ref, gate_ref, up_ref, down_ref,
    gain_ref, gain2_ref, fall_ref, rms_ref, bias_ref,
    grad_s, layer_s, sem,
):
    rows = grad_in.shape[0] // 4
    parts = [slice(j * rows, j * rows + rows) for j in range(4)]
    come, copies = [], []
    for src, mid, dst in ((grad_in, grad_s, grad_ref), (layer_in, layer_s, layer_ref)):
        for part in parts:
            come.append((load(src.at[part], mid.at[part], sem.at[len(come)]), mid.at[part], dst.at[part]))
    wout_ref[...] = wout_in[...]
    inner = q_ref.shape[1]
    for j, ref in enumerate((q_ref, k_ref, v_ref, o_ref)):
        for pair in range(inner // PAIR):
            lane = (pair * 4 + j) * PAIR
            ref[:, pair * PAIR : pair * PAIR + PAIR] = four_in[:, lane : lane + PAIR]
    units = gate_ref.shape[1]
    down_ref[...] = mlp_in[:, 0:units]
    gate_ref[...] = mlp_in[:, units : 2 * units]
    up_ref[:, 0:STEP] = mlp_in[:, 2 * units : 2 * units + STEP]
    up_ref[:, STEP:] = four_in[:, 4 * inner : 4 * inner + STEP]
    share, width = gain_ref.shape[1], sums_in.shape[1]
    row = lax.broadcasted_iota(jnp.int32, (width, share), 0)
    lane = lax.broadcasted_iota(jnp.int32, (width, share), 1)
    pick = jnp.where(row == lane + lax.axis_index("dp") * share, 1.0, 0.0)
    own = jnp.dot(
        sums_in[...], pick, precision=lax.Precision.HIGHEST, preferred_element_type=F32
    )
    gain_ref[...] = own[0:1]
    gain2_ref[...] = own[1:2]
    fall_ref[...] = own[3 : 3 + fall_ref.shape[0]]
    square = lambda row, at: sums_in[row : row + 1, at * PAIR : at * PAIR + NBUCKET]
    squares = jnp.concatenate([square(9, 0), square(9, 1), square(2, 0)], axis=0)
    rms_ref[...] = jnp.sqrt(squares / (square(9, 2) * width))
    bias_ref[...] = sums_in[10:11, 0 : bias_ref.shape[1]]
    for arrived, mid, dst in come:
        arrived.wait()
        copies.append(load(mid, dst, sem.at[8 + len(copies)]))
    for copy in copies:
        copy.wait()


def finish(grad, layer, out_share, share, mlp_share, sums, heads):
    rows, inner = out_share.shape
    units = mlp_share.shape[1] * 2 // 5
    return pl.pallas_call(
        finish_kernel,
        out_shape=[
            struct(*grad.shape), struct(*layer.shape, t=layer.dtype), *[struct(rows, inner)] * 5,
            *[struct(rows, units)] * 3, struct(1, rows), struct(1, rows), struct(heads, rows),
            struct(3, NBUCKET), struct(1, heads),
        ],
        in_specs=[HBM, HBM] + [VMEM] * 4,
        out_specs=[HBM, HBM] + [VMEM] * 13,
        scratch_shapes=[
            pltpu.VMEM(grad.shape, grad.dtype),
            pltpu.VMEM(layer.shape, layer.dtype),
            pltpu.SemaphoreType.DMA((16,)),
        ],
        compiler_params=pltpu.CompilerParams(vmem_limit_bytes=60 << 20),
    )(grad, layer, out_share, share, mlp_share, sums)


def per_device(
    tokens, lengths, buckets, out_cotangent, gain_attn, w_query, w_key, w_value, w_outgate,
    w_forget, b_forget, w_out, gain_mlp, w_gate, w_up, w_down,
):
    x, cotangent = tokens[0], out_cotangent[0]
    heads = w_forget.shape[1]
    gain_in, gain_mid = gain_attn[None], gain_mlp[None]
    weights = (w_query, w_key, w_value, w_outgate, w_forget.T)
    low, qn, kn, value, sig, attended, stat, decay, gated, w_full = forward_attention(
        x, lengths, gain_in, *weights, b_forget[None], w_out, 0
    )
    middle, mid_low, grad_rows, gate, up, hidden, mlp_local, squares = mlp_forward(
        x, cotangent, lengths, gated, gain_mid, w_full, w_gate, w_up, w_down
    )
    mid_local, g_down, g_gate, g_up, layer_own, mlp_square = mlp_backward(
        lengths, grad_rows, mid_low, gate, up, hidden, w_gate, w_up, w_down, mlp_local, middle, 1
    )
    grad_own, gg, mlp_share, mlp_gain = reduce_middle(
        mid_local, middle, grad_rows, gain_mid, w_full, [g_down, g_gate, g_up],
        ((0, 0), (0, 1), (1, 0), (1, 1), (2, 0)), 2,
    )
    in_local, g_four, g_out, g_fall, bias, layer_out = backward_attention(
        lengths, gg, low, qn, kn, value, sig, attended, stat, decay, *weights, grad_own, gated,
        layer_own, 3,
    )
    small = (mlp_gain, g_fall, squares, mlp_square, bias, lengths, buckets)
    input_grad, out_share, share, sums = reduce_input(
        in_local, x, grad_own, gain_in, small, [g_out, g_four, g_up],
        ((0, 0), (0, 1), (0, 2), (1, 0), (1, 1), (1, 2), (2, 1)), 4,
    )
    (
        input_grad, layer_out, g_out, g_query, g_key, g_value, g_outgate, g_gate, g_up, g_down,
        g_gain, g_gain_mid, g_fall, rms, bias,
    ) = finish(input_grad, layer_out, out_share, share, mlp_share, sums, heads)
    return (
        layer_out[None],
        input_grad[None],
        g_gain[0],
        g_query,
        g_key,
        g_value,
        g_outgate,
        g_fall.T,
        bias[0],
        g_out.T,
        g_gain_mid[0],
        g_gate,
        g_up,
        g_down.T,
        rms,
    )


def solution(mesh):
    placed = (
        P("dp", None, None),
        P("dp"),
        P("dp"),
        P("dp", None, None),
        P(),
        P(None, "mp"),
        P(None, "mp"),
        P(None, "mp"),
        P(None, "mp"),
        P(None, "mp"),
        P("mp"),
        P("mp", None),
        P(),
        P(None, "mp"),
        P(None, "mp"),
        P("mp", None),
    )
    return jax.shard_map(
        per_device,
        mesh=mesh,
        in_specs=placed,
        out_specs=(
            P("dp", None, None),
            P("dp", None, None),
            P("dp"),
            P("dp", "mp"),
            P("dp", "mp"),
            P("dp", "mp"),
            P("dp", "mp"),
            P("dp", "mp"),
            P("mp"),
            P("mp", "dp"),
            P("dp"),
            P("dp", "mp"),
            P("dp", "mp"),
            P("mp", "dp"),
            P(),
        ),
        check_vma=False,
    )
```

```python
import functools

import jax
import jax.numpy as jnp
from jax import lax
from jax.experimental import pallas as pl
from jax.experimental.pallas import tpu as pltpu
from jax.sharding import PartitionSpec as P

NBUCKET = 4


EPSILON = 1e-06


MESH = pl.DeviceIdType.MESH
F32 = jnp.float32
Y = 4
STEP = 512
HBM = pl.BlockSpec(memory_space=pl.ANY)
VMEM = pl.BlockSpec(memory_space=pltpu.VMEM)
STEPS = ("oR", "oL", "iR", "iL", "dR", "dL", "gRa", "gRb", "gLa", "gLb", "fR", "fL")


def rows_of(ref, start, count):
    return ref.at[pl.ds(pl.multiple_of(start, 8), count)]


def meet(devices):
    barrier = pltpu.get_barrier_semaphore()
    for device in devices:
        pl.semaphore_signal(barrier, inc=1, device_id=device, device_id_type=MESH)
    pl.semaphore_wait(barrier, len(devices))


def link(src, dst, ssem, rsem, at, device):
    return pltpu.make_async_remote_copy(
        src_ref=src,
        dst_ref=dst,
        send_sem=ssem.at[at],
        recv_sem=rsem.at[at],
        device_id=device,
        device_id_type=MESH,
    )


def push(*args):
    copy = link(*args)
    copy.start()
    return copy


class YRing:
    def __init__(self, rows, waves, ssem, rsem):
        self.sems = (ssem, rsem)
        self.dp, self.me = lax.axis_index("dp"), lax.axis_index("mp")
        self.right, self.left = lax.rem(self.me + 1, Y), lax.rem(self.me + 3, Y)
        self.far = lax.rem(self.me + 2, Y)
        self.quarter, self.half = rows // Y, rows // Y // 2
        self.tall = self.half // waves
        self.sent = {}

    def neighbours(self):
        return [(self.dp, self.right), (self.dp, self.left)]

    def send(self, name, wave, src, dst, to):
        kind, index = divmod(STEPS.index(name), 6)
        at = kind * 12 + wave * 6 + index
        self.sent[name, wave] = push(src, dst, *self.sems, at, (self.dp, to))

    def rows(self, x, owner, part, wave):
        return rows_of(x, owner * self.quarter + part * self.half + wave * self.tall, self.tall)

    def fetch(self, x, held, own, sem):
        self.loads = [
            load(rows_of(x, self.right * self.quarter, self.half), held.at[0], sem.at[0]),
            load(rows_of(x, self.left * self.quarter + self.half, self.half), held.at[1], sem.at[1]),
            load(rows_of(x, self.me * self.quarter, self.quarter), own, sem.at[2]),
        ]

    def start(self, x, opp, nbr, wave):
        w = slice(wave * self.tall, wave * self.tall + self.tall)
        low = slice(self.half + wave * self.tall, self.half + wave * self.tall + self.tall)
        self.send("oR", wave, self.rows(x, self.far, 0, wave), opp.at[0, w], self.right)
        self.send("oL", wave, self.rows(x, self.far, 1, wave), opp.at[1, w], self.left)
        self.send("iR", wave, self.rows(x, self.right, 1, wave), nbr.at[0, low], self.right)
        self.send("iL", wave, self.rows(x, self.left, 0, wave), nbr.at[1, w], self.left)

    def relay(self, opp, nbr, held, wave):
        w = slice(wave * self.tall, wave * self.tall + self.tall)
        low = slice(self.half + wave * self.tall, self.half + wave * self.tall + self.tall)
        for part, (come, go, into, to) in enumerate(
            (("oR", "dR", nbr.at[0, w], self.right), ("oL", "dL", nbr.at[1, low], self.left))
        ):
            self.sent[come, wave].wait_recv()
            if wave == 0:
                self.loads[part].wait()
            held[part, w] = held[part, w] + opp[part, w]
            self.send(go, wave, held.at[part, w], into, to)

    def collect(self, own, nbr, part, wave):
        if part == 0 and wave == 0:
            self.loads[2].wait()
        for name in (("dR", "iL"), ("iR", "dL"))[part]:
            self.sent[name, wave].wait_recv()
        start = part * self.half + wave * self.tall
        at = slice(start, start + self.tall)
        return at, own[at, :] + nbr[0, at] + nbr[1, at]

    def spread(self, part, wave, own, out):
        tag, into = "ab"[part], self.rows(out, self.me, part, wave)
        start = part * self.half + wave * self.tall
        mine = own.at[start : start + self.tall]
        self.send("gR" + tag, wave, mine, into, self.right)
        self.send("gL" + tag, wave, mine, into, self.left)

    def forward(self, wave, out):
        for come, go, owner, part, to in (
            ("gRa", "fR", self.left, 0, self.right),
            ("gLb", "fL", self.right, 1, self.left),
        ):
            self.sent[come, wave].wait_recv()
            block = self.rows(out, owner, part, wave)
            self.send(go, wave, block, block, to)

    def arrive(self, wave):
        for name in ("gRb", "gLa", "fR", "fL"):
            self.sent[name, wave].wait_recv()

    def finish(self):
        for copy in self.sent.values():
            copy.wait_send()


def ring_scratch(quarter, columns):
    return [
        pltpu.VMEM((2, quarter // 2, columns), F32),
        pltpu.VMEM((2, quarter, columns), F32),
        pltpu.VMEM((2, quarter // 2, columns), F32),
    ]


def sems(*counts):
    return [pltpu.SemaphoreType.DMA((n,)) for n in counts for _ in (0, 1)]


class Place:
    def __init__(self):
        self.dp, self.my = lax.axis_index("dp"), lax.axis_index("mp")
        c, z, x = lax.rem(self.dp, 2), lax.rem(self.dp // 2, 4), self.dp // 8
        self.c, self.sib, self.chip = c, self.dp + 1 - 2 * c, x * 4 + z
        self.st1, self.st2 = 4 - 3 * c, 1 + 3 * c
        self.p1, self.p2 = x + c * (z - x), z + c * (x - z)
        step = lambda p, by: lax.rem(p + by, 4)
        self.r1, self.l1, self.o1 = (step(self.p1, by) for by in (1, 3, 2))
        self.r2, self.l2, self.o2 = (step(self.p2, by) for by in (1, 3, 2))

    def device(self, a, b):
        return ((a * self.st1 + b * self.st2) * 2 + self.c, self.my)

    def peers(self):
        return [
            (self.sib, self.my),
            self.device(self.r1, self.p2),
            self.device(self.l1, self.p2),
            self.device(self.p1, self.r2),
            self.device(self.p1, self.l2),
        ]


class ScatterSum:
    def __init__(self, here, sources, own, other, near, last, asem, bsem, lsem, ssem, rsem):
        self.here, self.sources = here, sources
        self.own, self.other, self.near, self.last = own, other, near, last
        self.asem, self.bsem, self.lsem, self.ssem, self.rsem = asem, bsem, lsem, ssem, rsem
        self.n = own.shape[0]
        self.sibling, *to = here.peers()
        self.to = (to[0:2], to[2:4])

    def message(self, name, k, stage):
        at = (k * 2 + stage) * 6 + STEPS.index(name)
        device = self.to[stage][0 if name[1] == "R" else 1]
        here, own = self.here, self.own.at[k]
        if stage:
            own, into, cut = own.at[here.p1], self.last.at[k], (slice(0, 24), slice(24, 48))
            far, right, left = here.o2, here.r2, here.l2
        else:
            into, cut = self.near.at[k], (slice(0, 2), slice(2, 4))
            far, right, left = here.o1, here.r1, here.l1
        row, part, slot = {
            "oR": (far, 0, 0),
            "oL": (far, 1, 1),
            "iR": (right, 1, 3),
            "iL": (left, 0, 4),
            "dR": (right, 0, 2),
            "dL": (left, 1, 5),
        }[name]
        return link(own.at[row, cut[part]], into.at[slot], self.ssem, self.rsem, at, device)

    def whole(self, k):
        own, other = self.own.at[k], self.other.at[k]
        return link(own, other, self.asem, self.bsem, k, self.sibling)

    def exchange(self, k):
        here = self.here
        ref, start, width = self.sources[k]

        def source(block):
            return ref.at[pl.ds(pl.multiple_of(block * 48, 16), 48), pl.ds(start, width)]

        def cross(i, carry):
            a, b = i // 4, lax.rem(i, 4)
            block = source((a * here.st2 + b * here.st1) * 2 + 1 - here.c)
            push(block, self.other.at[k, a, b], self.asem, self.bsem, k, self.sibling)
            return carry

        def fetch(i, carry):
            a, b = i // 4, lax.rem(i, 4)
            block = source((a * here.st1 + b * here.st2) * 2 + here.c)
            pltpu.make_async_copy(block, self.own.at[k, a, b], self.lsem.at[k]).start()
            return carry

        lax.fori_loop(0, 16, cross, 0)
        lax.fori_loop(0, 16, fetch, 0)

    def first(self, k):
        here, own, other = self.here, self.own, self.other
        pltpu.make_async_copy(own.at[k], own.at[k], self.lsem.at[k]).wait()
        self.whole(k).wait_recv()

        def add(p):
            def body(b, carry):
                own[k, p, b] = own[k, p, b] + other[k, p, b]
                return carry

            lax.fori_loop(0, 4, body, 0)

        add(here.o1)
        self.message("oR", k, 0).start()
        self.message("oL", k, 0).start()
        add(here.r1)
        self.message("iR", k, 0).start()
        add(here.l1)
        self.message("iL", k, 0).start()
        add(here.p1)

    def first_relay(self, k):
        here, own, near = self.here, self.own, self.near

        def add(p, at, slot):
            def body(b, carry):
                own[k, p, at + b] = own[k, p, at + b] + near[k, slot, b]
                return carry

            lax.fori_loop(0, 2, body, 0)

        self.message("oR", k, 0).wait_recv()
        add(here.r1, 0, 0)
        self.message("dR", k, 0).start()
        self.message("oL", k, 0).wait_recv()
        add(here.l1, 2, 1)
        self.message("dL", k, 0).start()

    def second(self, k):
        here, own, near = self.here, self.own, self.near
        for name in ("iR", "dR", "iL", "dL"):
            self.message(name, k, 0).wait_recv()

        def add(p):
            h, b = p // 2, lax.rem(p, 2)
            own[k, here.p1, p] = own[k, here.p1, p] + near[k, 2 + h, b] + near[k, 4 + h, b]

        add(here.o2)
        self.message("oR", k, 1).start()
        self.message("oL", k, 1).start()
        add(here.r2)
        self.message("iR", k, 1).start()
        add(here.l2)
        self.message("iL", k, 1).start()
        add(here.p2)

    def second_relay(self, k):
        here, own, last = self.here, self.own, self.last
        self.message("oR", k, 1).wait_recv()
        own[k, here.p1, here.r2, 0:24] = own[k, here.p1, here.r2, 0:24] + last[k, 0]
        self.message("dR", k, 1).start()
        self.message("oL", k, 1).wait_recv()
        own[k, here.p1, here.l2, 24:48] = own[k, here.p1, here.l2, 24:48] + last[k, 1]
        self.message("dL", k, 1).start()

    def result(self, k, out, at):
        here, own, last = self.here, self.own, self.last
        width = own.shape[4]
        for name in ("iR", "dR", "iL", "dL"):
            self.message(name, k, 1).wait_recv()
        columns = pl.ds(pl.multiple_of(at * width, 128), width)
        out[0:24, columns] = own[k, here.p1, here.p2, 0:24] + last[k, 2] + last[k, 4]
        out[24:48, columns] = own[k, here.p1, here.p2, 24:48] + last[k, 3] + last[k, 5]

    def sent(self, k):
        self.whole(k).wait_send()
        for stage in (0, 1):
            for name in STEPS[:6]:
                self.message(name, k, stage).wait_send()


def each(low, high, step):
    def body(k, carry):
        step(k)
        return carry

    lax.fori_loop(low, high, body, 0)


class SmallSum:
    def __init__(self, here, bufs, landed, ssem, rsem):
        self.bufs, self.landed, self.ssem, self.rsem = bufs, landed, ssem, rsem
        turn = lambda p, by: lax.rem(p + by, 4)
        self.stages = [
            [(here.sib, here.my)],
            [here.device(turn(here.p1, by), here.p2) for by in (1, 2, 3)],
            [here.device(here.p1, turn(here.p2, by)) for by in (1, 2, 3)],
            [(here.dp, turn(here.my, by)) for by in (1, 2, 3)],
        ]
        self.far = [self.stages[1][1], self.stages[2][1], self.stages[3][1]]
        self.sent = []

    def send(self, stage):
        for to in self.stages[stage]:
            at = len(self.sent)
            copy = push(self.bufs.at[stage], self.landed.at[at], self.ssem, self.rsem, at, to)
            self.sent.append(copy)

    def take(self, stage):
        value, count = self.bufs[stage], len(self.stages[stage])
        for at in range(len(self.sent) - count, len(self.sent)):
            self.sent[at].wait_recv()
            value = value + self.landed[at]
        self.bufs[stage + 1] = value

    def finish(self):
        for copy in self.sent:
            copy.wait_send()


def scatter_scratch(n, w):
    return [
        pltpu.VMEM((n, 4, 4, 48, w), F32),
        pltpu.VMEM((n, 4, 4, 48, w), F32),
        pltpu.VMEM((n, 6, 2, 48, w), F32),
        pltpu.VMEM((n, 6, 24, w), F32),
        pltpu.SemaphoreType.DMA((n,)),
        pltpu.SemaphoreType.DMA((n,)),
        pltpu.SemaphoreType.DMA((n,)),
        pltpu.SemaphoreType.DMA((12 * n,)),
        pltpu.SemaphoreType.DMA((12 * n,)),
    ]


def scatter_sources(refs, pieces):
    return [(refs[which], at * STEP, STEP) for which, at in pieces]


def norm_back(value, source, base, gain):
    source = source.astype(F32)
    r = lax.rsqrt(jnp.mean(source * source, axis=1, keepdims=True) + EPSILON)
    n = source * r
    e = value * gain.astype(F32)
    inner = jnp.mean(e * n, axis=1, keepdims=True)
    return base.astype(F32) + r * (e - n * inner), jnp.sum(value * n, axis=0, keepdims=True)


def load(ref, scratch, sem):
    copy = pltpu.make_async_copy(ref, scratch, sem)
    copy.start()
    return copy


def middle_kernel(pieces, count, x_ref, source_ref, base_ref, gain_ref, w_ref, *refs):
    ins, refs = refs[:count], refs[count:]
    grad_ref, gg_ref, share_ref, sums_ref = refs[:4]
    source_s, base_s, w_s, opp, nbr, held, own_s, blocks, csem, *sem = refs[4:17]
    here, ring = Place(), YRing(x_ref.shape[0], 2, *sem[0:2])
    total = ScatterSum(here, scatter_sources(ins, pieces), *refs[17:])
    n = total.n
    far = (ring.dp, ring.far)
    meet(ring.neighbours() + [far] + here.peers())
    ring.start(x_ref, opp, nbr, 0)
    q, h = ring.quarter, ring.half
    ring.fetch(x_ref, held, own_s, csem)
    for k in range(n):
        total.exchange(k)
    loads = [
        load(rows_of(source_ref, ring.me * q, q), source_s, csem.at[3]),
        load(rows_of(base_ref, ring.me * q, q), base_s, csem.at[4]),
        load(w_ref, w_s, csem.at[5]),
    ]
    ring.relay(opp, nbr, held, 0)
    ring.start(x_ref, opp, nbr, 1)
    each(0, n, total.first)
    each(0, n - 2, total.first_relay)
    ring.relay(opp, nbr, held, 1)
    for copy in loads:
        copy.wait()
    sums, swaps, keeps = 0.0, [], []
    inner = gg_ref.shape[1]
    for wave in (0, 1):
        for part in (0, 1):
            at, value = ring.collect(own_s, nbr, part, wave)
            value, more = norm_back(value, source_s[at, :], base_s[at, :], gain_ref[...])
            grad_ref[at, :] = value
            sums = sums + more
        tall = ring.tall
        low = jnp.concatenate(
            [grad_ref[part * h + wave * tall : part * h + wave * tall + tall, :] for part in (0, 1)], axis=0
        ).astype(jnp.bfloat16)
        for j, by in enumerate((2, 1, 3, 0)):
            to = lax.rem(ring.me + by, Y)
            blocks[wave, j] = mm_t(low, rows_of(w_s, to * inner, inner)[...])
            for part in (0, 1):
                src = blocks.at[wave, j, part * tall : part * tall + tall]
                into = rows_of(gg_ref, ring.me * q + part * h + wave * tall, tall)
                if by:
                    at = (wave * 3 + j) * 2 + part
                    swaps.append(push(src, into, *sem[2:4], at, (ring.dp, to)))
                else:
                    keeps.append(load(src, into, csem.at[6 + wave * 2 + part]))
        if wave == 0:
            each(n - 2, n, total.first_relay)
    sums_ref[...] = sums
    each(0, n, total.second)
    each(0, n, total.second_relay)
    each(0, n, lambda k: total.result(k, share_ref, k))
    for copy in swaps:
        copy.wait_recv()
    for copy in keeps:
        copy.wait()
    for copy in swaps:
        copy.wait_send()
    ring.finish()
    each(0, n, total.sent)


def reduce_middle(partial, source, base, gain, w_full, grads, pieces, call_id):
    n = len(pieces)
    hbm, vmem = pl.BlockSpec(memory_space=pl.ANY), pl.BlockSpec(memory_space=pltpu.VMEM)
    rows, columns = partial.shape
    quarter, inner = rows // Y, w_full.shape[0] // Y
    return pl.pallas_call(
        functools.partial(middle_kernel, pieces, len(grads)),
        out_shape=[
            jax.ShapeDtypeStruct((quarter, columns), F32),
            jax.ShapeDtypeStruct((rows, inner), F32),
            jax.ShapeDtypeStruct((48, n * STEP), F32),
            jax.ShapeDtypeStruct((1, columns), F32),
        ],
        in_specs=[hbm, hbm, hbm, vmem, hbm] + [hbm] * len(grads),
        out_specs=[vmem, hbm, vmem, vmem],
        scratch_shapes=[
            pltpu.VMEM((quarter, columns), source.dtype),
            pltpu.VMEM((quarter, columns), base.dtype),
            pltpu.VMEM(w_full.shape, w_full.dtype),
        ]
        + ring_scratch(quarter, columns)
        + [
            pltpu.VMEM((quarter, columns), F32),
            pltpu.VMEM((2, 4, quarter // 2, inner), F32),
            pltpu.SemaphoreType.DMA((10,)),
        ]
        + sems(12, 12)
        + scatter_scratch(n, STEP),
        compiler_params=pltpu.CompilerParams(
            collective_id=call_id, has_side_effects=True, vmem_limit_bytes=56 << 20
        ),
    )(partial, source, base, gain, w_full, *grads)


def input_kernel(
    pieces, count, x_ref, source_ref, base_ref, gain_ref, other_ref, fall_ref, square_ref, more_ref,
    bias_ref, length_ref, bucket_ref, *refs
):
    ins, refs = refs[:count], refs[count:]
    out_ref, out_share_ref, share_ref, sums_ref = refs[:4]
    source_s, opp, nbr, held, own_s, mine_s, wide_s, landed, csem, *sem = refs[4:17]
    bufs, arrived, asem, bsem = refs[17:21]
    here, ring = Place(), YRing(x_ref.shape[0], 2, *sem[0:2])
    total = ScatterSum(here, scatter_sources(ins, pieces), *refs[21:])
    tiny = SmallSum(here, bufs, arrived, asem, bsem)
    n, first = total.n, wide_s.shape[1] // STEP
    meet(ring.neighbours() + here.peers() + tiny.far)
    ring.start(x_ref, opp, nbr, 0)
    q, h = ring.quarter, ring.half
    ring.fetch(x_ref, held, own_s, csem)
    copy = load(rows_of(source_ref, ring.me * q, q), source_s, csem.at[3])
    for k in range(n):
        total.exchange(k)
    ring.relay(opp, nbr, held, 0)
    ring.start(x_ref, opp, nbr, 1)
    each(0, n, total.first)
    ring.relay(opp, nbr, held, 1)
    each(0, n - 2, total.first_relay)
    copy.wait()
    sums = 0.0
    for wave in (0, 1):
        for part in (0, 1):
            at, value = ring.collect(own_s, nbr, part, wave)
            value, more = norm_back(value, source_s[at, :], base_ref[at, :], gain_ref[...])
            mine_s[at, :] = value
            ring.spread(part, wave, mine_s, out_ref)
            sums = sums + more
    kept = load(mine_s, rows_of(out_ref, ring.me * q, q), csem.at[4])
    bufs[0, 0:1, :] = sums
    bufs[0, 1:2, :] = other_ref[...]
    bufs[0, 8:16, :] = jnp.zeros_like(bufs[0, 8:16, :])
    bufs[0, 2:3, :] = jnp.zeros((1, sums_ref.shape[1]), F32)
    bufs[0, 3:9, :] = fall_ref[0:6, :]
    lane = lax.broadcasted_iota(jnp.int32, (1, PAIR), 1)
    both = jnp.sum(square_ref[...], axis=1, keepdims=True)
    in_bucket = lambda value: jnp.where(lane == bucket_ref[0], value, 0.0)
    bufs[0, 2:3, 0:PAIR] = in_bucket(jnp.sum(more_ref[...], axis=1, keepdims=True))
    for at, value in enumerate((both[0:1], both[1:2], length_ref[0].astype(F32))):
        bufs[0, 9:10, at * PAIR : at * PAIR + PAIR] = in_bucket(value)
    diagonal = lax.broadcasted_iota(jnp.int32, bias_ref.shape, 0) == lax.broadcasted_iota(
        jnp.int32, bias_ref.shape, 1
    )
    bufs[0, 10:11, 0:PAIR] = jnp.sum(jnp.where(diagonal, bias_ref[...], 0.0), axis=0, keepdims=True)
    tiny.send(0)
    each(n - 2, n, total.first_relay)
    ring.forward(0, out_ref)
    each(0, n, total.second)
    ring.forward(1, out_ref)
    tiny.take(0)
    tiny.send(1)
    each(0, n, total.second_relay)
    tiny.take(1)
    tiny.send(2)
    each(0, first, lambda k: total.result(k, wide_s, k))
    inner = landed.shape[2]
    swaps = []
    for j, by in enumerate((2, 1, 3)):
        to = lax.rem(ring.me + by, Y)
        columns = pl.ds(pl.multiple_of(to * inner, 128), inner)
        swaps.append(push(wide_s.at[:, columns], landed.at[j], *sem[2:4], j, (ring.dp, to)))
    each(first, n, lambda k: total.result(k, share_ref, k - first))
    tiny.take(2)
    tiny.send(3)
    own = wide_s[:, pl.ds(pl.multiple_of(ring.me * inner, 128), inner)]
    for j, copy in enumerate(swaps):
        copy.wait_recv()
        own = own + landed[j]
    out_share_ref[...] = own
    tiny.take(3)
    rows = lax.broadcasted_iota(jnp.int32, sums_ref.shape, 0)
    sums_ref[...] = jnp.where(rows < 3, bufs[4], bufs[3])
    ring.arrive(0)
    ring.arrive(1)
    kept.wait()
    for copy in swaps:
        copy.wait_send()
    tiny.finish()
    ring.finish()
    each(0, n, total.sent)


def reduce_input(partial, source, base, gain, small, grads, pieces, call_id):
    n = len(pieces)
    smem = pl.BlockSpec(memory_space=pltpu.SMEM)
    hbm, vmem = pl.BlockSpec(memory_space=pl.ANY), pl.BlockSpec(memory_space=pltpu.VMEM)
    rows, columns = partial.shape
    quarter, inner = rows // Y, grads[0].shape[1] // Y
    wide = grads[0].shape[1]
    shares = n * STEP - wide
    return pl.pallas_call(
        functools.partial(input_kernel, pieces, len(grads)),
        out_shape=[
            jax.ShapeDtypeStruct(partial.shape, F32),
            jax.ShapeDtypeStruct((48, inner), F32),
            jax.ShapeDtypeStruct((48, shares), F32),
            jax.ShapeDtypeStruct((16, columns), F32),
        ],
        in_specs=[hbm, hbm, vmem, vmem] + [vmem] * 5 + [smem] * 2 + [hbm] * len(grads),
        out_specs=[hbm] + [vmem] * 3,
        scratch_shapes=[pltpu.VMEM((quarter, columns), source.dtype)]
        + ring_scratch(quarter, columns)
        + [
            pltpu.VMEM((quarter, columns), F32),
            pltpu.VMEM((quarter, columns), F32),
            pltpu.VMEM((48, wide), F32),
            pltpu.VMEM((3, 48, inner), F32),
            pltpu.SemaphoreType.DMA((5,)),
        ]
        + sems(24, 3)
        + [pltpu.VMEM((5, 16, columns), F32), pltpu.VMEM((10, 16, columns), F32)]
        + sems(10)
        + scatter_scratch(n, STEP),
        compiler_params=pltpu.CompilerParams(
            collective_id=call_id, has_side_effects=True, vmem_limit_bytes=56 << 20
        ),
    )(partial, source, base, gain, *small, *grads)


HEAD = 64
PAIR = 128
NEG = -1e30


def rows_at(i, size):
    return pl.ds(pl.multiple_of(i * size, size), size)


def lane_is(shape, index):
    return lax.broadcasted_iota(jnp.int32, shape, len(shape) - 1) == index


def first_head(shape):
    return lax.broadcasted_iota(jnp.int32, shape, len(shape) - 1) < HEAD


def halves_mean(values):
    first = first_head(values.shape)
    low = jnp.sum(jnp.where(first, values, 0.0), axis=1, keepdims=True) * (1.0 / HEAD)
    high = jnp.sum(jnp.where(first, 0.0, values), axis=1, keepdims=True) * (1.0 / HEAD)
    return low, high


def one_row(ref, index):
    rows = ref[...]
    picked = lax.broadcasted_iota(jnp.int32, rows.shape, 0) == index
    return jnp.sum(jnp.where(picked, rows, 0.0), axis=0, keepdims=True)


def running_sum(values, backward=False):
    count = values.shape[1]
    at = lax.broadcasted_iota(jnp.int32, values.shape, 1)
    shift = 1
    while shift < count:
        if backward:
            moved = jnp.where(at < count - shift, pltpu.roll(values, count - shift, 1), 0.0)
        else:
            moved = jnp.where(at >= shift, pltpu.roll(values, shift, 1), 0.0)
        values = values + moved
        shift *= 2
    return values


def mm(left, right):
    return jnp.dot(left, right, preferred_element_type=F32)


def mm_t(left, right):
    return lax.dot_general(left, right, (((1,), (1,)), ((), ())), preferred_element_type=F32)


def t_mm(left, right):
    return lax.dot_general(left, right, (((0,), (0,)), ((), ())), preferred_element_type=F32)


def whole(shape):
    return pl.BlockSpec(shape, lambda *_: (0,) * len(shape), pipeline_mode=pl.Buffered(1))


def struct(*shape, t=F32):
    return jax.ShapeDtypeStruct(shape, t)


def local_call(kernel, grid, in_specs, out_specs, out_shape, scratch, limit, flops, moved, call_id=None):
    return pl.pallas_call(
        kernel,
        grid_spec=pltpu.PrefetchScalarGridSpec(
            num_scalar_prefetch=1,
            grid=(grid,),
            in_specs=in_specs,
            out_specs=out_specs,
            scratch_shapes=scratch,
        ),
        out_shape=out_shape,
        compiler_params=pltpu.CompilerParams(
            vmem_limit_bytes=limit << 20,
            collective_id=call_id,
            has_side_effects=call_id is not None,
        ),
        cost_estimate=pl.CostEstimate(
            flops=flops * 10**9, bytes_accessed=moved * 10**6, transcendentals=4 * 10**6
        ),
    )


def forward_kernel(
    length_ref, x_ref, gain_ref, wq_ref, wk_ref, wv_ref, wo_ref, wf_ref, bf_ref, w_ref,
    low_out, qn_ref, kn_ref, v_ref, sig_ref, att_ref, stat_ref, decay_ref, gated_out, full_out,
    top_s, row_s, q_s, k_s, w_s, pre_s, gs, ws, wf_s, bf_s, low_ref, gated_ref, full_ref, osem, *sem,
):
    step = pl.program_id(0)
    seq = x_ref.shape[0]
    length = length_ref[0]
    here = Place()
    me, right, left, far = (lax.rem(here.my + by, Y) for by in (0, 1, 3, 2))
    sibling, right1, left1, right2, left2 = here.peers()
    c, p1, p2, half = here.c, here.p1, here.p2, seq // 2
    mine = ws.at[c, p2, p1, me]
    cross_order = (p2, here.l2, here.r2, here.o2)

    def plane(j):
        return link(mine, mine, *sem[2:4], j, (here.dp, (right, far, left)[j]))

    def torus(stage, j):
        if stage == 0:
            at, spots, to = (lambda p: ws.at[c, p2, p]), (p1, here.l1, here.r1), (right1, left1)
        else:
            at, spots, to = (lambda p: ws.at[c, p]), (p2, here.l2, here.r2), (right2, left2)
        spot, part, side = ((0, 0, 0), (0, 1, 0), (0, 0, 1), (0, 1, 1), (1, 0, 0), (2, 1, 1))[j]
        piece = at(spots[spot]).at[2 * part : 2 * part + 2]
        return link(piece, piece, *sem[4 + 2 * stage : 6 + 2 * stage], j, to[side])

    def cross(j):
        piece = ws.at[c, cross_order[j]]
        return link(piece, piece, *sem[8:10], j, sibling)

    def gate(pair, j):
        owner, part, to = (
            (me, 0, right), (me, 1, right), (me, 0, left), (me, 1, left), (left, 0, right), (right, 1, left)
        )[j]
        piece = gs.at[pair, owner, part * half : part * half + half]
        return link(piece, piece, *sem[0:2], pair * 6 + j, (here.dp, to))

    def flush(j):
        src, dst = ((low_ref, low_out), (full_ref, full_out), (gated_ref, gated_out))[j]
        return pltpu.make_async_copy(src, dst, osem.at[j])

    def pass_on(make):
        make(0).wait_recv()
        make(4).start()
        make(3).wait_recv()
        make(5).start()

    def arrived(make):
        for j in (1, 2, 4, 5):
            make(j).wait_recv()

    @pl.when(step == 0)
    def _():
        tall, wide = ws.shape[4], ws.shape[5]
        two = w_ref[
            pl.ds(pl.multiple_of(here.chip // 2 * (2 * tall), 16), 2 * tall),
            pl.ds(pl.multiple_of(c * wide, 128), wide),
        ].astype(F32)
        mine[...] = jnp.where(lax.rem(here.chip, 2) == 0, two[0:tall], two[tall:])
        meet([(here.dp, right), (here.dp, left), (here.dp, far)] + here.peers())
        for j in range(3):
            plane(j).start()

    @pl.when(step == 0)
    def _():
        def norm(i, carry):
            at = rows_at(i, 128)
            x = x_ref[at, :].astype(F32)
            r = lax.rsqrt(jnp.mean(x * x, axis=1, keepdims=True) + EPSILON)
            low_ref[at, :] = (x * r * gain_ref[...].astype(F32)).astype(jnp.bfloat16)
            return carry

        lax.fori_loop(0, seq // 128, norm, 0)
        flush(0).start()
        heads = wf_ref.shape[0]
        wf_s[...] = jnp.zeros_like(wf_s)
        wf_s[0:heads, :] = wf_ref[...]
        bf_s[...] = jnp.zeros_like(bf_s)
        bf_s[:, 0:heads] = bf_ref[...].astype(F32)
        pre = mm_t(wf_s[...], low_ref[...])[0:8] + jnp.broadcast_to(bf_s[...], (PAIR, PAIR)).T[0:8, 0:1]
        fall = jnp.minimum(pre, 0.0) - jnp.log1p(jnp.exp(-jnp.abs(pre)))
        decay = running_sum(fall)
        column = lax.broadcasted_iota(jnp.int32, decay.shape, 1)
        decay_ref[0] = decay
        decay_ref[1] = jax.nn.sigmoid(-pre)
        row_s[...] = jnp.where(column < length, decay, -NEG)
        final = jnp.sum(jnp.where(column == length - 1, decay, 0.0), axis=1, keepdims=True)
        top = jnp.where(column < length, decay, final)
        top_s[...] = jnp.concatenate([top, jnp.zeros((PAIR - 8, seq), F32)], axis=0).T

    for j, ref in enumerate((wq_ref, wk_ref, wv_ref, wo_ref)):
        w_s[:, j * PAIR : j * PAIR + PAIR] = ref[...]
    pre_s[...] = mm(low_ref[...], w_s[...])

    def norms(i, carry):
        at = rows_at(i, 128)
        for j, n_ref, s, col in ((0, qn_ref, q_s, 0), (1, kn_ref, k_s, 2)):
            pre = pre_s[at, j * PAIR : j * PAIR + PAIR]
            a, b = halves_mean(pre * pre)
            a, b = lax.rsqrt(a + EPSILON), lax.rsqrt(b + EPSILON)
            n = pre * jnp.where(first_head(pre.shape), a, b)
            n_ref[at, :] = n
            s[at, :] = n.astype(jnp.bfloat16)
            here = jnp.where(lane_is(pre.shape, col), a, jnp.where(lane_is(pre.shape, col + 1), b, 0.0))
            stat_ref[at, :] = here if col == 0 else stat_ref[at, :] + here
        v_ref[at, :] = pre_s[at, 2 * PAIR : 3 * PAIR].astype(jnp.bfloat16)
        sig_ref[at, :] = jax.nn.sigmoid(pre_s[at, 3 * PAIR : 4 * PAIR])
        return carry

    lax.fori_loop(0, seq // 128, norms, 0)

    @pl.when(step == 0)
    def _():
        for j in range(3):
            plane(j).wait_recv()
        for j in range(4):
            torus(0, j).start()

    @pl.when(step == 1)
    def _():
        arrived(lambda j: torus(0, j))
        for j in range(4):
            torus(1, j).start()
        cross(0).start()

    @pl.when(step == 2)
    def _():
        pass_on(lambda j: torus(1, j))

    lines = [one_row(row_s, 2 * step + head) for head in (0, 1)]
    first = first_head((128, PAIR))
    zero = jnp.zeros((128, PAIR), jnp.bfloat16)
    upper = lax.broadcasted_iota(jnp.int32, (128, 128), 1) > lax.broadcasted_iota(
        jnp.int32, (128, 128), 0
    )
    for i in range(seq // 128):
        at, n = slice(i * 128, i * 128 + 128), i * 128 + 128
        q = q_s[at, :]
        both = []
        for head in (0, 1):
            own = jnp.where(first, q, zero) if head == 0 else jnp.where(first, zero, q)
            s = mm_t(own, k_s[0:n, :])
            column = jnp.sum(
                jnp.where(lane_is((128, PAIR), 2 * step + head), top_s[at, :], 0.0), axis=1, keepdims=True
            )
            s = s * (HEAD ** (-0.5)) + (column - lines[head][:, 0:n])
            diagonal = jnp.where(upper, NEG, s[:, n - 128 :])
            s = diagonal if i == 0 else jnp.concatenate([s[:, : n - 128], diagonal], axis=1)
            p = jnp.exp(s)
            p = p * (1.0 / jnp.sum(p, axis=1, keepdims=True))
            both.append(mm(p.astype(jnp.bfloat16), v_ref[0:n, :]))
        out = jnp.where(first, both[0], both[1])
        att_ref[at, :] = out
        gs[step, me, at, :] = (out * sig_ref[at, :]).astype(jnp.bfloat16).astype(F32)
        if n % half == 0:
            gate(step, n // half - 1).start()
            gate(step, n // half + 1).start()

    @pl.when(step == 0)
    def _():
        pass_on(lambda j: torus(0, j))

    @pl.when(step > 0)
    def _():
        pass_on(lambda j: gate(step - 1, j))

    @pl.when(step == pl.num_programs(0) - 1)
    def _():
        torus(1, 1).wait_recv()
        cross(1).start()
        torus(1, 2).wait_recv()
        cross(2).start()
        torus(1, 4).wait_recv()
        torus(1, 5).wait_recv()
        cross(3).start()
        pass_on(lambda j: gate(step, j))
        for j in range(4):
            cross(j).wait_recv()
        tall, wide, shard = ws.shape[4], ws.shape[5], w_ref.shape[0]

        def turn(k, carry):
            y, m = k // 8, lax.rem(k, 8)
            x, z = m // 2, lax.rem(m, 2) * 2
            rows = pl.ds(pl.multiple_of(y * shard + m * 2 * tall, 16), 2 * tall)
            for h, one, two in (
                (0, ws[0, z, x, y], ws[0, z + 1, x, y]),
                (1, ws[1, x, z, y], ws[1, x, z + 1, y]),
            ):
                both = jnp.concatenate([one, two], axis=0).astype(jnp.bfloat16)
                full_ref[rows, h * wide : h * wide + wide] = both
            return carry

        lax.fori_loop(0, 8 * Y, turn, 0)
        flush(1).start()
        pairs = gs.shape[0]
        for pair in range(pairs):
            arrived(lambda j: gate(pair, j))
            for y in range(Y):
                lane = (y * pairs + pair) * PAIR
                gated_ref[:, lane : lane + PAIR] = gs[pair, y].astype(jnp.bfloat16)
        flush(2).start()
        for j in range(3):
            flush(j).wait()
            plane(j).wait_send()
        for stage in (0, 1):
            for j in range(6):
                torus(stage, j).wait_send()
        for j in range(4):
            cross(j).wait_send()
        for pair in range(pairs):
            for j in range(6):
                gate(pair, j).wait_send()


def forward_attention(tokens, length, gain, wq, wk, wv, wo, wf, bf, w_out, call_id):
    seq, width = tokens.shape
    heads = wq.shape[1]
    weights = pl.BlockSpec((width, PAIR), lambda i, _: (0, i))
    lanes = pl.BlockSpec((seq, PAIR), lambda i, _: (0, i))
    low = jnp.bfloat16
    return local_call(
        forward_kernel,
        heads // PAIR,
        [whole((seq, width)), whole((1, width))] + [weights] * 4 + [whole(wf.shape), whole(bf.shape), whole(w_out.shape)],
        [HBM] + [lanes] * 6 + [whole((2, 8, seq)), HBM, HBM],
        [
            struct(seq, width, t=low), struct(seq, heads), struct(seq, heads), struct(seq, heads, t=low),
            struct(seq, heads), struct(seq, heads), struct(seq, heads),
            struct(2, 8, seq), struct(seq, heads * Y, t=low), struct(heads * Y, width, t=low),
        ],
        [
            pltpu.VMEM((seq, PAIR), F32),
            pltpu.VMEM((8, seq), F32),
            pltpu.VMEM((seq, PAIR), low),
            pltpu.VMEM((seq, PAIR), low),
            pltpu.VMEM((width, 4 * PAIR), low),
            pltpu.VMEM((seq, 4 * PAIR), F32),
            pltpu.VMEM((heads // PAIR, Y, seq, PAIR), F32),
            pltpu.VMEM((2, 4, 4, Y, heads // 16, width // 2), F32),
            pltpu.VMEM((16, width), low),
            pltpu.VMEM((1, PAIR), F32),
            pltpu.VMEM((seq, width), low),
            pltpu.VMEM((seq, width), low),
            pltpu.VMEM((heads * Y, width), low),
            pltpu.SemaphoreType.DMA((3,)),
        ]
        + sems(6 * (heads // PAIR), 3, 6, 6, 4),
        56, 6, 20, call_id,
    )(length, tokens, gain, wq, wk, wv, wo, wf, bf, w_out)


def copier(sem):
    count = iter(range(sem.shape[0]))

    def copy(src, dst):
        return load(src, dst, sem.at[next(count)])

    return copy


def mlp_forward_kernel(
    length_ref, x_in, cot_in, gated_in, gain_ref, wo_in, wg_in, wu_in, wd_in,
    mid_out, low_out, grad_out, gate_out, up_out, hid_out, out_out, sums_ref,
    x_ref, cot_ref, gated_ref, wo_ref, wg_ref, wu_ref, wd_ref,
    mid_ref, low_ref, grad_ref, gate_ref, up_ref, hid_ref, out_ref, sem,
):
    seq, width = x_ref.shape
    length = length_ref[0]
    tile, units = wo_ref.shape[2], hid_ref.shape[1] // 2
    copy = copier(sem)
    columns = lambda j, size: pl.ds(pl.multiple_of(j * size, size), size)
    outer = lambda j: pltpu.make_async_copy(
        wo_in.at[:, columns(j, tile)], wo_ref.at[j], sem.at[sem.shape[0] - 2 + j]
    )
    need = copy(gated_in, gated_ref)
    outer(0).start()
    need_x = copy(x_in, x_ref)
    need.wait()
    outer(1).start()
    need_cot = copy(cot_in, cot_ref)
    weights = [copy(wg_in, wg_ref), copy(wu_in, wu_ref), copy(wd_in, wd_ref)]
    kept = lax.broadcasted_iota(jnp.int32, (seq, 1), 0) < length
    flushes = []

    def project(j):
        at = columns(j, tile)
        outer(j).wait()
        branch = mm(gated_ref[...], wo_ref[j])
        x = x_ref[:, at].astype(F32)
        mid_ref[:, at] = x + branch
        sums_ref[0:1, at] = jnp.sum(jnp.where(kept, x * x, 0.0), axis=0, keepdims=True)
        sums_ref[1:2, at] = jnp.sum(jnp.where(kept, branch * branch, 0.0), axis=0, keepdims=True)

    need_x.wait()
    each(0, 2, project)
    flushes.append(copy(mid_ref, mid_out))

    def norm(i, carry):
        at = rows_at(i, 128)
        mid = mid_ref[at, :]
        r = lax.rsqrt(jnp.mean(mid * mid, axis=1, keepdims=True) + EPSILON)
        low_ref[at, :] = (mid * r * gain_ref[...].astype(F32)).astype(jnp.bfloat16)
        return carry

    lax.fori_loop(0, seq // 128, norm, 0)
    flushes.append(copy(low_ref, low_out))
    weights[0].wait()
    weights[1].wait()

    def hidden(j):
        at = columns(j, units)
        gate_ref[:, at] = mm(low_ref[...], wg_ref[:, at])
        up_ref[:, at] = mm(low_ref[...], wu_ref[:, at])
        gate = gate_ref[:, at]
        hid_ref[:, at] = (gate * jax.nn.sigmoid(gate) * up_ref[:, at]).astype(jnp.bfloat16)

    each(0, 2, hidden)
    for src, dst in ((gate_ref, gate_out), (up_ref, up_out), (hid_ref, hid_out)):
        flushes.append(copy(src, dst))
    need_cot.wait()
    grad_ref[...] = jnp.where(kept, cot_ref[...].astype(F32), 0.0).astype(jnp.bfloat16)
    flushes.append(copy(grad_ref, grad_out))
    weights[2].wait()
    result = lambda j: pltpu.make_async_copy(
        out_ref.at[:, columns(j, tile)], out_out.at[:, columns(j, tile)], sem.at[sem.shape[0] - 4 + j]
    )

    def project_out(j):
        at = columns(j, tile)
        out_ref[:, at] = mm(hid_ref[...], wd_ref[:, at])
        result(j).start()

    each(0, 2, project_out)
    flushes += [result(0), result(1)]
    for c in flushes:
        c.wait()


def mlp_forward(tokens, cotangent, length, gated, gain, wo, wg, wu, wd):
    seq, width = tokens.shape
    hidden = wg.shape[1]
    low = jnp.bfloat16
    smem = pl.BlockSpec(memory_space=pltpu.SMEM)
    outs = [
        struct(seq, width), struct(seq, width, t=low), struct(seq, width, t=low),
        struct(seq, hidden), struct(seq, hidden), struct(seq, hidden, t=low), struct(seq, width),
    ]
    return pl.pallas_call(
        mlp_forward_kernel,
        in_specs=[smem, HBM, HBM, HBM, VMEM] + [HBM] * 4,
        out_specs=[HBM] * 7 + [VMEM],
        out_shape=outs + [struct(2, width)],
        scratch_shapes=[
            pltpu.VMEM((seq, width), low),
            pltpu.VMEM((seq, width), low),
            pltpu.VMEM((seq, width), low),
            pltpu.VMEM((2, width, width // 2), low),
            pltpu.VMEM((width, hidden), low),
            pltpu.VMEM((width, hidden), low),
            pltpu.VMEM((hidden, width), low),
        ]
        + [pltpu.VMEM(out.shape, out.dtype) for out in outs]
        + [pltpu.SemaphoreType.DMA((18,))],
        compiler_params=pltpu.CompilerParams(vmem_limit_bytes=58 << 20),
    )(length, tokens, cotangent, gated, gain, wo, wg, wu, wd)


def reduce_links(rows, x, opp, nbr, held, sem):
    dp, me = lax.axis_index("dp"), lax.axis_index("mp")
    right, left, far = lax.rem(me + 1, Y), lax.rem(me + 3, Y), lax.rem(me + 2, Y)
    q, h = rows // Y, rows // Y // 2

    def message(name):
        src, dst, to = {
            "oR": (lambda: rows_of(x, far * q, h), lambda: opp.at[0], right),
            "oL": (lambda: rows_of(x, far * q + h, h), lambda: opp.at[1], left),
            "iR": (lambda: rows_of(x, right * q + h, h), lambda: nbr.at[0, h:q], right),
            "iL": (lambda: rows_of(x, left * q, h), lambda: nbr.at[1, 0:h], left),
            "dR": (lambda: held.at[0], lambda: nbr.at[0, 0:h], right),
            "dL": (lambda: held.at[1], lambda: nbr.at[1, h:q], left),
        }[name]
        return link(src(), dst(), *sem, STEPS.index(name), (dp, to))

    return message, me, right, left, [(dp, right), (dp, left)]


def mlp_backward_kernel(
    length_ref, grad_in, low_in, gate_in, up_in, hid_in, wd_in, wg_in, wu_in, x_ref, mid_ref,
    back_out, gd_out, gg_out, gu_out, layer_ref, square_ref,
    grad_ref, low_ref, gate_ref, up_ref, hid_ref, wd_ref, wg_ref, wu_ref,
    dg_s, du_s, back_s, bufs, opp, nbr, held, own_s, mid_s, csem, *sem,
):
    seq, width = grad_ref.shape
    units = wd_ref.shape[0] // 2
    low16 = jnp.bfloat16
    message, me, right, left, peers = reduce_links(seq, x_ref, opp, nbr, held, sem)
    q, h = seq // Y, seq // Y // 2
    copy = copier(csem)
    need = [
        copy(grad_in, grad_ref),
        copy(wd_in.at[0:units], wd_ref.at[0:units]),
        copy(gate_in.at[:, 0:units], gate_ref.at[:, 0:units]),
        copy(up_in.at[:, 0:units], up_ref.at[:, 0:units]),
    ]
    meet(peers)
    for name in STEPS[:4]:
        message(name).start()
    for c in need[0:2]:
        c.wait()
    next_low, next_hid = copy(low_in, low_ref), copy(hid_in, hid_ref)
    more = [
        copy(wd_in.at[units:], wd_ref.at[units:]),
        copy(gate_in.at[:, units:], gate_ref.at[:, units:]),
        copy(up_in.at[:, units:], up_ref.at[:, units:]),
    ]
    weights = [copy(wg_in, wg_ref), copy(wu_in, wu_ref)]
    adds = [
        copy(rows_of(x_ref, right * q, h), held.at[0]),
        copy(rows_of(x_ref, left * q + h, h), held.at[1]),
        copy(rows_of(x_ref, me * q, q), own_s),
        copy(rows_of(mid_ref, me * q, q), mid_s),
    ]
    spots = (gd_out, gg_out, gu_out)
    columns = lambda j: pl.ds(pl.multiple_of(j * units, units), units)
    flush = lambda j, which: pltpu.make_async_copy(
        bufs.at[which, j], spots[which].at[:, columns(j)], csem.at[csem.shape[0] - 6 + which * 2 + j]
    )

    def write(which, left_of, right_of, j):
        slot, at = bufs.at[which, j], columns(j)

        def rows(i, carry):
            part = rows_at(i, 768)
            slot[part, :] = t_mm(left_of[:, part], right_of[:, at])
            return carry

        lax.fori_loop(0, width // 768, rows, 0)
        flush(j, which).start()

    def tile(j):
        at = columns(j)

        @pl.when(j == 1)
        def _():
            for c in more:
                c.wait()

        grad = mm_t(grad_ref[...], wd_ref[at, :])

        @pl.when(j == 0)
        def _():
            for c in need[2:4]:
                c.wait()

        gate = gate_ref[:, at]
        sig = jax.nn.sigmoid(gate)
        dg_s[:, at] = (grad * up_ref[:, at] * (sig * (1.0 + gate * (1.0 - sig)))).astype(low16)
        du_s[:, at] = (grad * (gate * sig)).astype(low16)

        @pl.when(j == 0)
        def _():
            next_low.wait()
            next_hid.wait()

        write(0, grad_ref, hid_ref, j)
        write(1, low_ref, dg_s, j)

        @pl.when(j == 1)
        def _():
            for part, (come, go) in enumerate((("oR", "dR"), ("oL", "dL"))):
                message(come).wait_recv()
                adds[part].wait()
                held[part] = held[part] + opp[part]
                message(go).start()

        write(2, low_ref, du_s, j)

    each(0, 2, tile)
    for c in weights:
        c.wait()

    def back(i, carry):
        rows = rows_at(i, 768)
        back_s[:, rows] = mm_t(dg_s[...], wg_ref[rows, :])
        back_s[:, rows] = back_s[:, rows] + mm_t(du_s[...], wu_ref[rows, :])
        return carry

    lax.fori_loop(0, width // 768, back, 0)
    last = copy(back_s, back_out)
    adds[2].wait()
    adds[3].wait()
    sums = 0.0
    for part, names in enumerate((("dR", "iL"), ("iR", "dL"))):
        for name in names:
            message(name).wait_recv()
        at = slice(part * h, part * h + h)
        branch = own_s[at, :] + nbr[0, at] + nbr[1, at]
        layer_ref[at, :] = (mid_s[at, :] + branch).astype(low16).astype(F32)
        row = lax.broadcasted_iota(jnp.int32, (h, 1), 0) + (me * q + part * h)
        kept = jnp.where(row < length_ref[0], branch * branch, 0.0)
        sums = sums + jnp.sum(kept, axis=0, keepdims=True)
    square_ref[...] = sums
    last.wait()
    for j in (0, 1):
        for which in range(3):
            flush(j, which).wait()
    for name in STEPS[:6]:
        message(name).wait_send()


def mlp_backward(length, grad, low, gate, up, hid, wg, wu, wd, branch, mid, call_id):
    seq, width = low.shape
    hidden = wg.shape[1]
    quarter = seq // Y
    low16 = jnp.bfloat16
    smem = pl.BlockSpec(memory_space=pltpu.SMEM)
    inputs = (grad, low, gate, up, hid, wd, wg, wu)
    return pl.pallas_call(
        mlp_backward_kernel,
        in_specs=[smem] + [HBM] * 10,
        out_specs=[HBM] * 4 + [VMEM] * 2,
        out_shape=[struct(seq, width)] + [struct(width, hidden)] * 3
        + [struct(quarter, width), struct(1, width)],
        scratch_shapes=[pltpu.VMEM(a.shape, a.dtype) for a in inputs]
        + [pltpu.VMEM((seq, hidden), low16)] * 2
        + [pltpu.VMEM((seq, width), F32), pltpu.VMEM((3, 2, width, hidden // 2), F32)]
        + ring_scratch(quarter, width)
        + [pltpu.VMEM((quarter, width), F32)] * 2
        + [pltpu.SemaphoreType.DMA((22,))]
        + sems(6),
        compiler_params=pltpu.CompilerParams(
            vmem_limit_bytes=62 << 20, collective_id=call_id, has_side_effects=True
        ),
    )(length, *inputs, branch, mid)


def backward_kernel(
    length_ref, gg_ref, low_in, qn_ref, kn_ref, v_ref, sig_ref, att_ref, stat_ref,
    decay_ref, wq_ref, wk_ref, wv_ref, wo_ref, wf_ref, own_ref, gated_ref, layer_ref,
    back_out, four_out, gout_out, gf_ref, bias_ref, out_ref,
    k_s, do_s, line_s, top_s, dq_s, dk_s, dv_s, all_s, fall_s, w_s, wf_s, lay_s, back_ref, wide_s, low_ref, osem,
    *sem,
):
    step = pl.program_id(0)
    seq, width = low_ref.shape
    length = length_ref[0]
    low16 = jnp.bfloat16
    wide = 4 * PAIR
    dp, me = lax.axis_index("dp"), lax.axis_index("mp")
    right, left = lax.rem(me + 1, Y), lax.rem(me + 3, Y)
    q, h = seq // Y, seq // Y // 2

    def spread(j):
        owner, part, to = (
            (me, 0, right), (me, 1, right), (me, 0, left), (me, 1, left), (left, 0, right), (right, 1, left)
        )[j]
        piece = rows_of(lay_s, owner * q + part * h, h)
        source = layer_ref.at[part * h : part * h + h] if j < 4 else piece
        return link(source, piece, *sem, j, (dp, to))

    def fetch(j):
        pair = ((layer_ref, rows_of(lay_s, me * q, q)), (low_in, low_ref))[j]
        return pltpu.make_async_copy(*pair, osem.at[5 + j])

    @pl.when(step == 0)
    def _():
        meet([(dp, right), (dp, left)])
        for j in range(4):
            spread(j).start()
        for j in (0, 1):
            fetch(j).start()

    @pl.when(step == 2)
    def _():
        spread(0).wait_recv()
        spread(4).start()
        spread(3).wait_recv()
        spread(5).start()

    @pl.when(step == 0)
    def _():
        heads = wf_ref.shape[0]
        wf_s[...] = jnp.zeros_like(wf_s)
        wf_s[0:heads, :] = wf_ref[...]
        decay = decay_ref[0]
        column = lax.broadcasted_iota(jnp.int32, decay.shape, 1)
        final = jnp.sum(jnp.where(column == length - 1, decay, 0.0), axis=1, keepdims=True)
        line_s[...] = jnp.where(column < length, decay, final)
        masked = jnp.where(column < length, decay, -NEG)
        top_s[...] = jnp.concatenate([masked, jnp.zeros((PAIR - 8, seq), F32)], axis=0).T
        fall_s[...] = jnp.zeros_like(fall_s)

    base = pl.multiple_of(step * wide, wide)
    part = lambda j: pl.ds(pl.multiple_of(base + j * PAIR, PAIR), PAIR)
    for j, w_ref in enumerate((wq_ref, wk_ref, wv_ref, wo_ref)):
        w_s[:, part(j)] = w_ref[...]
    first = first_head((seq, PAIR))
    gg, sig = gg_ref[...], sig_ref[...]
    do_s[...] = (gg * sig).astype(low16)
    all_s[:, part(3)] = (gg * att_ref[...] * sig * (1.0 - sig)).astype(low16)
    k_s[...] = kn_ref[...].astype(low16)
    dk_s[...] = jnp.zeros_like(dk_s)
    dv_s[...] = jnp.zeros_like(dv_s)
    columns, lines = [], [one_row(line_s, 2 * step + head) for head in (0, 1)]
    for head in (0, 1):
        column = jnp.sum(
            jnp.where(lane_is((seq, PAIR), 2 * step + head), top_s[...], 0.0), axis=1, keepdims=True
        )
        columns.append(column)
    block = first_head((128, PAIR))
    zero = jnp.zeros((128, PAIR), low16)
    lower = lax.broadcasted_iota(jnp.int32, (128, 128), 0) > lax.broadcasted_iota(
        jnp.int32, (128, 128), 1
    )
    for i in range(seq // 128):
        at, n = slice(i * 128, i * 128 + 128), i * 128 + 128
        query = qn_ref[at, :].astype(low16)
        do = do_s[at, :]
        pieces = []
        for head in (0, 1):
            pick = (lambda t: jnp.where(block, t, zero)) if head == 0 else (lambda t: jnp.where(block, zero, t))
            own_q, own_do = pick(query), pick(do)
            one = jnp.where(lane_is((128, PAIR), 2 * step + head), 1.0, 0.0).astype(low16)
            s = mm_t(k_s[0:n, :], own_q)
            s = s * (HEAD ** (-0.5)) + (lines[head][:, at] - columns[head][0:n])
            diagonal = jnp.where(lower, NEG, s[n - 128 :, :])
            s = diagonal if i == 0 else jnp.concatenate([s[: n - 128, :], diagonal], axis=0)
            p = jnp.exp(s)
            p = p * (1.0 / jnp.sum(p, axis=0, keepdims=True))
            gp = mm_t(v_ref[0:n, :], own_do)
            ds = (p * (gp - jnp.sum(p * gp, axis=0, keepdims=True))).astype(low16)
            dv_s[0:n, :] = dv_s[0:n, :] + mm(p.astype(low16), own_do)
            dk_s[0:n, :] = dk_s[0:n, :] + mm(ds, jnp.concatenate([own_q, one], axis=1))
            mark = jnp.where(lane_is((n, PAIR), 2 * step + head), 1.0, 0.0).astype(low16)
            pieces.append(t_mm(ds, jnp.concatenate([k_s[0:n, :], mark], axis=1)))
        dq_s[at, :] = jnp.where(block, pieces[0][:, 0:PAIR], pieces[1][:, 0:PAIR])
        fall_s[at, :] = fall_s[at, :] + pieces[0][:, PAIR:] + pieces[1][:, PAIR:]
    fall_s[...] = fall_s[...] - dk_s[:, PAIR:]
    stat = stat_ref[...]
    for e, n_ref, col, to in ((dq_s, qn_ref, 0, 0), (dk_s, kn_ref, 2, 1)):
        e = e[:, 0:PAIR] * (HEAD ** (-0.5))
        n = n_ref[...]
        a, b = halves_mean(e * n)
        r = jnp.where(first, stat[:, col : col + 1], stat[:, col + 1 : col + 2])
        all_s[:, part(to)] = (r * (e - n * jnp.where(first, a, b))).astype(low16)
    all_s[:, part(2)] = dv_s[...].astype(low16)
    slot = lax.rem(step, 2)

    @pl.when(step == 0)
    def _():
        for j in (0, 1):
            fetch(j).wait()

    def flush(j, at, step):
        columns = pl.ds(pl.multiple_of(step * wide, wide), wide)
        out = (four_out, gout_out)[j].at[:, columns]
        return pltpu.make_async_copy(wide_s.at[at, j], out, osem.at[at * 2 + j])

    @pl.when(step == 2)
    def _():
        for j in (0, 1):
            flush(j, 0, 0).wait()

    def grads(k, carry):
        rows = rows_at(k, 768)
        wide_s[slot, 0, rows, :] = t_mm(low_ref[:, rows], all_s[:, pl.ds(base, wide)])
        wide_s[slot, 1, rows, :] = t_mm(own_ref[:, rows].astype(low16), gated_ref[...])
        return carry

    lax.fori_loop(0, width // 768, grads, 0)
    for j in (0, 1):
        flush(j, slot, step).start()

    @pl.when(step == pl.num_programs(0) - 1)
    def _():
        fall = running_sum(fall_s[...].T[0:8], backward=True) * decay_ref[1]
        fall = jnp.concatenate([fall, jnp.zeros_like(fall)], axis=0).astype(low16)
        bias = jnp.sum(fall.astype(F32), axis=1, keepdims=True)
        bias_ref[...] = jnp.broadcast_to(bias[0:8], (8, PAIR))
        gf_ref[...] = mm(fall, low_ref[...])[0:8]

        def tail(k, carry):
            rows = rows_at(k, 768)
            back_ref[:, rows] = mm_t(all_s[...], w_s[rows, :])
            back_ref[:, rows] = back_ref[:, rows] + t_mm(fall, wf_s[:, rows])
            return carry

        lax.fori_loop(0, width // 768, tail, 0)
        last = load(back_ref, back_out, osem.at[4])
        for j in (1, 2, 4, 5):
            spread(j).wait_recv()
        out_ref[...] = lay_s[...].astype(low16)
        for at, done in ((1, 1), (0, 2)):
            for j in (0, 1):
                flush(j, at, done).wait()
        last.wait()
        for j in range(6):
            spread(j).wait_send()


def backward_attention(place, gg, low, qn, kn, v, sig, att, stat, decay, wq, wk, wv, wo, wf, own, gated, layer, call_id):
    seq, width = low.shape
    heads = wq.shape[1]
    weights = pl.BlockSpec((width, PAIR), lambda i, _: (0, i))
    lanes = pl.BlockSpec((seq, PAIR), lambda i, _: (0, i))
    full = whole((seq, width))
    low16 = jnp.bfloat16
    return local_call(
        backward_kernel,
        heads // PAIR,
        [lanes, HBM] + [lanes] * 6 + [whole((2, 8, seq))] + [weights] * 4
        + [whole(wf.shape), whole(own.shape)]
        + [pl.BlockSpec((own.shape[0], 4 * PAIR), lambda i, _: (lax.axis_index("mp"), i)), HBM],
        [HBM, HBM, HBM, whole((8, width)), whole((8, PAIR)), full],
        [
            struct(seq, width), struct(width, 4 * heads), struct(width, width), struct(8, width),
            struct(8, PAIR), struct(seq, width, t=low16),
        ],
        [
            pltpu.VMEM((seq, PAIR), low16),
            pltpu.VMEM((seq, PAIR), low16),
            pltpu.VMEM((8, seq), F32),
            pltpu.VMEM((seq, PAIR), F32),
            pltpu.VMEM((seq, PAIR), F32),
            pltpu.VMEM((seq, 2 * PAIR), F32),
            pltpu.VMEM((seq, PAIR), F32),
            pltpu.VMEM((seq, 4 * heads), low16),
            pltpu.VMEM((seq, PAIR), F32),
            pltpu.VMEM((width, 4 * heads), low16),
            pltpu.VMEM((16, width), low16),
            pltpu.VMEM((seq, width), F32),
            pltpu.VMEM((seq, width), F32),
            pltpu.VMEM((2, 2, width, 4 * PAIR), F32),
            pltpu.VMEM((seq, width), low16),
            pltpu.SemaphoreType.DMA((7,)),
        ]
        + sems(6),
        62, 14, 50, call_id,
    )(place, gg, low, qn, kn, v, sig, att, stat, decay, wq, wk, wv, wo, wf, own, gated, layer)


def finish_kernel(
    grad_in, layer_in, wout_hbm, four_hbm, mlp_hbm, sums_hbm,
    grad_ref, layer_ref, wout_ref, q_ref, k_ref, v_ref, o_ref, gate_ref, up_ref, down_ref,
    gain_ref, gain2_ref, fall_ref, rms_ref, bias_ref,
    grad_s, layer_s, four_in, mlp_in, sums_in, sem,
):
    copy = copier(sem)
    rows = grad_in.shape[0] // 4
    parts = [slice(j * rows, j * rows + rows) for j in range(4)]
    come = [(copy(grad_in.at[p], grad_s.at[p]), grad_s.at[p], grad_ref.at[p]) for p in parts]
    small = [copy(wout_hbm, wout_ref), copy(four_hbm, four_in), copy(mlp_hbm, mlp_in), copy(sums_hbm, sums_in)]
    come += [(copy(layer_in.at[p], layer_s.at[p]), layer_s.at[p], layer_ref.at[p]) for p in parts]
    copies = []

    def leave(some):
        for arrived, mid, dst in some:
            arrived.wait()
            copies.append(copy(mid, dst))

    leave(come[0:4])
    for c in small:
        c.wait()
    inner = q_ref.shape[1]
    for j, ref in enumerate((q_ref, k_ref, v_ref, o_ref)):
        for pair in range(inner // PAIR):
            lane = (pair * 4 + j) * PAIR
            ref[:, pair * PAIR : pair * PAIR + PAIR] = four_in[:, lane : lane + PAIR]
    units = gate_ref.shape[1]
    down_ref[...] = mlp_in[:, 0:units]
    gate_ref[...] = mlp_in[:, units : 2 * units]
    up_ref[...] = four_in[:, 4 * inner : 4 * inner + units]
    leave(come[4:8])
    share, width = gain_ref.shape[1], sums_in.shape[1]
    row = lax.broadcasted_iota(jnp.int32, (width, share), 0)
    lane = lax.broadcasted_iota(jnp.int32, (width, share), 1)
    pick = jnp.where(row == lane + lax.axis_index("dp") * share, 1.0, 0.0)
    own = jnp.dot(
        sums_in[...], pick, precision=lax.Precision.HIGHEST, preferred_element_type=F32
    )
    gain_ref[...] = own[0:1]
    gain2_ref[...] = own[1:2]
    fall_ref[...] = own[3 : 3 + fall_ref.shape[0]]
    square = lambda row, at: sums_in[row : row + 1, at * PAIR : at * PAIR + NBUCKET]
    squares = jnp.concatenate([square(9, 0), square(9, 1), square(2, 0)], axis=0)
    rms_ref[...] = jnp.sqrt(squares / (square(9, 2) * width))
    bias_ref[...] = sums_in[10:11, 0 : bias_ref.shape[1]]
    for c in copies:
        c.wait()


def finish(grad, layer, out_share, share, mlp_share, sums, heads):
    rows, inner = out_share.shape
    units = mlp_share.shape[1] // 2
    return pl.pallas_call(
        finish_kernel,
        out_shape=[
            struct(*grad.shape), struct(*layer.shape, t=layer.dtype), *[struct(rows, inner)] * 5,
            *[struct(rows, units)] * 3, struct(1, rows), struct(1, rows), struct(heads, rows),
            struct(3, NBUCKET), struct(1, heads),
        ],
        in_specs=[HBM] * 6,
        out_specs=[HBM, HBM] + [VMEM] * 13,
        scratch_shapes=[pltpu.VMEM(a.shape, a.dtype) for a in (grad, layer, share, mlp_share, sums)]
        + [pltpu.SemaphoreType.DMA((20,))],
        compiler_params=pltpu.CompilerParams(vmem_limit_bytes=60 << 20),
    )(grad, layer, out_share, share, mlp_share, sums)


def per_device(
    tokens, lengths, buckets, out_cotangent, gain_attn, w_query, w_key, w_value, w_outgate,
    w_forget, b_forget, w_out, gain_mlp, w_gate, w_up, w_down,
):
    x, cotangent = tokens[0], out_cotangent[0]
    heads = w_forget.shape[1]
    gain_in, gain_mid = gain_attn[None], gain_mlp[None]
    weights = (w_query, w_key, w_value, w_outgate, w_forget.T)
    low, qn, kn, value, sig, attended, stat, decay, gated, w_full = forward_attention(
        x, lengths, gain_in, *weights, b_forget[None], w_out, 0
    )
    middle, mid_low, grad_rows, gate, up, hidden, mlp_local, squares = mlp_forward(
        x, cotangent, lengths, gated, gain_mid, w_full, w_gate, w_up, w_down
    )
    mid_local, g_down, g_gate, g_up, layer_own, mlp_square = mlp_backward(
        lengths, grad_rows, mid_low, gate, up, hidden, w_gate, w_up, w_down, mlp_local, middle, 1
    )
    grad_own, gg, mlp_share, mlp_gain = reduce_middle(
        mid_local, middle, grad_rows, gain_mid, w_full, [g_down, g_gate],
        ((0, 0), (0, 1), (1, 0), (1, 1)), 2,
    )
    in_local, g_four, g_out, g_fall, bias, layer_out = backward_attention(
        lengths, gg, low, qn, kn, value, sig, attended, stat, decay, *weights, grad_own, gated,
        layer_own, 3,
    )
    small = (mlp_gain, g_fall, squares, mlp_square, bias, lengths, buckets)
    input_grad, out_share, share, sums = reduce_input(
        in_local, x, grad_own, gain_in, small, [g_out, g_four, g_up],
        ((0, 0), (0, 1), (0, 2), (1, 0), (1, 1), (1, 2), (2, 0), (2, 1)), 4,
    )
    (
        input_grad, layer_out, g_out, g_query, g_key, g_value, g_outgate, g_gate, g_up, g_down,
        g_gain, g_gain_mid, g_fall, rms, bias,
    ) = finish(input_grad, layer_out, out_share, share, mlp_share, sums, heads)
    return (
        layer_out[None],
        input_grad[None],
        g_gain[0],
        g_query,
        g_key,
        g_value,
        g_outgate,
        g_fall.T,
        bias[0],
        g_out.T,
        g_gain_mid[0],
        g_gate,
        g_up,
        g_down.T,
        rms,
    )


def solution(mesh):
    placed = (
        P("dp", None, None),
        P("dp"),
        P("dp"),
        P("dp", None, None),
        P(),
        P(None, "mp"),
        P(None, "mp"),
        P(None, "mp"),
        P(None, "mp"),
        P(None, "mp"),
        P("mp"),
        P("mp", None),
        P(),
        P(None, "mp"),
        P(None, "mp"),
        P("mp", None),
    )
    return jax.shard_map(
        per_device,
        mesh=mesh,
        in_specs=placed,
        out_specs=(
            P("dp", None, None),
            P("dp", None, None),
            P("dp"),
            P("dp", "mp"),
            P("dp", "mp"),
            P("dp", "mp"),
            P("dp", "mp"),
            P("dp", "mp"),
            P("mp"),
            P("mp", "dp"),
            P("dp"),
            P("dp", "mp"),
            P("dp", "mp"),
            P("mp", "dp"),
            P(),
        ),
        check_vma=False,
    )
```

```python
import functools

import jax
import jax.numpy as jnp
from jax import lax
from jax.experimental import pallas as pl
from jax.experimental.pallas import tpu as pltpu
from jax.sharding import PartitionSpec as P

NBUCKET = 4


EPSILON = 1e-06


MESH = pl.DeviceIdType.MESH
F32 = jnp.float32
Y = 4
STEP = 512
HBM = pl.BlockSpec(memory_space=pl.ANY)
VMEM = pl.BlockSpec(memory_space=pltpu.VMEM)
STEPS = ("oR", "oL", "iR", "iL", "dR", "dL", "gRa", "gRb", "gLa", "gLb", "fR", "fL")


def rows_of(ref, start, count):
    return ref.at[pl.ds(pl.multiple_of(start, 8), count)]


def meet(devices):
    barrier = pltpu.get_barrier_semaphore()
    for device in devices:
        pl.semaphore_signal(barrier, inc=1, device_id=device, device_id_type=MESH)
    pl.semaphore_wait(barrier, len(devices))


def link(src, dst, ssem, rsem, at, device):
    return pltpu.make_async_remote_copy(
        src_ref=src,
        dst_ref=dst,
        send_sem=ssem.at[at],
        recv_sem=rsem.at[at],
        device_id=device,
        device_id_type=MESH,
    )


def push(*args):
    copy = link(*args)
    copy.start()
    return copy


class YRing:
    def __init__(self, rows, waves, ssem, rsem):
        self.sems = (ssem, rsem)
        self.dp, self.me = lax.axis_index("dp"), lax.axis_index("mp")
        self.right, self.left = lax.rem(self.me + 1, Y), lax.rem(self.me + 3, Y)
        self.far = lax.rem(self.me + 2, Y)
        self.quarter, self.half = rows // Y, rows // Y // 2
        self.tall = self.half // waves
        self.sent = {}

    def neighbours(self):
        return [(self.dp, self.right), (self.dp, self.left)]

    def send(self, name, wave, src, dst, to):
        kind, index = divmod(STEPS.index(name), 6)
        at = kind * 12 + wave * 6 + index
        self.sent[name, wave] = push(src, dst, *self.sems, at, (self.dp, to))

    def rows(self, x, owner, part, wave):
        return rows_of(x, owner * self.quarter + part * self.half + wave * self.tall, self.tall)

    def fetch(self, x, held, own, sem):
        self.loads = [
            load(rows_of(x, self.right * self.quarter, self.half), held.at[0], sem.at[0]),
            load(rows_of(x, self.left * self.quarter + self.half, self.half), held.at[1], sem.at[1]),
            load(rows_of(x, self.me * self.quarter, self.quarter), own, sem.at[2]),
        ]

    def start(self, x, opp, nbr, wave):
        w = slice(wave * self.tall, wave * self.tall + self.tall)
        low = slice(self.half + wave * self.tall, self.half + wave * self.tall + self.tall)
        self.send("oR", wave, self.rows(x, self.far, 0, wave), opp.at[0, w], self.right)
        self.send("oL", wave, self.rows(x, self.far, 1, wave), opp.at[1, w], self.left)
        self.send("iR", wave, self.rows(x, self.right, 1, wave), nbr.at[0, low], self.right)
        self.send("iL", wave, self.rows(x, self.left, 0, wave), nbr.at[1, w], self.left)

    def relay(self, opp, nbr, held, wave):
        w = slice(wave * self.tall, wave * self.tall + self.tall)
        low = slice(self.half + wave * self.tall, self.half + wave * self.tall + self.tall)
        for part, (come, go, into, to) in enumerate(
            (("oR", "dR", nbr.at[0, w], self.right), ("oL", "dL", nbr.at[1, low], self.left))
        ):
            self.sent[come, wave].wait_recv()
            if wave == 0:
                self.loads[part].wait()
            held[part, w] = held[part, w] + opp[part, w]
            self.send(go, wave, held.at[part, w], into, to)

    def collect(self, own, nbr, part, wave):
        if part == 0 and wave == 0:
            self.loads[2].wait()
        for name in (("dR", "iL"), ("iR", "dL"))[part]:
            self.sent[name, wave].wait_recv()
        start = part * self.half + wave * self.tall
        at = slice(start, start + self.tall)
        return at, own[at, :] + nbr[0, at] + nbr[1, at]

    def spread(self, part, wave, own, out):
        tag, into = "ab"[part], self.rows(out, self.me, part, wave)
        start = part * self.half + wave * self.tall
        mine = own.at[start : start + self.tall]
        self.send("gR" + tag, wave, mine, into, self.right)
        self.send("gL" + tag, wave, mine, into, self.left)

    def forward(self, wave, out):
        for come, go, owner, part, to in (
            ("gRa", "fR", self.left, 0, self.right),
            ("gLb", "fL", self.right, 1, self.left),
        ):
            self.sent[come, wave].wait_recv()
            block = self.rows(out, owner, part, wave)
            self.send(go, wave, block, block, to)

    def arrive(self, wave):
        for name in ("gRb", "gLa", "fR", "fL"):
            self.sent[name, wave].wait_recv()

    def finish(self):
        for copy in self.sent.values():
            copy.wait_send()


def ring_scratch(quarter, columns):
    return [
        pltpu.VMEM((2, quarter // 2, columns), F32),
        pltpu.VMEM((2, quarter, columns), F32),
        pltpu.VMEM((2, quarter // 2, columns), F32),
    ]


def sems(*counts):
    return [pltpu.SemaphoreType.DMA((n,)) for n in counts for _ in (0, 1)]


class Place:
    def __init__(self):
        self.dp, self.my = lax.axis_index("dp"), lax.axis_index("mp")
        c, z, x = lax.rem(self.dp, 2), lax.rem(self.dp // 2, 4), self.dp // 8
        self.c, self.sib, self.chip = c, self.dp + 1 - 2 * c, x * 4 + z
        self.st1, self.st2 = 4 - 3 * c, 1 + 3 * c
        self.p1, self.p2 = x + c * (z - x), z + c * (x - z)
        step = lambda p, by: lax.rem(p + by, 4)
        self.r1, self.l1, self.o1 = (step(self.p1, by) for by in (1, 3, 2))
        self.r2, self.l2, self.o2 = (step(self.p2, by) for by in (1, 3, 2))

    def device(self, a, b):
        return ((a * self.st1 + b * self.st2) * 2 + self.c, self.my)

    def peers(self):
        return [
            (self.sib, self.my),
            self.device(self.r1, self.p2),
            self.device(self.l1, self.p2),
            self.device(self.p1, self.r2),
            self.device(self.p1, self.l2),
        ]


class ScatterSum:
    def __init__(self, here, sources, own, other, near, last, asem, bsem, lsem, ssem, rsem):
        self.here, self.sources = here, sources
        self.own, self.other, self.near, self.last = own, other, near, last
        self.asem, self.bsem, self.lsem, self.ssem, self.rsem = asem, bsem, lsem, ssem, rsem
        self.n = own.shape[0]
        self.sibling, *to = here.peers()
        self.to = (to[0:2], to[2:4])

    def message(self, name, k, stage):
        at = (k * 2 + stage) * 6 + STEPS.index(name)
        device = self.to[stage][0 if name[1] == "R" else 1]
        here, own = self.here, self.own.at[k]
        if stage:
            own, into, cut = own.at[here.p1], self.last.at[k], (slice(0, 24), slice(24, 48))
            far, right, left = here.o2, here.r2, here.l2
        else:
            into, cut = self.near.at[k], (slice(0, 2), slice(2, 4))
            far, right, left = here.o1, here.r1, here.l1
        row, part, slot = {
            "oR": (far, 0, 0),
            "oL": (far, 1, 1),
            "iR": (right, 1, 3),
            "iL": (left, 0, 4),
            "dR": (right, 0, 2),
            "dL": (left, 1, 5),
        }[name]
        return link(own.at[row, cut[part]], into.at[slot], self.ssem, self.rsem, at, device)

    def whole(self, k):
        own, other = self.own.at[k], self.other.at[k]
        return link(own, other, self.asem, self.bsem, k, self.sibling)

    def exchange(self, k):
        here = self.here
        ref, start, width = self.sources[k]

        def source(block):
            return ref.at[pl.ds(pl.multiple_of(block * 48, 16), 48), pl.ds(start, width)]

        def cross(i, carry):
            a, b = i // 4, lax.rem(i, 4)
            block = source((a * here.st2 + b * here.st1) * 2 + 1 - here.c)
            push(block, self.other.at[k, a, b], self.asem, self.bsem, k, self.sibling)
            return carry

        def fetch(i, carry):
            a, b = i // 4, lax.rem(i, 4)
            block = source((a * here.st1 + b * here.st2) * 2 + here.c)
            pltpu.make_async_copy(block, self.own.at[k, a, b], self.lsem.at[k]).start()
            return carry

        lax.fori_loop(0, 16, cross, 0)
        lax.fori_loop(0, 16, fetch, 0)

    def first(self, k):
        here, own, other = self.here, self.own, self.other
        pltpu.make_async_copy(own.at[k], own.at[k], self.lsem.at[k]).wait()
        self.whole(k).wait_recv()

        def add(p):
            def body(b, carry):
                own[k, p, b] = own[k, p, b] + other[k, p, b]
                return carry

            lax.fori_loop(0, 4, body, 0)

        add(here.o1)
        self.message("oR", k, 0).start()
        self.message("oL", k, 0).start()
        add(here.r1)
        self.message("iR", k, 0).start()
        add(here.l1)
        self.message("iL", k, 0).start()
        add(here.p1)

    def first_relay(self, k):
        here, own, near = self.here, self.own, self.near

        def add(p, at, slot):
            def body(b, carry):
                own[k, p, at + b] = own[k, p, at + b] + near[k, slot, b]
                return carry

            lax.fori_loop(0, 2, body, 0)

        self.message("oR", k, 0).wait_recv()
        add(here.r1, 0, 0)
        self.message("dR", k, 0).start()
        self.message("oL", k, 0).wait_recv()
        add(here.l1, 2, 1)
        self.message("dL", k, 0).start()

    def second(self, k):
        here, own, near = self.here, self.own, self.near
        for name in ("iR", "dR", "iL", "dL"):
            self.message(name, k, 0).wait_recv()

        def add(p):
            h, b = p // 2, lax.rem(p, 2)
            own[k, here.p1, p] = own[k, here.p1, p] + near[k, 2 + h, b] + near[k, 4 + h, b]

        add(here.o2)
        self.message("oR", k, 1).start()
        self.message("oL", k, 1).start()
        add(here.r2)
        self.message("iR", k, 1).start()
        add(here.l2)
        self.message("iL", k, 1).start()
        add(here.p2)

    def second_relay(self, k):
        here, own, last = self.here, self.own, self.last
        self.message("oR", k, 1).wait_recv()
        own[k, here.p1, here.r2, 0:24] = own[k, here.p1, here.r2, 0:24] + last[k, 0]
        self.message("dR", k, 1).start()
        self.message("oL", k, 1).wait_recv()
        own[k, here.p1, here.l2, 24:48] = own[k, here.p1, here.l2, 24:48] + last[k, 1]
        self.message("dL", k, 1).start()

    def result(self, k, out, at):
        here, own, last = self.here, self.own, self.last
        width = own.shape[4]
        for name in ("iR", "dR", "iL", "dL"):
            self.message(name, k, 1).wait_recv()
        columns = pl.ds(pl.multiple_of(at * width, 128), width)
        out[0:24, columns] = own[k, here.p1, here.p2, 0:24] + last[k, 2] + last[k, 4]
        out[24:48, columns] = own[k, here.p1, here.p2, 24:48] + last[k, 3] + last[k, 5]

    def sent(self, k):
        self.whole(k).wait_send()
        for stage in (0, 1):
            for name in STEPS[:6]:
                self.message(name, k, stage).wait_send()


def each(low, high, step):
    def body(k, carry):
        step(k)
        return carry

    lax.fori_loop(low, high, body, 0)


class SmallSum:
    def __init__(self, here, bufs, landed, ssem, rsem):
        self.bufs, self.landed, self.ssem, self.rsem = bufs, landed, ssem, rsem
        turn = lambda p, by: lax.rem(p + by, 4)
        self.stages = [
            [(here.sib, here.my)],
            [here.device(turn(here.p1, by), here.p2) for by in (1, 2, 3)],
            [here.device(here.p1, turn(here.p2, by)) for by in (1, 2, 3)],
            [(here.dp, turn(here.my, by)) for by in (1, 2, 3)],
        ]
        self.far = [self.stages[1][1], self.stages[2][1], self.stages[3][1]]
        self.sent = []

    def send(self, stage):
        for to in self.stages[stage]:
            at = len(self.sent)
            copy = push(self.bufs.at[stage], self.landed.at[at], self.ssem, self.rsem, at, to)
            self.sent.append(copy)

    def take(self, stage):
        value, count = self.bufs[stage], len(self.stages[stage])
        for at in range(len(self.sent) - count, len(self.sent)):
            self.sent[at].wait_recv()
            value = value + self.landed[at]
        self.bufs[stage + 1] = value

    def finish(self):
        for copy in self.sent:
            copy.wait_send()


def scatter_scratch(n, w):
    return [
        pltpu.VMEM((n, 4, 4, 48, w), F32),
        pltpu.VMEM((n, 4, 4, 48, w), F32),
        pltpu.VMEM((n, 6, 2, 48, w), F32),
        pltpu.VMEM((n, 6, 24, w), F32),
        pltpu.SemaphoreType.DMA((n,)),
        pltpu.SemaphoreType.DMA((n,)),
        pltpu.SemaphoreType.DMA((n,)),
        pltpu.SemaphoreType.DMA((12 * n,)),
        pltpu.SemaphoreType.DMA((12 * n,)),
    ]


def scatter_sources(refs, pieces):
    return [(refs[which], at * STEP, STEP) for which, at in pieces]


def norm_back(value, source, base, gain):
    source = source.astype(F32)
    r = lax.rsqrt(jnp.mean(source * source, axis=1, keepdims=True) + EPSILON)
    n = source * r
    e = value * gain.astype(F32)
    inner = jnp.mean(e * n, axis=1, keepdims=True)
    return base.astype(F32) + r * (e - n * inner), jnp.sum(value * n, axis=0, keepdims=True)


def load(ref, scratch, sem):
    copy = pltpu.make_async_copy(ref, scratch, sem)
    copy.start()
    return copy


def middle_kernel(pieces, count, x_ref, source_ref, base_ref, gain_ref, w_ref, *refs):
    ins, refs = refs[:count], refs[count:]
    grad_ref, gg_ref, share_ref, sums_ref = refs[:4]
    source_s, base_s, w_s, opp, nbr, held, own_s, blocks, csem, *sem = refs[4:17]
    here, ring = Place(), YRing(x_ref.shape[0], 2, *sem[0:2])
    total = ScatterSum(here, scatter_sources(ins, pieces), *refs[17:])
    n = total.n
    far = (ring.dp, ring.far)
    meet(ring.neighbours() + [far] + here.peers())
    ring.start(x_ref, opp, nbr, 0)
    q, h = ring.quarter, ring.half
    ring.fetch(x_ref, held, own_s, csem)
    for k in range(n):
        total.exchange(k)
    loads = [
        load(rows_of(source_ref, ring.me * q, q), source_s, csem.at[3]),
        load(rows_of(base_ref, ring.me * q, q), base_s, csem.at[4]),
        load(w_ref, w_s, csem.at[5]),
    ]
    ring.relay(opp, nbr, held, 0)
    ring.start(x_ref, opp, nbr, 1)
    each(0, n, total.first)
    each(0, n - 2, total.first_relay)
    ring.relay(opp, nbr, held, 1)
    for copy in loads:
        copy.wait()
    sums, swaps, keeps = 0.0, [], []
    inner = gg_ref.shape[1]
    for wave in (0, 1):
        for part in (0, 1):
            at, value = ring.collect(own_s, nbr, part, wave)
            value, more = norm_back(value, source_s[at, :], base_s[at, :], gain_ref[...])
            grad_ref[at, :] = value
            sums = sums + more
        tall = ring.tall
        low = jnp.concatenate(
            [grad_ref[part * h + wave * tall : part * h + wave * tall + tall, :] for part in (0, 1)], axis=0
        ).astype(jnp.bfloat16)
        for j, by in enumerate((2, 1, 3, 0)):
            to = lax.rem(ring.me + by, Y)
            blocks[wave, j] = mm_t(low, rows_of(w_s, to * inner, inner)[...])
            for part in (0, 1):
                src = blocks.at[wave, j, part * tall : part * tall + tall]
                into = rows_of(gg_ref, ring.me * q + part * h + wave * tall, tall)
                if by:
                    at = (wave * 3 + j) * 2 + part
                    swaps.append(push(src, into, *sem[2:4], at, (ring.dp, to)))
                else:
                    keeps.append(load(src, into, csem.at[6 + wave * 2 + part]))
        if wave == 0:
            each(n - 2, n, total.first_relay)
    sums_ref[...] = sums
    each(0, n, total.second)
    each(0, n, total.second_relay)
    each(0, n, lambda k: total.result(k, share_ref, k))
    for copy in swaps:
        copy.wait_recv()
    for copy in keeps:
        copy.wait()
    for copy in swaps:
        copy.wait_send()
    ring.finish()
    each(0, n, total.sent)


def reduce_middle(partial, source, base, gain, w_full, grads, pieces, call_id):
    n = len(pieces)
    hbm, vmem = pl.BlockSpec(memory_space=pl.ANY), pl.BlockSpec(memory_space=pltpu.VMEM)
    rows, columns = partial.shape
    quarter, inner = rows // Y, w_full.shape[0] // Y
    return pl.pallas_call(
        functools.partial(middle_kernel, pieces, len(grads)),
        out_shape=[
            jax.ShapeDtypeStruct((quarter, columns), F32),
            jax.ShapeDtypeStruct((rows, inner), F32),
            jax.ShapeDtypeStruct((48, n * STEP), F32),
            jax.ShapeDtypeStruct((1, columns), F32),
        ],
        in_specs=[hbm, hbm, hbm, vmem, hbm] + [hbm] * len(grads),
        out_specs=[vmem, hbm, vmem, vmem],
        scratch_shapes=[
            pltpu.VMEM((quarter, columns), source.dtype),
            pltpu.VMEM((quarter, columns), base.dtype),
            pltpu.VMEM(w_full.shape, w_full.dtype),
        ]
        + ring_scratch(quarter, columns)
        + [
            pltpu.VMEM((quarter, columns), F32),
            pltpu.VMEM((2, 4, quarter // 2, inner), F32),
            pltpu.SemaphoreType.DMA((10,)),
        ]
        + sems(12, 12)
        + scatter_scratch(n, STEP),
        compiler_params=pltpu.CompilerParams(
            collective_id=call_id, has_side_effects=True, vmem_limit_bytes=56 << 20
        ),
    )(partial, source, base, gain, w_full, *grads)


def input_kernel(
    pieces, count, x_ref, source_ref, base_ref, gain_ref, other_ref, fall_ref, square_ref, more_ref,
    bias_ref, length_ref, bucket_ref, *refs
):
    ins, refs = refs[:count], refs[count:]
    out_ref, out_share_ref, share_ref, sums_ref = refs[:4]
    source_s, opp, nbr, held, own_s, mine_s, wide_s, landed, csem, *sem = refs[4:17]
    bufs, arrived, asem, bsem = refs[17:21]
    here, ring = Place(), YRing(x_ref.shape[0], 1, *sem[0:2])
    total = ScatterSum(here, scatter_sources(ins, pieces), *refs[21:])
    tiny = SmallSum(here, bufs, arrived, asem, bsem)
    n, first = total.n, wide_s.shape[1] // STEP
    meet(ring.neighbours() + here.peers() + tiny.far)
    ring.start(x_ref, opp, nbr, 0)
    q, h = ring.quarter, ring.half
    ring.fetch(x_ref, held, own_s, csem)
    copy = load(rows_of(source_ref, ring.me * q, q), source_s, csem.at[3])
    for k in range(n):
        total.exchange(k)
    each(0, n // 2, total.first)
    ring.relay(opp, nbr, held, 0)
    each(n // 2, n, total.first)
    each(0, n - 2, total.first_relay)
    copy.wait()
    sums = 0.0
    for wave in (0,):
        for part in (0, 1):
            at, value = ring.collect(own_s, nbr, part, wave)
            value, more = norm_back(value, source_s[at, :], base_ref[at, :], gain_ref[...])
            mine_s[at, :] = value
            ring.spread(part, wave, mine_s, out_ref)
            sums = sums + more
    kept = load(mine_s, rows_of(out_ref, ring.me * q, q), csem.at[4])
    bufs[0, 0:1, :] = sums
    bufs[0, 1:2, :] = other_ref[...]
    bufs[0, 8:16, :] = jnp.zeros_like(bufs[0, 8:16, :])
    bufs[0, 2:3, :] = jnp.zeros((1, sums_ref.shape[1]), F32)
    bufs[0, 3:9, :] = fall_ref[0:6, :]
    lane = lax.broadcasted_iota(jnp.int32, (1, PAIR), 1)
    both = jnp.sum(square_ref[...], axis=1, keepdims=True)
    in_bucket = lambda value: jnp.where(lane == bucket_ref[0], value, 0.0)
    bufs[0, 2:3, 0:PAIR] = in_bucket(jnp.sum(more_ref[...], axis=1, keepdims=True))
    for at, value in enumerate((both[0:1], both[1:2], length_ref[0].astype(F32))):
        bufs[0, 9:10, at * PAIR : at * PAIR + PAIR] = in_bucket(value)
    diagonal = lax.broadcasted_iota(jnp.int32, bias_ref.shape, 0) == lax.broadcasted_iota(
        jnp.int32, bias_ref.shape, 1
    )
    bufs[0, 10:11, 0:PAIR] = jnp.sum(jnp.where(diagonal, bias_ref[...], 0.0), axis=0, keepdims=True)
    tiny.send(0)
    each(n - 2, n, total.first_relay)
    each(0, n, total.second)
    ring.forward(0, out_ref)
    tiny.take(0)
    tiny.send(1)
    each(0, n, total.second_relay)
    tiny.take(1)
    tiny.send(2)
    each(0, first, lambda k: total.result(k, wide_s, k))
    inner = landed.shape[2]
    swaps = []
    for j, by in enumerate((2, 1, 3)):
        to = lax.rem(ring.me + by, Y)
        columns = pl.ds(pl.multiple_of(to * inner, 128), inner)
        swaps.append(push(wide_s.at[:, columns], landed.at[j], *sem[2:4], j, (ring.dp, to)))
    each(first, n, lambda k: total.result(k, share_ref, k - first))
    tiny.take(2)
    tiny.send(3)
    own = wide_s[:, pl.ds(pl.multiple_of(ring.me * inner, 128), inner)]
    for j, copy in enumerate(swaps):
        copy.wait_recv()
        own = own + landed[j]
    out_share_ref[...] = own
    tiny.take(3)
    rows = lax.broadcasted_iota(jnp.int32, sums_ref.shape, 0)
    sums_ref[...] = jnp.where(rows < 3, bufs[4], bufs[3])
    ring.arrive(0)
    kept.wait()
    for copy in swaps:
        copy.wait_send()
    tiny.finish()
    ring.finish()
    each(0, n, total.sent)


def reduce_input(partial, source, base, gain, small, grads, pieces, call_id):
    n = len(pieces)
    smem = pl.BlockSpec(memory_space=pltpu.SMEM)
    hbm, vmem = pl.BlockSpec(memory_space=pl.ANY), pl.BlockSpec(memory_space=pltpu.VMEM)
    rows, columns = partial.shape
    quarter, inner = rows // Y, grads[0].shape[1] // Y
    wide = grads[0].shape[1]
    shares = n * STEP - wide
    return pl.pallas_call(
        functools.partial(input_kernel, pieces, len(grads)),
        out_shape=[
            jax.ShapeDtypeStruct(partial.shape, F32),
            jax.ShapeDtypeStruct((48, inner), F32),
            jax.ShapeDtypeStruct((48, shares), F32),
            jax.ShapeDtypeStruct((16, columns), F32),
        ],
        in_specs=[hbm, hbm, vmem, vmem] + [vmem] * 5 + [smem] * 2 + [hbm] * len(grads),
        out_specs=[hbm] + [vmem] * 3,
        scratch_shapes=[pltpu.VMEM((quarter, columns), source.dtype)]
        + ring_scratch(quarter, columns)
        + [
            pltpu.VMEM((quarter, columns), F32),
            pltpu.VMEM((quarter, columns), F32),
            pltpu.VMEM((48, wide), F32),
            pltpu.VMEM((3, 48, inner), F32),
            pltpu.SemaphoreType.DMA((5,)),
        ]
        + sems(24, 3)
        + [pltpu.VMEM((5, 16, columns), F32), pltpu.VMEM((10, 16, columns), F32)]
        + sems(10)
        + scatter_scratch(n, STEP),
        compiler_params=pltpu.CompilerParams(
            collective_id=call_id, has_side_effects=True, vmem_limit_bytes=56 << 20
        ),
    )(partial, source, base, gain, *small, *grads)


HEAD = 64
PAIR = 128
NEG = -1e30


def rows_at(i, size):
    return pl.ds(pl.multiple_of(i * size, size), size)


def lane_is(shape, index):
    return lax.broadcasted_iota(jnp.int32, shape, len(shape) - 1) == index


def first_head(shape):
    return lax.broadcasted_iota(jnp.int32, shape, len(shape) - 1) < HEAD


def halves_mean(values):
    first = first_head(values.shape)
    low = jnp.sum(jnp.where(first, values, 0.0), axis=1, keepdims=True) * (1.0 / HEAD)
    high = jnp.sum(jnp.where(first, 0.0, values), axis=1, keepdims=True) * (1.0 / HEAD)
    return low, high


def one_row(ref, index):
    rows = ref[...]
    picked = lax.broadcasted_iota(jnp.int32, rows.shape, 0) == index
    return jnp.sum(jnp.where(picked, rows, 0.0), axis=0, keepdims=True)


def running_sum(values, backward=False):
    count = values.shape[1]
    at = lax.broadcasted_iota(jnp.int32, values.shape, 1)
    shift = 1
    while shift < count:
        if backward:
            moved = jnp.where(at < count - shift, pltpu.roll(values, count - shift, 1), 0.0)
        else:
            moved = jnp.where(at >= shift, pltpu.roll(values, shift, 1), 0.0)
        values = values + moved
        shift *= 2
    return values


def mm(left, right):
    return jnp.dot(left, right, preferred_element_type=F32)


def mm_t(left, right):
    return lax.dot_general(left, right, (((1,), (1,)), ((), ())), preferred_element_type=F32)


def t_mm(left, right):
    return lax.dot_general(left, right, (((0,), (0,)), ((), ())), preferred_element_type=F32)


def whole(shape):
    return pl.BlockSpec(shape, lambda *_: (0,) * len(shape), pipeline_mode=pl.Buffered(1))


def struct(*shape, t=F32):
    return jax.ShapeDtypeStruct(shape, t)


def local_call(kernel, grid, in_specs, out_specs, out_shape, scratch, limit, flops, moved, call_id=None):
    return pl.pallas_call(
        kernel,
        grid_spec=pltpu.PrefetchScalarGridSpec(
            num_scalar_prefetch=1,
            grid=(grid,),
            in_specs=in_specs,
            out_specs=out_specs,
            scratch_shapes=scratch,
        ),
        out_shape=out_shape,
        compiler_params=pltpu.CompilerParams(
            vmem_limit_bytes=limit << 20,
            collective_id=call_id,
            has_side_effects=call_id is not None,
        ),
        cost_estimate=pl.CostEstimate(
            flops=flops * 10**9, bytes_accessed=moved * 10**6, transcendentals=4 * 10**6
        ),
    )


def forward_kernel(
    length_ref, x_ref, gain_ref, wq_ref, wk_ref, wv_ref, wo_ref, wf_ref, bf_ref, w_ref,
    low_out, qn_ref, kn_ref, v_ref, sig_ref, att_ref, stat_ref, decay_ref, gated_out, full_out,
    top_s, row_s, q_s, k_s, w_s, pre_s, gs, ws, wf_s, bf_s, low_ref, gated_ref, full_ref, osem, *sem,
):
    step = pl.program_id(0)
    seq = x_ref.shape[0]
    length = length_ref[0]
    here = Place()
    me, right, left, far = (lax.rem(here.my + by, Y) for by in (0, 1, 3, 2))
    sibling, right1, left1, right2, left2 = here.peers()
    c, p1, p2, half = here.c, here.p1, here.p2, seq // 2
    mine = ws.at[c, p2, p1, me]
    cross_order = (p2, here.l2, here.r2, here.o2)

    def plane(j):
        return link(mine, mine, *sem[2:4], j, (here.dp, (right, far, left)[j]))

    def torus(stage, j):
        if stage == 0:
            at, spots, to = (lambda p: ws.at[c, p2, p]), (p1, here.l1, here.r1), (right1, left1)
        else:
            at, spots, to = (lambda p: ws.at[c, p]), (p2, here.l2, here.r2), (right2, left2)
        spot, part, side = ((0, 0, 0), (0, 1, 0), (0, 0, 1), (0, 1, 1), (1, 0, 0), (2, 1, 1))[j]
        piece = at(spots[spot]).at[2 * part : 2 * part + 2]
        return link(piece, piece, *sem[4 + 2 * stage : 6 + 2 * stage], j, to[side])

    def cross(j):
        piece = ws.at[c, cross_order[j]]
        return link(piece, piece, *sem[8:10], j, sibling)

    def gate(pair, j):
        owner, part, to = (
            (me, 0, right), (me, 1, right), (me, 0, left), (me, 1, left), (left, 0, right), (right, 1, left)
        )[j]
        piece = gs.at[pair, owner, part * half : part * half + half]
        return link(piece, piece, *sem[0:2], pair * 6 + j, (here.dp, to))

    def flush(j):
        src, dst = ((low_ref, low_out), (full_ref, full_out), (gated_ref, gated_out))[j]
        return pltpu.make_async_copy(src, dst, osem.at[j])

    def pass_on(make):
        make(0).wait_recv()
        make(4).start()
        make(3).wait_recv()
        make(5).start()

    def arrived(make):
        for j in (1, 2, 4, 5):
            make(j).wait_recv()

    @pl.when(step == 0)
    def _():
        tall, wide = ws.shape[4], ws.shape[5]
        two = w_ref[
            pl.ds(pl.multiple_of(here.chip // 2 * (2 * tall), 16), 2 * tall),
            pl.ds(pl.multiple_of(c * wide, 128), wide),
        ].astype(F32)
        mine[...] = jnp.where(lax.rem(here.chip, 2) == 0, two[0:tall], two[tall:])
        meet([(here.dp, right), (here.dp, left), (here.dp, far)] + here.peers())
        for j in range(3):
            plane(j).start()

    @pl.when(step == 0)
    def _():
        def norm(i, carry):
            at = rows_at(i, 128)
            x = x_ref[at, :].astype(F32)
            r = lax.rsqrt(jnp.mean(x * x, axis=1, keepdims=True) + EPSILON)
            low_ref[at, :] = (x * r * gain_ref[...].astype(F32)).astype(jnp.bfloat16)
            return carry

        lax.fori_loop(0, seq // 128, norm, 0)
        flush(0).start()
        heads = wf_ref.shape[0]
        wf_s[...] = jnp.zeros_like(wf_s)
        wf_s[0:heads, :] = wf_ref[...]
        bf_s[...] = jnp.zeros_like(bf_s)
        bf_s[:, 0:heads] = bf_ref[...].astype(F32)
        pre = mm_t(wf_s[...], low_ref[...])[0:8] + jnp.broadcast_to(bf_s[...], (PAIR, PAIR)).T[0:8, 0:1]
        fall = jnp.minimum(pre, 0.0) - jnp.log1p(jnp.exp(-jnp.abs(pre)))
        decay = running_sum(fall)
        column = lax.broadcasted_iota(jnp.int32, decay.shape, 1)
        decay_ref[0] = decay
        decay_ref[1] = jax.nn.sigmoid(-pre)
        row_s[...] = jnp.where(column < length, decay, -NEG)
        final = jnp.sum(jnp.where(column == length - 1, decay, 0.0), axis=1, keepdims=True)
        top = jnp.where(column < length, decay, final)
        top_s[...] = jnp.concatenate([top, jnp.zeros((PAIR - 8, seq), F32)], axis=0).T

    for j, ref in enumerate((wq_ref, wk_ref, wv_ref, wo_ref)):
        w_s[:, j * PAIR : j * PAIR + PAIR] = ref[...]
    pre_s[...] = mm(low_ref[...], w_s[...])

    def norms(i, carry):
        at = rows_at(i, 128)
        for j, n_ref, s, col in ((0, qn_ref, q_s, 0), (1, kn_ref, k_s, 2)):
            pre = pre_s[at, j * PAIR : j * PAIR + PAIR]
            a, b = halves_mean(pre * pre)
            a, b = lax.rsqrt(a + EPSILON), lax.rsqrt(b + EPSILON)
            n = pre * jnp.where(first_head(pre.shape), a, b)
            n_ref[at, :] = n
            s[at, :] = n.astype(jnp.bfloat16)
            here = jnp.where(lane_is(pre.shape, col), a, jnp.where(lane_is(pre.shape, col + 1), b, 0.0))
            stat_ref[at, :] = here if col == 0 else stat_ref[at, :] + here
        v_ref[at, :] = pre_s[at, 2 * PAIR : 3 * PAIR].astype(jnp.bfloat16)
        sig_ref[at, :] = jax.nn.sigmoid(pre_s[at, 3 * PAIR : 4 * PAIR])
        return carry

    lax.fori_loop(0, seq // 128, norms, 0)

    @pl.when(step == 0)
    def _():
        for j in range(3):
            plane(j).wait_recv()
        for j in range(4):
            torus(0, j).start()

    @pl.when(step == 1)
    def _():
        arrived(lambda j: torus(0, j))
        for j in range(4):
            torus(1, j).start()
        cross(0).start()

    @pl.when(step == 2)
    def _():
        pass_on(lambda j: torus(1, j))

    lines = [one_row(row_s, 2 * step + head) for head in (0, 1)]
    first = first_head((128, PAIR))
    zero = jnp.zeros((128, PAIR), jnp.bfloat16)
    upper = lax.broadcasted_iota(jnp.int32, (128, 128), 1) > lax.broadcasted_iota(
        jnp.int32, (128, 128), 0
    )
    for i in range(seq // 128):
        at, n = slice(i * 128, i * 128 + 128), i * 128 + 128
        q = q_s[at, :]
        both = []
        for head in (0, 1):
            own = jnp.where(first, q, zero) if head == 0 else jnp.where(first, zero, q)
            s = mm_t(own, k_s[0:n, :])
            column = jnp.sum(
                jnp.where(lane_is((128, PAIR), 2 * step + head), top_s[at, :], 0.0), axis=1, keepdims=True
            )
            s = s * (HEAD ** (-0.5)) + (column - lines[head][:, 0:n])
            diagonal = jnp.where(upper, NEG, s[:, n - 128 :])
            s = diagonal if i == 0 else jnp.concatenate([s[:, : n - 128], diagonal], axis=1)
            p = jnp.exp(s)
            p = p * (1.0 / jnp.sum(p, axis=1, keepdims=True))
            both.append(mm(p.astype(jnp.bfloat16), v_ref[0:n, :]))
        out = jnp.where(first, both[0], both[1])
        att_ref[at, :] = out
        gs[step, me, at, :] = (out * sig_ref[at, :]).astype(jnp.bfloat16).astype(F32)
        if n % half == 0:
            gate(step, n // half - 1).start()
            gate(step, n // half + 1).start()

    @pl.when(step == 0)
    def _():
        pass_on(lambda j: torus(0, j))

    @pl.when(step > 0)
    def _():
        pass_on(lambda j: gate(step - 1, j))

    @pl.when(step == pl.num_programs(0) - 1)
    def _():
        torus(1, 1).wait_recv()
        cross(1).start()
        torus(1, 2).wait_recv()
        cross(2).start()
        torus(1, 4).wait_recv()
        torus(1, 5).wait_recv()
        cross(3).start()
        pass_on(lambda j: gate(step, j))
        for j in range(4):
            cross(j).wait_recv()
        tall, wide, shard = ws.shape[4], ws.shape[5], w_ref.shape[0]

        def turn(k, carry):
            y, m = k // 8, lax.rem(k, 8)
            x, z = m // 2, lax.rem(m, 2) * 2
            rows = pl.ds(pl.multiple_of(y * shard + m * 2 * tall, 16), 2 * tall)
            for h, one, two in (
                (0, ws[0, z, x, y], ws[0, z + 1, x, y]),
                (1, ws[1, x, z, y], ws[1, x, z + 1, y]),
            ):
                both = jnp.concatenate([one, two], axis=0).astype(jnp.bfloat16)
                full_ref[rows, h * wide : h * wide + wide] = both
            return carry

        lax.fori_loop(0, 8 * Y, turn, 0)
        flush(1).start()
        pairs = gs.shape[0]
        for pair in range(pairs):
            arrived(lambda j: gate(pair, j))
            for y in range(Y):
                lane = (y * pairs + pair) * PAIR
                gated_ref[:, lane : lane + PAIR] = gs[pair, y].astype(jnp.bfloat16)
        flush(2).start()
        for j in range(3):
            flush(j).wait()
            plane(j).wait_send()
        for stage in (0, 1):
            for j in range(6):
                torus(stage, j).wait_send()
        for j in range(4):
            cross(j).wait_send()
        for pair in range(pairs):
            for j in range(6):
                gate(pair, j).wait_send()


def forward_attention(tokens, length, gain, wq, wk, wv, wo, wf, bf, w_out, call_id):
    seq, width = tokens.shape
    heads = wq.shape[1]
    weights = pl.BlockSpec((width, PAIR), lambda i, _: (0, i))
    lanes = pl.BlockSpec((seq, PAIR), lambda i, _: (0, i))
    low = jnp.bfloat16
    return local_call(
        forward_kernel,
        heads // PAIR,
        [whole((seq, width)), whole((1, width))] + [weights] * 4 + [whole(wf.shape), whole(bf.shape), whole(w_out.shape)],
        [HBM] + [lanes] * 6 + [whole((2, 8, seq)), HBM, HBM],
        [
            struct(seq, width, t=low), struct(seq, heads), struct(seq, heads), struct(seq, heads, t=low),
            struct(seq, heads), struct(seq, heads), struct(seq, heads),
            struct(2, 8, seq), struct(seq, heads * Y, t=low), struct(heads * Y, width, t=low),
        ],
        [
            pltpu.VMEM((seq, PAIR), F32),
            pltpu.VMEM((8, seq), F32),
            pltpu.VMEM((seq, PAIR), low),
            pltpu.VMEM((seq, PAIR), low),
            pltpu.VMEM((width, 4 * PAIR), low),
            pltpu.VMEM((seq, 4 * PAIR), F32),
            pltpu.VMEM((heads // PAIR, Y, seq, PAIR), F32),
            pltpu.VMEM((2, 4, 4, Y, heads // 16, width // 2), F32),
            pltpu.VMEM((16, width), low),
            pltpu.VMEM((1, PAIR), F32),
            pltpu.VMEM((seq, width), low),
            pltpu.VMEM((seq, width), low),
            pltpu.VMEM((heads * Y, width), low),
            pltpu.SemaphoreType.DMA((3,)),
        ]
        + sems(6 * (heads // PAIR), 3, 6, 6, 4),
        56, 6, 20, call_id,
    )(length, tokens, gain, wq, wk, wv, wo, wf, bf, w_out)


def copier(sem):
    count = iter(range(sem.shape[0]))

    def copy(src, dst):
        return load(src, dst, sem.at[next(count)])

    return copy


def mlp_forward_kernel(
    length_ref, x_in, cot_in, gated_in, gain_ref, wo_in, wg_in, wu_in, wd_in,
    mid_out, low_out, grad_out, gate_out, up_out, hid_out, out_out, sums_ref,
    x_ref, cot_ref, gated_ref, wo_ref, wg_ref, wu_ref, wd_ref,
    mid_ref, low_ref, grad_ref, gate_ref, up_ref, hid_ref, out_ref, sem,
):
    seq, width = x_ref.shape
    length = length_ref[0]
    tile, units = wo_ref.shape[2], hid_ref.shape[1] // 2
    copy = copier(sem)
    columns = lambda j, size: pl.ds(pl.multiple_of(j * size, size), size)
    outer = lambda j: pltpu.make_async_copy(
        wo_in.at[:, columns(j, tile)], wo_ref.at[j], sem.at[sem.shape[0] - 2 + j]
    )
    need = copy(gated_in, gated_ref)
    outer(0).start()
    need_x = copy(x_in, x_ref)
    need.wait()
    outer(1).start()
    need_cot = copy(cot_in, cot_ref)
    weights = [copy(wg_in, wg_ref), copy(wu_in, wu_ref), copy(wd_in, wd_ref)]
    kept = lax.broadcasted_iota(jnp.int32, (seq, 1), 0) < length
    flushes = []

    def project(j):
        at = columns(j, tile)
        outer(j).wait()
        branch = mm(gated_ref[...], wo_ref[j])
        x = x_ref[:, at].astype(F32)
        mid_ref[:, at] = x + branch
        sums_ref[0:1, at] = jnp.sum(jnp.where(kept, x * x, 0.0), axis=0, keepdims=True)
        sums_ref[1:2, at] = jnp.sum(jnp.where(kept, branch * branch, 0.0), axis=0, keepdims=True)

    need_x.wait()
    each(0, 2, project)
    flushes.append(copy(mid_ref, mid_out))

    def norm(i, carry):
        at = rows_at(i, 128)
        mid = mid_ref[at, :]
        r = lax.rsqrt(jnp.mean(mid * mid, axis=1, keepdims=True) + EPSILON)
        low_ref[at, :] = (mid * r * gain_ref[...].astype(F32)).astype(jnp.bfloat16)
        return carry

    lax.fori_loop(0, seq // 128, norm, 0)
    flushes.append(copy(low_ref, low_out))
    weights[0].wait()
    weights[1].wait()

    def hidden(j):
        at = columns(j, units)
        gate_ref[:, at] = mm(low_ref[...], wg_ref[:, at])
        up_ref[:, at] = mm(low_ref[...], wu_ref[:, at])
        gate = gate_ref[:, at]
        hid_ref[:, at] = (gate * jax.nn.sigmoid(gate) * up_ref[:, at]).astype(jnp.bfloat16)

    each(0, 2, hidden)
    for src, dst in ((gate_ref, gate_out), (up_ref, up_out), (hid_ref, hid_out)):
        flushes.append(copy(src, dst))
    need_cot.wait()
    grad_ref[...] = jnp.where(kept, cot_ref[...].astype(F32), 0.0).astype(jnp.bfloat16)
    flushes.append(copy(grad_ref, grad_out))
    weights[2].wait()
    result = lambda j: pltpu.make_async_copy(
        out_ref.at[:, columns(j, tile)], out_out.at[:, columns(j, tile)], sem.at[sem.shape[0] - 4 + j]
    )

    def project_out(j):
        at = columns(j, tile)
        out_ref[:, at] = mm(hid_ref[...], wd_ref[:, at])
        result(j).start()

    each(0, 2, project_out)
    flushes += [result(0), result(1)]
    for c in flushes:
        c.wait()


def mlp_forward(tokens, cotangent, length, gated, gain, wo, wg, wu, wd):
    seq, width = tokens.shape
    hidden = wg.shape[1]
    low = jnp.bfloat16
    smem = pl.BlockSpec(memory_space=pltpu.SMEM)
    outs = [
        struct(seq, width), struct(seq, width, t=low), struct(seq, width, t=low),
        struct(seq, hidden), struct(seq, hidden), struct(seq, hidden, t=low), struct(seq, width),
    ]
    return pl.pallas_call(
        mlp_forward_kernel,
        in_specs=[smem, HBM, HBM, HBM, VMEM] + [HBM] * 4,
        out_specs=[HBM] * 7 + [VMEM],
        out_shape=outs + [struct(2, width)],
        scratch_shapes=[
            pltpu.VMEM((seq, width), low),
            pltpu.VMEM((seq, width), low),
            pltpu.VMEM((seq, width), low),
            pltpu.VMEM((2, width, width // 2), low),
            pltpu.VMEM((width, hidden), low),
            pltpu.VMEM((width, hidden), low),
            pltpu.VMEM((hidden, width), low),
        ]
        + [pltpu.VMEM(out.shape, out.dtype) for out in outs]
        + [pltpu.SemaphoreType.DMA((18,))],
        compiler_params=pltpu.CompilerParams(vmem_limit_bytes=58 << 20),
    )(length, tokens, cotangent, gated, gain, wo, wg, wu, wd)


def reduce_links(rows, x, opp, nbr, held, sem):
    dp, me = lax.axis_index("dp"), lax.axis_index("mp")
    right, left, far = lax.rem(me + 1, Y), lax.rem(me + 3, Y), lax.rem(me + 2, Y)
    q, h = rows // Y, rows // Y // 2

    def message(name):
        src, dst, to = {
            "oR": (lambda: rows_of(x, far * q, h), lambda: opp.at[0], right),
            "oL": (lambda: rows_of(x, far * q + h, h), lambda: opp.at[1], left),
            "iR": (lambda: rows_of(x, right * q + h, h), lambda: nbr.at[0, h:q], right),
            "iL": (lambda: rows_of(x, left * q, h), lambda: nbr.at[1, 0:h], left),
            "dR": (lambda: held.at[0], lambda: nbr.at[0, 0:h], right),
            "dL": (lambda: held.at[1], lambda: nbr.at[1, h:q], left),
        }[name]
        return link(src(), dst(), *sem, STEPS.index(name), (dp, to))

    return message, me, right, left, [(dp, right), (dp, left)]


def mlp_backward_kernel(
    length_ref, grad_in, low_in, gate_in, up_in, hid_in, wd_in, wg_in, wu_in, x_ref, mid_ref,
    back_out, gd_out, gg_out, gu_out, layer_ref, square_ref,
    grad_ref, low_ref, gate_ref, up_ref, hid_ref, wd_ref, wg_ref, wu_ref,
    dg_s, du_s, back_s, bufs, opp, nbr, held, own_s, mid_s, csem, *sem,
):
    seq, width = grad_ref.shape
    units = wd_ref.shape[0] // 2
    low16 = jnp.bfloat16
    message, me, right, left, peers = reduce_links(seq, x_ref, opp, nbr, held, sem)
    q, h = seq // Y, seq // Y // 2
    copy = copier(csem)
    need = [
        copy(grad_in, grad_ref),
        copy(wd_in.at[0:units], wd_ref.at[0:units]),
        copy(gate_in.at[:, 0:units], gate_ref.at[:, 0:units]),
        copy(up_in.at[:, 0:units], up_ref.at[:, 0:units]),
    ]
    meet(peers)
    for name in STEPS[:4]:
        message(name).start()
    for c in need[0:2]:
        c.wait()
    next_low, next_hid = copy(low_in, low_ref), copy(hid_in, hid_ref)
    more = [
        copy(wd_in.at[units:], wd_ref.at[units:]),
        copy(gate_in.at[:, units:], gate_ref.at[:, units:]),
        copy(up_in.at[:, units:], up_ref.at[:, units:]),
    ]
    weights = [copy(wg_in, wg_ref), copy(wu_in, wu_ref)]
    adds = [
        copy(rows_of(x_ref, right * q, h), held.at[0]),
        copy(rows_of(x_ref, left * q + h, h), held.at[1]),
        copy(rows_of(x_ref, me * q, q), own_s),
        copy(rows_of(mid_ref, me * q, q), mid_s),
    ]
    spots = (gd_out, gg_out, gu_out)
    columns = lambda j: pl.ds(pl.multiple_of(j * units, units), units)
    flush = lambda j, which: pltpu.make_async_copy(
        bufs.at[which, j], spots[which].at[:, columns(j)], csem.at[csem.shape[0] - 6 + which * 2 + j]
    )

    def write(which, left_of, right_of, j):
        slot, at = bufs.at[which, j], columns(j)

        def rows(i, carry):
            part = rows_at(i, 768)
            slot[part, :] = t_mm(left_of[:, part], right_of[:, at])
            return carry

        lax.fori_loop(0, width // 768, rows, 0)
        flush(j, which).start()

    def tile(j):
        at = columns(j)

        @pl.when(j == 1)
        def _():
            for c in more:
                c.wait()

        grad = mm_t(grad_ref[...], wd_ref[at, :])

        @pl.when(j == 0)
        def _():
            for c in need[2:4]:
                c.wait()

        gate = gate_ref[:, at]
        sig = jax.nn.sigmoid(gate)
        dg_s[:, at] = (grad * up_ref[:, at] * (sig * (1.0 + gate * (1.0 - sig)))).astype(low16)
        du_s[:, at] = (grad * (gate * sig)).astype(low16)

        @pl.when(j == 0)
        def _():
            next_low.wait()
            next_hid.wait()

        write(0, grad_ref, hid_ref, j)
        write(1, low_ref, dg_s, j)

        @pl.when(j == 1)
        def _():
            for part, (come, go) in enumerate((("oR", "dR"), ("oL", "dL"))):
                message(come).wait_recv()
                adds[part].wait()
                held[part] = held[part] + opp[part]
                message(go).start()

        write(2, low_ref, du_s, j)

    each(0, 2, tile)
    for c in weights:
        c.wait()

    def back(i, carry):
        rows = rows_at(i, 768)
        back_s[:, rows] = mm_t(dg_s[...], wg_ref[rows, :])
        back_s[:, rows] = back_s[:, rows] + mm_t(du_s[...], wu_ref[rows, :])
        return carry

    lax.fori_loop(0, width // 768, back, 0)
    last = copy(back_s, back_out)
    adds[2].wait()
    adds[3].wait()
    sums = 0.0
    for part, names in enumerate((("dR", "iL"), ("iR", "dL"))):
        for name in names:
            message(name).wait_recv()
        at = slice(part * h, part * h + h)
        branch = own_s[at, :] + nbr[0, at] + nbr[1, at]
        layer_ref[at, :] = (mid_s[at, :] + branch).astype(low16).astype(F32)
        row = lax.broadcasted_iota(jnp.int32, (h, 1), 0) + (me * q + part * h)
        kept = jnp.where(row < length_ref[0], branch * branch, 0.0)
        sums = sums + jnp.sum(kept, axis=0, keepdims=True)
    square_ref[...] = sums
    last.wait()
    for j in (0, 1):
        for which in range(3):
            flush(j, which).wait()
    for name in STEPS[:6]:
        message(name).wait_send()


def mlp_backward(length, grad, low, gate, up, hid, wg, wu, wd, branch, mid, call_id):
    seq, width = low.shape
    hidden = wg.shape[1]
    quarter = seq // Y
    low16 = jnp.bfloat16
    smem = pl.BlockSpec(memory_space=pltpu.SMEM)
    inputs = (grad, low, gate, up, hid, wd, wg, wu)
    return pl.pallas_call(
        mlp_backward_kernel,
        in_specs=[smem] + [HBM] * 10,
        out_specs=[HBM] * 4 + [VMEM] * 2,
        out_shape=[struct(seq, width)] + [struct(width, hidden)] * 3
        + [struct(quarter, width), struct(1, width)],
        scratch_shapes=[pltpu.VMEM(a.shape, a.dtype) for a in inputs]
        + [pltpu.VMEM((seq, hidden), low16)] * 2
        + [pltpu.VMEM((seq, width), F32), pltpu.VMEM((3, 2, width, hidden // 2), F32)]
        + ring_scratch(quarter, width)
        + [pltpu.VMEM((quarter, width), F32)] * 2
        + [pltpu.SemaphoreType.DMA((22,))]
        + sems(6),
        compiler_params=pltpu.CompilerParams(
            vmem_limit_bytes=62 << 20, collective_id=call_id, has_side_effects=True
        ),
    )(length, *inputs, branch, mid)


def backward_kernel(
    length_ref, gg_ref, low_in, qn_ref, kn_ref, v_ref, sig_ref, att_ref, stat_ref,
    decay_ref, wq_ref, wk_ref, wv_ref, wo_ref, wf_ref, own_ref, gated_ref, layer_ref,
    back_out, four_out, gout_out, gf_ref, bias_ref, out_ref,
    k_s, do_s, line_s, top_s, dq_s, dk_s, dv_s, all_s, fall_s, w_s, wf_s, lay_s, back_ref, wide_s, low_ref, osem,
    *sem,
):
    step = pl.program_id(0)
    seq, width = low_ref.shape
    length = length_ref[0]
    low16 = jnp.bfloat16
    wide = 4 * PAIR
    dp, me = lax.axis_index("dp"), lax.axis_index("mp")
    right, left = lax.rem(me + 1, Y), lax.rem(me + 3, Y)
    q, h = seq // Y, seq // Y // 2

    def spread(j):
        owner, part, to = (
            (me, 0, right), (me, 1, right), (me, 0, left), (me, 1, left), (left, 0, right), (right, 1, left)
        )[j]
        piece = rows_of(lay_s, owner * q + part * h, h)
        source = layer_ref.at[part * h : part * h + h] if j < 4 else piece
        return link(source, piece, *sem, j, (dp, to))

    def fetch(j):
        pair = ((layer_ref, rows_of(lay_s, me * q, q)), (low_in, low_ref))[j]
        return pltpu.make_async_copy(*pair, osem.at[5 + j])

    @pl.when(step == 0)
    def _():
        meet([(dp, right), (dp, left)])
        for j in range(4):
            spread(j).start()
        for j in (0, 1):
            fetch(j).start()

    @pl.when(step == 2)
    def _():
        spread(0).wait_recv()
        spread(4).start()
        spread(3).wait_recv()
        spread(5).start()

    @pl.when(step == 0)
    def _():
        heads = wf_ref.shape[0]
        wf_s[...] = jnp.zeros_like(wf_s)
        wf_s[0:heads, :] = wf_ref[...]
        decay = decay_ref[0]
        column = lax.broadcasted_iota(jnp.int32, decay.shape, 1)
        final = jnp.sum(jnp.where(column == length - 1, decay, 0.0), axis=1, keepdims=True)
        line_s[...] = jnp.where(column < length, decay, final)
        masked = jnp.where(column < length, decay, -NEG)
        top_s[...] = jnp.concatenate([masked, jnp.zeros((PAIR - 8, seq), F32)], axis=0).T
        fall_s[...] = jnp.zeros_like(fall_s)

    base = pl.multiple_of(step * wide, wide)
    part = lambda j: pl.ds(pl.multiple_of(base + j * PAIR, PAIR), PAIR)
    for j, w_ref in enumerate((wq_ref, wk_ref, wv_ref, wo_ref)):
        w_s[:, part(j)] = w_ref[...]
    first = first_head((seq, PAIR))
    gg, sig = gg_ref[...], sig_ref[...]
    do_s[...] = (gg * sig).astype(low16)
    all_s[:, part(3)] = (gg * att_ref[...] * sig * (1.0 - sig)).astype(low16)
    k_s[...] = kn_ref[...].astype(low16)
    dk_s[...] = jnp.zeros_like(dk_s)
    dv_s[...] = jnp.zeros_like(dv_s)
    columns, lines = [], [one_row(line_s, 2 * step + head) for head in (0, 1)]
    for head in (0, 1):
        column = jnp.sum(
            jnp.where(lane_is((seq, PAIR), 2 * step + head), top_s[...], 0.0), axis=1, keepdims=True
        )
        columns.append(column)
    block = first_head((128, PAIR))
    zero = jnp.zeros((128, PAIR), low16)
    lower = lax.broadcasted_iota(jnp.int32, (128, 128), 0) > lax.broadcasted_iota(
        jnp.int32, (128, 128), 1
    )
    for i in range(seq // 128):
        at, n = slice(i * 128, i * 128 + 128), i * 128 + 128
        query = qn_ref[at, :].astype(low16)
        do = do_s[at, :]
        pieces = []
        for head in (0, 1):
            pick = (lambda t: jnp.where(block, t, zero)) if head == 0 else (lambda t: jnp.where(block, zero, t))
            own_q, own_do = pick(query), pick(do)
            one = jnp.where(lane_is((128, PAIR), 2 * step + head), 1.0, 0.0).astype(low16)
            s = mm_t(k_s[0:n, :], own_q)
            s = s * (HEAD ** (-0.5)) + (lines[head][:, at] - columns[head][0:n])
            diagonal = jnp.where(lower, NEG, s[n - 128 :, :])
            s = diagonal if i == 0 else jnp.concatenate([s[: n - 128, :], diagonal], axis=0)
            p = jnp.exp(s)
            p = p * (1.0 / jnp.sum(p, axis=0, keepdims=True))
            gp = mm_t(v_ref[0:n, :], own_do)
            ds = (p * (gp - jnp.sum(p * gp, axis=0, keepdims=True))).astype(low16)
            dv_s[0:n, :] = dv_s[0:n, :] + mm(p.astype(low16), own_do)
            dk_s[0:n, :] = dk_s[0:n, :] + mm(ds, jnp.concatenate([own_q, one], axis=1))
            mark = jnp.where(lane_is((n, PAIR), 2 * step + head), 1.0, 0.0).astype(low16)
            pieces.append(t_mm(ds, jnp.concatenate([k_s[0:n, :], mark], axis=1)))
        dq_s[at, :] = jnp.where(block, pieces[0][:, 0:PAIR], pieces[1][:, 0:PAIR])
        fall_s[at, :] = fall_s[at, :] + pieces[0][:, PAIR:] + pieces[1][:, PAIR:]
    fall_s[...] = fall_s[...] - dk_s[:, PAIR:]
    stat = stat_ref[...]
    for e, n_ref, col, to in ((dq_s, qn_ref, 0, 0), (dk_s, kn_ref, 2, 1)):
        e = e[:, 0:PAIR] * (HEAD ** (-0.5))
        n = n_ref[...]
        a, b = halves_mean(e * n)
        r = jnp.where(first, stat[:, col : col + 1], stat[:, col + 1 : col + 2])
        all_s[:, part(to)] = (r * (e - n * jnp.where(first, a, b))).astype(low16)
    all_s[:, part(2)] = dv_s[...].astype(low16)
    slot = lax.rem(step, 2)

    @pl.when(step == 0)
    def _():
        for j in (0, 1):
            fetch(j).wait()

    def flush(j, at, step):
        columns = pl.ds(pl.multiple_of(step * wide, wide), wide)
        out = (four_out, gout_out)[j].at[:, columns]
        return pltpu.make_async_copy(wide_s.at[at, j], out, osem.at[at * 2 + j])

    @pl.when(step == 2)
    def _():
        for j in (0, 1):
            flush(j, 0, 0).wait()

    def grads(k, carry):
        rows = rows_at(k, 768)
        wide_s[slot, 0, rows, :] = t_mm(low_ref[:, rows], all_s[:, pl.ds(base, wide)])
        wide_s[slot, 1, rows, :] = t_mm(own_ref[:, rows].astype(low16), gated_ref[...])
        return carry

    lax.fori_loop(0, width // 768, grads, 0)
    for j in (0, 1):
        flush(j, slot, step).start()

    @pl.when(step == pl.num_programs(0) - 1)
    def _():
        fall = running_sum(fall_s[...].T[0:8], backward=True) * decay_ref[1]
        fall = jnp.concatenate([fall, jnp.zeros_like(fall)], axis=0).astype(low16)
        bias = jnp.sum(fall.astype(F32), axis=1, keepdims=True)
        bias_ref[...] = jnp.broadcast_to(bias[0:8], (8, PAIR))
        gf_ref[...] = mm(fall, low_ref[...])[0:8]

        def tail(k, carry):
            rows = rows_at(k, 768)
            back_ref[:, rows] = mm_t(all_s[...], w_s[rows, :])
            back_ref[:, rows] = back_ref[:, rows] + t_mm(fall, wf_s[:, rows])
            return carry

        lax.fori_loop(0, width // 768, tail, 0)
        last = load(back_ref, back_out, osem.at[4])
        for j in (1, 2, 4, 5):
            spread(j).wait_recv()
        out_ref[...] = lay_s[...].astype(low16)
        for at, done in ((1, 1), (0, 2)):
            for j in (0, 1):
                flush(j, at, done).wait()
        last.wait()
        for j in range(6):
            spread(j).wait_send()


def backward_attention(place, gg, low, qn, kn, v, sig, att, stat, decay, wq, wk, wv, wo, wf, own, gated, layer, call_id):
    seq, width = low.shape
    heads = wq.shape[1]
    weights = pl.BlockSpec((width, PAIR), lambda i, _: (0, i))
    lanes = pl.BlockSpec((seq, PAIR), lambda i, _: (0, i))
    full = whole((seq, width))
    low16 = jnp.bfloat16
    return local_call(
        backward_kernel,
        heads // PAIR,
        [lanes, HBM] + [lanes] * 6 + [whole((2, 8, seq))] + [weights] * 4
        + [whole(wf.shape), whole(own.shape)]
        + [pl.BlockSpec((own.shape[0], 4 * PAIR), lambda i, _: (lax.axis_index("mp"), i)), HBM],
        [HBM, HBM, HBM, whole((8, width)), whole((8, PAIR)), full],
        [
            struct(seq, width), struct(width, 4 * heads), struct(width, width), struct(8, width),
            struct(8, PAIR), struct(seq, width, t=low16),
        ],
        [
            pltpu.VMEM((seq, PAIR), low16),
            pltpu.VMEM((seq, PAIR), low16),
            pltpu.VMEM((8, seq), F32),
            pltpu.VMEM((seq, PAIR), F32),
            pltpu.VMEM((seq, PAIR), F32),
            pltpu.VMEM((seq, 2 * PAIR), F32),
            pltpu.VMEM((seq, PAIR), F32),
            pltpu.VMEM((seq, 4 * heads), low16),
            pltpu.VMEM((seq, PAIR), F32),
            pltpu.VMEM((width, 4 * heads), low16),
            pltpu.VMEM((16, width), low16),
            pltpu.VMEM((seq, width), F32),
            pltpu.VMEM((seq, width), F32),
            pltpu.VMEM((2, 2, width, 4 * PAIR), F32),
            pltpu.VMEM((seq, width), low16),
            pltpu.SemaphoreType.DMA((7,)),
        ]
        + sems(6),
        62, 14, 50, call_id,
    )(place, gg, low, qn, kn, v, sig, att, stat, decay, wq, wk, wv, wo, wf, own, gated, layer)


def finish_kernel(
    grad_in, layer_in, wout_hbm, four_hbm, mlp_hbm, sums_hbm,
    grad_ref, layer_ref, wout_ref, q_ref, k_ref, v_ref, o_ref, gate_ref, up_ref, down_ref,
    gain_ref, gain2_ref, fall_ref, rms_ref, bias_ref,
    grad_s, layer_s, four_in, mlp_in, sums_in, sem,
):
    copy = copier(sem)
    rows = grad_in.shape[0] // 4
    parts = [slice(j * rows, j * rows + rows) for j in range(4)]
    come = [(copy(grad_in.at[p], grad_s.at[p]), grad_s.at[p], grad_ref.at[p]) for p in parts]
    small = [copy(wout_hbm, wout_ref), copy(four_hbm, four_in), copy(mlp_hbm, mlp_in), copy(sums_hbm, sums_in)]
    come += [(copy(layer_in.at[p], layer_s.at[p]), layer_s.at[p], layer_ref.at[p]) for p in parts]
    copies = []

    def leave(some):
        for arrived, mid, dst in some:
            arrived.wait()
            copies.append(copy(mid, dst))

    leave(come[0:4])
    for c in small:
        c.wait()
    inner = q_ref.shape[1]
    for j, ref in enumerate((q_ref, k_ref, v_ref, o_ref)):
        for pair in range(inner // PAIR):
            lane = (pair * 4 + j) * PAIR
            ref[:, pair * PAIR : pair * PAIR + PAIR] = four_in[:, lane : lane + PAIR]
    units = gate_ref.shape[1]
    down_ref[...] = mlp_in[:, 0:units]
    gate_ref[...] = mlp_in[:, units : 2 * units]
    up_ref[...] = four_in[:, 4 * inner : 4 * inner + units]
    leave(come[4:8])
    share, width = gain_ref.shape[1], sums_in.shape[1]
    row = lax.broadcasted_iota(jnp.int32, (width, share), 0)
    lane = lax.broadcasted_iota(jnp.int32, (width, share), 1)
    pick = jnp.where(row == lane + lax.axis_index("dp") * share, 1.0, 0.0)
    own = jnp.dot(
        sums_in[...], pick, precision=lax.Precision.HIGHEST, preferred_element_type=F32
    )
    gain_ref[...] = own[0:1]
    gain2_ref[...] = own[1:2]
    fall_ref[...] = own[3 : 3 + fall_ref.shape[0]]
    square = lambda row, at: sums_in[row : row + 1, at * PAIR : at * PAIR + NBUCKET]
    squares = jnp.concatenate([square(9, 0), square(9, 1), square(2, 0)], axis=0)
    rms_ref[...] = jnp.sqrt(squares / (square(9, 2) * width))
    bias_ref[...] = sums_in[10:11, 0 : bias_ref.shape[1]]
    for c in copies:
        c.wait()


def finish(grad, layer, out_share, share, mlp_share, sums, heads):
    rows, inner = out_share.shape
    units = mlp_share.shape[1] // 2
    return pl.pallas_call(
        finish_kernel,
        out_shape=[
            struct(*grad.shape), struct(*layer.shape, t=layer.dtype), *[struct(rows, inner)] * 5,
            *[struct(rows, units)] * 3, struct(1, rows), struct(1, rows), struct(heads, rows),
            struct(3, NBUCKET), struct(1, heads),
        ],
        in_specs=[HBM] * 6,
        out_specs=[HBM, HBM] + [VMEM] * 13,
        scratch_shapes=[pltpu.VMEM(a.shape, a.dtype) for a in (grad, layer, share, mlp_share, sums)]
        + [pltpu.SemaphoreType.DMA((20,))],
        compiler_params=pltpu.CompilerParams(vmem_limit_bytes=60 << 20),
    )(grad, layer, out_share, share, mlp_share, sums)


def per_device(
    tokens, lengths, buckets, out_cotangent, gain_attn, w_query, w_key, w_value, w_outgate,
    w_forget, b_forget, w_out, gain_mlp, w_gate, w_up, w_down,
):
    x, cotangent = tokens[0], out_cotangent[0]
    heads = w_forget.shape[1]
    gain_in, gain_mid = gain_attn[None], gain_mlp[None]
    weights = (w_query, w_key, w_value, w_outgate, w_forget.T)
    low, qn, kn, value, sig, attended, stat, decay, gated, w_full = forward_attention(
        x, lengths, gain_in, *weights, b_forget[None], w_out, 0
    )
    middle, mid_low, grad_rows, gate, up, hidden, mlp_local, squares = mlp_forward(
        x, cotangent, lengths, gated, gain_mid, w_full, w_gate, w_up, w_down
    )
    mid_local, g_down, g_gate, g_up, layer_own, mlp_square = mlp_backward(
        lengths, grad_rows, mid_low, gate, up, hidden, w_gate, w_up, w_down, mlp_local, middle, 1
    )
    grad_own, gg, mlp_share, mlp_gain = reduce_middle(
        mid_local, middle, grad_rows, gain_mid, w_full, [g_down, g_gate],
        ((0, 0), (0, 1), (1, 0), (1, 1)), 2,
    )
    in_local, g_four, g_out, g_fall, bias, layer_out = backward_attention(
        lengths, gg, low, qn, kn, value, sig, attended, stat, decay, *weights, grad_own, gated,
        layer_own, 3,
    )
    small = (mlp_gain, g_fall, squares, mlp_square, bias, lengths, buckets)
    input_grad, out_share, share, sums = reduce_input(
        in_local, x, grad_own, gain_in, small, [g_out, g_four, g_up],
        ((0, 0), (0, 1), (0, 2), (1, 0), (1, 1), (1, 2), (2, 0), (2, 1)), 4,
    )
    (
        input_grad, layer_out, g_out, g_query, g_key, g_value, g_outgate, g_gate, g_up, g_down,
        g_gain, g_gain_mid, g_fall, rms, bias,
    ) = finish(input_grad, layer_out, out_share, share, mlp_share, sums, heads)
    return (
        layer_out[None],
        input_grad[None],
        g_gain[0],
        g_query,
        g_key,
        g_value,
        g_outgate,
        g_fall.T,
        bias[0],
        g_out.T,
        g_gain_mid[0],
        g_gate,
        g_up,
        g_down.T,
        rms,
    )


def solution(mesh):
    placed = (
        P("dp", None, None),
        P("dp"),
        P("dp"),
        P("dp", None, None),
        P(),
        P(None, "mp"),
        P(None, "mp"),
        P(None, "mp"),
        P(None, "mp"),
        P(None, "mp"),
        P("mp"),
        P("mp", None),
        P(),
        P(None, "mp"),
        P(None, "mp"),
        P("mp", None),
    )
    return jax.shard_map(
        per_device,
        mesh=mesh,
        in_specs=placed,
        out_specs=(
            P("dp", None, None),
            P("dp", None, None),
            P("dp"),
            P("dp", "mp"),
            P("dp", "mp"),
            P("dp", "mp"),
            P("dp", "mp"),
            P("dp", "mp"),
            P("mp"),
            P("mp", "dp"),
            P("dp"),
            P("dp", "mp"),
            P("dp", "mp"),
            P("mp", "dp"),
            P(),
        ),
        check_vma=False,
    )
```

```python
import functools

import jax
import jax.numpy as jnp
from jax import lax
from jax.experimental import pallas as pl
from jax.experimental.pallas import tpu as pltpu
from jax.sharding import PartitionSpec as P

NBUCKET = 4


EPSILON = 1e-06


MESH = pl.DeviceIdType.MESH
F32 = jnp.float32
Y = 4
STEP = 512
HBM = pl.BlockSpec(memory_space=pl.ANY)
VMEM = pl.BlockSpec(memory_space=pltpu.VMEM)
STEPS = ("oR", "oL", "iR", "iL", "dR", "dL", "gRa", "gRb", "gLa", "gLb", "fR", "fL")


def rows_of(ref, start, count):
    return ref.at[pl.ds(pl.multiple_of(start, 8), count)]


def meet(devices):
    barrier = pltpu.get_barrier_semaphore()
    for device in devices:
        pl.semaphore_signal(barrier, inc=1, device_id=device, device_id_type=MESH)
    pl.semaphore_wait(barrier, len(devices))


def link(src, dst, ssem, rsem, at, device):
    return pltpu.make_async_remote_copy(
        src_ref=src,
        dst_ref=dst,
        send_sem=ssem.at[at],
        recv_sem=rsem.at[at],
        device_id=device,
        device_id_type=MESH,
    )


def push(*args):
    copy = link(*args)
    copy.start()
    return copy


class YRing:
    def __init__(self, rows, waves, ssem, rsem):
        self.sems = (ssem, rsem)
        self.dp, self.me = lax.axis_index("dp"), lax.axis_index("mp")
        self.right, self.left = lax.rem(self.me + 1, Y), lax.rem(self.me + 3, Y)
        self.far = lax.rem(self.me + 2, Y)
        self.quarter, self.half = rows // Y, rows // Y // 2
        self.tall = self.half // waves
        self.sent = {}

    def neighbours(self):
        return [(self.dp, self.right), (self.dp, self.left)]

    def send(self, name, wave, src, dst, to):
        kind, index = divmod(STEPS.index(name), 6)
        at = kind * 12 + wave * 6 + index
        self.sent[name, wave] = push(src, dst, *self.sems, at, (self.dp, to))

    def rows(self, x, owner, part, wave):
        return rows_of(x, owner * self.quarter + part * self.half + wave * self.tall, self.tall)

    def fetch(self, x, held, own, sem):
        self.loads = [
            load(rows_of(x, self.right * self.quarter, self.half), held.at[0], sem.at[0]),
            load(rows_of(x, self.left * self.quarter + self.half, self.half), held.at[1], sem.at[1]),
            load(rows_of(x, self.me * self.quarter, self.quarter), own, sem.at[2]),
        ]

    def start(self, x, opp, nbr, wave):
        w = slice(wave * self.tall, wave * self.tall + self.tall)
        low = slice(self.half + wave * self.tall, self.half + wave * self.tall + self.tall)
        self.send("oR", wave, self.rows(x, self.far, 0, wave), opp.at[0, w], self.right)
        self.send("oL", wave, self.rows(x, self.far, 1, wave), opp.at[1, w], self.left)
        self.send("iR", wave, self.rows(x, self.right, 1, wave), nbr.at[0, low], self.right)
        self.send("iL", wave, self.rows(x, self.left, 0, wave), nbr.at[1, w], self.left)

    def relay(self, opp, nbr, held, wave):
        w = slice(wave * self.tall, wave * self.tall + self.tall)
        low = slice(self.half + wave * self.tall, self.half + wave * self.tall + self.tall)
        for part, (come, go, into, to) in enumerate(
            (("oR", "dR", nbr.at[0, w], self.right), ("oL", "dL", nbr.at[1, low], self.left))
        ):
            self.sent[come, wave].wait_recv()
            if wave == 0:
                self.loads[part].wait()
            held[part, w] = held[part, w] + opp[part, w]
            self.send(go, wave, held.at[part, w], into, to)

    def collect(self, own, nbr, part, wave):
        if part == 0 and wave == 0:
            self.loads[2].wait()
        for name in (("dR", "iL"), ("iR", "dL"))[part]:
            self.sent[name, wave].wait_recv()
        start = part * self.half + wave * self.tall
        at = slice(start, start + self.tall)
        return at, own[at, :] + nbr[0, at] + nbr[1, at]

    def spread(self, part, wave, own, out):
        tag, into = "ab"[part], self.rows(out, self.me, part, wave)
        start = part * self.half + wave * self.tall
        mine = own.at[start : start + self.tall]
        self.send("gR" + tag, wave, mine, into, self.right)
        self.send("gL" + tag, wave, mine, into, self.left)

    def forward(self, wave, out):
        for come, go, owner, part, to in (
            ("gRa", "fR", self.left, 0, self.right),
            ("gLb", "fL", self.right, 1, self.left),
        ):
            self.sent[come, wave].wait_recv()
            block = self.rows(out, owner, part, wave)
            self.send(go, wave, block, block, to)

    def arrive(self, wave):
        for name in ("gRb", "gLa", "fR", "fL"):
            self.sent[name, wave].wait_recv()

    def finish(self):
        for copy in self.sent.values():
            copy.wait_send()


def ring_scratch(quarter, columns):
    return [
        pltpu.VMEM((2, quarter // 2, columns), F32),
        pltpu.VMEM((2, quarter, columns), F32),
        pltpu.VMEM((2, quarter // 2, columns), F32),
    ]


def sems(*counts):
    return [pltpu.SemaphoreType.DMA((n,)) for n in counts for _ in (0, 1)]


class Place:
    def __init__(self):
        self.dp, self.my = lax.axis_index("dp"), lax.axis_index("mp")
        c, z, x = lax.rem(self.dp, 2), lax.rem(self.dp // 2, 4), self.dp // 8
        self.c, self.sib, self.chip = c, self.dp + 1 - 2 * c, x * 4 + z
        self.st1, self.st2 = 4 - 3 * c, 1 + 3 * c
        self.p1, self.p2 = x + c * (z - x), z + c * (x - z)
        step = lambda p, by: lax.rem(p + by, 4)
        self.r1, self.l1, self.o1 = (step(self.p1, by) for by in (1, 3, 2))
        self.r2, self.l2, self.o2 = (step(self.p2, by) for by in (1, 3, 2))

    def device(self, a, b):
        return ((a * self.st1 + b * self.st2) * 2 + self.c, self.my)

    def peers(self):
        return [
            (self.sib, self.my),
            self.device(self.r1, self.p2),
            self.device(self.l1, self.p2),
            self.device(self.p1, self.r2),
            self.device(self.p1, self.l2),
        ]


class ScatterSum:
    def __init__(self, here, sources, own, other, near, last, asem, bsem, lsem, ssem, rsem):
        self.here, self.sources = here, sources
        self.own, self.other, self.near, self.last = own, other, near, last
        self.asem, self.bsem, self.lsem, self.ssem, self.rsem = asem, bsem, lsem, ssem, rsem
        self.n = own.shape[0]
        self.sibling, *to = here.peers()
        self.to = (to[0:2], to[2:4])

    def message(self, name, k, stage):
        at = (k * 2 + stage) * 6 + STEPS.index(name)
        device = self.to[stage][0 if name[1] == "R" else 1]
        here, own = self.here, self.own.at[k]
        if stage:
            own, into, cut = own.at[here.p1], self.last.at[k], (slice(0, 24), slice(24, 48))
            far, right, left = here.o2, here.r2, here.l2
        else:
            into, cut = self.near.at[k], (slice(0, 2), slice(2, 4))
            far, right, left = here.o1, here.r1, here.l1
        row, part, slot = {
            "oR": (far, 0, 0),
            "oL": (far, 1, 1),
            "iR": (right, 1, 3),
            "iL": (left, 0, 4),
            "dR": (right, 0, 2),
            "dL": (left, 1, 5),
        }[name]
        return link(own.at[row, cut[part]], into.at[slot], self.ssem, self.rsem, at, device)

    def whole(self, k):
        own, other = self.own.at[k], self.other.at[k]
        return link(own, other, self.asem, self.bsem, k, self.sibling)

    def exchange(self, k):
        here = self.here
        ref, start, width = self.sources[k]

        def source(block):
            return ref.at[pl.ds(pl.multiple_of(block * 48, 16), 48), pl.ds(start, width)]

        def cross(i, carry):
            a, b = i // 4, lax.rem(i, 4)
            block = source((a * here.st2 + b * here.st1) * 2 + 1 - here.c)
            push(block, self.other.at[k, a, b], self.asem, self.bsem, k, self.sibling)
            return carry

        def fetch(i, carry):
            a, b = i // 4, lax.rem(i, 4)
            block = source((a * here.st1 + b * here.st2) * 2 + here.c)
            pltpu.make_async_copy(block, self.own.at[k, a, b], self.lsem.at[k]).start()
            return carry

        lax.fori_loop(0, 16, cross, 0)
        lax.fori_loop(0, 16, fetch, 0)

    def first(self, k):
        here, own, other = self.here, self.own, self.other
        pltpu.make_async_copy(own.at[k], own.at[k], self.lsem.at[k]).wait()
        self.whole(k).wait_recv()

        def add(p):
            def body(b, carry):
                own[k, p, b] = own[k, p, b] + other[k, p, b]
                return carry

            lax.fori_loop(0, 4, body, 0)

        add(here.o1)
        self.message("oR", k, 0).start()
        self.message("oL", k, 0).start()
        add(here.r1)
        self.message("iR", k, 0).start()
        add(here.l1)
        self.message("iL", k, 0).start()
        add(here.p1)

    def first_relay(self, k):
        here, own, near = self.here, self.own, self.near

        def add(p, at, slot):
            def body(b, carry):
                own[k, p, at + b] = own[k, p, at + b] + near[k, slot, b]
                return carry

            lax.fori_loop(0, 2, body, 0)

        self.message("oR", k, 0).wait_recv()
        add(here.r1, 0, 0)
        self.message("dR", k, 0).start()
        self.message("oL", k, 0).wait_recv()
        add(here.l1, 2, 1)
        self.message("dL", k, 0).start()

    def second(self, k):
        here, own, near = self.here, self.own, self.near
        for name in ("iR", "dR", "iL", "dL"):
            self.message(name, k, 0).wait_recv()

        def add(p):
            h, b = p // 2, lax.rem(p, 2)
            own[k, here.p1, p] = own[k, here.p1, p] + near[k, 2 + h, b] + near[k, 4 + h, b]

        add(here.o2)
        self.message("oR", k, 1).start()
        self.message("oL", k, 1).start()
        add(here.r2)
        self.message("iR", k, 1).start()
        add(here.l2)
        self.message("iL", k, 1).start()
        add(here.p2)

    def second_relay(self, k):
        here, own, last = self.here, self.own, self.last
        self.message("oR", k, 1).wait_recv()
        own[k, here.p1, here.r2, 0:24] = own[k, here.p1, here.r2, 0:24] + last[k, 0]
        self.message("dR", k, 1).start()
        self.message("oL", k, 1).wait_recv()
        own[k, here.p1, here.l2, 24:48] = own[k, here.p1, here.l2, 24:48] + last[k, 1]
        self.message("dL", k, 1).start()

    def result(self, k, out, at):
        here, own, last = self.here, self.own, self.last
        width = own.shape[4]
        for name in ("iR", "dR", "iL", "dL"):
            self.message(name, k, 1).wait_recv()
        columns = pl.ds(pl.multiple_of(at * width, 128), width)
        out[0:24, columns] = own[k, here.p1, here.p2, 0:24] + last[k, 2] + last[k, 4]
        out[24:48, columns] = own[k, here.p1, here.p2, 24:48] + last[k, 3] + last[k, 5]

    def sent(self, k):
        self.whole(k).wait_send()
        for stage in (0, 1):
            for name in STEPS[:6]:
                self.message(name, k, stage).wait_send()


def each(low, high, step):
    def body(k, carry):
        step(k)
        return carry

    lax.fori_loop(low, high, body, 0)


class SmallSum:
    def __init__(self, here, bufs, landed, ssem, rsem):
        self.bufs, self.landed, self.ssem, self.rsem = bufs, landed, ssem, rsem
        turn = lambda p, by: lax.rem(p + by, 4)
        self.stages = [
            [(here.sib, here.my)],
            [here.device(turn(here.p1, by), here.p2) for by in (1, 2, 3)],
            [here.device(here.p1, turn(here.p2, by)) for by in (1, 2, 3)],
            [(here.dp, turn(here.my, by)) for by in (1, 2, 3)],
        ]
        self.far = [self.stages[1][1], self.stages[2][1], self.stages[3][1]]
        self.sent = []

    def send(self, stage):
        for to in self.stages[stage]:
            at = len(self.sent)
            copy = push(self.bufs.at[stage], self.landed.at[at], self.ssem, self.rsem, at, to)
            self.sent.append(copy)

    def take(self, stage):
        value, count = self.bufs[stage], len(self.stages[stage])
        for at in range(len(self.sent) - count, len(self.sent)):
            self.sent[at].wait_recv()
            value = value + self.landed[at]
        self.bufs[stage + 1] = value

    def finish(self):
        for copy in self.sent:
            copy.wait_send()


def scatter_scratch(n, w):
    return [
        pltpu.VMEM((n, 4, 4, 48, w), F32),
        pltpu.VMEM((n, 4, 4, 48, w), F32),
        pltpu.VMEM((n, 6, 2, 48, w), F32),
        pltpu.VMEM((n, 6, 24, w), F32),
        pltpu.SemaphoreType.DMA((n,)),
        pltpu.SemaphoreType.DMA((n,)),
        pltpu.SemaphoreType.DMA((n,)),
        pltpu.SemaphoreType.DMA((12 * n,)),
        pltpu.SemaphoreType.DMA((12 * n,)),
    ]


def scatter_sources(refs, pieces):
    return [(refs[which], at * STEP, STEP) for which, at in pieces]


def norm_back(value, source, base, gain):
    source = source.astype(F32)
    r = lax.rsqrt(jnp.mean(source * source, axis=1, keepdims=True) + EPSILON)
    n = source * r
    e = value * gain.astype(F32)
    inner = jnp.mean(e * n, axis=1, keepdims=True)
    return base.astype(F32) + r * (e - n * inner), jnp.sum(value * n, axis=0, keepdims=True)


def load(ref, scratch, sem):
    copy = pltpu.make_async_copy(ref, scratch, sem)
    copy.start()
    return copy


def middle_kernel(pieces, count, x_ref, source_ref, base_ref, gain_ref, w_ref, *refs):
    ins, refs = refs[:count], refs[count:]
    grad_ref, gg_ref, share_ref, sums_ref = refs[:4]
    source_s, base_s, w_s, opp, nbr, held, own_s, blocks, csem, *sem = refs[4:17]
    here, ring = Place(), YRing(x_ref.shape[0], 2, *sem[0:2])
    total = ScatterSum(here, scatter_sources(ins, pieces), *refs[17:])
    n = total.n
    far = (ring.dp, ring.far)
    meet(ring.neighbours() + [far] + here.peers())
    ring.start(x_ref, opp, nbr, 0)
    q, h = ring.quarter, ring.half
    ring.fetch(x_ref, held, own_s, csem)
    for k in range(n):
        total.exchange(k)
    loads = [
        load(rows_of(source_ref, ring.me * q, q), source_s, csem.at[3]),
        load(rows_of(base_ref, ring.me * q, q), base_s, csem.at[4]),
        load(w_ref, w_s, csem.at[5]),
    ]
    ring.relay(opp, nbr, held, 0)
    ring.start(x_ref, opp, nbr, 1)
    each(0, n, total.first)
    each(0, n - 2, total.first_relay)
    ring.relay(opp, nbr, held, 1)
    for copy in loads:
        copy.wait()
    sums, swaps, keeps = 0.0, [], []
    inner = gg_ref.shape[1]
    for wave in (0, 1):
        for part in (0, 1):
            at, value = ring.collect(own_s, nbr, part, wave)
            value, more = norm_back(value, source_s[at, :], base_s[at, :], gain_ref[...])
            grad_ref[at, :] = value
            sums = sums + more
        tall = ring.tall
        low = jnp.concatenate(
            [grad_ref[part * h + wave * tall : part * h + wave * tall + tall, :] for part in (0, 1)], axis=0
        ).astype(jnp.bfloat16)
        for j, by in enumerate((2, 1, 3, 0)):
            to = lax.rem(ring.me + by, Y)
            blocks[wave, j] = mm_t(low, rows_of(w_s, to * inner, inner)[...])
            for part in (0, 1):
                src = blocks.at[wave, j, part * tall : part * tall + tall]
                into = rows_of(gg_ref, ring.me * q + part * h + wave * tall, tall)
                if by:
                    at = (wave * 3 + j) * 2 + part
                    swaps.append(push(src, into, *sem[2:4], at, (ring.dp, to)))
                else:
                    keeps.append(load(src, into, csem.at[6 + wave * 2 + part]))
        if wave == 0:
            each(n - 2, n, total.first_relay)
    sums_ref[...] = sums
    each(0, n, total.second)
    each(0, n, total.second_relay)
    each(0, n, lambda k: total.result(k, share_ref, k))
    for copy in swaps:
        copy.wait_recv()
    for copy in keeps:
        copy.wait()
    for copy in swaps:
        copy.wait_send()
    ring.finish()
    each(0, n, total.sent)


def reduce_middle(partial, source, base, gain, w_full, grads, pieces, call_id):
    n = len(pieces)
    hbm, vmem = pl.BlockSpec(memory_space=pl.ANY), pl.BlockSpec(memory_space=pltpu.VMEM)
    rows, columns = partial.shape
    quarter, inner = rows // Y, w_full.shape[0] // Y
    return pl.pallas_call(
        functools.partial(middle_kernel, pieces, len(grads)),
        out_shape=[
            jax.ShapeDtypeStruct((quarter, columns), F32),
            jax.ShapeDtypeStruct((rows, inner), F32),
            jax.ShapeDtypeStruct((48, n * STEP), F32),
            jax.ShapeDtypeStruct((1, columns), F32),
        ],
        in_specs=[hbm, hbm, hbm, vmem, hbm] + [hbm] * len(grads),
        out_specs=[vmem, hbm, vmem, vmem],
        scratch_shapes=[
            pltpu.VMEM((quarter, columns), source.dtype),
            pltpu.VMEM((quarter, columns), base.dtype),
            pltpu.VMEM(w_full.shape, w_full.dtype),
        ]
        + ring_scratch(quarter, columns)
        + [
            pltpu.VMEM((quarter, columns), F32),
            pltpu.VMEM((2, 4, quarter // 2, inner), F32),
            pltpu.SemaphoreType.DMA((10,)),
        ]
        + sems(12, 12)
        + scatter_scratch(n, STEP),
        compiler_params=pltpu.CompilerParams(
            collective_id=call_id, has_side_effects=True, vmem_limit_bytes=56 << 20
        ),
    )(partial, source, base, gain, w_full, *grads)


def input_kernel(
    pieces, count, x_ref, source_ref, base_ref, gain_ref, other_ref, fall_ref, square_ref, more_ref,
    bias_ref, length_ref, bucket_ref, *refs
):
    ins, refs = refs[:count], refs[count:]
    out_ref, out_share_ref, share_ref, sums_ref = refs[:4]
    source_s, opp, nbr, held, own_s, mine_s, wide_s, landed, csem, *sem = refs[4:17]
    bufs, arrived, asem, bsem = refs[17:21]
    here, ring = Place(), YRing(x_ref.shape[0], 1, *sem[0:2])
    total = ScatterSum(here, scatter_sources(ins, pieces), *refs[21:])
    tiny = SmallSum(here, bufs, arrived, asem, bsem)
    n, first = total.n, wide_s.shape[1] // STEP
    meet(ring.neighbours() + here.peers() + tiny.far)
    ring.start(x_ref, opp, nbr, 0)
    q, h = ring.quarter, ring.half
    ring.fetch(x_ref, held, own_s, csem)
    copy = load(rows_of(source_ref, ring.me * q, q), source_s, csem.at[3])
    for k in range(n):
        total.exchange(k)
    each(0, n // 2, total.first)
    ring.relay(opp, nbr, held, 0)
    each(n // 2, n, total.first)
    each(0, n - 2, total.first_relay)
    copy.wait()
    sums = 0.0
    for wave in (0,):
        for part in (0, 1):
            at, value = ring.collect(own_s, nbr, part, wave)
            value, more = norm_back(value, source_s[at, :], base_ref[at, :], gain_ref[...])
            mine_s[at, :] = value
            ring.spread(part, wave, mine_s, out_ref)
            sums = sums + more
    kept = load(mine_s, rows_of(out_ref, ring.me * q, q), csem.at[4])
    bufs[0, 0:1, :] = sums
    bufs[0, 1:2, :] = other_ref[...]
    bufs[0, 8:16, :] = jnp.zeros_like(bufs[0, 8:16, :])
    bufs[0, 2:3, :] = jnp.zeros((1, sums_ref.shape[1]), F32)
    bufs[0, 3:9, :] = fall_ref[0:6, :]
    lane = lax.broadcasted_iota(jnp.int32, (1, PAIR), 1)
    both = jnp.sum(square_ref[...], axis=1, keepdims=True)
    in_bucket = lambda value: jnp.where(lane == bucket_ref[0], value, 0.0)
    bufs[0, 2:3, 0:PAIR] = in_bucket(jnp.sum(more_ref[...], axis=1, keepdims=True))
    for at, value in enumerate((both[0:1], both[1:2], length_ref[0].astype(F32))):
        bufs[0, 9:10, at * PAIR : at * PAIR + PAIR] = in_bucket(value)
    diagonal = lax.broadcasted_iota(jnp.int32, bias_ref.shape, 0) == lax.broadcasted_iota(
        jnp.int32, bias_ref.shape, 1
    )
    bufs[0, 10:11, 0:PAIR] = jnp.sum(jnp.where(diagonal, bias_ref[...], 0.0), axis=0, keepdims=True)
    tiny.send(0)
    each(n - 2, n, total.first_relay)
    each(0, n, total.second)
    ring.forward(0, out_ref)
    tiny.take(0)
    tiny.send(1)
    each(0, n, total.second_relay)
    tiny.take(1)
    tiny.send(2)
    each(0, first, lambda k: total.result(k, wide_s, k))
    inner = landed.shape[2]
    swaps = []
    for j, by in enumerate((2, 1, 3)):
        to = lax.rem(ring.me + by, Y)
        columns = pl.ds(pl.multiple_of(to * inner, 128), inner)
        swaps.append(push(wide_s.at[:, columns], landed.at[j], *sem[2:4], j, (ring.dp, to)))
    each(first, n, lambda k: total.result(k, share_ref, k - first))
    tiny.take(2)
    tiny.send(3)
    own = wide_s[:, pl.ds(pl.multiple_of(ring.me * inner, 128), inner)]
    for j, copy in enumerate(swaps):
        copy.wait_recv()
        own = own + landed[j]
    out_share_ref[...] = own
    tiny.take(3)
    rows = lax.broadcasted_iota(jnp.int32, sums_ref.shape, 0)
    sums_ref[...] = jnp.where(rows < 3, bufs[4], bufs[3])
    ring.arrive(0)
    kept.wait()
    for copy in swaps:
        copy.wait_send()
    tiny.finish()
    ring.finish()
    each(0, n, total.sent)


def reduce_input(partial, source, base, gain, small, grads, pieces, call_id):
    n = len(pieces)
    smem = pl.BlockSpec(memory_space=pltpu.SMEM)
    hbm, vmem = pl.BlockSpec(memory_space=pl.ANY), pl.BlockSpec(memory_space=pltpu.VMEM)
    rows, columns = partial.shape
    quarter, inner = rows // Y, grads[0].shape[1] // Y
    wide = grads[0].shape[1]
    shares = n * STEP - wide
    return pl.pallas_call(
        functools.partial(input_kernel, pieces, len(grads)),
        out_shape=[
            jax.ShapeDtypeStruct(partial.shape, F32),
            jax.ShapeDtypeStruct((48, inner), F32),
            jax.ShapeDtypeStruct((48, shares), F32),
            jax.ShapeDtypeStruct((16, columns), F32),
        ],
        in_specs=[hbm, hbm, vmem, vmem] + [vmem] * 5 + [smem] * 2 + [hbm] * len(grads),
        out_specs=[hbm] + [vmem] * 3,
        scratch_shapes=[pltpu.VMEM((quarter, columns), source.dtype)]
        + ring_scratch(quarter, columns)
        + [
            pltpu.VMEM((quarter, columns), F32),
            pltpu.VMEM((quarter, columns), F32),
            pltpu.VMEM((48, wide), F32),
            pltpu.VMEM((3, 48, inner), F32),
            pltpu.SemaphoreType.DMA((5,)),
        ]
        + sems(24, 3)
        + [pltpu.VMEM((5, 16, columns), F32), pltpu.VMEM((10, 16, columns), F32)]
        + sems(10)
        + scatter_scratch(n, STEP),
        compiler_params=pltpu.CompilerParams(
            collective_id=call_id, has_side_effects=True, vmem_limit_bytes=56 << 20
        ),
    )(partial, source, base, gain, *small, *grads)


HEAD = 64
PAIR = 128
NEG = -1e30


def rows_at(i, size):
    return pl.ds(pl.multiple_of(i * size, size), size)


def lane_is(shape, index):
    return lax.broadcasted_iota(jnp.int32, shape, len(shape) - 1) == index


def first_head(shape):
    return lax.broadcasted_iota(jnp.int32, shape, len(shape) - 1) < HEAD


def halves_mean(values):
    first = first_head(values.shape)
    low = jnp.sum(jnp.where(first, values, 0.0), axis=1, keepdims=True) * (1.0 / HEAD)
    high = jnp.sum(jnp.where(first, 0.0, values), axis=1, keepdims=True) * (1.0 / HEAD)
    return low, high


def one_row(ref, index):
    rows = ref[...]
    picked = lax.broadcasted_iota(jnp.int32, rows.shape, 0) == index
    return jnp.sum(jnp.where(picked, rows, 0.0), axis=0, keepdims=True)


def running_sum(values, backward=False):
    count = values.shape[1]
    at = lax.broadcasted_iota(jnp.int32, values.shape, 1)
    shift = 1
    while shift < count:
        if backward:
            moved = jnp.where(at < count - shift, pltpu.roll(values, count - shift, 1), 0.0)
        else:
            moved = jnp.where(at >= shift, pltpu.roll(values, shift, 1), 0.0)
        values = values + moved
        shift *= 2
    return values


def mm(left, right):
    return jnp.dot(left, right, preferred_element_type=F32)


def mm_t(left, right):
    return lax.dot_general(left, right, (((1,), (1,)), ((), ())), preferred_element_type=F32)


def t_mm(left, right):
    return lax.dot_general(left, right, (((0,), (0,)), ((), ())), preferred_element_type=F32)


def whole(shape):
    return pl.BlockSpec(shape, lambda *_: (0,) * len(shape), pipeline_mode=pl.Buffered(1))


def struct(*shape, t=F32):
    return jax.ShapeDtypeStruct(shape, t)


def local_call(kernel, grid, in_specs, out_specs, out_shape, scratch, limit, flops, moved, call_id=None):
    return pl.pallas_call(
        kernel,
        grid_spec=pltpu.PrefetchScalarGridSpec(
            num_scalar_prefetch=1,
            grid=(grid,),
            in_specs=in_specs,
            out_specs=out_specs,
            scratch_shapes=scratch,
        ),
        out_shape=out_shape,
        compiler_params=pltpu.CompilerParams(
            vmem_limit_bytes=limit << 20,
            collective_id=call_id,
            has_side_effects=call_id is not None,
        ),
        cost_estimate=pl.CostEstimate(
            flops=flops * 10**9, bytes_accessed=moved * 10**6, transcendentals=4 * 10**6
        ),
    )


def forward_kernel(
    length_ref, x_ref, gain_ref, wq_ref, wk_ref, wv_ref, wo_ref, wf_ref, bf_ref, w_ref,
    gain2_ref, cot_in, wg_in, wu_in, wd_in,
    low_out, qn_ref, kn_ref, v_ref, sig_ref, att_ref, stat_ref, decay_ref, gated_out, full_out,
    mid_out, normed_out, grad_out, gate_out, up_out, hid_out, mlp_out, sums_ref,
    top_s, row_s, q_s, k_s, w_s, pre_s, gs, ws, wf_s, bf_s, low_ref, gated_ref, full_ref,
    wg_s, wu_s, wd_s, cot_s, mid_s, normed_s, grad_s, gate_s, up_s, hid_s, mlp_s, osem, *sem,
):
    step = pl.program_id(0)
    seq = x_ref.shape[0]
    length = length_ref[0]
    here = Place()
    me, right, left, far = (lax.rem(here.my + by, Y) for by in (0, 1, 3, 2))
    sibling, right1, left1, right2, left2 = here.peers()
    c, p1, p2, half, quarter = here.c, here.p1, here.p2, seq // 2, seq // Y
    mine = ws.at[c, p2, p1, me]
    cross_order = (p2, here.l2, here.r2, here.o2)

    def plane(j):
        return link(mine, mine, *sem[2:4], j, (here.dp, (right, far, left)[j]))

    def torus(stage, j):
        if stage == 0:
            at, spots, to = (lambda p: ws.at[c, p2, p]), (p1, here.l1, here.r1), (right1, left1)
        else:
            at, spots, to = (lambda p: ws.at[c, p]), (p2, here.l2, here.r2), (right2, left2)
        spot, part, side = ((0, 0, 0), (0, 1, 0), (0, 0, 1), (0, 1, 1), (1, 0, 0), (2, 1, 1))[j]
        piece = at(spots[spot]).at[2 * part : 2 * part + 2]
        return link(piece, piece, *sem[4 + 2 * stage : 6 + 2 * stage], j, to[side])

    def cross(j):
        piece = ws.at[c, cross_order[j]]
        return link(piece, piece, *sem[8:10], j, sibling)

    def gate(pair, chunk, j):
        owner, part, to = (
            (me, 0, right), (me, 1, right), (me, 0, left), (me, 1, left), (left, 0, right), (right, 1, left)
        )[j]
        start = pl.multiple_of(chunk * half + part * quarter, quarter)
        piece = gs.at[pair, owner, pl.ds(start, quarter)]
        return link(piece, piece, *sem[0:2], (pair * 2 + chunk) * 6 + j, (here.dp, to))

    def offer(pair, chunk):
        for j in range(4):
            gate(pair, chunk, j).start()

    def flush(j):
        src, dst = (
            (low_ref, low_out),
            (full_ref, full_out),
            (rows_of(gated_ref, me * quarter, quarter), gated_out),
            (wg_in, wg_s),
            (wu_in, wu_s),
            (wd_in, wd_s),
        )[j]
        return pltpu.make_async_copy(src, dst, osem.at[j])

    def leave(j, chunk):
        src, dst = (
            (mid_s, mid_out), (normed_s, normed_out), (grad_s, grad_out), (gate_s, gate_out),
            (up_s, up_out), (hid_s, hid_out), (mlp_s, mlp_out),
        )[j]
        return pltpu.make_async_copy(src, dst.at[rows_at(chunk, half)], osem.at[6 + j])

    def come(chunk):
        return pltpu.make_async_copy(cot_in.at[rows_at(chunk, half)], cot_s, osem.at[13])

    def pass_on(make):
        make(0).wait_recv()
        make(4).start()
        make(3).wait_recv()
        make(5).start()

    def arrived(make):
        for j in (1, 2, 4, 5):
            make(j).wait_recv()

    @pl.when(step == 0)
    def _():
        tall, wide = ws.shape[4], ws.shape[5]
        two = w_ref[
            pl.ds(pl.multiple_of(here.chip // 2 * (2 * tall), 16), 2 * tall),
            pl.ds(pl.multiple_of(c * wide, 128), wide),
        ].astype(F32)
        mine[...] = jnp.where(lax.rem(here.chip, 2) == 0, two[0:tall], two[tall:])
        meet([(here.dp, right), (here.dp, left), (here.dp, far)] + here.peers())
        for j in range(3):
            plane(j).start()

    @pl.when(step == 0)
    def _():
        def norm(i, carry):
            at = rows_at(i, 128)
            x = x_ref[at, :].astype(F32)
            r = lax.rsqrt(jnp.mean(x * x, axis=1, keepdims=True) + EPSILON)
            low_ref[at, :] = (x * r * gain_ref[...].astype(F32)).astype(jnp.bfloat16)
            return carry

        lax.fori_loop(0, seq // 128, norm, 0)
        flush(0).start()
        heads = wf_ref.shape[0]
        wf_s[...] = jnp.zeros_like(wf_s)
        wf_s[0:heads, :] = wf_ref[...]
        bf_s[...] = jnp.zeros_like(bf_s)
        bf_s[:, 0:heads] = bf_ref[...].astype(F32)
        pre = mm_t(wf_s[...], low_ref[...])[0:8] + jnp.broadcast_to(bf_s[...], (PAIR, PAIR)).T[0:8, 0:1]
        fall = jnp.minimum(pre, 0.0) - jnp.log1p(jnp.exp(-jnp.abs(pre)))
        decay = running_sum(fall)
        column = lax.broadcasted_iota(jnp.int32, decay.shape, 1)
        decay_ref[0] = decay
        decay_ref[1] = jax.nn.sigmoid(-pre)
        row_s[...] = jnp.where(column < length, decay, -NEG)
        final = jnp.sum(jnp.where(column == length - 1, decay, 0.0), axis=1, keepdims=True)
        top = jnp.where(column < length, decay, final)
        top_s[...] = jnp.concatenate([top, jnp.zeros((PAIR - 8, seq), F32)], axis=0).T

    for j, ref in enumerate((wq_ref, wk_ref, wv_ref, wo_ref)):
        w_s[:, j * PAIR : j * PAIR + PAIR] = ref[...]
    pre_s[...] = mm(low_ref[...], w_s[...])

    def norms(i, carry):
        at = rows_at(i, 128)
        for j, n_ref, s, col in ((0, qn_ref, q_s, 0), (1, kn_ref, k_s, 2)):
            pre = pre_s[at, j * PAIR : j * PAIR + PAIR]
            a, b = halves_mean(pre * pre)
            a, b = lax.rsqrt(a + EPSILON), lax.rsqrt(b + EPSILON)
            n = pre * jnp.where(first_head(pre.shape), a, b)
            n_ref[at, :] = n
            s[at, :] = n.astype(jnp.bfloat16)
            here = jnp.where(lane_is(pre.shape, col), a, jnp.where(lane_is(pre.shape, col + 1), b, 0.0))
            stat_ref[at, :] = here if col == 0 else stat_ref[at, :] + here
        v_ref[at, :] = pre_s[at, 2 * PAIR : 3 * PAIR].astype(jnp.bfloat16)
        sig_ref[at, :] = jax.nn.sigmoid(pre_s[at, 3 * PAIR : 4 * PAIR])
        return carry

    lax.fori_loop(0, seq // 128, norms, 0)

    @pl.when(step == 0)
    def _():
        for j in range(3):
            plane(j).wait_recv()
        for j in range(4):
            torus(0, j).start()

    @pl.when(step == 1)
    def _():
        arrived(lambda j: torus(0, j))
        for j in range(4):
            torus(1, j).start()
        cross(0).start()
        for j in (3, 4, 5):
            flush(j).start()
        come(0).start()

    @pl.when(step == 2)
    def _():
        pass_on(lambda j: torus(1, j))

    lines = [one_row(row_s, 2 * step + head) for head in (0, 1)]
    first = first_head((128, PAIR))
    zero = jnp.zeros((128, PAIR), jnp.bfloat16)
    upper = lax.broadcasted_iota(jnp.int32, (128, 128), 1) > lax.broadcasted_iota(
        jnp.int32, (128, 128), 0
    )
    for i in range(seq // 128):
        at, n = slice(i * 128, i * 128 + 128), i * 128 + 128
        q = q_s[at, :]
        both = []
        for head in (0, 1):
            own = jnp.where(first, q, zero) if head == 0 else jnp.where(first, zero, q)
            s = mm_t(own, k_s[0:n, :])
            column = jnp.sum(
                jnp.where(lane_is((128, PAIR), 2 * step + head), top_s[at, :], 0.0), axis=1, keepdims=True
            )
            s = s * (HEAD ** (-0.5)) + (column - lines[head][:, 0:n])
            diagonal = jnp.where(upper, NEG, s[:, n - 128 :])
            s = diagonal if i == 0 else jnp.concatenate([s[:, : n - 128], diagonal], axis=1)
            p = jnp.exp(s)
            p = p * (1.0 / jnp.sum(p, axis=1, keepdims=True))
            both.append(mm(p.astype(jnp.bfloat16), v_ref[0:n, :]))
        out = jnp.where(first, both[0], both[1])
        att_ref[at, :] = out
        gs[step, me, at, :] = (out * sig_ref[at, :]).astype(jnp.bfloat16).astype(F32)
        if n == half:
            offer(step, 0)

    @pl.when(step == 0)
    def _():
        offer(0, 1)
        pass_on(lambda j: torus(0, j))

    @pl.when(step > 0)
    def _():
        pass_on(lambda j: gate(step - 1, 0, j))

    @pl.when(step == pl.num_programs(0) - 1)
    def _():
        torus(1, 1).wait_recv()
        cross(1).start()
        torus(1, 2).wait_recv()
        cross(2).start()
        torus(1, 4).wait_recv()
        torus(1, 5).wait_recv()
        cross(3).start()
        pass_on(lambda j: gate(step, 0, j))
        pairs = gs.shape[0]
        for pair in range(1, pairs):
            offer(pair, 1)
        for j in range(4):
            cross(j).wait_recv()
        tall, wide, shard = ws.shape[4], ws.shape[5], w_ref.shape[0]

        def turn(k, carry):
            y, m = k // 8, lax.rem(k, 8)
            x, z = m // 2, lax.rem(m, 2) * 2
            rows = pl.ds(pl.multiple_of(y * shard + m * 2 * tall, 16), 2 * tall)
            for h, one, two in (
                (0, ws[0, z, x, y], ws[0, z + 1, x, y]),
                (1, ws[1, x, z, y], ws[1, x, z + 1, y]),
            ):
                both = jnp.concatenate([one, two], axis=0).astype(jnp.bfloat16)
                full_ref[rows, h * wide : h * wide + wide] = both
            return carry

        lax.fori_loop(0, 8 * Y, turn, 0)
        flush(1).start()
        for j in (3, 4, 5):
            flush(j).wait()
        outer, inner = full_ref.shape[1] // 2, wg_s.shape[1] // 2
        columns = lambda k, size: pl.ds(pl.multiple_of(k * size, size), size)
        sums_ref[...] = jnp.zeros_like(sums_ref)

        def feed_forward(chunk):
            rows = rows_at(chunk, half)
            for pair in range(pairs):
                arrived(lambda j: gate(pair, chunk, j))
                for y in range(Y):
                    lane = (y * pairs + pair) * PAIR
                    gated_ref[rows, lane : lane + PAIR] = gs[pair, y, rows, :].astype(jnp.bfloat16)

            @pl.when(chunk == 1)
            def _():
                flush(2).start()
                for j in range(7):
                    leave(j, 0).wait()
                come(1).start()

            kept = lax.broadcasted_iota(jnp.int32, (half, 1), 0) + chunk * half < length

            def project(k):
                at = columns(k, outer)
                branch = mm(gated_ref[rows, :], full_ref[:, at])
                x = x_ref[rows, at].astype(F32)
                mid_s[:, at] = x + branch
                for row, value in ((0, x), (1, branch)):
                    value = jnp.where(kept, value * value, 0.0)
                    sums_ref[row : row + 1, at] = sums_ref[row : row + 1, at] + jnp.sum(
                        value, axis=0, keepdims=True
                    )

            each(0, 2, project)
            leave(0, chunk).start()

            def norm(i, carry):
                at = rows_at(i, 128)
                mid = mid_s[at, :]
                r = lax.rsqrt(jnp.mean(mid * mid, axis=1, keepdims=True) + EPSILON)
                normed_s[at, :] = (mid * r * gain2_ref[...].astype(F32)).astype(jnp.bfloat16)
                return carry

            lax.fori_loop(0, half // 128, norm, 0)
            leave(1, chunk).start()

            @pl.when(chunk == 0)
            def _():
                pass_on(lambda j: gate(0, 1, j))

            def hidden(k):
                at = columns(k, inner)
                gate_s[:, at] = mm(normed_s[...], wg_s[:, at])
                up_s[:, at] = mm(normed_s[...], wu_s[:, at])
                pre = gate_s[:, at]
                hid_s[:, at] = (pre * jax.nn.sigmoid(pre) * up_s[:, at]).astype(jnp.bfloat16)

            each(0, 2, hidden)
            for j in (3, 4, 5):
                leave(j, chunk).start()

            @pl.when(chunk == 0)
            def _():
                for pair in range(1, pairs):
                    pass_on(lambda j: gate(pair, 1, j))

            come(chunk).wait()
            grad_s[...] = jnp.where(kept, cot_s[...].astype(F32), 0.0).astype(jnp.bfloat16)
            leave(2, chunk).start()

            def project_out(k):
                at = columns(k, outer)
                mlp_s[:, at] = mm(hid_s[...], wd_s[:, at])

            each(0, 2, project_out)
            leave(6, chunk).start()

        each(0, 2, feed_forward)
        for j in range(7):
            leave(j, 1).wait()
        for j in range(3):
            flush(j).wait()
            plane(j).wait_send()
        for stage in (0, 1):
            for j in range(6):
                torus(stage, j).wait_send()
        for j in range(4):
            cross(j).wait_send()
        for pair in range(pairs):
            for chunk in (0, 1):
                for j in range(6):
                    gate(pair, chunk, j).wait_send()


def forward(
    tokens, cotangent, length, gain, wq, wk, wv, wo, wf, bf, w_out, gain2, wg, wu, wd, call_id
):
    seq, width = tokens.shape
    heads, hidden, half = wq.shape[1], wg.shape[1], seq // 2
    weights = pl.BlockSpec((width, PAIR), lambda i, _: (0, i))
    lanes = pl.BlockSpec((seq, PAIR), lambda i, _: (0, i))
    low = jnp.bfloat16
    half_rows = lambda w, t=F32: pltpu.VMEM((half, w), t)
    return local_call(
        forward_kernel,
        heads // PAIR,
        [whole((seq, width)), whole((1, width))] + [weights] * 4
        + [whole(wf.shape), whole(bf.shape), whole(w_out.shape), whole((1, width))] + [HBM] * 4,
        [HBM] + [lanes] * 6 + [whole((2, 8, seq))] + [HBM] * 9 + [whole((2, width))],
        [
            struct(seq, width, t=low), struct(seq, heads), struct(seq, heads), struct(seq, heads, t=low),
            struct(seq, heads), struct(seq, heads), struct(seq, heads),
            struct(2, 8, seq), struct(seq // Y, heads * Y, t=low), struct(heads * Y, width, t=low),
            struct(seq, width), struct(seq, width, t=low), struct(seq, width, t=low),
            struct(seq, hidden), struct(seq, hidden), struct(seq, hidden, t=low), struct(seq, width),
            struct(2, width),
        ],
        [
            pltpu.VMEM((seq, PAIR), F32),
            pltpu.VMEM((8, seq), F32),
            pltpu.VMEM((seq, PAIR), low),
            pltpu.VMEM((seq, PAIR), low),
            pltpu.VMEM((width, 4 * PAIR), low),
            pltpu.VMEM((seq, 4 * PAIR), F32),
            pltpu.VMEM((heads // PAIR, Y, seq, PAIR), F32),
            pltpu.VMEM((2, 4, 4, Y, heads // 16, width // 2), F32),
            pltpu.VMEM((16, width), low),
            pltpu.VMEM((1, PAIR), F32),
            pltpu.VMEM((seq, width), low),
            pltpu.VMEM((seq, width), low),
            pltpu.VMEM((heads * Y, width), low),
            pltpu.VMEM((width, hidden), low),
            pltpu.VMEM((width, hidden), low),
            pltpu.VMEM((hidden, width), low),
            half_rows(width, low), half_rows(width), half_rows(width, low), half_rows(width, low),
            half_rows(hidden), half_rows(hidden), half_rows(hidden, low), half_rows(width),
            pltpu.SemaphoreType.DMA((14,)),
        ]
        + sems(12 * (heads // PAIR), 3, 6, 6, 4),
        63, 17, 60, call_id,
    )(length, tokens, gain, wq, wk, wv, wo, wf, bf, w_out, gain2, cotangent, wg, wu, wd)


def copier(sem):
    count = iter(range(sem.shape[0]))

    def copy(src, dst):
        return load(src, dst, sem.at[next(count)])

    return copy


def reduce_links(rows, x, opp, nbr, held, sem):
    dp, me = lax.axis_index("dp"), lax.axis_index("mp")
    right, left, far = lax.rem(me + 1, Y), lax.rem(me + 3, Y), lax.rem(me + 2, Y)
    q, h = rows // Y, rows // Y // 2

    def message(name):
        src, dst, to = {
            "oR": (lambda: rows_of(x, far * q, h), lambda: opp.at[0], right),
            "oL": (lambda: rows_of(x, far * q + h, h), lambda: opp.at[1], left),
            "iR": (lambda: rows_of(x, right * q + h, h), lambda: nbr.at[0, h:q], right),
            "iL": (lambda: rows_of(x, left * q, h), lambda: nbr.at[1, 0:h], left),
            "dR": (lambda: held.at[0], lambda: nbr.at[0, 0:h], right),
            "dL": (lambda: held.at[1], lambda: nbr.at[1, h:q], left),
        }[name]
        return link(src(), dst(), *sem, STEPS.index(name), (dp, to))

    return message, me, right, left, [(dp, right), (dp, left)]


def mlp_backward_kernel(
    length_ref, grad_in, low_in, gate_in, up_in, hid_in, wd_in, wg_in, wu_in, x_ref, mid_ref,
    back_out, gd_out, gg_out, gu_out, layer_ref, square_ref,
    grad_ref, low_ref, gate_ref, up_ref, hid_ref, wd_ref, wg_ref, wu_ref,
    dg_s, du_s, back_s, bufs, opp, nbr, held, own_s, mid_s, csem, *sem,
):
    seq, width = grad_ref.shape
    units = wd_ref.shape[0] // 2
    low16 = jnp.bfloat16
    message, me, right, left, peers = reduce_links(seq, x_ref, opp, nbr, held, sem)
    q, h = seq // Y, seq // Y // 2
    copy = copier(csem)
    need = [
        copy(grad_in, grad_ref),
        copy(wd_in.at[0:units], wd_ref.at[0:units]),
        copy(gate_in.at[:, 0:units], gate_ref.at[:, 0:units]),
        copy(up_in.at[:, 0:units], up_ref.at[:, 0:units]),
    ]
    meet(peers)
    for name in STEPS[:4]:
        message(name).start()
    for c in need[0:2]:
        c.wait()
    next_low, next_hid = copy(low_in, low_ref), copy(hid_in, hid_ref)
    more = [
        copy(wd_in.at[units:], wd_ref.at[units:]),
        copy(gate_in.at[:, units:], gate_ref.at[:, units:]),
        copy(up_in.at[:, units:], up_ref.at[:, units:]),
    ]
    weights = [copy(wg_in, wg_ref), copy(wu_in, wu_ref)]
    adds = [
        copy(rows_of(x_ref, right * q, h), held.at[0]),
        copy(rows_of(x_ref, left * q + h, h), held.at[1]),
        copy(rows_of(x_ref, me * q, q), own_s),
        copy(rows_of(mid_ref, me * q, q), mid_s),
    ]
    spots = (gd_out, gg_out, gu_out)
    columns = lambda j: pl.ds(pl.multiple_of(j * units, units), units)
    flush = lambda j, which: pltpu.make_async_copy(
        bufs.at[which, j], spots[which].at[:, columns(j)], csem.at[csem.shape[0] - 6 + which * 2 + j]
    )

    def write(which, left_of, right_of, j):
        slot, at = bufs.at[which, j], columns(j)

        def rows(i, carry):
            part = rows_at(i, 768)
            slot[part, :] = t_mm(left_of[:, part], right_of[:, at])
            return carry

        lax.fori_loop(0, width // 768, rows, 0)
        flush(j, which).start()

    def tile(j):
        at = columns(j)

        @pl.when(j == 1)
        def _():
            for c in more:
                c.wait()

        grad = mm_t(grad_ref[...], wd_ref[at, :])

        @pl.when(j == 0)
        def _():
            for c in need[2:4]:
                c.wait()

        gate = gate_ref[:, at]
        sig = jax.nn.sigmoid(gate)
        dg_s[:, at] = (grad * up_ref[:, at] * (sig * (1.0 + gate * (1.0 - sig)))).astype(low16)
        du_s[:, at] = (grad * (gate * sig)).astype(low16)

        @pl.when(j == 0)
        def _():
            next_low.wait()
            next_hid.wait()

        write(0, grad_ref, hid_ref, j)
        write(1, low_ref, dg_s, j)

        @pl.when(j == 1)
        def _():
            for part, (come, go) in enumerate((("oR", "dR"), ("oL", "dL"))):
                message(come).wait_recv()
                adds[part].wait()
                held[part] = held[part] + opp[part]
                message(go).start()

        write(2, low_ref, du_s, j)

    each(0, 2, tile)
    for c in weights:
        c.wait()

    def back(i, carry):
        rows = rows_at(i, 768)
        back_s[:, rows] = mm_t(dg_s[...], wg_ref[rows, :])
        back_s[:, rows] = back_s[:, rows] + mm_t(du_s[...], wu_ref[rows, :])
        return carry

    lax.fori_loop(0, width // 768, back, 0)
    last = copy(back_s, back_out)
    adds[2].wait()
    adds[3].wait()
    sums = 0.0
    for part, names in enumerate((("dR", "iL"), ("iR", "dL"))):
        for name in names:
            message(name).wait_recv()
        at = slice(part * h, part * h + h)
        branch = own_s[at, :] + nbr[0, at] + nbr[1, at]
        layer_ref[at, :] = (mid_s[at, :] + branch).astype(low16).astype(F32)
        row = lax.broadcasted_iota(jnp.int32, (h, 1), 0) + (me * q + part * h)
        kept = jnp.where(row < length_ref[0], branch * branch, 0.0)
        sums = sums + jnp.sum(kept, axis=0, keepdims=True)
    square_ref[...] = sums
    last.wait()
    for j in (0, 1):
        for which in range(3):
            flush(j, which).wait()
    for name in STEPS[:6]:
        message(name).wait_send()


def mlp_backward(length, grad, low, gate, up, hid, wg, wu, wd, branch, mid, call_id):
    seq, width = low.shape
    hidden = wg.shape[1]
    quarter = seq // Y
    low16 = jnp.bfloat16
    smem = pl.BlockSpec(memory_space=pltpu.SMEM)
    inputs = (grad, low, gate, up, hid, wd, wg, wu)
    return pl.pallas_call(
        mlp_backward_kernel,
        in_specs=[smem] + [HBM] * 10,
        out_specs=[HBM] * 4 + [VMEM] * 2,
        out_shape=[struct(seq, width)] + [struct(width, hidden)] * 3
        + [struct(quarter, width), struct(1, width)],
        scratch_shapes=[pltpu.VMEM(a.shape, a.dtype) for a in inputs]
        + [pltpu.VMEM((seq, hidden), low16)] * 2
        + [pltpu.VMEM((seq, width), F32), pltpu.VMEM((3, 2, width, hidden // 2), F32)]
        + ring_scratch(quarter, width)
        + [pltpu.VMEM((quarter, width), F32)] * 2
        + [pltpu.SemaphoreType.DMA((22,))]
        + sems(6),
        compiler_params=pltpu.CompilerParams(
            vmem_limit_bytes=62 << 20, collective_id=call_id, has_side_effects=True
        ),
    )(length, *inputs, branch, mid)


def backward_kernel(
    length_ref, gg_ref, low_in, qn_ref, kn_ref, v_ref, sig_ref, att_ref, stat_ref,
    decay_ref, wq_ref, wk_ref, wv_ref, wo_ref, wf_ref, own_ref, gated_ref, layer_ref,
    back_out, four_out, gout_out, gf_ref, bias_ref, out_ref,
    k_s, do_s, line_s, top_s, dq_s, dk_s, dv_s, all_s, fall_s, w_s, wf_s, lay_s, back_ref, wide_s, low_ref, osem,
    *sem,
):
    step = pl.program_id(0)
    seq, width = low_ref.shape
    length = length_ref[0]
    low16 = jnp.bfloat16
    wide = 4 * PAIR
    dp, me = lax.axis_index("dp"), lax.axis_index("mp")
    right, left = lax.rem(me + 1, Y), lax.rem(me + 3, Y)
    q, h = seq // Y, seq // Y // 2

    def spread(j):
        owner, part, to = (
            (me, 0, right), (me, 1, right), (me, 0, left), (me, 1, left), (left, 0, right), (right, 1, left)
        )[j]
        piece = rows_of(lay_s, owner * q + part * h, h)
        source = layer_ref.at[part * h : part * h + h] if j < 4 else piece
        return link(source, piece, *sem, j, (dp, to))

    def fetch(j):
        pair = ((layer_ref, rows_of(lay_s, me * q, q)), (low_in, low_ref))[j]
        return pltpu.make_async_copy(*pair, osem.at[5 + j])

    @pl.when(step == 0)
    def _():
        meet([(dp, right), (dp, left)])
        for j in range(4):
            spread(j).start()
        for j in (0, 1):
            fetch(j).start()

    @pl.when(step == 2)
    def _():
        spread(0).wait_recv()
        spread(4).start()
        spread(3).wait_recv()
        spread(5).start()

    @pl.when(step == 0)
    def _():
        heads = wf_ref.shape[0]
        wf_s[...] = jnp.zeros_like(wf_s)
        wf_s[0:heads, :] = wf_ref[...]
        decay = decay_ref[0]
        column = lax.broadcasted_iota(jnp.int32, decay.shape, 1)
        final = jnp.sum(jnp.where(column == length - 1, decay, 0.0), axis=1, keepdims=True)
        line_s[...] = jnp.where(column < length, decay, final)
        masked = jnp.where(column < length, decay, -NEG)
        top_s[...] = jnp.concatenate([masked, jnp.zeros((PAIR - 8, seq), F32)], axis=0).T
        fall_s[...] = jnp.zeros_like(fall_s)

    base = pl.multiple_of(step * wide, wide)
    part = lambda j: pl.ds(pl.multiple_of(base + j * PAIR, PAIR), PAIR)
    for j, w_ref in enumerate((wq_ref, wk_ref, wv_ref, wo_ref)):
        w_s[:, part(j)] = w_ref[...]
    first = first_head((seq, PAIR))
    gg, sig = gg_ref[...], sig_ref[...]
    do_s[...] = (gg * sig).astype(low16)
    all_s[:, part(3)] = (gg * att_ref[...] * sig * (1.0 - sig)).astype(low16)
    k_s[...] = kn_ref[...].astype(low16)
    dk_s[...] = jnp.zeros_like(dk_s)
    dv_s[...] = jnp.zeros_like(dv_s)
    columns, lines = [], [one_row(line_s, 2 * step + head) for head in (0, 1)]
    for head in (0, 1):
        column = jnp.sum(
            jnp.where(lane_is((seq, PAIR), 2 * step + head), top_s[...], 0.0), axis=1, keepdims=True
        )
        columns.append(column)
    block = first_head((128, PAIR))
    zero = jnp.zeros((128, PAIR), low16)
    lower = lax.broadcasted_iota(jnp.int32, (128, 128), 0) > lax.broadcasted_iota(
        jnp.int32, (128, 128), 1
    )
    for i in range(seq // 128):
        at, n = slice(i * 128, i * 128 + 128), i * 128 + 128
        query = qn_ref[at, :].astype(low16)
        do = do_s[at, :]
        pieces = []
        for head in (0, 1):
            pick = (lambda t: jnp.where(block, t, zero)) if head == 0 else (lambda t: jnp.where(block, zero, t))
            own_q, own_do = pick(query), pick(do)
            one = jnp.where(lane_is((128, PAIR), 2 * step + head), 1.0, 0.0).astype(low16)
            s = mm_t(k_s[0:n, :], own_q)
            s = s * (HEAD ** (-0.5)) + (lines[head][:, at] - columns[head][0:n])
            diagonal = jnp.where(lower, NEG, s[n - 128 :, :])
            s = diagonal if i == 0 else jnp.concatenate([s[: n - 128, :], diagonal], axis=0)
            p = jnp.exp(s)
            p = p * (1.0 / jnp.sum(p, axis=0, keepdims=True))
            gp = mm_t(v_ref[0:n, :], own_do)
            ds = (p * (gp - jnp.sum(p * gp, axis=0, keepdims=True))).astype(low16)
            dv_s[0:n, :] = dv_s[0:n, :] + mm(p.astype(low16), own_do)
            dk_s[0:n, :] = dk_s[0:n, :] + mm(ds, jnp.concatenate([own_q, one], axis=1))
            mark = jnp.where(lane_is((n, PAIR), 2 * step + head), 1.0, 0.0).astype(low16)
            pieces.append(t_mm(ds, jnp.concatenate([k_s[0:n, :], mark], axis=1)))
        dq_s[at, :] = jnp.where(block, pieces[0][:, 0:PAIR], pieces[1][:, 0:PAIR])
        fall_s[at, :] = fall_s[at, :] + pieces[0][:, PAIR:] + pieces[1][:, PAIR:]
    fall_s[...] = fall_s[...] - dk_s[:, PAIR:]
    stat = stat_ref[...]
    for e, n_ref, col, to in ((dq_s, qn_ref, 0, 0), (dk_s, kn_ref, 2, 1)):
        e = e[:, 0:PAIR] * (HEAD ** (-0.5))
        n = n_ref[...]
        a, b = halves_mean(e * n)
        r = jnp.where(first, stat[:, col : col + 1], stat[:, col + 1 : col + 2])
        all_s[:, part(to)] = (r * (e - n * jnp.where(first, a, b))).astype(low16)
    all_s[:, part(2)] = dv_s[...].astype(low16)
    slot = lax.rem(step, 2)

    @pl.when(step == 0)
    def _():
        for j in (0, 1):
            fetch(j).wait()

    def flush(j, at, step):
        columns = pl.ds(pl.multiple_of(step * wide, wide), wide)
        out = (four_out, gout_out)[j].at[:, columns]
        return pltpu.make_async_copy(wide_s.at[at, j], out, osem.at[at * 2 + j])

    @pl.when(step == 2)
    def _():
        for j in (0, 1):
            flush(j, 0, 0).wait()

    def grads(k, carry):
        rows = rows_at(k, 768)
        wide_s[slot, 0, rows, :] = t_mm(low_ref[:, rows], all_s[:, pl.ds(base, wide)])
        wide_s[slot, 1, rows, :] = t_mm(own_ref[:, rows].astype(low16), gated_ref[...])
        return carry

    lax.fori_loop(0, width // 768, grads, 0)
    for j in (0, 1):
        flush(j, slot, step).start()

    @pl.when(step == pl.num_programs(0) - 1)
    def _():
        fall = running_sum(fall_s[...].T[0:8], backward=True) * decay_ref[1]
        fall = jnp.concatenate([fall, jnp.zeros_like(fall)], axis=0).astype(low16)
        bias = jnp.sum(fall.astype(F32), axis=1, keepdims=True)
        bias_ref[...] = jnp.broadcast_to(bias[0:8], (8, PAIR))
        gf_ref[...] = mm(fall, low_ref[...])[0:8]

        def tail(k, carry):
            rows = rows_at(k, 768)
            back_ref[:, rows] = mm_t(all_s[...], w_s[rows, :])
            back_ref[:, rows] = back_ref[:, rows] + t_mm(fall, wf_s[:, rows])
            return carry

        lax.fori_loop(0, width // 768, tail, 0)
        last = load(back_ref, back_out, osem.at[4])
        for j in (1, 2, 4, 5):
            spread(j).wait_recv()
        out_ref[...] = lay_s[...].astype(low16)
        for at, done in ((1, 1), (0, 2)):
            for j in (0, 1):
                flush(j, at, done).wait()
        last.wait()
        for j in range(6):
            spread(j).wait_send()


def backward_attention(place, gg, low, qn, kn, v, sig, att, stat, decay, wq, wk, wv, wo, wf, own, gated, layer, call_id):
    seq, width = low.shape
    heads = wq.shape[1]
    weights = pl.BlockSpec((width, PAIR), lambda i, _: (0, i))
    lanes = pl.BlockSpec((seq, PAIR), lambda i, _: (0, i))
    full = whole((seq, width))
    low16 = jnp.bfloat16
    return local_call(
        backward_kernel,
        heads // PAIR,
        [lanes, HBM] + [lanes] * 6 + [whole((2, 8, seq))] + [weights] * 4
        + [whole(wf.shape), whole(own.shape)]
        + [pl.BlockSpec((own.shape[0], 4 * PAIR), lambda i, _: (0, i)), HBM],
        [HBM, HBM, HBM, whole((8, width)), whole((8, PAIR)), full],
        [
            struct(seq, width), struct(width, 4 * heads), struct(width, width), struct(8, width),
            struct(8, PAIR), struct(seq, width, t=low16),
        ],
        [
            pltpu.VMEM((seq, PAIR), low16),
            pltpu.VMEM((seq, PAIR), low16),
            pltpu.VMEM((8, seq), F32),
            pltpu.VMEM((seq, PAIR), F32),
            pltpu.VMEM((seq, PAIR), F32),
            pltpu.VMEM((seq, 2 * PAIR), F32),
            pltpu.VMEM((seq, PAIR), F32),
            pltpu.VMEM((seq, 4 * heads), low16),
            pltpu.VMEM((seq, PAIR), F32),
            pltpu.VMEM((width, 4 * heads), low16),
            pltpu.VMEM((16, width), low16),
            pltpu.VMEM((seq, width), F32),
            pltpu.VMEM((seq, width), F32),
            pltpu.VMEM((2, 2, width, 4 * PAIR), F32),
            pltpu.VMEM((seq, width), low16),
            pltpu.SemaphoreType.DMA((7,)),
        ]
        + sems(6),
        62, 14, 50, call_id,
    )(place, gg, low, qn, kn, v, sig, att, stat, decay, wq, wk, wv, wo, wf, own, gated, layer)


def finish_kernel(
    grad_in, layer_in, wout_hbm, four_hbm, mlp_hbm, sums_hbm,
    grad_ref, layer_ref, wout_ref, q_ref, k_ref, v_ref, o_ref, gate_ref, up_ref, down_ref,
    gain_ref, gain2_ref, fall_ref, rms_ref, bias_ref,
    grad_s, layer_s, four_in, mlp_in, sums_in, sem,
):
    copy = copier(sem)
    rows = grad_in.shape[0] // 4
    parts = [slice(j * rows, j * rows + rows) for j in range(4)]
    come = [(copy(grad_in.at[p], grad_s.at[p]), grad_s.at[p], grad_ref.at[p]) for p in parts]
    small = [copy(wout_hbm, wout_ref), copy(four_hbm, four_in), copy(mlp_hbm, mlp_in), copy(sums_hbm, sums_in)]
    come += [(copy(layer_in.at[p], layer_s.at[p]), layer_s.at[p], layer_ref.at[p]) for p in parts]
    copies = []

    def leave(some):
        for arrived, mid, dst in some:
            arrived.wait()
            copies.append(copy(mid, dst))

    leave(come[0:4])
    for c in small:
        c.wait()
    inner = q_ref.shape[1]
    for j, ref in enumerate((q_ref, k_ref, v_ref, o_ref)):
        for pair in range(inner // PAIR):
            lane = (pair * 4 + j) * PAIR
            ref[:, pair * PAIR : pair * PAIR + PAIR] = four_in[:, lane : lane + PAIR]
    units = gate_ref.shape[1]
    down_ref[...] = mlp_in[:, 0:units]
    gate_ref[...] = mlp_in[:, units : 2 * units]
    up_ref[...] = four_in[:, 4 * inner : 4 * inner + units]
    leave(come[4:8])
    share, width = gain_ref.shape[1], sums_in.shape[1]
    row = lax.broadcasted_iota(jnp.int32, (width, share), 0)
    lane = lax.broadcasted_iota(jnp.int32, (width, share), 1)
    pick = jnp.where(row == lane + lax.axis_index("dp") * share, 1.0, 0.0)
    own = jnp.dot(
        sums_in[...], pick, precision=lax.Precision.HIGHEST, preferred_element_type=F32
    )
    gain_ref[...] = own[0:1]
    gain2_ref[...] = own[1:2]
    fall_ref[...] = own[3 : 3 + fall_ref.shape[0]]
    square = lambda row, at: sums_in[row : row + 1, at * PAIR : at * PAIR + NBUCKET]
    squares = jnp.concatenate([square(9, 0), square(9, 1), square(2, 0)], axis=0)
    rms_ref[...] = jnp.sqrt(squares / (square(9, 2) * width))
    bias_ref[...] = sums_in[10:11, 0 : bias_ref.shape[1]]
    for c in copies:
        c.wait()


def finish(grad, layer, out_share, share, mlp_share, sums, heads):
    rows, inner = out_share.shape
    units = mlp_share.shape[1] // 2
    return pl.pallas_call(
        finish_kernel,
        out_shape=[
            struct(*grad.shape), struct(*layer.shape, t=layer.dtype), *[struct(rows, inner)] * 5,
            *[struct(rows, units)] * 3, struct(1, rows), struct(1, rows), struct(heads, rows),
            struct(3, NBUCKET), struct(1, heads),
        ],
        in_specs=[HBM] * 6,
        out_specs=[HBM, HBM] + [VMEM] * 13,
        scratch_shapes=[pltpu.VMEM(a.shape, a.dtype) for a in (grad, layer, share, mlp_share, sums)]
        + [pltpu.SemaphoreType.DMA((20,))],
        compiler_params=pltpu.CompilerParams(vmem_limit_bytes=60 << 20),
    )(grad, layer, out_share, share, mlp_share, sums)


def per_device(
    tokens, lengths, buckets, out_cotangent, gain_attn, w_query, w_key, w_value, w_outgate,
    w_forget, b_forget, w_out, gain_mlp, w_gate, w_up, w_down,
):
    x, cotangent = tokens[0], out_cotangent[0]
    heads = w_forget.shape[1]
    gain_in, gain_mid = gain_attn[None], gain_mlp[None]
    weights = (w_query, w_key, w_value, w_outgate, w_forget.T)
    (
        low, qn, kn, value, sig, attended, stat, decay, gated, w_full,
        middle, mid_low, grad_rows, gate, up, hidden, mlp_local, squares,
    ) = forward(
        x, cotangent, lengths, gain_in, *weights, b_forget[None], w_out, gain_mid, w_gate, w_up, w_down, 0
    )
    mid_local, g_down, g_gate, g_up, layer_own, mlp_square = mlp_backward(
        lengths, grad_rows, mid_low, gate, up, hidden, w_gate, w_up, w_down, mlp_local, middle, 1
    )
    grad_own, gg, mlp_share, mlp_gain = reduce_middle(
        mid_local, middle, grad_rows, gain_mid, w_full, [g_down, g_gate],
        ((0, 0), (0, 1), (1, 0), (1, 1)), 2,
    )
    in_local, g_four, g_out, g_fall, bias, layer_out = backward_attention(
        lengths, gg, low, qn, kn, value, sig, attended, stat, decay, *weights, grad_own, gated,
        layer_own, 3,
    )
    small = (mlp_gain, g_fall, squares, mlp_square, bias, lengths, buckets)
    input_grad, out_share, share, sums = reduce_input(
        in_local, x, grad_own, gain_in, small, [g_out, g_four, g_up],
        ((0, 0), (0, 1), (0, 2), (1, 0), (1, 1), (1, 2), (2, 0), (2, 1)), 4,
    )
    (
        input_grad, layer_out, g_out, g_query, g_key, g_value, g_outgate, g_gate, g_up, g_down,
        g_gain, g_gain_mid, g_fall, rms, bias,
    ) = finish(input_grad, layer_out, out_share, share, mlp_share, sums, heads)
    return (
        layer_out[None],
        input_grad[None],
        g_gain[0],
        g_query,
        g_key,
        g_value,
        g_outgate,
        g_fall.T,
        bias[0],
        g_out.T,
        g_gain_mid[0],
        g_gate,
        g_up,
        g_down.T,
        rms,
    )


def solution(mesh):
    placed = (
        P("dp", None, None),
        P("dp"),
        P("dp"),
        P("dp", None, None),
        P(),
        P(None, "mp"),
        P(None, "mp"),
        P(None, "mp"),
        P(None, "mp"),
        P(None, "mp"),
        P("mp"),
        P("mp", None),
        P(),
        P(None, "mp"),
        P(None, "mp"),
        P("mp", None),
    )
    return jax.shard_map(
        per_device,
        mesh=mesh,
        in_specs=placed,
        out_specs=(
            P("dp", None, None),
            P("dp", None, None),
            P("dp"),
            P("dp", "mp"),
            P("dp", "mp"),
            P("dp", "mp"),
            P("dp", "mp"),
            P("dp", "mp"),
            P("mp"),
            P("mp", "dp"),
            P("dp"),
            P("dp", "mp"),
            P("dp", "mp"),
            P("mp", "dp"),
            P(),
        ),
        check_vma=False,
    )
```

```python
import functools

import jax
import jax.numpy as jnp
from jax import lax
from jax.experimental import pallas as pl
from jax.experimental.pallas import tpu as pltpu
from jax.sharding import PartitionSpec as P

NBUCKET = 4


EPSILON = 1e-06


MESH = pl.DeviceIdType.MESH
F32 = jnp.float32
Y = 4
STEP = 512
HBM = pl.BlockSpec(memory_space=pl.ANY)
VMEM = pl.BlockSpec(memory_space=pltpu.VMEM)
STEPS = ("oR", "oL", "iR", "iL", "dR", "dL", "gRa", "gRb", "gLa", "gLb", "fR", "fL")


def rows_of(ref, start, count):
    return ref.at[pl.ds(pl.multiple_of(start, 8), count)]


def meet(devices):
    barrier = pltpu.get_barrier_semaphore()
    for device in devices:
        pl.semaphore_signal(barrier, inc=1, device_id=device, device_id_type=MESH)
    pl.semaphore_wait(barrier, len(devices))


def link(src, dst, ssem, rsem, at, device):
    return pltpu.make_async_remote_copy(
        src_ref=src,
        dst_ref=dst,
        send_sem=ssem.at[at],
        recv_sem=rsem.at[at],
        device_id=device,
        device_id_type=MESH,
    )


def push(*args):
    copy = link(*args)
    copy.start()
    return copy


class YRing:
    def __init__(self, rows, waves, ssem, rsem):
        self.sems = (ssem, rsem)
        self.dp, self.me = lax.axis_index("dp"), lax.axis_index("mp")
        self.right, self.left = lax.rem(self.me + 1, Y), lax.rem(self.me + 3, Y)
        self.far = lax.rem(self.me + 2, Y)
        self.quarter, self.half = rows // Y, rows // Y // 2
        self.tall = self.half // waves
        self.sent = {}

    def neighbours(self):
        return [(self.dp, self.right), (self.dp, self.left)]

    def send(self, name, wave, src, dst, to):
        kind, index = divmod(STEPS.index(name), 6)
        at = kind * 12 + wave * 6 + index
        self.sent[name, wave] = push(src, dst, *self.sems, at, (self.dp, to))

    def rows(self, x, owner, part, wave):
        return rows_of(x, owner * self.quarter + part * self.half + wave * self.tall, self.tall)

    def fetch(self, x, held, own, sem):
        self.loads = [
            load(rows_of(x, self.right * self.quarter, self.half), held.at[0], sem.at[0]),
            load(rows_of(x, self.left * self.quarter + self.half, self.half), held.at[1], sem.at[1]),
            load(rows_of(x, self.me * self.quarter, self.quarter), own, sem.at[2]),
        ]

    def start(self, x, opp, nbr, wave):
        w = slice(wave * self.tall, wave * self.tall + self.tall)
        low = slice(self.half + wave * self.tall, self.half + wave * self.tall + self.tall)
        self.send("oR", wave, self.rows(x, self.far, 0, wave), opp.at[0, w], self.right)
        self.send("oL", wave, self.rows(x, self.far, 1, wave), opp.at[1, w], self.left)
        self.send("iR", wave, self.rows(x, self.right, 1, wave), nbr.at[0, low], self.right)
        self.send("iL", wave, self.rows(x, self.left, 0, wave), nbr.at[1, w], self.left)

    def relay(self, opp, nbr, held, wave):
        w = slice(wave * self.tall, wave * self.tall + self.tall)
        low = slice(self.half + wave * self.tall, self.half + wave * self.tall + self.tall)
        for part, (come, go, into, to) in enumerate(
            (("oR", "dR", nbr.at[0, w], self.right), ("oL", "dL", nbr.at[1, low], self.left))
        ):
            self.sent[come, wave].wait_recv()
            if wave == 0:
                self.loads[part].wait()
            held[part, w] = held[part, w] + opp[part, w]
            self.send(go, wave, held.at[part, w], into, to)

    def collect(self, own, nbr, part, wave):
        if part == 0 and wave == 0:
            self.loads[2].wait()
        for name in (("dR", "iL"), ("iR", "dL"))[part]:
            self.sent[name, wave].wait_recv()
        start = part * self.half + wave * self.tall
        at = slice(start, start + self.tall)
        return at, own[at, :] + nbr[0, at] + nbr[1, at]

    def spread(self, part, wave, own, out):
        tag, into = "ab"[part], self.rows(out, self.me, part, wave)
        start = part * self.half + wave * self.tall
        mine = own.at[start : start + self.tall]
        self.send("gR" + tag, wave, mine, into, self.right)
        self.send("gL" + tag, wave, mine, into, self.left)

    def forward(self, wave, out):
        for come, go, owner, part, to in (
            ("gRa", "fR", self.left, 0, self.right),
            ("gLb", "fL", self.right, 1, self.left),
        ):
            self.sent[come, wave].wait_recv()
            block = self.rows(out, owner, part, wave)
            self.send(go, wave, block, block, to)

    def arrive(self, wave):
        for name in ("gRb", "gLa", "fR", "fL"):
            self.sent[name, wave].wait_recv()

    def finish(self):
        for copy in self.sent.values():
            copy.wait_send()


def ring_scratch(quarter, columns):
    return [
        pltpu.VMEM((2, quarter // 2, columns), F32),
        pltpu.VMEM((2, quarter, columns), F32),
        pltpu.VMEM((2, quarter // 2, columns), F32),
    ]


def sems(*counts):
    return [pltpu.SemaphoreType.DMA((n,)) for n in counts for _ in (0, 1)]


class Place:
    def __init__(self):
        self.dp, self.my = lax.axis_index("dp"), lax.axis_index("mp")
        c, z, x = lax.rem(self.dp, 2), lax.rem(self.dp // 2, 4), self.dp // 8
        self.c, self.sib, self.chip = c, self.dp + 1 - 2 * c, x * 4 + z
        self.st1, self.st2 = 4 - 3 * c, 1 + 3 * c
        self.p1, self.p2 = x + c * (z - x), z + c * (x - z)
        step = lambda p, by: lax.rem(p + by, 4)
        self.r1, self.l1, self.o1 = (step(self.p1, by) for by in (1, 3, 2))
        self.r2, self.l2, self.o2 = (step(self.p2, by) for by in (1, 3, 2))

    def device(self, a, b):
        return ((a * self.st1 + b * self.st2) * 2 + self.c, self.my)

    def peers(self):
        return [
            (self.sib, self.my),
            self.device(self.r1, self.p2),
            self.device(self.l1, self.p2),
            self.device(self.p1, self.r2),
            self.device(self.p1, self.l2),
        ]


class ScatterSum:
    def __init__(self, here, sources, own, other, near, last, asem, bsem, lsem, ssem, rsem):
        self.here, self.sources = here, sources
        self.own, self.other, self.near, self.last = own, other, near, last
        self.asem, self.bsem, self.lsem, self.ssem, self.rsem = asem, bsem, lsem, ssem, rsem
        self.n = own.shape[0]
        self.sibling, *to = here.peers()
        self.to = (to[0:2], to[2:4])

    def message(self, name, k, stage):
        at = (k * 2 + stage) * 6 + STEPS.index(name)
        device = self.to[stage][0 if name[1] == "R" else 1]
        here, own = self.here, self.own.at[k]
        if stage:
            own, into, cut = own.at[here.p1], self.last.at[k], (slice(0, 24), slice(24, 48))
            far, right, left = here.o2, here.r2, here.l2
        else:
            into, cut = self.near.at[k], (slice(0, 2), slice(2, 4))
            far, right, left = here.o1, here.r1, here.l1
        row, part, slot = {
            "oR": (far, 0, 0),
            "oL": (far, 1, 1),
            "iR": (right, 1, 3),
            "iL": (left, 0, 4),
            "dR": (right, 0, 2),
            "dL": (left, 1, 5),
        }[name]
        return link(own.at[row, cut[part]], into.at[slot], self.ssem, self.rsem, at, device)

    def whole(self, k):
        own, other = self.own.at[k], self.other.at[k]
        return link(own, other, self.asem, self.bsem, k, self.sibling)

    def exchange(self, k):
        here = self.here
        ref, start, width = self.sources[k]

        def source(block):
            return ref.at[pl.ds(pl.multiple_of(block * 48, 16), 48), pl.ds(start, width)]

        def cross(i, carry):
            a, b = i // 4, lax.rem(i, 4)
            block = source((a * here.st2 + b * here.st1) * 2 + 1 - here.c)
            push(block, self.other.at[k, a, b], self.asem, self.bsem, k, self.sibling)
            return carry

        def fetch(i, carry):
            a, b = i // 4, lax.rem(i, 4)
            block = source((a * here.st1 + b * here.st2) * 2 + here.c)
            pltpu.make_async_copy(block, self.own.at[k, a, b], self.lsem.at[k]).start()
            return carry

        lax.fori_loop(0, 16, cross, 0)
        lax.fori_loop(0, 16, fetch, 0)

    def first(self, k):
        here, own, other = self.here, self.own, self.other
        pltpu.make_async_copy(own.at[k], own.at[k], self.lsem.at[k]).wait()
        self.whole(k).wait_recv()

        def add(p):
            def body(b, carry):
                own[k, p, b] = own[k, p, b] + other[k, p, b]
                return carry

            lax.fori_loop(0, 4, body, 0)

        add(here.o1)
        self.message("oR", k, 0).start()
        self.message("oL", k, 0).start()
        add(here.r1)
        self.message("iR", k, 0).start()
        add(here.l1)
        self.message("iL", k, 0).start()
        add(here.p1)

    def first_relay(self, k):
        here, own, near = self.here, self.own, self.near

        def add(p, at, slot):
            def body(b, carry):
                own[k, p, at + b] = own[k, p, at + b] + near[k, slot, b]
                return carry

            lax.fori_loop(0, 2, body, 0)

        self.message("oR", k, 0).wait_recv()
        add(here.r1, 0, 0)
        self.message("dR", k, 0).start()
        self.message("oL", k, 0).wait_recv()
        add(here.l1, 2, 1)
        self.message("dL", k, 0).start()

    def second(self, k):
        here, own, near = self.here, self.own, self.near
        for name in ("iR", "dR", "iL", "dL"):
            self.message(name, k, 0).wait_recv()

        def add(p):
            h, b = p // 2, lax.rem(p, 2)
            own[k, here.p1, p] = own[k, here.p1, p] + near[k, 2 + h, b] + near[k, 4 + h, b]

        add(here.o2)
        self.message("oR", k, 1).start()
        self.message("oL", k, 1).start()
        add(here.r2)
        self.message("iR", k, 1).start()
        add(here.l2)
        self.message("iL", k, 1).start()
        add(here.p2)

    def second_relay(self, k):
        here, own, last = self.here, self.own, self.last
        self.message("oR", k, 1).wait_recv()
        own[k, here.p1, here.r2, 0:24] = own[k, here.p1, here.r2, 0:24] + last[k, 0]
        self.message("dR", k, 1).start()
        self.message("oL", k, 1).wait_recv()
        own[k, here.p1, here.l2, 24:48] = own[k, here.p1, here.l2, 24:48] + last[k, 1]
        self.message("dL", k, 1).start()

    def result(self, k, out, at):
        here, own, last = self.here, self.own, self.last
        width = own.shape[4]
        for name in ("iR", "dR", "iL", "dL"):
            self.message(name, k, 1).wait_recv()
        columns = pl.ds(pl.multiple_of(at * width, 128), width)
        out[0:24, columns] = own[k, here.p1, here.p2, 0:24] + last[k, 2] + last[k, 4]
        out[24:48, columns] = own[k, here.p1, here.p2, 24:48] + last[k, 3] + last[k, 5]

    def sent(self, k):
        self.whole(k).wait_send()
        for stage in (0, 1):
            for name in STEPS[:6]:
                self.message(name, k, stage).wait_send()


def each(low, high, step):
    def body(k, carry):
        step(k)
        return carry

    lax.fori_loop(low, high, body, 0)


class SmallSum:
    def __init__(self, here, bufs, landed, ssem, rsem):
        self.bufs, self.landed, self.ssem, self.rsem = bufs, landed, ssem, rsem
        turn = lambda p, by: lax.rem(p + by, 4)
        self.stages = [
            [(here.sib, here.my)],
            [here.device(turn(here.p1, by), here.p2) for by in (1, 2, 3)],
            [here.device(here.p1, turn(here.p2, by)) for by in (1, 2, 3)],
            [(here.dp, turn(here.my, by)) for by in (1, 2, 3)],
        ]
        self.far = [self.stages[1][1], self.stages[2][1], self.stages[3][1]]
        self.sent = []

    def send(self, stage):
        for to in self.stages[stage]:
            at = len(self.sent)
            copy = push(self.bufs.at[stage], self.landed.at[at], self.ssem, self.rsem, at, to)
            self.sent.append(copy)

    def take(self, stage):
        value, count = self.bufs[stage], len(self.stages[stage])
        for at in range(len(self.sent) - count, len(self.sent)):
            self.sent[at].wait_recv()
            value = value + self.landed[at]
        self.bufs[stage + 1] = value

    def finish(self):
        for copy in self.sent:
            copy.wait_send()


def scatter_scratch(n, w):
    return [
        pltpu.VMEM((n, 4, 4, 48, w), F32),
        pltpu.VMEM((n, 4, 4, 48, w), F32),
        pltpu.VMEM((n, 6, 2, 48, w), F32),
        pltpu.VMEM((n, 6, 24, w), F32),
        pltpu.SemaphoreType.DMA((n,)),
        pltpu.SemaphoreType.DMA((n,)),
        pltpu.SemaphoreType.DMA((n,)),
        pltpu.SemaphoreType.DMA((12 * n,)),
        pltpu.SemaphoreType.DMA((12 * n,)),
    ]


def scatter_sources(refs, pieces):
    return [(refs[which], at * STEP, STEP) for which, at in pieces]


def norm_back(value, source, base, gain):
    source = source.astype(F32)
    r = lax.rsqrt(jnp.mean(source * source, axis=1, keepdims=True) + EPSILON)
    n = source * r
    e = value * gain.astype(F32)
    inner = jnp.mean(e * n, axis=1, keepdims=True)
    return base.astype(F32) + r * (e - n * inner), jnp.sum(value * n, axis=0, keepdims=True)


def load(ref, scratch, sem):
    copy = pltpu.make_async_copy(ref, scratch, sem)
    copy.start()
    return copy


def middle_kernel(pieces, count, x_ref, source_ref, base_ref, gain_ref, w_ref, *refs):
    ins, refs = refs[:count], refs[count:]
    grad_ref, gg_ref, share_ref, sums_ref = refs[:4]
    source_s, base_s, w_s, opp, nbr, held, own_s, blocks, csem, *sem = refs[4:17]
    here, ring = Place(), YRing(x_ref.shape[0], 2, *sem[0:2])
    total = ScatterSum(here, scatter_sources(ins, pieces), *refs[17:])
    n = total.n
    far = (ring.dp, ring.far)
    meet(ring.neighbours() + [far] + here.peers())
    ring.start(x_ref, opp, nbr, 0)
    q, h = ring.quarter, ring.half
    ring.fetch(x_ref, held, own_s, csem)
    for k in range(n):
        total.exchange(k)
    loads = [
        load(rows_of(source_ref, ring.me * q, q), source_s, csem.at[3]),
        load(rows_of(base_ref, ring.me * q, q), base_s, csem.at[4]),
        load(w_ref, w_s, csem.at[5]),
    ]
    ring.relay(opp, nbr, held, 0)
    ring.start(x_ref, opp, nbr, 1)
    each(0, n, total.first)
    each(0, n - 2, total.first_relay)
    ring.relay(opp, nbr, held, 1)
    for copy in loads:
        copy.wait()
    sums, swaps, keeps = 0.0, [], []
    inner = gg_ref.shape[1]
    for wave in (0, 1):
        for part in (0, 1):
            at, value = ring.collect(own_s, nbr, part, wave)
            value, more = norm_back(value, source_s[at, :], base_s[at, :], gain_ref[...])
            grad_ref[at, :] = value
            sums = sums + more
        tall = ring.tall
        low = jnp.concatenate(
            [grad_ref[part * h + wave * tall : part * h + wave * tall + tall, :] for part in (0, 1)], axis=0
        ).astype(jnp.bfloat16)
        for j, by in enumerate((2, 1, 3, 0)):
            to = lax.rem(ring.me + by, Y)
            blocks[wave, j] = mm_t(low, rows_of(w_s, to * inner, inner)[...])
            for part in (0, 1):
                src = blocks.at[wave, j, part * tall : part * tall + tall]
                into = rows_of(gg_ref, ring.me * q + part * h + wave * tall, tall)
                if by:
                    at = (wave * 3 + j) * 2 + part
                    swaps.append(push(src, into, *sem[2:4], at, (ring.dp, to)))
                else:
                    keeps.append(load(src, into, csem.at[6 + wave * 2 + part]))
        if wave == 0:
            each(n - 2, n, total.first_relay)
    sums_ref[...] = sums
    each(0, n, total.second)
    each(0, n, total.second_relay)
    each(0, n, lambda k: total.result(k, share_ref, k))
    for copy in swaps:
        copy.wait_recv()
    for copy in keeps:
        copy.wait()
    for copy in swaps:
        copy.wait_send()
    ring.finish()
    each(0, n, total.sent)


def reduce_middle(partial, source, base, gain, w_full, grads, pieces, call_id):
    n = len(pieces)
    hbm, vmem = pl.BlockSpec(memory_space=pl.ANY), pl.BlockSpec(memory_space=pltpu.VMEM)
    rows, columns = partial.shape
    quarter, inner = rows // Y, w_full.shape[0] // Y
    return pl.pallas_call(
        functools.partial(middle_kernel, pieces, len(grads)),
        out_shape=[
            jax.ShapeDtypeStruct((quarter, columns), F32),
            jax.ShapeDtypeStruct((rows, inner), F32),
            jax.ShapeDtypeStruct((48, n * STEP), F32),
            jax.ShapeDtypeStruct((1, columns), F32),
        ],
        in_specs=[hbm, hbm, hbm, vmem, hbm] + [hbm] * len(grads),
        out_specs=[vmem, hbm, vmem, vmem],
        scratch_shapes=[
            pltpu.VMEM((quarter, columns), source.dtype),
            pltpu.VMEM((quarter, columns), base.dtype),
            pltpu.VMEM(w_full.shape, w_full.dtype),
        ]
        + ring_scratch(quarter, columns)
        + [
            pltpu.VMEM((quarter, columns), F32),
            pltpu.VMEM((2, 4, quarter // 2, inner), F32),
            pltpu.SemaphoreType.DMA((10,)),
        ]
        + sems(12, 12)
        + scatter_scratch(n, STEP),
        compiler_params=pltpu.CompilerParams(
            collective_id=call_id, has_side_effects=True, vmem_limit_bytes=56 << 20
        ),
    )(partial, source, base, gain, w_full, *grads)


def input_kernel(
    pieces, count, x_ref, source_ref, base_ref, gain_ref, other_ref, fall_ref, square_ref, more_ref,
    bias_ref, length_ref, bucket_ref, *refs
):
    ins, refs = refs[:count], refs[count:]
    out_ref, out_share_ref, share_ref, sums_ref = refs[:4]
    source_s, opp, nbr, held, own_s, mine_s, wide_s, landed, csem, *sem = refs[4:17]
    bufs, arrived, asem, bsem = refs[17:21]
    here, ring = Place(), YRing(x_ref.shape[0], 1, *sem[0:2])
    total = ScatterSum(here, scatter_sources(ins, pieces), *refs[21:])
    tiny = SmallSum(here, bufs, arrived, asem, bsem)
    n, first = total.n, wide_s.shape[1] // STEP
    meet(ring.neighbours() + here.peers() + tiny.far)
    ring.start(x_ref, opp, nbr, 0)
    q, h = ring.quarter, ring.half
    ring.fetch(x_ref, held, own_s, csem)
    copy = load(rows_of(source_ref, ring.me * q, q), source_s, csem.at[3])
    for k in range(n):
        total.exchange(k)
    each(0, n // 2, total.first)
    ring.relay(opp, nbr, held, 0)
    each(n // 2, n, total.first)
    each(0, n - 2, total.first_relay)
    copy.wait()
    sums = 0.0
    for wave in (0,):
        for part in (0, 1):
            at, value = ring.collect(own_s, nbr, part, wave)
            value, more = norm_back(value, source_s[at, :], base_ref[at, :], gain_ref[...])
            mine_s[at, :] = value
            ring.spread(part, wave, mine_s, out_ref)
            sums = sums + more
    kept = load(mine_s, rows_of(out_ref, ring.me * q, q), csem.at[4])
    bufs[0, 0:1, :] = sums
    bufs[0, 1:2, :] = other_ref[...]
    bufs[0, 8:16, :] = jnp.zeros_like(bufs[0, 8:16, :])
    bufs[0, 2:3, :] = jnp.zeros((1, sums_ref.shape[1]), F32)
    bufs[0, 3:9, :] = fall_ref[0:6, :]
    lane = lax.broadcasted_iota(jnp.int32, (1, PAIR), 1)
    both = jnp.sum(square_ref[...], axis=1, keepdims=True)
    in_bucket = lambda value: jnp.where(lane == bucket_ref[0], value, 0.0)
    bufs[0, 2:3, 0:PAIR] = in_bucket(jnp.sum(more_ref[...], axis=1, keepdims=True))
    for at, value in enumerate((both[0:1], both[1:2], length_ref[0].astype(F32))):
        bufs[0, 9:10, at * PAIR : at * PAIR + PAIR] = in_bucket(value)
    diagonal = lax.broadcasted_iota(jnp.int32, bias_ref.shape, 0) == lax.broadcasted_iota(
        jnp.int32, bias_ref.shape, 1
    )
    bufs[0, 10:11, 0:PAIR] = jnp.sum(jnp.where(diagonal, bias_ref[...], 0.0), axis=0, keepdims=True)
    tiny.send(0)
    each(n - 2, n, total.first_relay)
    each(0, n, total.second)
    ring.forward(0, out_ref)
    tiny.take(0)
    tiny.send(1)
    each(0, n, total.second_relay)
    tiny.take(1)
    tiny.send(2)
    each(0, first, lambda k: total.result(k, wide_s, k))
    inner = landed.shape[2]
    swaps = []
    for j, by in enumerate((2, 1, 3)):
        to = lax.rem(ring.me + by, Y)
        columns = pl.ds(pl.multiple_of(to * inner, 128), inner)
        swaps.append(push(wide_s.at[:, columns], landed.at[j], *sem[2:4], j, (ring.dp, to)))
    each(first, n, lambda k: total.result(k, share_ref, k - first))
    tiny.take(2)
    tiny.send(3)
    own = wide_s[:, pl.ds(pl.multiple_of(ring.me * inner, 128), inner)]
    for j, copy in enumerate(swaps):
        copy.wait_recv()
        own = own + landed[j]
    out_share_ref[...] = own
    tiny.take(3)
    rows = lax.broadcasted_iota(jnp.int32, sums_ref.shape, 0)
    sums_ref[...] = jnp.where(rows < 3, bufs[4], bufs[3])
    ring.arrive(0)
    kept.wait()
    for copy in swaps:
        copy.wait_send()
    tiny.finish()
    ring.finish()
    each(0, n, total.sent)


def reduce_input(partial, source, base, gain, small, grads, pieces, call_id):
    n = len(pieces)
    smem = pl.BlockSpec(memory_space=pltpu.SMEM)
    hbm, vmem = pl.BlockSpec(memory_space=pl.ANY), pl.BlockSpec(memory_space=pltpu.VMEM)
    rows, columns = partial.shape
    quarter, inner = rows // Y, grads[0].shape[1] // Y
    wide = grads[0].shape[1]
    shares = n * STEP - wide
    return pl.pallas_call(
        functools.partial(input_kernel, pieces, len(grads)),
        out_shape=[
            jax.ShapeDtypeStruct(partial.shape, F32),
            jax.ShapeDtypeStruct((48, inner), F32),
            jax.ShapeDtypeStruct((48, shares), F32),
            jax.ShapeDtypeStruct((16, columns), F32),
        ],
        in_specs=[hbm, hbm, vmem, vmem] + [vmem] * 5 + [smem] * 2 + [hbm] * len(grads),
        out_specs=[hbm] + [vmem] * 3,
        scratch_shapes=[pltpu.VMEM((quarter, columns), source.dtype)]
        + ring_scratch(quarter, columns)
        + [
            pltpu.VMEM((quarter, columns), F32),
            pltpu.VMEM((quarter, columns), F32),
            pltpu.VMEM((48, wide), F32),
            pltpu.VMEM((3, 48, inner), F32),
            pltpu.SemaphoreType.DMA((5,)),
        ]
        + sems(24, 3)
        + [pltpu.VMEM((5, 16, columns), F32), pltpu.VMEM((10, 16, columns), F32)]
        + sems(10)
        + scatter_scratch(n, STEP),
        compiler_params=pltpu.CompilerParams(
            collective_id=call_id, has_side_effects=True, vmem_limit_bytes=56 << 20
        ),
    )(partial, source, base, gain, *small, *grads)


HEAD = 64
PAIR = 128
NEG = -1e30


def rows_at(i, size):
    return pl.ds(pl.multiple_of(i * size, size), size)


def lane_is(shape, index):
    return lax.broadcasted_iota(jnp.int32, shape, len(shape) - 1) == index


def first_head(shape):
    return lax.broadcasted_iota(jnp.int32, shape, len(shape) - 1) < HEAD


def halves_mean(values):
    first = first_head(values.shape)
    low = jnp.sum(jnp.where(first, values, 0.0), axis=1, keepdims=True) * (1.0 / HEAD)
    high = jnp.sum(jnp.where(first, 0.0, values), axis=1, keepdims=True) * (1.0 / HEAD)
    return low, high


def one_row(ref, index):
    rows = ref[...]
    picked = lax.broadcasted_iota(jnp.int32, rows.shape, 0) == index
    return jnp.sum(jnp.where(picked, rows, 0.0), axis=0, keepdims=True)


def running_sum(values, backward=False):
    count = values.shape[1]
    at = lax.broadcasted_iota(jnp.int32, values.shape, 1)
    shift = 1
    while shift < count:
        if backward:
            moved = jnp.where(at < count - shift, pltpu.roll(values, count - shift, 1), 0.0)
        else:
            moved = jnp.where(at >= shift, pltpu.roll(values, shift, 1), 0.0)
        values = values + moved
        shift *= 2
    return values


def mm(left, right):
    return jnp.dot(left, right, preferred_element_type=F32)


def mm_t(left, right):
    return lax.dot_general(left, right, (((1,), (1,)), ((), ())), preferred_element_type=F32)


def t_mm(left, right):
    return lax.dot_general(left, right, (((0,), (0,)), ((), ())), preferred_element_type=F32)


def whole(shape):
    return pl.BlockSpec(shape, lambda *_: (0,) * len(shape), pipeline_mode=pl.Buffered(1))


def struct(*shape, t=F32):
    return jax.ShapeDtypeStruct(shape, t)


def local_call(kernel, grid, in_specs, out_specs, out_shape, scratch, limit, flops, moved, call_id=None):
    return pl.pallas_call(
        kernel,
        grid_spec=pltpu.PrefetchScalarGridSpec(
            num_scalar_prefetch=1,
            grid=(grid,),
            in_specs=in_specs,
            out_specs=out_specs,
            scratch_shapes=scratch,
        ),
        out_shape=out_shape,
        compiler_params=pltpu.CompilerParams(
            vmem_limit_bytes=limit << 20,
            collective_id=call_id,
            has_side_effects=call_id is not None,
        ),
        cost_estimate=pl.CostEstimate(
            flops=flops * 10**9, bytes_accessed=moved * 10**6, transcendentals=4 * 10**6
        ),
    )


def forward_kernel(
    length_ref, x_ref, gain_ref, wq_ref, wk_ref, wv_ref, wo_ref, wf_ref, bf_ref, w_ref,
    gain2_ref, cot_in, wg_in, wu_in, wd_in,
    low_out, qn_ref, kn_ref, v_ref, sig_ref, att_ref, stat_ref, decay_ref, gated_out, full_out,
    mid_out, normed_out, grad_out, gate_out, up_out, hid_out, mlp_out, sums_ref,
    top_s, row_s, q_s, k_s, w_s, pre_s, gs, ws, wf_s, bf_s, low_ref, gated_ref, full_ref,
    wg_s, wu_s, wd_s, cot_s, mid_s, normed_s, grad_s, gate_s, up_s, hid_s, mlp_s, osem, *sem,
):
    step = pl.program_id(0)
    seq = x_ref.shape[0]
    length = length_ref[0]
    here = Place()
    me, right, left, far = (lax.rem(here.my + by, Y) for by in (0, 1, 3, 2))
    sibling, right1, left1, right2, left2 = here.peers()
    c, p1, p2, half, quarter = here.c, here.p1, here.p2, seq // 2, seq // Y
    mine = ws.at[c, p2, p1, me]
    cross_order = (p2, here.l2, here.r2, here.o2)

    def plane(j):
        return link(mine, mine, *sem[2:4], j, (here.dp, (right, far, left)[j]))

    def torus(stage, j):
        if stage == 0:
            at, spots, to = (lambda p: ws.at[c, p2, p]), (p1, here.l1, here.r1), (right1, left1)
        else:
            at, spots, to = (lambda p: ws.at[c, p]), (p2, here.l2, here.r2), (right2, left2)
        spot, part, side = ((0, 0, 0), (0, 1, 0), (0, 0, 1), (0, 1, 1), (1, 0, 0), (2, 1, 1))[j]
        piece = at(spots[spot]).at[2 * part : 2 * part + 2]
        return link(piece, piece, *sem[4 + 2 * stage : 6 + 2 * stage], j, to[side])

    def cross(j):
        piece = ws.at[c, cross_order[j]]
        return link(piece, piece, *sem[8:10], j, sibling)

    def gate(pair, j):
        owner, part, to = (
            (me, 0, right), (me, 1, right), (me, 0, left), (me, 1, left), (left, 0, right), (right, 1, left)
        )[j]
        piece = gs.at[pair, owner, part * half : part * half + half]
        return link(piece, piece, *sem[0:2], pair * 6 + j, (here.dp, to))

    def hand_on(pair, come, go):
        gate(pair, come).wait_recv()
        gate(pair, go).start()

    def flush(j):
        src, dst = (
            (low_ref, low_out),
            (full_ref, full_out),
            (rows_of(gated_ref, me * quarter, quarter), gated_out),
            (wg_in, wg_s),
            (wu_in, wu_s),
            (wd_in, wd_s),
        )[j]
        return pltpu.make_async_copy(src, dst, osem.at[j])

    def leave(j, chunk):
        src, dst = (
            (mid_s, mid_out), (normed_s, normed_out), (grad_s, grad_out), (gate_s, gate_out),
            (up_s, up_out), (hid_s, hid_out), (mlp_s, mlp_out),
        )[j]
        return pltpu.make_async_copy(src, dst.at[rows_at(chunk, half)], osem.at[6 + j])

    def come(chunk):
        return pltpu.make_async_copy(cot_in.at[rows_at(chunk, half)], cot_s, osem.at[13])

    def pass_on(make):
        make(0).wait_recv()
        make(4).start()
        make(3).wait_recv()
        make(5).start()

    def arrived(make):
        for j in (1, 2, 4, 5):
            make(j).wait_recv()

    @pl.when(step == 0)
    def _():
        tall, wide = ws.shape[4], ws.shape[5]
        two = w_ref[
            pl.ds(pl.multiple_of(here.chip // 2 * (2 * tall), 16), 2 * tall),
            pl.ds(pl.multiple_of(c * wide, 128), wide),
        ].astype(F32)
        mine[...] = jnp.where(lax.rem(here.chip, 2) == 0, two[0:tall], two[tall:])
        meet([(here.dp, right), (here.dp, left), (here.dp, far)] + here.peers())
        for j in range(3):
            plane(j).start()

    @pl.when(step == 0)
    def _():
        def norm(i, carry):
            at = rows_at(i, 128)
            x = x_ref[at, :].astype(F32)
            r = lax.rsqrt(jnp.mean(x * x, axis=1, keepdims=True) + EPSILON)
            low_ref[at, :] = (x * r * gain_ref[...].astype(F32)).astype(jnp.bfloat16)
            return carry

        lax.fori_loop(0, seq // 128, norm, 0)
        flush(0).start()
        heads = wf_ref.shape[0]
        wf_s[...] = jnp.zeros_like(wf_s)
        wf_s[0:heads, :] = wf_ref[...]
        bf_s[...] = jnp.zeros_like(bf_s)
        bf_s[:, 0:heads] = bf_ref[...].astype(F32)
        pre = mm_t(wf_s[...], low_ref[...])[0:8] + jnp.broadcast_to(bf_s[...], (PAIR, PAIR)).T[0:8, 0:1]
        fall = jnp.minimum(pre, 0.0) - jnp.log1p(jnp.exp(-jnp.abs(pre)))
        decay = running_sum(fall)
        column = lax.broadcasted_iota(jnp.int32, decay.shape, 1)
        decay_ref[0] = decay
        decay_ref[1] = jax.nn.sigmoid(-pre)
        row_s[...] = jnp.where(column < length, decay, -NEG)
        final = jnp.sum(jnp.where(column == length - 1, decay, 0.0), axis=1, keepdims=True)
        top = jnp.where(column < length, decay, final)
        top_s[...] = jnp.concatenate([top, jnp.zeros((PAIR - 8, seq), F32)], axis=0).T

    for j, ref in enumerate((wq_ref, wk_ref, wv_ref, wo_ref)):
        w_s[:, j * PAIR : j * PAIR + PAIR] = ref[...]
    pre_s[...] = mm(low_ref[...], w_s[...])

    def norms(i, carry):
        at = rows_at(i, 128)
        for j, n_ref, s, col in ((0, qn_ref, q_s, 0), (1, kn_ref, k_s, 2)):
            pre = pre_s[at, j * PAIR : j * PAIR + PAIR]
            a, b = halves_mean(pre * pre)
            a, b = lax.rsqrt(a + EPSILON), lax.rsqrt(b + EPSILON)
            n = pre * jnp.where(first_head(pre.shape), a, b)
            n_ref[at, :] = n
            s[at, :] = n.astype(jnp.bfloat16)
            here = jnp.where(lane_is(pre.shape, col), a, jnp.where(lane_is(pre.shape, col + 1), b, 0.0))
            stat_ref[at, :] = here if col == 0 else stat_ref[at, :] + here
        v_ref[at, :] = pre_s[at, 2 * PAIR : 3 * PAIR].astype(jnp.bfloat16)
        sig_ref[at, :] = jax.nn.sigmoid(pre_s[at, 3 * PAIR : 4 * PAIR])
        return carry

    lax.fori_loop(0, seq // 128, norms, 0)

    @pl.when(step == 0)
    def _():
        for j in range(3):
            plane(j).wait_recv()
        for j in range(4):
            torus(0, j).start()

    @pl.when(step == 1)
    def _():
        arrived(lambda j: torus(0, j))
        for j in range(4):
            torus(1, j).start()
        cross(0).start()
        for j in (3, 4, 5):
            flush(j).start()
        come(0).start()

    @pl.when(step == 2)
    def _():
        pass_on(lambda j: torus(1, j))

    lines = [one_row(row_s, 2 * step + head) for head in (0, 1)]
    first = first_head((128, PAIR))
    zero = jnp.zeros((128, PAIR), jnp.bfloat16)
    upper = lax.broadcasted_iota(jnp.int32, (128, 128), 1) > lax.broadcasted_iota(
        jnp.int32, (128, 128), 0
    )
    for i in range(seq // 128):
        at, n = slice(i * 128, i * 128 + 128), i * 128 + 128
        q = q_s[at, :]
        two = jnp.concatenate([jnp.where(first, q, zero), jnp.where(first, zero, q)], axis=0)
        raw = mm_t(two, k_s[0:n, :]) * (HEAD ** (-0.5))
        probs = []
        for head in (0, 1):
            column = jnp.sum(
                jnp.where(lane_is((128, PAIR), 2 * step + head), top_s[at, :], 0.0), axis=1, keepdims=True
            )
            s = raw[head * 128 : head * 128 + 128] + (column - lines[head][:, 0:n])
            diagonal = jnp.where(upper, NEG, s[:, n - 128 :])
            s = diagonal if i == 0 else jnp.concatenate([s[:, : n - 128], diagonal], axis=1)
            p = jnp.exp(s)
            probs.append((p * (1.0 / jnp.sum(p, axis=1, keepdims=True))).astype(jnp.bfloat16))
        both = mm(jnp.concatenate(probs, axis=0), v_ref[0:n, :])
        out = jnp.where(first, both[0:128], both[128:])
        att_ref[at, :] = out
        gs[step, me, at, :] = (out * sig_ref[at, :]).astype(jnp.bfloat16).astype(F32)
        if n == half:
            gate(step, 0).start()
            gate(step, 2).start()

            @pl.when(step > 0)
            def _():
                hand_on(step - 1, 0, 4)


    gate(step, 3).start()

    @pl.when(step == 0)
    def _():
        gate(0, 1).start()
        pass_on(lambda j: torus(0, j))

    @pl.when(step > 0)
    def _():
        hand_on(step - 1, 3, 5)

    @pl.when(step == pl.num_programs(0) - 1)
    def _():
        torus(1, 1).wait_recv()
        cross(1).start()
        torus(1, 2).wait_recv()
        cross(2).start()
        torus(1, 4).wait_recv()
        torus(1, 5).wait_recv()
        cross(3).start()
        hand_on(step, 0, 4)
        pairs = gs.shape[0]
        for pair in range(1, pairs):
            gate(pair, 1).start()
        hand_on(step, 3, 5)
        for j in range(4):
            cross(j).wait_recv()
        tall, wide, shard = ws.shape[4], ws.shape[5], w_ref.shape[0]

        def turn(k, carry):
            y, m = k // 8, lax.rem(k, 8)
            x, z = m // 2, lax.rem(m, 2) * 2
            rows = pl.ds(pl.multiple_of(y * shard + m * 2 * tall, 16), 2 * tall)
            for h, one, two in (
                (0, ws[0, z, x, y], ws[0, z + 1, x, y]),
                (1, ws[1, x, z, y], ws[1, x, z + 1, y]),
            ):
                both = jnp.concatenate([one, two], axis=0).astype(jnp.bfloat16)
                full_ref[rows, h * wide : h * wide + wide] = both
            return carry

        lax.fori_loop(0, 8 * Y, turn, 0)
        flush(1).start()
        for j in (3, 4, 5):
            flush(j).wait()
        outer, inner = full_ref.shape[1] // 2, wg_s.shape[1] // 2
        columns = lambda k, size: pl.ds(pl.multiple_of(k * size, size), size)
        sums_ref[...] = jnp.zeros_like(sums_ref)

        def feed_forward(chunk):
            rows = rows_at(chunk, half)
            for part, names in enumerate(((2, 4), (1, 5))):

                @pl.when(chunk == part)
                def _():
                    for pair in range(pairs):
                        for j in names:
                            gate(pair, j).wait_recv()

            for pair in range(pairs):
                for y in range(Y):
                    lane = (y * pairs + pair) * PAIR
                    gated_ref[rows, lane : lane + PAIR] = gs[pair, y, rows, :].astype(jnp.bfloat16)

            @pl.when(chunk == 1)
            def _():
                flush(2).start()
                for j in range(7):
                    leave(j, 0).wait()
                come(1).start()

            kept = lax.broadcasted_iota(jnp.int32, (half, 1), 0) + chunk * half < length

            def project(k):
                at = columns(k, outer)
                branch = mm(gated_ref[rows, :], full_ref[:, at])
                x = x_ref[rows, at].astype(F32)
                mid_s[:, at] = x + branch
                for row, value in ((0, x), (1, branch)):
                    value = jnp.where(kept, value * value, 0.0)
                    sums_ref[row : row + 1, at] = sums_ref[row : row + 1, at] + jnp.sum(
                        value, axis=0, keepdims=True
                    )

            each(0, 2, project)
            leave(0, chunk).start()

            def norm(i, carry):
                at = rows_at(i, 128)
                mid = mid_s[at, :]
                r = lax.rsqrt(jnp.mean(mid * mid, axis=1, keepdims=True) + EPSILON)
                normed_s[at, :] = (mid * r * gain2_ref[...].astype(F32)).astype(jnp.bfloat16)
                return carry

            lax.fori_loop(0, half // 128, norm, 0)
            leave(1, chunk).start()

            def hidden(k):
                at = columns(k, inner)
                gate_s[:, at] = mm(normed_s[...], wg_s[:, at])
                up_s[:, at] = mm(normed_s[...], wu_s[:, at])
                pre = gate_s[:, at]
                hid_s[:, at] = (pre * jax.nn.sigmoid(pre) * up_s[:, at]).astype(jnp.bfloat16)

            each(0, 2, hidden)
            for j in (3, 4, 5):
                leave(j, chunk).start()

            come(chunk).wait()
            grad_s[...] = jnp.where(kept, cot_s[...].astype(F32), 0.0).astype(jnp.bfloat16)
            leave(2, chunk).start()

            def project_out(k):
                at = columns(k, outer)
                mlp_s[:, at] = mm(hid_s[...], wd_s[:, at])

            each(0, 2, project_out)
            leave(6, chunk).start()

        each(0, 2, feed_forward)
        for j in range(7):
            leave(j, 1).wait()
        for j in range(3):
            flush(j).wait()
            plane(j).wait_send()
        for stage in (0, 1):
            for j in range(6):
                torus(stage, j).wait_send()
        for j in range(4):
            cross(j).wait_send()
        for pair in range(pairs):
            for j in range(6):
                gate(pair, j).wait_send()


def forward(
    tokens, cotangent, length, gain, wq, wk, wv, wo, wf, bf, w_out, gain2, wg, wu, wd, call_id
):
    seq, width = tokens.shape
    heads, hidden, half = wq.shape[1], wg.shape[1], seq // 2
    weights = pl.BlockSpec((width, PAIR), lambda i, _: (0, i))
    lanes = pl.BlockSpec((seq, PAIR), lambda i, _: (0, i))
    low = jnp.bfloat16
    half_rows = lambda w, t=F32: pltpu.VMEM((half, w), t)
    return local_call(
        forward_kernel,
        heads // PAIR,
        [whole((seq, width)), whole((1, width))] + [weights] * 4
        + [whole(wf.shape), whole(bf.shape), whole(w_out.shape), whole((1, width))] + [HBM] * 4,
        [HBM] + [lanes] * 6 + [whole((2, 8, seq))] + [HBM] * 9 + [whole((2, width))],
        [
            struct(seq, width, t=low), struct(seq, heads), struct(seq, heads), struct(seq, heads, t=low),
            struct(seq, heads), struct(seq, heads), struct(seq, heads),
            struct(2, 8, seq), struct(seq // Y, heads * Y, t=low), struct(heads * Y, width, t=low),
            struct(seq, width), struct(seq, width, t=low), struct(seq, width, t=low),
            struct(seq, hidden), struct(seq, hidden), struct(seq, hidden, t=low), struct(seq, width),
            struct(2, width),
        ],
        [
            pltpu.VMEM((seq, PAIR), F32),
            pltpu.VMEM((8, seq), F32),
            pltpu.VMEM((seq, PAIR), low),
            pltpu.VMEM((seq, PAIR), low),
            pltpu.VMEM((width, 4 * PAIR), low),
            pltpu.VMEM((seq, 4 * PAIR), F32),
            pltpu.VMEM((heads // PAIR, Y, seq, PAIR), F32),
            pltpu.VMEM((2, 4, 4, Y, heads // 16, width // 2), F32),
            pltpu.VMEM((16, width), low),
            pltpu.VMEM((1, PAIR), F32),
            pltpu.VMEM((seq, width), low),
            pltpu.VMEM((seq, width), low),
            pltpu.VMEM((heads * Y, width), low),
            pltpu.VMEM((width, hidden), low),
            pltpu.VMEM((width, hidden), low),
            pltpu.VMEM((hidden, width), low),
            half_rows(width, low), half_rows(width), half_rows(width, low), half_rows(width, low),
            half_rows(hidden), half_rows(hidden), half_rows(hidden, low), half_rows(width),
            pltpu.SemaphoreType.DMA((14,)),
        ]
        + sems(6 * (heads // PAIR), 3, 6, 6, 4),
        63, 17, 60, call_id,
    )(length, tokens, gain, wq, wk, wv, wo, wf, bf, w_out, gain2, cotangent, wg, wu, wd)


def copier(sem):
    count = iter(range(sem.shape[0]))

    def copy(src, dst):
        return load(src, dst, sem.at[next(count)])

    return copy


def reduce_links(rows, x, opp, nbr, held, sem):
    dp, me = lax.axis_index("dp"), lax.axis_index("mp")
    right, left, far = lax.rem(me + 1, Y), lax.rem(me + 3, Y), lax.rem(me + 2, Y)
    q, h = rows // Y, rows // Y // 2

    def message(name):
        src, dst, to = {
            "oR": (lambda: rows_of(x, far * q, h), lambda: opp.at[0], right),
            "oL": (lambda: rows_of(x, far * q + h, h), lambda: opp.at[1], left),
            "iR": (lambda: rows_of(x, right * q + h, h), lambda: nbr.at[0, h:q], right),
            "iL": (lambda: rows_of(x, left * q, h), lambda: nbr.at[1, 0:h], left),
            "dR": (lambda: held.at[0], lambda: nbr.at[0, 0:h], right),
            "dL": (lambda: held.at[1], lambda: nbr.at[1, h:q], left),
        }[name]
        return link(src(), dst(), *sem, STEPS.index(name), (dp, to))

    return message, me, right, left, [(dp, right), (dp, left)]


def mlp_backward_kernel(
    length_ref, grad_in, low_in, gate_in, up_in, hid_in, wd_in, wg_in, wu_in, x_ref, mid_ref,
    back_out, gd_out, gg_out, gu_out, layer_ref, square_ref,
    grad_ref, low_ref, gate_ref, up_ref, hid_ref, wd_ref, wg_ref, wu_ref,
    dg_s, du_s, back_s, bufs, opp, nbr, held, own_s, mid_s, csem, *sem,
):
    seq, width = grad_ref.shape
    units = wd_ref.shape[0] // 2
    low16 = jnp.bfloat16
    message, me, right, left, peers = reduce_links(seq, x_ref, opp, nbr, held, sem)
    q, h = seq // Y, seq // Y // 2
    copy = copier(csem)
    need = [
        copy(grad_in, grad_ref),
        copy(wd_in.at[0:units], wd_ref.at[0:units]),
        copy(gate_in.at[:, 0:units], gate_ref.at[:, 0:units]),
        copy(up_in.at[:, 0:units], up_ref.at[:, 0:units]),
    ]
    meet(peers)
    for name in STEPS[:4]:
        message(name).start()
    for c in need[0:2]:
        c.wait()
    next_low, next_hid = copy(low_in, low_ref), copy(hid_in, hid_ref)
    more = [
        copy(wd_in.at[units:], wd_ref.at[units:]),
        copy(gate_in.at[:, units:], gate_ref.at[:, units:]),
        copy(up_in.at[:, units:], up_ref.at[:, units:]),
    ]
    weights = [copy(wg_in, wg_ref), copy(wu_in, wu_ref)]
    adds = [
        copy(rows_of(x_ref, right * q, h), held.at[0]),
        copy(rows_of(x_ref, left * q + h, h), held.at[1]),
        copy(rows_of(x_ref, me * q, q), own_s),
        copy(rows_of(mid_ref, me * q, q), mid_s),
    ]
    spots = (gd_out, gg_out, gu_out)
    columns = lambda j: pl.ds(pl.multiple_of(j * units, units), units)
    flush = lambda j, which: pltpu.make_async_copy(
        bufs.at[which, j], spots[which].at[:, columns(j)], csem.at[csem.shape[0] - 6 + which * 2 + j]
    )

    def write(which, left_of, right_of, j):
        slot, at = bufs.at[which, j], columns(j)

        def rows(i, carry):
            part = rows_at(i, 768)
            slot[part, :] = t_mm(left_of[:, part], right_of[:, at])
            return carry

        lax.fori_loop(0, width // 768, rows, 0)
        flush(j, which).start()

    def tile(j):
        at = columns(j)

        @pl.when(j == 1)
        def _():
            for c in more:
                c.wait()

        grad = mm_t(grad_ref[...], wd_ref[at, :])

        @pl.when(j == 0)
        def _():
            for c in need[2:4]:
                c.wait()

        gate = gate_ref[:, at]
        sig = jax.nn.sigmoid(gate)
        dg_s[:, at] = (grad * up_ref[:, at] * (sig * (1.0 + gate * (1.0 - sig)))).astype(low16)
        du_s[:, at] = (grad * (gate * sig)).astype(low16)

        @pl.when(j == 0)
        def _():
            next_low.wait()
            next_hid.wait()

        write(0, grad_ref, hid_ref, j)
        write(1, low_ref, dg_s, j)

        @pl.when(j == 1)
        def _():
            for part, (come, go) in enumerate((("oR", "dR"), ("oL", "dL"))):
                message(come).wait_recv()
                adds[part].wait()
                held[part] = held[part] + opp[part]
                message(go).start()

        write(2, low_ref, du_s, j)

    each(0, 2, tile)
    for c in weights:
        c.wait()

    def back(i, carry):
        rows = rows_at(i, 768)
        back_s[:, rows] = mm_t(dg_s[...], wg_ref[rows, :])
        back_s[:, rows] = back_s[:, rows] + mm_t(du_s[...], wu_ref[rows, :])
        return carry

    lax.fori_loop(0, width // 768, back, 0)
    last = copy(back_s, back_out)
    adds[2].wait()
    adds[3].wait()
    sums = 0.0
    for part, names in enumerate((("dR", "iL"), ("iR", "dL"))):
        for name in names:
            message(name).wait_recv()
        at = slice(part * h, part * h + h)
        branch = own_s[at, :] + nbr[0, at] + nbr[1, at]
        layer_ref[at, :] = (mid_s[at, :] + branch).astype(low16).astype(F32)
        row = lax.broadcasted_iota(jnp.int32, (h, 1), 0) + (me * q + part * h)
        kept = jnp.where(row < length_ref[0], branch * branch, 0.0)
        sums = sums + jnp.sum(kept, axis=0, keepdims=True)
    square_ref[...] = sums
    last.wait()
    for j in (0, 1):
        for which in range(3):
            flush(j, which).wait()
    for name in STEPS[:6]:
        message(name).wait_send()


def mlp_backward(length, grad, low, gate, up, hid, wg, wu, wd, branch, mid, call_id):
    seq, width = low.shape
    hidden = wg.shape[1]
    quarter = seq // Y
    low16 = jnp.bfloat16
    smem = pl.BlockSpec(memory_space=pltpu.SMEM)
    inputs = (grad, low, gate, up, hid, wd, wg, wu)
    return pl.pallas_call(
        mlp_backward_kernel,
        in_specs=[smem] + [HBM] * 10,
        out_specs=[HBM] * 4 + [VMEM] * 2,
        out_shape=[struct(seq, width)] + [struct(width, hidden)] * 3
        + [struct(quarter, width), struct(1, width)],
        scratch_shapes=[pltpu.VMEM(a.shape, a.dtype) for a in inputs]
        + [pltpu.VMEM((seq, hidden), low16)] * 2
        + [pltpu.VMEM((seq, width), F32), pltpu.VMEM((3, 2, width, hidden // 2), F32)]
        + ring_scratch(quarter, width)
        + [pltpu.VMEM((quarter, width), F32)] * 2
        + [pltpu.SemaphoreType.DMA((22,))]
        + sems(6),
        compiler_params=pltpu.CompilerParams(
            vmem_limit_bytes=62 << 20, collective_id=call_id, has_side_effects=True
        ),
    )(length, *inputs, branch, mid)


def backward_kernel(
    length_ref, gg_ref, low_in, qn_ref, kn_ref, v_ref, sig_ref, att_ref, stat_ref,
    decay_ref, wq_ref, wk_ref, wv_ref, wo_ref, wf_ref, own_ref, gated_ref, layer_ref,
    back_out, four_out, gout_out, gf_ref, bias_ref, out_ref,
    k_s, do_s, line_s, top_s, both_s, dq_s, dk_s, dv_s, all_s, fall_s, w_s, wf_s, lay_s, back_ref, wide_s, low_ref, osem,
    *sem,
):
    step = pl.program_id(0)
    seq, width = low_ref.shape
    length = length_ref[0]
    low16 = jnp.bfloat16
    wide = 4 * PAIR
    dp, me = lax.axis_index("dp"), lax.axis_index("mp")
    right, left = lax.rem(me + 1, Y), lax.rem(me + 3, Y)
    q, h = seq // Y, seq // Y // 2

    def spread(j):
        owner, part, to = (
            (me, 0, right), (me, 1, right), (me, 0, left), (me, 1, left), (left, 0, right), (right, 1, left)
        )[j]
        piece = rows_of(lay_s, owner * q + part * h, h)
        source = layer_ref.at[part * h : part * h + h] if j < 4 else piece
        return link(source, piece, *sem, j, (dp, to))

    def fetch(j):
        pair = ((layer_ref, rows_of(lay_s, me * q, q)), (low_in, low_ref))[j]
        return pltpu.make_async_copy(*pair, osem.at[5 + j])

    @pl.when(step == 0)
    def _():
        meet([(dp, right), (dp, left)])
        for j in range(4):
            spread(j).start()
        for j in (0, 1):
            fetch(j).start()

    @pl.when(step == 2)
    def _():
        spread(0).wait_recv()
        spread(4).start()
        spread(3).wait_recv()
        spread(5).start()

    @pl.when(step == 0)
    def _():
        heads = wf_ref.shape[0]
        wf_s[...] = jnp.zeros_like(wf_s)
        wf_s[0:heads, :] = wf_ref[...]
        decay = decay_ref[0]
        column = lax.broadcasted_iota(jnp.int32, decay.shape, 1)
        final = jnp.sum(jnp.where(column == length - 1, decay, 0.0), axis=1, keepdims=True)
        line_s[...] = jnp.where(column < length, decay, final)
        masked = jnp.where(column < length, decay, -NEG)
        top_s[...] = jnp.concatenate([masked, jnp.zeros((PAIR - 8, seq), F32)], axis=0).T
        fall_s[...] = jnp.zeros_like(fall_s)

    base = pl.multiple_of(step * wide, wide)
    part = lambda j: pl.ds(pl.multiple_of(base + j * PAIR, PAIR), PAIR)
    for j, w_ref in enumerate((wq_ref, wk_ref, wv_ref, wo_ref)):
        w_s[:, part(j)] = w_ref[...]
    first = first_head((seq, PAIR))
    gg, sig = gg_ref[...], sig_ref[...]
    do_s[...] = (gg * sig).astype(low16)
    all_s[:, part(3)] = (gg * att_ref[...] * sig * (1.0 - sig)).astype(low16)
    k_s[...] = kn_ref[...].astype(low16)
    dk_s[...] = jnp.zeros_like(dk_s)
    dv_s[...] = jnp.zeros_like(dv_s)
    columns, lines = [], [one_row(line_s, 2 * step + head) for head in (0, 1)]
    for head in (0, 1):
        column = jnp.sum(
            jnp.where(lane_is((seq, PAIR), 2 * step + head), top_s[...], 0.0), axis=1, keepdims=True
        )
        columns.append(column)
    both_s[...] = jnp.concatenate([jnp.broadcast_to(column, (seq, PAIR)) for column in columns], axis=1)
    ones = jnp.concatenate(
        [jnp.where(lane_is((128, PAIR), 2 * step + head), 1.0, 0.0) for head in (0, 1)], axis=0
    ).astype(low16)
    lanes = lax.broadcasted_iota(jnp.int32, (seq, PAIR), 1)
    marks = jnp.where(lanes // 2 == step, 1.0, 0.0).astype(low16)
    block = first_head((128, PAIR))
    zero = jnp.zeros((128, PAIR), low16)
    lower = lax.broadcasted_iota(jnp.int32, (128, 256), 0) > lax.rem(
        lax.broadcasted_iota(jnp.int32, (128, 256), 1), 128
    )
    for i in range(seq // 128):
        at, n = slice(i * 128, i * 128 + 128), i * 128 + 128
        query = qn_ref[at, :].astype(low16)
        do = do_s[at, :]
        two_q, two_do = (
            jnp.concatenate([jnp.where(block, t, zero), jnp.where(block, zero, t)], axis=0)
            for t in (query, do)
        )
        s = mm_t(k_s[0:n, :], two_q) * (HEAD ** (-0.5))
        s = s + (jnp.concatenate([line[:, at] for line in lines], axis=1) - both_s[0:n, :])
        diagonal = jnp.where(lower, NEG, s[n - 128 :, :])
        s = diagonal if i == 0 else jnp.concatenate([s[: n - 128, :], diagonal], axis=0)
        p = jnp.exp(s)
        p = p * (1.0 / jnp.sum(p, axis=0, keepdims=True))
        gp = mm_t(v_ref[0:n, :], two_do)
        ds = (p * (gp - jnp.sum(p * gp, axis=0, keepdims=True))).astype(low16)
        dv_s[0:n, :] = dv_s[0:n, :] + mm(p.astype(low16), two_do)
        dk_s[0:n, :] = dk_s[0:n, :] + mm(ds, jnp.concatenate([two_q, ones], axis=1))
        pieces = t_mm(ds, jnp.concatenate([k_s[0:n, :], marks[0:n]], axis=1))
        one, two = pieces[0:128], pieces[128:]
        dq_s[at, :] = jnp.where(block, one[:, 0:PAIR], two[:, 0:PAIR])
        fall_s[at, :] = fall_s[at, :] + (
            jnp.where(lane_is((128, PAIR), 2 * step), one[:, PAIR:], 0.0)
            + jnp.where(lane_is((128, PAIR), 2 * step + 1), two[:, PAIR:], 0.0)
        )
    fall_s[...] = fall_s[...] - dk_s[:, PAIR:]
    stat = stat_ref[...]
    for e, n_ref, col, to in ((dq_s, qn_ref, 0, 0), (dk_s, kn_ref, 2, 1)):
        e = e[:, 0:PAIR] * (HEAD ** (-0.5))
        n = n_ref[...]
        a, b = halves_mean(e * n)
        r = jnp.where(first, stat[:, col : col + 1], stat[:, col + 1 : col + 2])
        all_s[:, part(to)] = (r * (e - n * jnp.where(first, a, b))).astype(low16)
    all_s[:, part(2)] = dv_s[...].astype(low16)
    slot = lax.rem(step, 2)

    @pl.when(step == 0)
    def _():
        for j in (0, 1):
            fetch(j).wait()

    def flush(j, at, step):
        columns = pl.ds(pl.multiple_of(step * wide, wide), wide)
        out = (four_out, gout_out)[j].at[:, columns]
        return pltpu.make_async_copy(wide_s.at[at, j], out, osem.at[at * 2 + j])

    @pl.when(step == 2)
    def _():
        for j in (0, 1):
            flush(j, 0, 0).wait()

    def grads(k, carry):
        rows = rows_at(k, 768)
        wide_s[slot, 0, rows, :] = t_mm(low_ref[:, rows], all_s[:, pl.ds(base, wide)])
        wide_s[slot, 1, rows, :] = t_mm(own_ref[:, rows].astype(low16), gated_ref[...])
        return carry

    lax.fori_loop(0, width // 768, grads, 0)
    for j in (0, 1):
        flush(j, slot, step).start()

    @pl.when(step == pl.num_programs(0) - 1)
    def _():
        fall = running_sum(fall_s[...].T[0:8], backward=True) * decay_ref[1]
        fall = jnp.concatenate([fall, jnp.zeros_like(fall)], axis=0).astype(low16)
        bias = jnp.sum(fall.astype(F32), axis=1, keepdims=True)
        bias_ref[...] = jnp.broadcast_to(bias[0:8], (8, PAIR))
        gf_ref[...] = mm(fall, low_ref[...])[0:8]

        def tail(k, carry):
            rows = rows_at(k, 768)
            back_ref[:, rows] = mm_t(all_s[...], w_s[rows, :])
            back_ref[:, rows] = back_ref[:, rows] + t_mm(fall, wf_s[:, rows])
            return carry

        lax.fori_loop(0, width // 768, tail, 0)
        last = load(back_ref, back_out, osem.at[4])
        for j in (1, 2, 4, 5):
            spread(j).wait_recv()
        out_ref[...] = lay_s[...].astype(low16)
        for at, done in ((1, 1), (0, 2)):
            for j in (0, 1):
                flush(j, at, done).wait()
        last.wait()
        for j in range(6):
            spread(j).wait_send()


def backward_attention(place, gg, low, qn, kn, v, sig, att, stat, decay, wq, wk, wv, wo, wf, own, gated, layer, call_id):
    seq, width = low.shape
    heads = wq.shape[1]
    weights = pl.BlockSpec((width, PAIR), lambda i, _: (0, i))
    lanes = pl.BlockSpec((seq, PAIR), lambda i, _: (0, i))
    full = whole((seq, width))
    low16 = jnp.bfloat16
    return local_call(
        backward_kernel,
        heads // PAIR,
        [lanes, HBM] + [lanes] * 6 + [whole((2, 8, seq))] + [weights] * 4
        + [whole(wf.shape), whole(own.shape)]
        + [pl.BlockSpec((own.shape[0], 4 * PAIR), lambda i, _: (0, i)), HBM],
        [HBM, HBM, HBM, whole((8, width)), whole((8, PAIR)), full],
        [
            struct(seq, width), struct(width, 4 * heads), struct(width, width), struct(8, width),
            struct(8, PAIR), struct(seq, width, t=low16),
        ],
        [
            pltpu.VMEM((seq, PAIR), low16),
            pltpu.VMEM((seq, PAIR), low16),
            pltpu.VMEM((8, seq), F32),
            pltpu.VMEM((seq, PAIR), F32),
            pltpu.VMEM((seq, 2 * PAIR), F32),
            pltpu.VMEM((seq, PAIR), F32),
            pltpu.VMEM((seq, 2 * PAIR), F32),
            pltpu.VMEM((seq, PAIR), F32),
            pltpu.VMEM((seq, 4 * heads), low16),
            pltpu.VMEM((seq, PAIR), F32),
            pltpu.VMEM((width, 4 * heads), low16),
            pltpu.VMEM((16, width), low16),
            pltpu.VMEM((seq, width), F32),
            pltpu.VMEM((seq, width), F32),
            pltpu.VMEM((2, 2, width, 4 * PAIR), F32),
            pltpu.VMEM((seq, width), low16),
            pltpu.SemaphoreType.DMA((7,)),
        ]
        + sems(6),
        62, 14, 50, call_id,
    )(place, gg, low, qn, kn, v, sig, att, stat, decay, wq, wk, wv, wo, wf, own, gated, layer)


def finish_kernel(
    grad_in, layer_in, wout_hbm, four_hbm, mlp_hbm, sums_hbm,
    grad_ref, layer_ref, wout_ref, q_ref, k_ref, v_ref, o_ref, gate_ref, up_ref, down_ref,
    gain_ref, gain2_ref, fall_ref, rms_ref, bias_ref,
    grad_s, layer_s, four_in, mlp_in, sums_in, sem,
):
    copy = copier(sem)
    rows = grad_in.shape[0] // 4
    parts = [slice(j * rows, j * rows + rows) for j in range(4)]
    come = [(copy(grad_in.at[p], grad_s.at[p]), grad_s.at[p], grad_ref.at[p]) for p in parts]
    small = [copy(wout_hbm, wout_ref), copy(four_hbm, four_in), copy(mlp_hbm, mlp_in), copy(sums_hbm, sums_in)]
    come += [(copy(layer_in.at[p], layer_s.at[p]), layer_s.at[p], layer_ref.at[p]) for p in parts]
    copies = []

    def leave(some):
        for arrived, mid, dst in some:
            arrived.wait()
            copies.append(copy(mid, dst))

    leave(come[0:4])
    for c in small:
        c.wait()
    inner = q_ref.shape[1]
    for j, ref in enumerate((q_ref, k_ref, v_ref, o_ref)):
        for pair in range(inner // PAIR):
            lane = (pair * 4 + j) * PAIR
            ref[:, pair * PAIR : pair * PAIR + PAIR] = four_in[:, lane : lane + PAIR]
    units = gate_ref.shape[1]
    down_ref[...] = mlp_in[:, 0:units]
    gate_ref[...] = mlp_in[:, units : 2 * units]
    up_ref[...] = four_in[:, 4 * inner : 4 * inner + units]
    leave(come[4:8])
    share, width = gain_ref.shape[1], sums_in.shape[1]
    row = lax.broadcasted_iota(jnp.int32, (width, share), 0)
    lane = lax.broadcasted_iota(jnp.int32, (width, share), 1)
    pick = jnp.where(row == lane + lax.axis_index("dp") * share, 1.0, 0.0)
    own = jnp.dot(
        sums_in[...], pick, precision=lax.Precision.HIGHEST, preferred_element_type=F32
    )
    gain_ref[...] = own[0:1]
    gain2_ref[...] = own[1:2]
    fall_ref[...] = own[3 : 3 + fall_ref.shape[0]]
    square = lambda row, at: sums_in[row : row + 1, at * PAIR : at * PAIR + NBUCKET]
    squares = jnp.concatenate([square(9, 0), square(9, 1), square(2, 0)], axis=0)
    rms_ref[...] = jnp.sqrt(squares / (square(9, 2) * width))
    bias_ref[...] = sums_in[10:11, 0 : bias_ref.shape[1]]
    for c in copies:
        c.wait()


def finish(grad, layer, out_share, share, mlp_share, sums, heads):
    rows, inner = out_share.shape
    units = mlp_share.shape[1] // 2
    return pl.pallas_call(
        finish_kernel,
        out_shape=[
            struct(*grad.shape), struct(*layer.shape, t=layer.dtype), *[struct(rows, inner)] * 5,
            *[struct(rows, units)] * 3, struct(1, rows), struct(1, rows), struct(heads, rows),
            struct(3, NBUCKET), struct(1, heads),
        ],
        in_specs=[HBM] * 6,
        out_specs=[HBM, HBM] + [VMEM] * 13,
        scratch_shapes=[pltpu.VMEM(a.shape, a.dtype) for a in (grad, layer, share, mlp_share, sums)]
        + [pltpu.SemaphoreType.DMA((20,))],
        compiler_params=pltpu.CompilerParams(vmem_limit_bytes=60 << 20),
    )(grad, layer, out_share, share, mlp_share, sums)


def per_device(
    tokens, lengths, buckets, out_cotangent, gain_attn, w_query, w_key, w_value, w_outgate,
    w_forget, b_forget, w_out, gain_mlp, w_gate, w_up, w_down,
):
    x, cotangent = tokens[0], out_cotangent[0]
    heads = w_forget.shape[1]
    gain_in, gain_mid = gain_attn[None], gain_mlp[None]
    weights = (w_query, w_key, w_value, w_outgate, w_forget.T)
    (
        low, qn, kn, value, sig, attended, stat, decay, gated, w_full,
        middle, mid_low, grad_rows, gate, up, hidden, mlp_local, squares,
    ) = forward(
        x, cotangent, lengths, gain_in, *weights, b_forget[None], w_out, gain_mid, w_gate, w_up, w_down, 0
    )
    mid_local, g_down, g_gate, g_up, layer_own, mlp_square = mlp_backward(
        lengths, grad_rows, mid_low, gate, up, hidden, w_gate, w_up, w_down, mlp_local, middle, 1
    )
    grad_own, gg, mlp_share, mlp_gain = reduce_middle(
        mid_local, middle, grad_rows, gain_mid, w_full, [g_down, g_gate],
        ((0, 0), (0, 1), (1, 0), (1, 1)), 2,
    )
    in_local, g_four, g_out, g_fall, bias, layer_out = backward_attention(
        lengths, gg, low, qn, kn, value, sig, attended, stat, decay, *weights, grad_own, gated,
        layer_own, 3,
    )
    small = (mlp_gain, g_fall, squares, mlp_square, bias, lengths, buckets)
    input_grad, out_share, share, sums = reduce_input(
        in_local, x, grad_own, gain_in, small, [g_out, g_four, g_up],
        ((0, 0), (0, 1), (0, 2), (1, 0), (1, 1), (1, 2), (2, 0), (2, 1)), 4,
    )
    (
        input_grad, layer_out, g_out, g_query, g_key, g_value, g_outgate, g_gate, g_up, g_down,
        g_gain, g_gain_mid, g_fall, rms, bias,
    ) = finish(input_grad, layer_out, out_share, share, mlp_share, sums, heads)
    return (
        layer_out[None],
        input_grad[None],
        g_gain[0],
        g_query,
        g_key,
        g_value,
        g_outgate,
        g_fall.T,
        bias[0],
        g_out.T,
        g_gain_mid[0],
        g_gate,
        g_up,
        g_down.T,
        rms,
    )


def solution(mesh):
    placed = (
        P("dp", None, None),
        P("dp"),
        P("dp"),
        P("dp", None, None),
        P(),
        P(None, "mp"),
        P(None, "mp"),
        P(None, "mp"),
        P(None, "mp"),
        P(None, "mp"),
        P("mp"),
        P("mp", None),
        P(),
        P(None, "mp"),
        P(None, "mp"),
        P("mp", None),
    )
    return jax.shard_map(
        per_device,
        mesh=mesh,
        in_specs=placed,
        out_specs=(
            P("dp", None, None),
            P("dp", None, None),
            P("dp"),
            P("dp", "mp"),
            P("dp", "mp"),
            P("dp", "mp"),
            P("dp", "mp"),
            P("dp", "mp"),
            P("mp"),
            P("mp", "dp"),
            P("dp"),
            P("dp", "mp"),
            P("dp", "mp"),
            P("mp", "dp"),
            P(),
        ),
        check_vma=False,
    )
```

```python
import functools

import jax
import jax.numpy as jnp
from jax import lax
from jax.experimental import pallas as pl
from jax.experimental.pallas import tpu as pltpu
from jax.sharding import PartitionSpec as P

NBUCKET = 4


EPSILON = 1e-06


MESH = pl.DeviceIdType.MESH
F32 = jnp.float32
Y = 4
STEP = 512
HBM = pl.BlockSpec(memory_space=pl.ANY)
VMEM = pl.BlockSpec(memory_space=pltpu.VMEM)
STEPS = ("oR", "oL", "iR", "iL", "dR", "dL", "gRa", "gRb", "gLa", "gLb", "fR", "fL")


def gain_row(ref):
    return ref[...].astype(F32).reshape(1, ref.shape[0])


def rows_of(ref, start, count):
    return ref.at[pl.ds(pl.multiple_of(start, 8), count)]


def meet(devices):
    barrier = pltpu.get_barrier_semaphore()
    for device in devices:
        pl.semaphore_signal(barrier, inc=1, device_id=device, device_id_type=MESH)
    pl.semaphore_wait(barrier, len(devices))


def link(src, dst, ssem, rsem, at, device):
    return pltpu.make_async_remote_copy(
        src_ref=src,
        dst_ref=dst,
        send_sem=ssem.at[at],
        recv_sem=rsem.at[at],
        device_id=device,
        device_id_type=MESH,
    )


def push(*args):
    copy = link(*args)
    copy.start()
    return copy


class YRing:
    def __init__(self, rows, waves, ssem, rsem):
        self.sems = (ssem, rsem)
        self.dp, self.me = lax.axis_index("dp"), lax.axis_index("mp")
        self.right, self.left = lax.rem(self.me + 1, Y), lax.rem(self.me + 3, Y)
        self.far = lax.rem(self.me + 2, Y)
        self.quarter, self.half = rows // Y, rows // Y // 2
        self.tall = self.half // waves
        self.sent = {}

    def neighbours(self):
        return [(self.dp, self.right), (self.dp, self.left)]

    def send(self, name, wave, src, dst, to):
        kind, index = divmod(STEPS.index(name), 6)
        at = kind * 12 + wave * 6 + index
        self.sent[name, wave] = push(src, dst, *self.sems, at, (self.dp, to))

    def rows(self, x, owner, part, wave):
        return rows_of(x, owner * self.quarter + part * self.half + wave * self.tall, self.tall)

    def fetch(self, x, held, own, sem):
        self.loads = [
            load(rows_of(x, self.right * self.quarter, self.half), held.at[0], sem.at[0]),
            load(rows_of(x, self.left * self.quarter + self.half, self.half), held.at[1], sem.at[1]),
            load(rows_of(x, self.me * self.quarter, self.quarter), own, sem.at[2]),
        ]

    def start(self, x, opp, nbr, wave):
        w = slice(wave * self.tall, wave * self.tall + self.tall)
        low = slice(self.half + wave * self.tall, self.half + wave * self.tall + self.tall)
        self.send("oR", wave, self.rows(x, self.far, 0, wave), opp.at[0, w], self.right)
        self.send("oL", wave, self.rows(x, self.far, 1, wave), opp.at[1, w], self.left)
        self.send("iR", wave, self.rows(x, self.right, 1, wave), nbr.at[0, low], self.right)
        self.send("iL", wave, self.rows(x, self.left, 0, wave), nbr.at[1, w], self.left)

    def relay(self, opp, nbr, held, wave):
        w = slice(wave * self.tall, wave * self.tall + self.tall)
        low = slice(self.half + wave * self.tall, self.half + wave * self.tall + self.tall)
        for part, (come, go, into, to) in enumerate(
            (("oR", "dR", nbr.at[0, w], self.right), ("oL", "dL", nbr.at[1, low], self.left))
        ):
            self.sent[come, wave].wait_recv()
            if wave == 0:
                self.loads[part].wait()
            held[part, w] = held[part, w] + opp[part, w]
            self.send(go, wave, held.at[part, w], into, to)

    def collect(self, own, nbr, part, wave):
        if part == 0 and wave == 0:
            self.loads[2].wait()
        for name in (("dR", "iL"), ("iR", "dL"))[part]:
            self.sent[name, wave].wait_recv()
        start = part * self.half + wave * self.tall
        at = slice(start, start + self.tall)
        return at, own[at, :] + nbr[0, at] + nbr[1, at]

    def spread(self, part, wave, own, out):
        tag, into = "ab"[part], self.rows(out, self.me, part, wave)
        start = part * self.half + wave * self.tall
        mine = own.at[start : start + self.tall]
        self.send("gR" + tag, wave, mine, into, self.right)
        self.send("gL" + tag, wave, mine, into, self.left)

    def forward(self, wave, out):
        for come, go, owner, part, to in (
            ("gRa", "fR", self.left, 0, self.right),
            ("gLb", "fL", self.right, 1, self.left),
        ):
            self.sent[come, wave].wait_recv()
            block = self.rows(out, owner, part, wave)
            self.send(go, wave, block, block, to)

    def arrive(self, wave):
        for name in ("gRb", "gLa", "fR", "fL"):
            self.sent[name, wave].wait_recv()

    def finish(self):
        for copy in self.sent.values():
            copy.wait_send()


def ring_scratch(quarter, columns):
    return [
        pltpu.VMEM((2, quarter // 2, columns), F32),
        pltpu.VMEM((2, quarter, columns), F32),
        pltpu.VMEM((2, quarter // 2, columns), F32),
    ]


def sems(*counts):
    return [pltpu.SemaphoreType.DMA((n,)) for n in counts for _ in (0, 1)]


class Place:
    def __init__(self):
        self.dp, self.my = lax.axis_index("dp"), lax.axis_index("mp")
        c, z, x = lax.rem(self.dp, 2), lax.rem(self.dp // 2, 4), self.dp // 8
        self.c, self.sib, self.chip = c, self.dp + 1 - 2 * c, x * 4 + z
        self.st1, self.st2 = 4 - 3 * c, 1 + 3 * c
        self.p1, self.p2 = x + c * (z - x), z + c * (x - z)
        step = lambda p, by: lax.rem(p + by, 4)
        self.r1, self.l1, self.o1 = (step(self.p1, by) for by in (1, 3, 2))
        self.r2, self.l2, self.o2 = (step(self.p2, by) for by in (1, 3, 2))

    def device(self, a, b):
        return ((a * self.st1 + b * self.st2) * 2 + self.c, self.my)

    def peers(self):
        return [
            (self.sib, self.my),
            self.device(self.r1, self.p2),
            self.device(self.l1, self.p2),
            self.device(self.p1, self.r2),
            self.device(self.p1, self.l2),
        ]


class ScatterSum:
    def __init__(self, here, sources, own, other, near, last, asem, bsem, lsem, ssem, rsem):
        self.here, self.sources = here, sources
        self.own, self.other, self.near, self.last = own, other, near, last
        self.asem, self.bsem, self.lsem, self.ssem, self.rsem = asem, bsem, lsem, ssem, rsem
        self.n = own.shape[0]
        self.sibling, *to = here.peers()
        self.to = (to[0:2], to[2:4])

    def message(self, name, k, stage):
        at = (k * 2 + stage) * 6 + STEPS.index(name)
        device = self.to[stage][0 if name[1] == "R" else 1]
        here, own = self.here, self.own.at[k]
        if stage:
            own, into, cut = own.at[here.p1], self.last.at[k], (slice(0, 24), slice(24, 48))
            far, right, left = here.o2, here.r2, here.l2
        else:
            into, cut = self.near.at[k], (slice(0, 2), slice(2, 4))
            far, right, left = here.o1, here.r1, here.l1
        row, part, slot = {
            "oR": (far, 0, 0),
            "oL": (far, 1, 1),
            "iR": (right, 1, 3),
            "iL": (left, 0, 4),
            "dR": (right, 0, 2),
            "dL": (left, 1, 5),
        }[name]
        return link(own.at[row, cut[part]], into.at[slot], self.ssem, self.rsem, at, device)

    def whole(self, k):
        own, other = self.own.at[k], self.other.at[k]
        return link(own, other, self.asem, self.bsem, k, self.sibling)

    def exchange(self, k):
        here = self.here
        ref, start, width = self.sources[k]

        def source(block):
            return ref.at[pl.ds(pl.multiple_of(block * 48, 16), 48), pl.ds(start, width)]

        def cross(i, carry):
            a, b = i // 4, lax.rem(i, 4)
            block = source((a * here.st2 + b * here.st1) * 2 + 1 - here.c)
            push(block, self.other.at[k, a, b], self.asem, self.bsem, k, self.sibling)
            return carry

        def fetch(i, carry):
            a, b = i // 4, lax.rem(i, 4)
            block = source((a * here.st1 + b * here.st2) * 2 + here.c)
            pltpu.make_async_copy(block, self.own.at[k, a, b], self.lsem.at[k]).start()
            return carry

        lax.fori_loop(0, 16, cross, 0)
        lax.fori_loop(0, 16, fetch, 0)

    def first(self, k):
        here, own, other = self.here, self.own, self.other
        pltpu.make_async_copy(own.at[k], own.at[k], self.lsem.at[k]).wait()
        self.whole(k).wait_recv()

        def add(p):
            def body(b, carry):
                own[k, p, b] = own[k, p, b] + other[k, p, b]
                return carry

            lax.fori_loop(0, 4, body, 0)

        add(here.o1)
        self.message("oR", k, 0).start()
        self.message("oL", k, 0).start()
        add(here.r1)
        self.message("iR", k, 0).start()
        add(here.l1)
        self.message("iL", k, 0).start()
        add(here.p1)

    def first_relay(self, k):
        here, own, near = self.here, self.own, self.near

        def add(p, at, slot):
            def body(b, carry):
                own[k, p, at + b] = own[k, p, at + b] + near[k, slot, b]
                return carry

            lax.fori_loop(0, 2, body, 0)

        self.message("oR", k, 0).wait_recv()
        add(here.r1, 0, 0)
        self.message("dR", k, 0).start()
        self.message("oL", k, 0).wait_recv()
        add(here.l1, 2, 1)
        self.message("dL", k, 0).start()

    def second(self, k):
        here, own, near = self.here, self.own, self.near
        for name in ("iR", "dR", "iL", "dL"):
            self.message(name, k, 0).wait_recv()

        def add(p):
            h, b = p // 2, lax.rem(p, 2)
            own[k, here.p1, p] = own[k, here.p1, p] + near[k, 2 + h, b] + near[k, 4 + h, b]

        add(here.o2)
        self.message("oR", k, 1).start()
        self.message("oL", k, 1).start()
        add(here.r2)
        self.message("iR", k, 1).start()
        add(here.l2)
        self.message("iL", k, 1).start()
        add(here.p2)

    def second_relay(self, k):
        here, own, last = self.here, self.own, self.last
        self.message("oR", k, 1).wait_recv()
        own[k, here.p1, here.r2, 0:24] = own[k, here.p1, here.r2, 0:24] + last[k, 0]
        self.message("dR", k, 1).start()
        self.message("oL", k, 1).wait_recv()
        own[k, here.p1, here.l2, 24:48] = own[k, here.p1, here.l2, 24:48] + last[k, 1]
        self.message("dL", k, 1).start()

    def result(self, k, out, at):
        here, own, last = self.here, self.own, self.last
        width = own.shape[4]
        for name in ("iR", "dR", "iL", "dL"):
            self.message(name, k, 1).wait_recv()
        columns = pl.ds(pl.multiple_of(at * width, 128), width)
        out[0:24, columns] = own[k, here.p1, here.p2, 0:24] + last[k, 2] + last[k, 4]
        out[24:48, columns] = own[k, here.p1, here.p2, 24:48] + last[k, 3] + last[k, 5]

    def sent(self, k):
        self.whole(k).wait_send()
        for stage in (0, 1):
            for name in STEPS[:6]:
                self.message(name, k, stage).wait_send()


def each(low, high, step):
    def body(k, carry):
        step(k)
        return carry

    lax.fori_loop(low, high, body, 0)


class SmallSum:
    def __init__(self, here, bufs, landed, ssem, rsem):
        self.bufs, self.landed, self.ssem, self.rsem = bufs, landed, ssem, rsem
        turn = lambda p, by: lax.rem(p + by, 4)
        self.stages = [
            [(here.sib, here.my)],
            [here.device(turn(here.p1, by), here.p2) for by in (1, 2, 3)],
            [here.device(here.p1, turn(here.p2, by)) for by in (1, 2, 3)],
            [(here.dp, turn(here.my, by)) for by in (1, 2, 3)],
        ]
        self.far = [self.stages[1][1], self.stages[2][1], self.stages[3][1]]
        self.sent = []

    def send(self, stage):
        for to in self.stages[stage]:
            at = len(self.sent)
            copy = push(self.bufs.at[stage], self.landed.at[at], self.ssem, self.rsem, at, to)
            self.sent.append(copy)

    def take(self, stage):
        value, count = self.bufs[stage], len(self.stages[stage])
        for at in range(len(self.sent) - count, len(self.sent)):
            self.sent[at].wait_recv()
            value = value + self.landed[at]
        self.bufs[stage + 1] = value

    def finish(self):
        for copy in self.sent:
            copy.wait_send()


def scatter_scratch(n, w):
    return [
        pltpu.VMEM((n, 4, 4, 48, w), F32),
        pltpu.VMEM((n, 4, 4, 48, w), F32),
        pltpu.VMEM((n, 6, 2, 48, w), F32),
        pltpu.VMEM((n, 6, 24, w), F32),
        pltpu.SemaphoreType.DMA((n,)),
        pltpu.SemaphoreType.DMA((n,)),
        pltpu.SemaphoreType.DMA((n,)),
        pltpu.SemaphoreType.DMA((12 * n,)),
        pltpu.SemaphoreType.DMA((12 * n,)),
    ]


def scatter_sources(refs, pieces):
    return [(refs[which], at * STEP, STEP) for which, at in pieces]


def norm_back(value, source, base, gain):
    source = source.astype(F32)
    r = lax.rsqrt(jnp.mean(source * source, axis=1, keepdims=True) + EPSILON)
    n = source * r
    e = value * gain
    inner = jnp.mean(e * n, axis=1, keepdims=True)
    return base.astype(F32) + r * (e - n * inner), jnp.sum(value * n, axis=0, keepdims=True)


def load(ref, scratch, sem):
    copy = pltpu.make_async_copy(ref, scratch, sem)
    copy.start()
    return copy


def middle_kernel(pieces, count, x_ref, source_ref, base_ref, gain_ref, w_ref, *refs):
    ins, refs = refs[:count], refs[count:]
    grad_ref, gg_ref, share_ref, sums_ref = refs[:4]
    source_s, base_s, w_s, opp, nbr, held, own_s, blocks, csem, *sem = refs[4:17]
    here, ring = Place(), YRing(x_ref.shape[0], 2, *sem[0:2])
    total = ScatterSum(here, scatter_sources(ins, pieces), *refs[17:])
    n = total.n
    far = (ring.dp, ring.far)
    meet(ring.neighbours() + [far] + here.peers())
    ring.start(x_ref, opp, nbr, 0)
    q, h = ring.quarter, ring.half
    ring.fetch(x_ref, held, own_s, csem)
    for k in range(n):
        total.exchange(k)
    loads = [
        load(rows_of(source_ref, ring.me * q, q), source_s, csem.at[3]),
        load(rows_of(base_ref, ring.me * q, q), base_s, csem.at[4]),
        load(w_ref, w_s, csem.at[5]),
    ]
    ring.relay(opp, nbr, held, 0)
    ring.start(x_ref, opp, nbr, 1)
    each(0, n, total.first)
    each(0, n - 2, total.first_relay)
    ring.relay(opp, nbr, held, 1)
    for copy in loads:
        copy.wait()
    sums, swaps, keeps = 0.0, [], []
    inner = gg_ref.shape[1]
    for wave in (0, 1):
        for part in (0, 1):
            at, value = ring.collect(own_s, nbr, part, wave)
            value, more = norm_back(value, source_s[at, :], base_s[at, :], gain_row(gain_ref))
            grad_ref[at, :] = value
            sums = sums + more
        tall = ring.tall
        low = jnp.concatenate(
            [grad_ref[part * h + wave * tall : part * h + wave * tall + tall, :] for part in (0, 1)], axis=0
        ).astype(jnp.bfloat16)
        for j, by in enumerate((2, 1, 3, 0)):
            to = lax.rem(ring.me + by, Y)
            blocks[wave, j] = mm_t(low, rows_of(w_s, to * inner, inner)[...])
            for part in (0, 1):
                src = blocks.at[wave, j, part * tall : part * tall + tall]
                into = rows_of(gg_ref, ring.me * q + part * h + wave * tall, tall)
                if by:
                    at = (wave * 3 + j) * 2 + part
                    swaps.append(push(src, into, *sem[2:4], at, (ring.dp, to)))
                else:
                    keeps.append(load(src, into, csem.at[6 + wave * 2 + part]))
        if wave == 0:
            each(n - 2, n, total.first_relay)
    sums_ref[...] = sums
    each(0, n, total.second)
    each(0, n, total.second_relay)
    each(0, n, lambda k: total.result(k, share_ref, k))
    for copy in swaps:
        copy.wait_recv()
    for copy in keeps:
        copy.wait()
    for copy in swaps:
        copy.wait_send()
    ring.finish()
    each(0, n, total.sent)


def reduce_middle(partial, source, base, gain, w_full, grads, pieces, call_id):
    n = len(pieces)
    hbm, vmem = pl.BlockSpec(memory_space=pl.ANY), pl.BlockSpec(memory_space=pltpu.VMEM)
    rows, columns = partial.shape
    quarter, inner = rows // Y, w_full.shape[0] // Y
    return pl.pallas_call(
        functools.partial(middle_kernel, pieces, len(grads)),
        out_shape=[
            jax.ShapeDtypeStruct((quarter, columns), F32),
            jax.ShapeDtypeStruct((rows, inner), F32),
            jax.ShapeDtypeStruct((48, n * STEP), F32),
            jax.ShapeDtypeStruct((1, columns), F32),
        ],
        in_specs=[hbm, hbm, hbm, vmem, hbm] + [hbm] * len(grads),
        out_specs=[vmem, hbm, vmem, vmem],
        scratch_shapes=[
            pltpu.VMEM((quarter, columns), source.dtype),
            pltpu.VMEM((quarter, columns), base.dtype),
            pltpu.VMEM(w_full.shape, w_full.dtype),
        ]
        + ring_scratch(quarter, columns)
        + [
            pltpu.VMEM((quarter, columns), F32),
            pltpu.VMEM((2, 4, quarter // 2, inner), F32),
            pltpu.SemaphoreType.DMA((10,)),
        ]
        + sems(12, 12)
        + scatter_scratch(n, STEP),
        compiler_params=pltpu.CompilerParams(
            collective_id=call_id, has_side_effects=True, vmem_limit_bytes=56 << 20
        ),
    )(partial, source, base, gain, w_full, *grads)


def input_kernel(
    pieces, count, x_ref, source_ref, base_ref, gain_ref, other_ref, fall_ref, square_ref, more_ref,
    bias_ref, length_ref, bucket_ref, *refs
):
    ins, refs = refs[:count], refs[count:]
    out_ref, out_share_ref, share_ref, sums_ref = refs[:4]
    source_s, opp, nbr, held, own_s, mine_s, wide_s, landed, csem, *sem = refs[4:17]
    bufs, arrived, asem, bsem = refs[17:21]
    here, ring = Place(), YRing(x_ref.shape[0], 1, *sem[0:2])
    total = ScatterSum(here, scatter_sources(ins, pieces), *refs[21:])
    tiny = SmallSum(here, bufs, arrived, asem, bsem)
    n, first = total.n, wide_s.shape[1] // STEP
    meet(ring.neighbours() + here.peers() + tiny.far)
    ring.start(x_ref, opp, nbr, 0)
    q, h = ring.quarter, ring.half
    ring.fetch(x_ref, held, own_s, csem)
    copy = load(rows_of(source_ref, ring.me * q, q), source_s, csem.at[3])
    for k in range(n):
        total.exchange(k)
    each(0, n // 2, total.first)
    ring.relay(opp, nbr, held, 0)
    each(n // 2, n, total.first)
    each(0, n - 2, total.first_relay)
    copy.wait()
    sums = 0.0
    for wave in (0,):
        for part in (0, 1):
            at, value = ring.collect(own_s, nbr, part, wave)
            value, more = norm_back(value, source_s[at, :], base_ref[at, :], gain_row(gain_ref))
            mine_s[at, :] = value
            ring.spread(part, wave, mine_s, out_ref)
            sums = sums + more
    kept = load(mine_s, rows_of(out_ref, ring.me * q, q), csem.at[4])
    bufs[0, 0:1, :] = sums
    bufs[0, 1:2, :] = other_ref[...]
    bufs[0, 8:16, :] = jnp.zeros_like(bufs[0, 8:16, :])
    bufs[0, 2:3, :] = jnp.zeros((1, sums_ref.shape[1]), F32)
    bufs[0, 3:9, :] = fall_ref[0:6, :]
    lane = lax.broadcasted_iota(jnp.int32, (1, PAIR), 1)
    both = jnp.sum(square_ref[...], axis=1, keepdims=True)
    in_bucket = lambda value: jnp.where(lane == bucket_ref[0], value, 0.0)
    bufs[0, 2:3, 0:PAIR] = in_bucket(jnp.sum(more_ref[...], axis=1, keepdims=True))
    for at, value in enumerate((both[0:1], both[1:2], length_ref[0].astype(F32))):
        bufs[0, 9:10, at * PAIR : at * PAIR + PAIR] = in_bucket(value)
    diagonal = lax.broadcasted_iota(jnp.int32, bias_ref.shape, 0) == lax.broadcasted_iota(
        jnp.int32, bias_ref.shape, 1
    )
    bufs[0, 10:11, 0:PAIR] = jnp.sum(jnp.where(diagonal, bias_ref[...], 0.0), axis=0, keepdims=True)
    tiny.send(0)
    each(n - 2, n, total.first_relay)
    each(0, n, total.second)
    ring.forward(0, out_ref)
    tiny.take(0)
    tiny.send(1)
    each(0, n, total.second_relay)
    tiny.take(1)
    tiny.send(2)
    each(0, first, lambda k: total.result(k, wide_s, k))
    inner = landed.shape[2]
    swaps = []
    for j, by in enumerate((2, 1, 3)):
        to = lax.rem(ring.me + by, Y)
        columns = pl.ds(pl.multiple_of(to * inner, 128), inner)
        swaps.append(push(wide_s.at[:, columns], landed.at[j], *sem[2:4], j, (ring.dp, to)))
    each(first, n, lambda k: total.result(k, share_ref, k - first))
    tiny.take(2)
    tiny.send(3)
    own = wide_s[:, pl.ds(pl.multiple_of(ring.me * inner, 128), inner)]
    for j, copy in enumerate(swaps):
        copy.wait_recv()
        own = own + landed[j]
    out_share_ref[...] = own
    tiny.take(3)
    rows = lax.broadcasted_iota(jnp.int32, sums_ref.shape, 0)
    sums_ref[...] = jnp.where(rows < 3, bufs[4], bufs[3])
    ring.arrive(0)
    kept.wait()
    for copy in swaps:
        copy.wait_send()
    tiny.finish()
    ring.finish()
    each(0, n, total.sent)


def reduce_input(partial, source, base, gain, small, grads, pieces, call_id):
    n = len(pieces)
    smem = pl.BlockSpec(memory_space=pltpu.SMEM)
    hbm, vmem = pl.BlockSpec(memory_space=pl.ANY), pl.BlockSpec(memory_space=pltpu.VMEM)
    rows, columns = partial.shape
    quarter, inner = rows // Y, grads[0].shape[1] // Y
    wide = grads[0].shape[1]
    shares = n * STEP - wide
    return pl.pallas_call(
        functools.partial(input_kernel, pieces, len(grads)),
        out_shape=[
            jax.ShapeDtypeStruct(partial.shape, F32),
            jax.ShapeDtypeStruct((48, inner), F32),
            jax.ShapeDtypeStruct((48, shares), F32),
            jax.ShapeDtypeStruct((16, columns), F32),
        ],
        in_specs=[hbm, hbm, vmem, vmem] + [vmem] * 5 + [smem] * 2 + [hbm] * len(grads),
        out_specs=[hbm] + [vmem] * 3,
        scratch_shapes=[pltpu.VMEM((quarter, columns), source.dtype)]
        + ring_scratch(quarter, columns)
        + [
            pltpu.VMEM((quarter, columns), F32),
            pltpu.VMEM((quarter, columns), F32),
            pltpu.VMEM((48, wide), F32),
            pltpu.VMEM((3, 48, inner), F32),
            pltpu.SemaphoreType.DMA((5,)),
        ]
        + sems(24, 3)
        + [pltpu.VMEM((5, 16, columns), F32), pltpu.VMEM((10, 16, columns), F32)]
        + sems(10)
        + scatter_scratch(n, STEP),
        compiler_params=pltpu.CompilerParams(
            collective_id=call_id, has_side_effects=True, vmem_limit_bytes=56 << 20
        ),
    )(partial, source, base, gain, *small, *grads)


HEAD = 64
PAIR = 128
NEG = -1e30


def rows_at(i, size):
    return pl.ds(pl.multiple_of(i * size, size), size)


def lane_is(shape, index):
    return lax.broadcasted_iota(jnp.int32, shape, len(shape) - 1) == index


def first_head(shape):
    return lax.broadcasted_iota(jnp.int32, shape, len(shape) - 1) < HEAD


def halves_mean(values):
    first = first_head(values.shape)
    low = jnp.sum(jnp.where(first, values, 0.0), axis=1, keepdims=True) * (1.0 / HEAD)
    high = jnp.sum(jnp.where(first, 0.0, values), axis=1, keepdims=True) * (1.0 / HEAD)
    return low, high


def one_row(ref, index):
    rows = ref[...]
    picked = lax.broadcasted_iota(jnp.int32, rows.shape, 0) == index
    return jnp.sum(jnp.where(picked, rows, 0.0), axis=0, keepdims=True)


def running_sum(values, backward=False):
    count = values.shape[1]
    at = lax.broadcasted_iota(jnp.int32, values.shape, 1)
    shift = 1
    while shift < count:
        if backward:
            moved = jnp.where(at < count - shift, pltpu.roll(values, count - shift, 1), 0.0)
        else:
            moved = jnp.where(at >= shift, pltpu.roll(values, shift, 1), 0.0)
        values = values + moved
        shift *= 2
    return values


def mm(left, right):
    return jnp.dot(left, right, preferred_element_type=F32)


def mm_t(left, right):
    return lax.dot_general(left, right, (((1,), (1,)), ((), ())), preferred_element_type=F32)


def t_mm(left, right):
    return lax.dot_general(left, right, (((0,), (0,)), ((), ())), preferred_element_type=F32)


def whole(shape):
    return pl.BlockSpec(shape, lambda *_: (0,) * len(shape), pipeline_mode=pl.Buffered(1))


def struct(*shape, t=F32):
    return jax.ShapeDtypeStruct(shape, t)


def local_call(kernel, grid, in_specs, out_specs, out_shape, scratch, limit, flops, moved, call_id=None):
    return pl.pallas_call(
        kernel,
        grid_spec=pltpu.PrefetchScalarGridSpec(
            num_scalar_prefetch=1,
            grid=(grid,),
            in_specs=in_specs,
            out_specs=out_specs,
            scratch_shapes=scratch,
        ),
        out_shape=out_shape,
        compiler_params=pltpu.CompilerParams(
            vmem_limit_bytes=limit << 20,
            collective_id=call_id,
            has_side_effects=call_id is not None,
        ),
        cost_estimate=pl.CostEstimate(
            flops=flops * 10**9, bytes_accessed=moved * 10**6, transcendentals=4 * 10**6
        ),
    )


def forward_kernel(
    length_ref, x_ref, gain_ref, wq_ref, wk_ref, wv_ref, wo_ref, wf_ref, bf_ref, w_ref,
    gain2_ref, cot_in, wg_in, wu_in, wd_in,
    low_out, qn_ref, kn_ref, v_ref, sig_ref, att_ref, stat_ref, decay_ref, gated_out, full_out,
    mid_out, normed_out, grad_out, gate_out, up_out, hid_out, mlp_out, sums_ref,
    top_s, row_s, q_s, k_s, w_s, pre_s, gs, ws, mine, wf_s, bf_s, low_ref, gated_ref, full_ref,
    wg_s, wu_s, wd_s, cot_s, mid_s, normed_s, grad_s, gate_s, up_s, hid_s, mlp_s, osem, *sem,
):
    step = pl.program_id(0)
    seq = x_ref.shape[0]
    length = length_ref[0]
    here = Place()
    me, right, left, far = (lax.rem(here.my + by, Y) for by in (0, 1, 3, 2))
    sibling, right1, left1, right2, left2 = here.peers()
    c, p1, p2, half, quarter = here.c, here.p1, here.p2, seq // 2, seq // Y
    cross_order = (p2, here.l2, here.r2, here.o2)

    def plane(j):
        return link(mine, ws.at[c, p2, p1, 2 - j], *sem[2:4], j, (here.dp, (right, far, left)[j]))

    def torus(stage, j):
        if stage == 0:
            at, spots, to = (lambda p: ws.at[c, p2, p]), (p1, here.l1, here.r1), (right1, left1)
        else:
            at, spots, to = (lambda p: ws.at[c, p]), (p2, here.l2, here.r2), (right2, left2)
        spot, part, side = ((0, 0, 0), (0, 1, 0), (0, 0, 1), (0, 1, 1), (1, 0, 0), (2, 1, 1))[j]
        cut = (slice(0, 2), slice(2, 4 if stage else 3))[part]
        piece = at(spots[spot]).at[cut]
        return link(piece, piece, *sem[4 + 2 * stage : 6 + 2 * stage], j, to[side])

    def cross(j):
        piece = ws.at[c, cross_order[j]]
        return link(piece, piece, *sem[8:10], j, sibling)

    def gate(pair, j):
        owner, part, to = (
            (me, 0, right), (me, 1, right), (me, 0, left), (me, 1, left), (left, 0, right), (right, 1, left)
        )[j]
        piece = gs.at[pair, owner, part * half : part * half + half]
        return link(piece, piece, *sem[0:2], pair * 6 + j, (here.dp, to))

    def hand_on(pair, come, go):
        gate(pair, come).wait_recv()
        gate(pair, go).start()

    def flush(j):
        src, dst = (
            (low_ref, low_out),
            (full_ref, full_out),
            (rows_of(gated_ref, me * quarter, quarter), gated_out),
            (wg_in, wg_s),
            (wu_in, wu_s),
            (wd_in, wd_s),
        )[j]
        return pltpu.make_async_copy(src, dst, osem.at[j])

    def leave(j, chunk):
        src, dst = (
            (mid_s, mid_out), (normed_s, normed_out), (grad_s, grad_out), (gate_s, gate_out),
            (up_s, up_out), (hid_s, hid_out), (mlp_s, mlp_out),
        )[j]
        return pltpu.make_async_copy(src, dst.at[rows_at(chunk, half)], osem.at[6 + j])

    def come(chunk):
        return pltpu.make_async_copy(cot_in.at[rows_at(chunk, half)], cot_s, osem.at[13])

    def pass_on(make):
        make(0).wait_recv()
        make(4).start()
        make(3).wait_recv()
        make(5).start()

    def arrived(make):
        for j in (1, 2, 4, 5):
            make(j).wait_recv()

    @pl.when(step == 0)
    def _():
        tall, wide = ws.shape[4], ws.shape[5]
        two = w_ref[
            pl.ds(pl.multiple_of(here.chip // 2 * (2 * tall), 16), 2 * tall),
            pl.ds(pl.multiple_of(c * wide, 128), wide),
        ].astype(F32)
        mine[...] = jnp.where(lax.rem(here.chip, 2) == 0, two[0:tall], two[tall:])
        meet([(here.dp, right), (here.dp, left), (here.dp, far)] + here.peers())
        for j in range(3):
            plane(j).start()

    @pl.when(step == 0)
    def _():
        def norm(i, carry):
            at = rows_at(i, 128)
            x = x_ref[at, :].astype(F32)
            r = lax.rsqrt(jnp.mean(x * x, axis=1, keepdims=True) + EPSILON)
            low_ref[at, :] = (x * r * gain_row(gain_ref)).astype(jnp.bfloat16)
            return carry

        lax.fori_loop(0, seq // 128, norm, 0)
        flush(0).start()
        heads = wf_ref.shape[0]
        wf_s[...] = jnp.zeros_like(wf_s)
        wf_s[0:heads, :] = wf_ref[...]
        bf_s[...] = jnp.zeros_like(bf_s)
        bf_s[:, 0:heads] = bf_ref[...].astype(F32)
        for j in range(3):
            plane(j).wait_recv()
        for j in range(4):
            torus(0, j).start()
        pre = mm_t(wf_s[...], low_ref[...])[0:8] + jnp.broadcast_to(bf_s[...], (PAIR, PAIR)).T[0:8, 0:1]
        fall = jnp.minimum(pre, 0.0) - jnp.log1p(jnp.exp(-jnp.abs(pre)))
        decay = running_sum(fall)
        column = lax.broadcasted_iota(jnp.int32, decay.shape, 1)
        decay_ref[0] = decay
        decay_ref[1] = jax.nn.sigmoid(-pre)
        row_s[...] = jnp.where(column < length, decay, -NEG)
        final = jnp.sum(jnp.where(column == length - 1, decay, 0.0), axis=1, keepdims=True)
        top = jnp.where(column < length, decay, final)
        top_s[...] = jnp.concatenate([top, jnp.zeros((PAIR - 8, seq), F32)], axis=0).T

    for j, ref in enumerate((wq_ref, wk_ref, wv_ref, wo_ref)):
        w_s[:, j * PAIR : j * PAIR + PAIR] = ref[...]
    pre_s[...] = mm(low_ref[...], w_s[...])

    def norms(i, carry):
        at = rows_at(i, 128)
        for j, n_ref, s, col in ((0, qn_ref, q_s, 0), (1, kn_ref, k_s, 2)):
            pre = pre_s[at, j * PAIR : j * PAIR + PAIR]
            a, b = halves_mean(pre * pre)
            a, b = lax.rsqrt(a + EPSILON), lax.rsqrt(b + EPSILON)
            n = pre * jnp.where(first_head(pre.shape), a, b)
            n_ref[at, :] = n
            s[at, :] = n.astype(jnp.bfloat16)
            here = jnp.where(lane_is(pre.shape, col), a, jnp.where(lane_is(pre.shape, col + 1), b, 0.0))
            stat_ref[at, :] = here if col == 0 else stat_ref[at, :] + here
        v_ref[at, :] = pre_s[at, 2 * PAIR : 3 * PAIR].astype(jnp.bfloat16)
        sig_ref[at, :] = jax.nn.sigmoid(pre_s[at, 3 * PAIR : 4 * PAIR])
        return carry

    lax.fori_loop(0, seq // 128, norms, 0)

    @pl.when(step == 1)
    def _():
        for j in (3, 4, 5):
            flush(j).start()
        come(0).start()

    lines = [one_row(row_s, 2 * step + head) for head in (0, 1)]
    first = first_head((128, PAIR))
    zero = jnp.zeros((128, PAIR), jnp.bfloat16)
    upper = lax.broadcasted_iota(jnp.int32, (128, 128), 1) > lax.broadcasted_iota(
        jnp.int32, (128, 128), 0
    )
    for i in range(seq // 128):
        at, n = slice(i * 128, i * 128 + 128), i * 128 + 128
        q = q_s[at, :]
        two = jnp.concatenate([jnp.where(first, q, zero), jnp.where(first, zero, q)], axis=0)
        raw = mm_t(two, k_s[0:n, :]) * (HEAD ** (-0.5))
        probs = []
        for head in (0, 1):
            column = jnp.sum(
                jnp.where(lane_is((128, PAIR), 2 * step + head), top_s[at, :], 0.0), axis=1, keepdims=True
            )
            s = raw[head * 128 : head * 128 + 128] + (column - lines[head][:, 0:n])
            diagonal = jnp.where(upper, NEG, s[:, n - 128 :])
            s = diagonal if i == 0 else jnp.concatenate([s[:, : n - 128], diagonal], axis=1)
            p = jnp.exp(s)
            probs.append((p * (1.0 / jnp.sum(p, axis=1, keepdims=True))).astype(jnp.bfloat16))
        both = mm(jnp.concatenate(probs, axis=0), v_ref[0:n, :])
        out = jnp.where(first, both[0:128], both[128:])
        att_ref[at, :] = out
        gs[step, me, at, :] = (out * sig_ref[at, :]).astype(jnp.bfloat16).astype(F32)
        if n == half:
            gate(step, 0).start()
            gate(step, 2).start()

            @pl.when(step > 0)
            def _():
                hand_on(step - 1, 0, 4)

            @pl.when(step == 0)
            def _():
                pass_on(lambda j: torus(0, j))


    gate(step, 3).start()

    @pl.when(step == 0)
    def _():
        gate(0, 1).start()
        arrived(lambda j: torus(0, j))
        for j in range(4):
            torus(1, j).start()
        cross(0).start()

    @pl.when(step > 0)
    def _():
        hand_on(step - 1, 3, 5)

    @pl.when(step == pl.num_programs(0) - 1)
    def _():
        pairs = gs.shape[0]
        pass_on(lambda j: torus(1, j))
        torus(1, 1).wait_recv()
        cross(1).start()
        torus(1, 2).wait_recv()
        cross(2).start()
        hand_on(step, 0, 4)
        for pair in range(1, pairs):
            gate(pair, 1).start()
        hand_on(step, 3, 5)
        torus(1, 4).wait_recv()
        torus(1, 5).wait_recv()
        cross(3).start()
        for j in range(4):
            cross(j).wait_recv()
        tall, wide, shard = ws.shape[4], ws.shape[5], w_ref.shape[0]

        rows_of(full_ref, me * shard, shard)[...] = w_ref[...]

        def turn(k, carry):
            on, m = k // 8, lax.rem(k, 8)
            x, z = m // 2, lax.rem(m, 2) * 2
            y = lax.rem(me + on + 1, Y)
            rows = pl.ds(pl.multiple_of(y * shard + m * 2 * tall, 16), 2 * tall)
            for h, one, two in (
                (0, ws[0, z, x, on], ws[0, z + 1, x, on]),
                (1, ws[1, x, z, on], ws[1, x, z + 1, on]),
            ):
                both = jnp.concatenate([one, two], axis=0).astype(jnp.bfloat16)
                full_ref[rows, h * wide : h * wide + wide] = both
            return carry

        lax.fori_loop(0, 8 * (Y - 1), turn, 0)
        flush(1).start()
        for j in (3, 4, 5):
            flush(j).wait()
        outer, inner = full_ref.shape[1] // 2, wg_s.shape[1] // 2
        columns = lambda k, size: pl.ds(pl.multiple_of(k * size, size), size)
        sums_ref[...] = jnp.zeros_like(sums_ref)

        def feed_forward(chunk):
            rows = rows_at(chunk, half)
            for part, names in enumerate(((2, 4), (1, 5))):

                @pl.when(chunk == part)
                def _():
                    for pair in range(pairs):
                        for j in names:
                            gate(pair, j).wait_recv()

            for pair in range(pairs):
                for y in range(Y):
                    lane = (y * pairs + pair) * PAIR
                    gated_ref[rows, lane : lane + PAIR] = gs[pair, y, rows, :].astype(jnp.bfloat16)

            @pl.when(chunk == 1)
            def _():
                flush(2).start()
                for j in range(7):
                    leave(j, 0).wait()
                come(1).start()

            kept = lax.broadcasted_iota(jnp.int32, (half, 1), 0) + chunk * half < length

            def project(k):
                at = columns(k, outer)
                branch = mm(gated_ref[rows, :], full_ref[:, at])
                x = x_ref[rows, at].astype(F32)
                mid_s[:, at] = x + branch
                for row, value in ((0, x), (1, branch)):
                    value = jnp.where(kept, value * value, 0.0)
                    sums_ref[row : row + 1, at] = sums_ref[row : row + 1, at] + jnp.sum(
                        value, axis=0, keepdims=True
                    )

            each(0, 2, project)
            leave(0, chunk).start()

            def norm(i, carry):
                at = rows_at(i, 128)
                mid = mid_s[at, :]
                r = lax.rsqrt(jnp.mean(mid * mid, axis=1, keepdims=True) + EPSILON)
                normed_s[at, :] = (mid * r * gain_row(gain2_ref)).astype(jnp.bfloat16)
                return carry

            lax.fori_loop(0, half // 128, norm, 0)
            leave(1, chunk).start()

            def hidden(k):
                at = columns(k, inner)
                gate_s[:, at] = mm(normed_s[...], wg_s[:, at])
                up_s[:, at] = mm(normed_s[...], wu_s[:, at])
                pre = gate_s[:, at]
                hid_s[:, at] = (pre * jax.nn.sigmoid(pre) * up_s[:, at]).astype(jnp.bfloat16)

            each(0, 2, hidden)
            for j in (3, 4, 5):
                leave(j, chunk).start()

            come(chunk).wait()
            grad_s[...] = jnp.where(kept, cot_s[...].astype(F32), 0.0).astype(jnp.bfloat16)
            leave(2, chunk).start()

            def project_out(k):
                at = columns(k, outer)
                mlp_s[:, at] = mm(hid_s[...], wd_s[:, at])

            each(0, 2, project_out)
            leave(6, chunk).start()

        each(0, 2, feed_forward)
        for j in range(7):
            leave(j, 1).wait()
        for j in range(3):
            flush(j).wait()
            plane(j).wait_send()
        for stage in (0, 1):
            for j in range(6):
                torus(stage, j).wait_send()
        for j in range(4):
            cross(j).wait_send()
        for pair in range(pairs):
            for j in range(6):
                gate(pair, j).wait_send()


def forward(
    tokens, cotangent, length, gain, wq, wk, wv, wo, wf, bf, w_out, gain2, wg, wu, wd, call_id
):
    seq, width = tokens.shape
    heads, hidden, half = wq.shape[1], wg.shape[1], seq // 2
    weights = pl.BlockSpec((width, PAIR), lambda i, _: (0, i))
    lanes = pl.BlockSpec((seq, PAIR), lambda i, _: (0, i))
    low = jnp.bfloat16
    half_rows = lambda w, t=F32: pltpu.VMEM((half, w), t)
    return local_call(
        forward_kernel,
        heads // PAIR,
        [whole((seq, width)), whole((width,))] + [weights] * 4
        + [whole(wf.shape), whole(bf.shape), whole(w_out.shape), whole((width,))] + [HBM] * 4,
        [HBM] + [lanes] * 6 + [whole((2, 8, seq))] + [HBM] * 9 + [whole((2, width))],
        [
            struct(seq, width, t=low), struct(seq, heads), struct(seq, heads), struct(seq, heads, t=low),
            struct(seq, heads), struct(seq, heads), struct(seq, heads),
            struct(2, 8, seq), struct(seq // Y, heads * Y, t=low), struct(heads * Y, width, t=low),
            struct(seq, width), struct(seq, width, t=low), struct(seq, width, t=low),
            struct(seq, hidden), struct(seq, hidden), struct(seq, hidden, t=low), struct(seq, width),
            struct(2, width),
        ],
        [
            pltpu.VMEM((seq, PAIR), F32),
            pltpu.VMEM((8, seq), F32),
            pltpu.VMEM((seq, PAIR), low),
            pltpu.VMEM((seq, PAIR), low),
            pltpu.VMEM((width, 4 * PAIR), low),
            pltpu.VMEM((seq, 4 * PAIR), F32),
            pltpu.VMEM((heads // PAIR, Y, seq, PAIR), F32),
            pltpu.VMEM((2, 4, 4, Y - 1, heads // 16, width // 2), F32),
            pltpu.VMEM((heads // 16, width // 2), F32),
            pltpu.VMEM((16, width), low),
            pltpu.VMEM((1, PAIR), F32),
            pltpu.VMEM((seq, width), low),
            pltpu.VMEM((seq, width), low),
            pltpu.VMEM((heads * Y, width), low),
            pltpu.VMEM((width, hidden), low),
            pltpu.VMEM((width, hidden), low),
            pltpu.VMEM((hidden, width), low),
            half_rows(width, low), half_rows(width), half_rows(width, low), half_rows(width, low),
            half_rows(hidden), half_rows(hidden), half_rows(hidden, low), half_rows(width),
            pltpu.SemaphoreType.DMA((14,)),
        ]
        + sems(6 * (heads // PAIR), 3, 6, 6, 4),
        63, 17, 60, call_id,
    )(length, tokens, gain, wq, wk, wv, wo, wf, bf, w_out, gain2, cotangent, wg, wu, wd)


def copier(sem):
    count = iter(range(sem.shape[0]))

    def copy(src, dst):
        return load(src, dst, sem.at[next(count)])

    return copy


def reduce_links(rows, x, opp, nbr, held, sem):
    dp, me = lax.axis_index("dp"), lax.axis_index("mp")
    right, left, far = lax.rem(me + 1, Y), lax.rem(me + 3, Y), lax.rem(me + 2, Y)
    q, h = rows // Y, rows // Y // 2

    def message(name):
        src, dst, to = {
            "oR": (lambda: rows_of(x, far * q, h), lambda: opp.at[0], right),
            "oL": (lambda: rows_of(x, far * q + h, h), lambda: opp.at[1], left),
            "iR": (lambda: rows_of(x, right * q + h, h), lambda: nbr.at[0, h:q], right),
            "iL": (lambda: rows_of(x, left * q, h), lambda: nbr.at[1, 0:h], left),
            "dR": (lambda: held.at[0], lambda: nbr.at[0, 0:h], right),
            "dL": (lambda: held.at[1], lambda: nbr.at[1, h:q], left),
        }[name]
        return link(src(), dst(), *sem, STEPS.index(name), (dp, to))

    return message, me, right, left, [(dp, right), (dp, left)]


def mlp_backward_kernel(
    length_ref, grad_in, low_in, gate_in, up_in, hid_in, wd_in, wg_in, wu_in, x_ref, mid_ref,
    back_out, gd_out, gg_out, gu_out, layer_ref, square_ref,
    grad_ref, low_ref, gate_ref, up_ref, hid_ref, wd_ref, wg_ref, wu_ref,
    dg_s, du_s, back_s, bufs, opp, nbr, held, own_s, mid_s, csem, *sem,
):
    seq, width = grad_ref.shape
    units = wd_ref.shape[0] // 2
    low16 = jnp.bfloat16
    message, me, right, left, peers = reduce_links(seq, x_ref, opp, nbr, held, sem)
    q, h = seq // Y, seq // Y // 2
    copy = copier(csem)
    need = [
        copy(grad_in, grad_ref),
        copy(wd_in.at[0:units], wd_ref.at[0:units]),
        copy(gate_in.at[:, 0:units], gate_ref.at[:, 0:units]),
        copy(up_in.at[:, 0:units], up_ref.at[:, 0:units]),
    ]
    meet(peers)
    for name in STEPS[:4]:
        message(name).start()
    for c in need[0:2]:
        c.wait()
    next_low, next_hid = copy(low_in, low_ref), copy(hid_in, hid_ref)
    more = [
        copy(wd_in.at[units:], wd_ref.at[units:]),
        copy(gate_in.at[:, units:], gate_ref.at[:, units:]),
        copy(up_in.at[:, units:], up_ref.at[:, units:]),
    ]
    weights = [copy(wg_in, wg_ref), copy(wu_in, wu_ref)]
    adds = [
        copy(rows_of(x_ref, right * q, h), held.at[0]),
        copy(rows_of(x_ref, left * q + h, h), held.at[1]),
        copy(rows_of(x_ref, me * q, q), own_s),
        copy(rows_of(mid_ref, me * q, q), mid_s),
    ]
    spots = (gd_out, gg_out, gu_out)
    columns = lambda j: pl.ds(pl.multiple_of(j * units, units), units)
    flush = lambda j, which: pltpu.make_async_copy(
        bufs.at[which, j], spots[which].at[:, columns(j)], csem.at[csem.shape[0] - 6 + which * 2 + j]
    )

    def write(which, left_of, right_of, j):
        slot, at = bufs.at[which, j], columns(j)

        def rows(i, carry):
            part = rows_at(i, 768)
            slot[part, :] = t_mm(left_of[:, part], right_of[:, at])
            return carry

        lax.fori_loop(0, width // 768, rows, 0)
        flush(j, which).start()

    def tile(j):
        at = columns(j)

        @pl.when(j == 1)
        def _():
            for c in more:
                c.wait()

        grad = mm_t(grad_ref[...], wd_ref[at, :])

        @pl.when(j == 0)
        def _():
            for c in need[2:4]:
                c.wait()

        gate = gate_ref[:, at]
        sig = jax.nn.sigmoid(gate)
        dg_s[:, at] = (grad * up_ref[:, at] * (sig * (1.0 + gate * (1.0 - sig)))).astype(low16)
        du_s[:, at] = (grad * (gate * sig)).astype(low16)

        @pl.when(j == 0)
        def _():
            next_low.wait()
            next_hid.wait()

        write(0, grad_ref, hid_ref, j)
        write(1, low_ref, dg_s, j)

        @pl.when(j == 1)
        def _():
            for part, (come, go) in enumerate((("oR", "dR"), ("oL", "dL"))):
                message(come).wait_recv()
                adds[part].wait()
                held[part] = held[part] + opp[part]
                message(go).start()

        write(2, low_ref, du_s, j)

    each(0, 2, tile)
    for c in weights:
        c.wait()

    def back(i, carry):
        rows = rows_at(i, 768)
        back_s[:, rows] = mm_t(dg_s[...], wg_ref[rows, :])
        back_s[:, rows] = back_s[:, rows] + mm_t(du_s[...], wu_ref[rows, :])
        return carry

    lax.fori_loop(0, width // 768, back, 0)
    last = copy(back_s, back_out)
    adds[2].wait()
    adds[3].wait()
    sums = 0.0
    for part, names in enumerate((("dR", "iL"), ("iR", "dL"))):
        for name in names:
            message(name).wait_recv()
        at = slice(part * h, part * h + h)
        branch = own_s[at, :] + nbr[0, at] + nbr[1, at]
        layer_ref[at, :] = (mid_s[at, :] + branch).astype(low16).astype(F32)
        row = lax.broadcasted_iota(jnp.int32, (h, 1), 0) + (me * q + part * h)
        kept = jnp.where(row < length_ref[0], branch * branch, 0.0)
        sums = sums + jnp.sum(kept, axis=0, keepdims=True)
    square_ref[...] = sums
    last.wait()
    for j in (0, 1):
        for which in range(3):
            flush(j, which).wait()
    for name in STEPS[:6]:
        message(name).wait_send()


def mlp_backward(length, grad, low, gate, up, hid, wg, wu, wd, branch, mid, call_id):
    seq, width = low.shape
    hidden = wg.shape[1]
    quarter = seq // Y
    low16 = jnp.bfloat16
    smem = pl.BlockSpec(memory_space=pltpu.SMEM)
    inputs = (grad, low, gate, up, hid, wd, wg, wu)
    return pl.pallas_call(
        mlp_backward_kernel,
        in_specs=[smem] + [HBM] * 10,
        out_specs=[HBM] * 4 + [VMEM] * 2,
        out_shape=[struct(seq, width)] + [struct(width, hidden)] * 3
        + [struct(quarter, width), struct(1, width)],
        scratch_shapes=[pltpu.VMEM(a.shape, a.dtype) for a in inputs]
        + [pltpu.VMEM((seq, hidden), low16)] * 2
        + [pltpu.VMEM((seq, width), F32), pltpu.VMEM((3, 2, width, hidden // 2), F32)]
        + ring_scratch(quarter, width)
        + [pltpu.VMEM((quarter, width), F32)] * 2
        + [pltpu.SemaphoreType.DMA((22,))]
        + sems(6),
        compiler_params=pltpu.CompilerParams(
            vmem_limit_bytes=62 << 20, collective_id=call_id, has_side_effects=True
        ),
    )(length, *inputs, branch, mid)


def backward_kernel(
    length_ref, gg_ref, low_in, qn_ref, kn_ref, v_ref, sig_ref, att_ref, stat_ref,
    decay_ref, wq_ref, wk_ref, wv_ref, wo_ref, wf_ref, own_ref, gated_ref, layer_ref,
    back_out, four_out, gout_out, gf_ref, bias_ref, out_ref,
    k_s, do_s, line_s, top_s, both_s, dq_s, dk_s, dv_s, all_s, fall_s, w_s, wf_s, lay_s, back_ref, wide_s, low_ref, osem,
    *sem,
):
    step = pl.program_id(0)
    seq, width = low_ref.shape
    length = length_ref[0]
    low16 = jnp.bfloat16
    wide = 4 * PAIR
    dp, me = lax.axis_index("dp"), lax.axis_index("mp")
    right, left = lax.rem(me + 1, Y), lax.rem(me + 3, Y)
    q, h = seq // Y, seq // Y // 2

    def spread(j):
        owner, part, to = (
            (me, 0, right), (me, 1, right), (me, 0, left), (me, 1, left), (left, 0, right), (right, 1, left)
        )[j]
        piece = rows_of(lay_s, owner * q + part * h, h)
        source = layer_ref.at[part * h : part * h + h] if j < 4 else piece
        return link(source, piece, *sem, j, (dp, to))

    def fetch(j):
        pair = ((layer_ref, rows_of(lay_s, me * q, q)), (low_in, low_ref))[j]
        return pltpu.make_async_copy(*pair, osem.at[5 + j])

    @pl.when(step == 0)
    def _():
        meet([(dp, right), (dp, left)])
        for j in range(4):
            spread(j).start()
        for j in (0, 1):
            fetch(j).start()

    @pl.when(step == 2)
    def _():
        spread(0).wait_recv()
        spread(4).start()
        spread(3).wait_recv()
        spread(5).start()

    @pl.when(step == 0)
    def _():
        heads = wf_ref.shape[0]
        wf_s[...] = jnp.zeros_like(wf_s)
        wf_s[0:heads, :] = wf_ref[...]
        decay = decay_ref[0]
        column = lax.broadcasted_iota(jnp.int32, decay.shape, 1)
        final = jnp.sum(jnp.where(column == length - 1, decay, 0.0), axis=1, keepdims=True)
        line_s[...] = jnp.where(column < length, decay, final)
        masked = jnp.where(column < length, decay, -NEG)
        top_s[...] = jnp.concatenate([masked, jnp.zeros((PAIR - 8, seq), F32)], axis=0).T
        fall_s[...] = jnp.zeros_like(fall_s)

    base = pl.multiple_of(step * wide, wide)
    part = lambda j: pl.ds(pl.multiple_of(base + j * PAIR, PAIR), PAIR)
    for j, w_ref in enumerate((wq_ref, wk_ref, wv_ref, wo_ref)):
        w_s[:, part(j)] = w_ref[...]
    first = first_head((seq, PAIR))
    gg, sig = gg_ref[...], sig_ref[...]
    do_s[...] = (gg * sig).astype(low16)
    all_s[:, part(3)] = (gg * att_ref[...] * sig * (1.0 - sig)).astype(low16)
    k_s[...] = kn_ref[...].astype(low16)
    dk_s[...] = jnp.zeros_like(dk_s)
    dv_s[...] = jnp.zeros_like(dv_s)
    columns, lines = [], [one_row(line_s, 2 * step + head) for head in (0, 1)]
    for head in (0, 1):
        column = jnp.sum(
            jnp.where(lane_is((seq, PAIR), 2 * step + head), top_s[...], 0.0), axis=1, keepdims=True
        )
        columns.append(column)
    both_s[...] = jnp.concatenate([jnp.broadcast_to(column, (seq, PAIR)) for column in columns], axis=1)
    ones = jnp.concatenate(
        [jnp.where(lane_is((128, PAIR), 2 * step + head), 1.0, 0.0) for head in (0, 1)], axis=0
    ).astype(low16)
    lanes = lax.broadcasted_iota(jnp.int32, (seq, PAIR), 1)
    marks = jnp.where(lanes // 2 == step, 1.0, 0.0).astype(low16)
    block = first_head((128, PAIR))
    zero = jnp.zeros((128, PAIR), low16)
    lower = lax.broadcasted_iota(jnp.int32, (128, 256), 0) > lax.rem(
        lax.broadcasted_iota(jnp.int32, (128, 256), 1), 128
    )
    for i in range(seq // 128):
        at, n = slice(i * 128, i * 128 + 128), i * 128 + 128
        query = qn_ref[at, :].astype(low16)
        do = do_s[at, :]
        two_q, two_do = (
            jnp.concatenate([jnp.where(block, t, zero), jnp.where(block, zero, t)], axis=0)
            for t in (query, do)
        )
        s = mm_t(k_s[0:n, :], two_q) * (HEAD ** (-0.5))
        s = s + (jnp.concatenate([line[:, at] for line in lines], axis=1) - both_s[0:n, :])
        diagonal = jnp.where(lower, NEG, s[n - 128 :, :])
        s = diagonal if i == 0 else jnp.concatenate([s[: n - 128, :], diagonal], axis=0)
        p = jnp.exp(s)
        p = p * (1.0 / jnp.sum(p, axis=0, keepdims=True))
        gp = mm_t(v_ref[0:n, :], two_do)
        ds = (p * (gp - jnp.sum(p * gp, axis=0, keepdims=True))).astype(low16)
        dv_s[0:n, :] = dv_s[0:n, :] + mm(p.astype(low16), two_do)
        dk_s[0:n, :] = dk_s[0:n, :] + mm(ds, jnp.concatenate([two_q, ones], axis=1))
        pieces = t_mm(ds, jnp.concatenate([k_s[0:n, :], marks[0:n]], axis=1))
        one, two = pieces[0:128], pieces[128:]
        dq_s[at, :] = jnp.where(block, one[:, 0:PAIR], two[:, 0:PAIR])
        fall_s[at, :] = fall_s[at, :] + (
            jnp.where(lane_is((128, PAIR), 2 * step), one[:, PAIR:], 0.0)
            + jnp.where(lane_is((128, PAIR), 2 * step + 1), two[:, PAIR:], 0.0)
        )
    fall_s[...] = fall_s[...] - dk_s[:, PAIR:]
    stat = stat_ref[...]
    for e, n_ref, col, to in ((dq_s, qn_ref, 0, 0), (dk_s, kn_ref, 2, 1)):
        e = e[:, 0:PAIR] * (HEAD ** (-0.5))
        n = n_ref[...]
        a, b = halves_mean(e * n)
        r = jnp.where(first, stat[:, col : col + 1], stat[:, col + 1 : col + 2])
        all_s[:, part(to)] = (r * (e - n * jnp.where(first, a, b))).astype(low16)
    all_s[:, part(2)] = dv_s[...].astype(low16)
    slot = lax.rem(step, 2)

    @pl.when(step == 0)
    def _():
        for j in (0, 1):
            fetch(j).wait()

    def flush(j, at, step):
        columns = pl.ds(pl.multiple_of(step * wide, wide), wide)
        out = (four_out, gout_out)[j].at[:, columns]
        return pltpu.make_async_copy(wide_s.at[at, j], out, osem.at[at * 2 + j])

    @pl.when(step == 2)
    def _():
        for j in (0, 1):
            flush(j, 0, 0).wait()

    def grads(k, carry):
        rows = rows_at(k, 768)
        wide_s[slot, 0, rows, :] = t_mm(low_ref[:, rows], all_s[:, pl.ds(base, wide)])
        wide_s[slot, 1, rows, :] = t_mm(own_ref[:, rows].astype(low16), gated_ref[...])
        return carry

    lax.fori_loop(0, width // 768, grads, 0)
    for j in (0, 1):
        flush(j, slot, step).start()

    @pl.when(step == pl.num_programs(0) - 1)
    def _():
        fall = running_sum(fall_s[...].T[0:8], backward=True) * decay_ref[1]
        fall = jnp.concatenate([fall, jnp.zeros_like(fall)], axis=0).astype(low16)
        bias = jnp.sum(fall.astype(F32), axis=1, keepdims=True)
        bias_ref[...] = jnp.broadcast_to(bias[0:8], (8, PAIR))
        gf_ref[...] = mm(fall, low_ref[...])[0:8]

        def tail(k, carry):
            rows = rows_at(k, 768)
            back_ref[:, rows] = mm_t(all_s[...], w_s[rows, :])
            back_ref[:, rows] = back_ref[:, rows] + t_mm(fall, wf_s[:, rows])
            return carry

        lax.fori_loop(0, width // 768, tail, 0)
        last = load(back_ref, back_out, osem.at[4])
        for j in (1, 2, 4, 5):
            spread(j).wait_recv()
        out_ref[...] = lay_s[...].astype(low16)
        for at, done in ((1, 1), (0, 2)):
            for j in (0, 1):
                flush(j, at, done).wait()
        last.wait()
        for j in range(6):
            spread(j).wait_send()


def backward_attention(place, gg, low, qn, kn, v, sig, att, stat, decay, wq, wk, wv, wo, wf, own, gated, layer, call_id):
    seq, width = low.shape
    heads = wq.shape[1]
    weights = pl.BlockSpec((width, PAIR), lambda i, _: (0, i))
    lanes = pl.BlockSpec((seq, PAIR), lambda i, _: (0, i))
    full = whole((seq, width))
    low16 = jnp.bfloat16
    return local_call(
        backward_kernel,
        heads // PAIR,
        [lanes, HBM] + [lanes] * 6 + [whole((2, 8, seq))] + [weights] * 4
        + [whole(wf.shape), whole(own.shape)]
        + [pl.BlockSpec((own.shape[0], 4 * PAIR), lambda i, _: (0, i)), HBM],
        [HBM, HBM, HBM, whole((8, width)), whole((8, PAIR)), full],
        [
            struct(seq, width), struct(width, 4 * heads), struct(width, width), struct(8, width),
            struct(8, PAIR), struct(seq, width, t=low16),
        ],
        [
            pltpu.VMEM((seq, PAIR), low16),
            pltpu.VMEM((seq, PAIR), low16),
            pltpu.VMEM((8, seq), F32),
            pltpu.VMEM((seq, PAIR), F32),
            pltpu.VMEM((seq, 2 * PAIR), F32),
            pltpu.VMEM((seq, PAIR), F32),
            pltpu.VMEM((seq, 2 * PAIR), F32),
            pltpu.VMEM((seq, PAIR), F32),
            pltpu.VMEM((seq, 4 * heads), low16),
            pltpu.VMEM((seq, PAIR), F32),
            pltpu.VMEM((width, 4 * heads), low16),
            pltpu.VMEM((16, width), low16),
            pltpu.VMEM((seq, width), F32),
            pltpu.VMEM((seq, width), F32),
            pltpu.VMEM((2, 2, width, 4 * PAIR), F32),
            pltpu.VMEM((seq, width), low16),
            pltpu.SemaphoreType.DMA((7,)),
        ]
        + sems(6),
        62, 14, 50, call_id,
    )(place, gg, low, qn, kn, v, sig, att, stat, decay, wq, wk, wv, wo, wf, own, gated, layer)


def finish_kernel(
    grad_in, layer_in, wout_hbm, four_hbm, mlp_hbm, sums_hbm,
    grad_ref, layer_ref, wout_ref, q_ref, k_ref, v_ref, o_ref, gate_ref, up_ref, down_ref,
    gain_ref, gain2_ref, fall_ref, rms_ref, bias_ref,
    grad_s, layer_s, four_in, mlp_in, sums_in, sem,
):
    copy = copier(sem)
    rows = grad_in.shape[0] // 4
    parts = [slice(j * rows, j * rows + rows) for j in range(4)]
    come = [(copy(grad_in.at[p], grad_s.at[p]), grad_s.at[p], grad_ref.at[p]) for p in parts]
    small = [copy(wout_hbm, wout_ref), copy(four_hbm, four_in), copy(mlp_hbm, mlp_in), copy(sums_hbm, sums_in)]
    come += [(copy(layer_in.at[p], layer_s.at[p]), layer_s.at[p], layer_ref.at[p]) for p in parts]
    copies = []

    def leave(some):
        for arrived, mid, dst in some:
            arrived.wait()
            copies.append(copy(mid, dst))

    leave(come[0:4])
    for c in small:
        c.wait()
    inner = q_ref.shape[1]
    for j, ref in enumerate((q_ref, k_ref, v_ref, o_ref)):
        for pair in range(inner // PAIR):
            lane = (pair * 4 + j) * PAIR
            ref[:, pair * PAIR : pair * PAIR + PAIR] = four_in[:, lane : lane + PAIR]
    units = gate_ref.shape[1]
    down_ref[...] = mlp_in[:, 0:units]
    gate_ref[...] = mlp_in[:, units : 2 * units]
    up_ref[...] = four_in[:, 4 * inner : 4 * inner + units]
    leave(come[4:8])
    share, width = gain_ref.shape[1], sums_in.shape[1]
    row = lax.broadcasted_iota(jnp.int32, (width, share), 0)
    lane = lax.broadcasted_iota(jnp.int32, (width, share), 1)
    pick = jnp.where(row == lane + lax.axis_index("dp") * share, 1.0, 0.0)
    own = jnp.dot(
        sums_in[...], pick, precision=lax.Precision.HIGHEST, preferred_element_type=F32
    )
    gain_ref[...] = own[0:1]
    gain2_ref[...] = own[1:2]
    fall_ref[...] = own[3 : 3 + fall_ref.shape[0]]
    square = lambda row, at: sums_in[row : row + 1, at * PAIR : at * PAIR + NBUCKET]
    squares = jnp.concatenate([square(9, 0), square(9, 1), square(2, 0)], axis=0)
    rms_ref[...] = jnp.sqrt(squares / (square(9, 2) * width))
    bias_ref[...] = sums_in[10:11, 0 : bias_ref.shape[1]]
    for c in copies:
        c.wait()


def finish(grad, layer, out_share, share, mlp_share, sums, heads):
    rows, inner = out_share.shape
    units = mlp_share.shape[1] // 2
    return pl.pallas_call(
        finish_kernel,
        out_shape=[
            struct(*grad.shape), struct(*layer.shape, t=layer.dtype), *[struct(rows, inner)] * 5,
            *[struct(rows, units)] * 3, struct(1, rows), struct(1, rows), struct(heads, rows),
            struct(3, NBUCKET), struct(1, heads),
        ],
        in_specs=[HBM] * 6,
        out_specs=[HBM, HBM] + [VMEM] * 13,
        scratch_shapes=[pltpu.VMEM(a.shape, a.dtype) for a in (grad, layer, share, mlp_share, sums)]
        + [pltpu.SemaphoreType.DMA((20,))],
        compiler_params=pltpu.CompilerParams(vmem_limit_bytes=60 << 20),
    )(grad, layer, out_share, share, mlp_share, sums)


def per_device(
    tokens, lengths, buckets, out_cotangent, gain_attn, w_query, w_key, w_value, w_outgate,
    w_forget, b_forget, w_out, gain_mlp, w_gate, w_up, w_down,
):
    x, cotangent = tokens[0], out_cotangent[0]
    heads = w_forget.shape[1]
    gain_in, gain_mid = gain_attn, gain_mlp
    weights = (w_query, w_key, w_value, w_outgate, w_forget.T)
    (
        low, qn, kn, value, sig, attended, stat, decay, gated, w_full,
        middle, mid_low, grad_rows, gate, up, hidden, mlp_local, squares,
    ) = forward(
        x, cotangent, lengths, gain_in, *weights, b_forget[None], w_out, gain_mid, w_gate, w_up, w_down, 0
    )
    mid_local, g_down, g_gate, g_up, layer_own, mlp_square = mlp_backward(
        lengths, grad_rows, mid_low, gate, up, hidden, w_gate, w_up, w_down, mlp_local, middle, 1
    )
    grad_own, gg, mlp_share, mlp_gain = reduce_middle(
        mid_local, middle, grad_rows, gain_mid, w_full, [g_down, g_gate],
        ((0, 0), (0, 1), (1, 0), (1, 1)), 2,
    )
    in_local, g_four, g_out, g_fall, bias, layer_out = backward_attention(
        lengths, gg, low, qn, kn, value, sig, attended, stat, decay, *weights, grad_own, gated,
        layer_own, 3,
    )
    small = (mlp_gain, g_fall, squares, mlp_square, bias, lengths, buckets)
    input_grad, out_share, share, sums = reduce_input(
        in_local, x, grad_own, gain_in, small, [g_out, g_four, g_up],
        ((0, 0), (0, 1), (0, 2), (1, 0), (1, 1), (1, 2), (2, 0), (2, 1)), 4,
    )
    (
        input_grad, layer_out, g_out, g_query, g_key, g_value, g_outgate, g_gate, g_up, g_down,
        g_gain, g_gain_mid, g_fall, rms, bias,
    ) = finish(input_grad, layer_out, out_share, share, mlp_share, sums, heads)
    return (
        layer_out[None],
        input_grad[None],
        g_gain[0],
        g_query,
        g_key,
        g_value,
        g_outgate,
        g_fall.T,
        bias[0],
        g_out.T,
        g_gain_mid[0],
        g_gate,
        g_up,
        g_down.T,
        rms,
    )


def solution(mesh):
    placed = (
        P("dp", None, None),
        P("dp"),
        P("dp"),
        P("dp", None, None),
        P(),
        P(None, "mp"),
        P(None, "mp"),
        P(None, "mp"),
        P(None, "mp"),
        P(None, "mp"),
        P("mp"),
        P("mp", None),
        P(),
        P(None, "mp"),
        P(None, "mp"),
        P("mp", None),
    )
    return jax.shard_map(
        per_device,
        mesh=mesh,
        in_specs=placed,
        out_specs=(
            P("dp", None, None),
            P("dp", None, None),
            P("dp"),
            P("dp", "mp"),
            P("dp", "mp"),
            P("dp", "mp"),
            P("dp", "mp"),
            P("dp", "mp"),
            P("mp"),
            P("mp", "dp"),
            P("dp"),
            P("dp", "mp"),
            P("dp", "mp"),
            P("mp", "dp"),
            P(),
        ),
        check_vma=False,
    )
```

```python
import functools

import jax
import jax.numpy as jnp
from jax import lax
from jax.experimental import pallas as pl
from jax.experimental.pallas import tpu as pltpu
from jax.sharding import PartitionSpec as P

NBUCKET = 4


EPSILON = 1e-06


MESH = pl.DeviceIdType.MESH
F32 = jnp.float32
Y = 4
STEP = 512
HBM = pl.BlockSpec(memory_space=pl.ANY)
VMEM = pl.BlockSpec(memory_space=pltpu.VMEM)
STEPS = ("oR", "oL", "iR", "iL", "dR", "dL", "gRa", "gRb", "gLa", "gLb", "fR", "fL")


def gain_row(ref):
    return ref[...].astype(F32).reshape(1, ref.shape[0])


def rows_of(ref, start, count):
    return ref.at[pl.ds(pl.multiple_of(start, 8), count)]


def meet(devices):
    barrier = pltpu.get_barrier_semaphore()
    for device in devices:
        pl.semaphore_signal(barrier, inc=1, device_id=device, device_id_type=MESH)
    pl.semaphore_wait(barrier, len(devices))


def link(src, dst, ssem, rsem, at, device):
    return pltpu.make_async_remote_copy(
        src_ref=src,
        dst_ref=dst,
        send_sem=ssem.at[at],
        recv_sem=rsem.at[at],
        device_id=device,
        device_id_type=MESH,
    )


def push(*args):
    copy = link(*args)
    copy.start()
    return copy


class YRing:
    def __init__(self, rows, waves, ssem, rsem):
        self.sems = (ssem, rsem)
        self.dp, self.me = lax.axis_index("dp"), lax.axis_index("mp")
        self.right, self.left = lax.rem(self.me + 1, Y), lax.rem(self.me + 3, Y)
        self.far = lax.rem(self.me + 2, Y)
        self.quarter, self.half = rows // Y, rows // Y // 2
        self.tall = self.half // waves
        self.sent = {}

    def neighbours(self):
        return [(self.dp, self.right), (self.dp, self.left)]

    def send(self, name, wave, src, dst, to):
        kind, index = divmod(STEPS.index(name), 6)
        at = kind * 12 + wave * 6 + index
        self.sent[name, wave] = push(src, dst, *self.sems, at, (self.dp, to))

    def rows(self, x, owner, part, wave):
        return rows_of(x, owner * self.quarter + part * self.half + wave * self.tall, self.tall)

    def fetch(self, x, held, own, sem):
        self.loads = [
            load(rows_of(x, self.right * self.quarter, self.half), held.at[0], sem.at[0]),
            load(rows_of(x, self.left * self.quarter + self.half, self.half), held.at[1], sem.at[1]),
            load(rows_of(x, self.me * self.quarter, self.quarter), own, sem.at[2]),
        ]

    def start(self, x, opp, nbr, wave):
        w = slice(wave * self.tall, wave * self.tall + self.tall)
        low = slice(self.half + wave * self.tall, self.half + wave * self.tall + self.tall)
        self.send("oR", wave, self.rows(x, self.far, 0, wave), opp.at[0, w], self.right)
        self.send("oL", wave, self.rows(x, self.far, 1, wave), opp.at[1, w], self.left)
        self.send("iR", wave, self.rows(x, self.right, 1, wave), nbr.at[0, low], self.right)
        self.send("iL", wave, self.rows(x, self.left, 0, wave), nbr.at[1, w], self.left)

    def relay(self, opp, nbr, held, wave):
        w = slice(wave * self.tall, wave * self.tall + self.tall)
        low = slice(self.half + wave * self.tall, self.half + wave * self.tall + self.tall)
        for part, (come, go, into, to) in enumerate(
            (("oR", "dR", nbr.at[0, w], self.right), ("oL", "dL", nbr.at[1, low], self.left))
        ):
            self.sent[come, wave].wait_recv()
            if wave == 0:
                self.loads[part].wait()
            held[part, w] = held[part, w] + opp[part, w]
            self.send(go, wave, held.at[part, w], into, to)

    def collect(self, own, nbr, part, wave):
        if part == 0 and wave == 0:
            self.loads[2].wait()
        for name in (("dR", "iL"), ("iR", "dL"))[part]:
            self.sent[name, wave].wait_recv()
        start = part * self.half + wave * self.tall
        at = slice(start, start + self.tall)
        return at, own[at, :] + nbr[0, at] + nbr[1, at]

    def spread(self, part, wave, own, out):
        tag, into = "ab"[part], self.rows(out, self.me, part, wave)
        start = part * self.half + wave * self.tall
        mine = own.at[start : start + self.tall]
        self.send("gR" + tag, wave, mine, into, self.right)
        self.send("gL" + tag, wave, mine, into, self.left)

    def forward(self, wave, out):
        for come, go, owner, part, to in (
            ("gRa", "fR", self.left, 0, self.right),
            ("gLb", "fL", self.right, 1, self.left),
        ):
            self.sent[come, wave].wait_recv()
            block = self.rows(out, owner, part, wave)
            self.send(go, wave, block, block, to)

    def arrive(self, wave):
        for name in ("gRb", "gLa", "fR", "fL"):
            self.sent[name, wave].wait_recv()

    def finish(self):
        for copy in self.sent.values():
            copy.wait_send()


def ring_scratch(quarter, columns):
    return [
        pltpu.VMEM((2, quarter // 2, columns), F32),
        pltpu.VMEM((2, quarter, columns), F32),
        pltpu.VMEM((2, quarter // 2, columns), F32),
    ]


def sems(*counts):
    return [pltpu.SemaphoreType.DMA((n,)) for n in counts for _ in (0, 1)]


class Place:
    def __init__(self):
        self.dp, self.my = lax.axis_index("dp"), lax.axis_index("mp")
        c, z, x = lax.rem(self.dp, 2), lax.rem(self.dp // 2, 4), self.dp // 8
        self.c, self.sib, self.chip = c, self.dp + 1 - 2 * c, x * 4 + z
        self.st1, self.st2 = 4 - 3 * c, 1 + 3 * c
        self.p1, self.p2 = x + c * (z - x), z + c * (x - z)
        step = lambda p, by: lax.rem(p + by, 4)
        self.r1, self.l1, self.o1 = (step(self.p1, by) for by in (1, 3, 2))
        self.r2, self.l2, self.o2 = (step(self.p2, by) for by in (1, 3, 2))

    def device(self, a, b):
        return ((a * self.st1 + b * self.st2) * 2 + self.c, self.my)

    def peers(self):
        return [
            (self.sib, self.my),
            self.device(self.r1, self.p2),
            self.device(self.l1, self.p2),
            self.device(self.p1, self.r2),
            self.device(self.p1, self.l2),
        ]


class ScatterSum:
    def __init__(self, here, sources, own, other, near, last, asem, bsem, lsem, ssem, rsem):
        self.here, self.sources = here, sources
        self.own, self.other, self.near, self.last = own, other, near, last
        self.asem, self.bsem, self.lsem, self.ssem, self.rsem = asem, bsem, lsem, ssem, rsem
        self.n = own.shape[0]
        self.sibling, *to = here.peers()
        self.to = (to[0:2], to[2:4])

    def message(self, name, k, stage):
        at = (k * 2 + stage) * 6 + STEPS.index(name)
        device = self.to[stage][0 if name[1] == "R" else 1]
        here, own = self.here, self.own.at[k]
        if stage:
            own, into, cut = own.at[here.p1], self.last.at[k], (slice(0, 24), slice(24, 48))
            far, right, left = here.o2, here.r2, here.l2
        else:
            into, cut = self.near.at[k], (slice(0, 2), slice(2, 4))
            far, right, left = here.o1, here.r1, here.l1
        row, part, slot = {
            "oR": (far, 0, 0),
            "oL": (far, 1, 1),
            "iR": (right, 1, 3),
            "iL": (left, 0, 4),
            "dR": (right, 0, 2),
            "dL": (left, 1, 5),
        }[name]
        return link(own.at[row, cut[part]], into.at[slot], self.ssem, self.rsem, at, device)

    def whole(self, k):
        own, other = self.own.at[k], self.other.at[k]
        return link(own, other, self.asem, self.bsem, k, self.sibling)

    def exchange(self, k):
        here = self.here
        ref, start, width = self.sources[k]

        def source(block):
            return ref.at[pl.ds(pl.multiple_of(block * 48, 16), 48), pl.ds(start, width)]

        def cross(i, carry):
            a, b = i // 4, lax.rem(i, 4)
            block = source((a * here.st2 + b * here.st1) * 2 + 1 - here.c)
            push(block, self.other.at[k, a, b], self.asem, self.bsem, k, self.sibling)
            return carry

        def fetch(i, carry):
            a, b = i // 4, lax.rem(i, 4)
            block = source((a * here.st1 + b * here.st2) * 2 + here.c)
            pltpu.make_async_copy(block, self.own.at[k, a, b], self.lsem.at[k]).start()
            return carry

        lax.fori_loop(0, 16, cross, 0)
        lax.fori_loop(0, 16, fetch, 0)

    def first(self, k):
        here, own, other = self.here, self.own, self.other
        pltpu.make_async_copy(own.at[k], own.at[k], self.lsem.at[k]).wait()
        self.whole(k).wait_recv()

        def add(p):
            def body(b, carry):
                own[k, p, b] = own[k, p, b] + other[k, p, b]
                return carry

            lax.fori_loop(0, 4, body, 0)

        add(here.o1)
        self.message("oR", k, 0).start()
        self.message("oL", k, 0).start()
        add(here.r1)
        self.message("iR", k, 0).start()
        add(here.l1)
        self.message("iL", k, 0).start()
        add(here.p1)

    def first_relay(self, k):
        here, own, near = self.here, self.own, self.near

        def add(p, at, slot):
            def body(b, carry):
                own[k, p, at + b] = own[k, p, at + b] + near[k, slot, b]
                return carry

            lax.fori_loop(0, 2, body, 0)

        self.message("oR", k, 0).wait_recv()
        add(here.r1, 0, 0)
        self.message("dR", k, 0).start()
        self.message("oL", k, 0).wait_recv()
        add(here.l1, 2, 1)
        self.message("dL", k, 0).start()

    def second(self, k):
        here, own, near = self.here, self.own, self.near
        for name in ("iR", "dR", "iL", "dL"):
            self.message(name, k, 0).wait_recv()

        def add(p):
            h, b = p // 2, lax.rem(p, 2)
            own[k, here.p1, p] = own[k, here.p1, p] + near[k, 2 + h, b] + near[k, 4 + h, b]

        add(here.o2)
        self.message("oR", k, 1).start()
        self.message("oL", k, 1).start()
        add(here.r2)
        self.message("iR", k, 1).start()
        add(here.l2)
        self.message("iL", k, 1).start()
        add(here.p2)

    def second_relay(self, k):
        here, own, last = self.here, self.own, self.last
        self.message("oR", k, 1).wait_recv()
        own[k, here.p1, here.r2, 0:24] = own[k, here.p1, here.r2, 0:24] + last[k, 0]
        self.message("dR", k, 1).start()
        self.message("oL", k, 1).wait_recv()
        own[k, here.p1, here.l2, 24:48] = own[k, here.p1, here.l2, 24:48] + last[k, 1]
        self.message("dL", k, 1).start()

    def result(self, k, out, at):
        here, own, last = self.here, self.own, self.last
        width = own.shape[4]
        for name in ("iR", "dR", "iL", "dL"):
            self.message(name, k, 1).wait_recv()
        columns = pl.ds(pl.multiple_of(at * width, 128), width)
        out[0:24, columns] = own[k, here.p1, here.p2, 0:24] + last[k, 2] + last[k, 4]
        out[24:48, columns] = own[k, here.p1, here.p2, 24:48] + last[k, 3] + last[k, 5]

    def sent(self, k):
        self.whole(k).wait_send()
        for stage in (0, 1):
            for name in STEPS[:6]:
                self.message(name, k, stage).wait_send()


def each(low, high, step):
    def body(k, carry):
        step(k)
        return carry

    lax.fori_loop(low, high, body, 0)


class SmallSum:
    def __init__(self, here, bufs, landed, ssem, rsem):
        self.bufs, self.landed, self.ssem, self.rsem = bufs, landed, ssem, rsem
        turn = lambda p, by: lax.rem(p + by, 4)
        self.stages = [
            [(here.sib, here.my)],
            [here.device(turn(here.p1, by), here.p2) for by in (1, 2, 3)],
            [here.device(here.p1, turn(here.p2, by)) for by in (1, 2, 3)],
            [(here.dp, turn(here.my, by)) for by in (1, 2, 3)],
        ]
        self.far = [self.stages[1][1], self.stages[2][1], self.stages[3][1]]
        self.sent = []

    def send(self, stage):
        for to in self.stages[stage]:
            at = len(self.sent)
            copy = push(self.bufs.at[stage], self.landed.at[at], self.ssem, self.rsem, at, to)
            self.sent.append(copy)

    def take(self, stage):
        value, count = self.bufs[stage], len(self.stages[stage])
        for at in range(len(self.sent) - count, len(self.sent)):
            self.sent[at].wait_recv()
            value = value + self.landed[at]
        self.bufs[stage + 1] = value

    def finish(self):
        for copy in self.sent:
            copy.wait_send()


def scatter_scratch(n, w):
    return [
        pltpu.VMEM((n, 4, 4, 48, w), F32),
        pltpu.VMEM((n, 4, 4, 48, w), F32),
        pltpu.VMEM((n, 6, 2, 48, w), F32),
        pltpu.VMEM((n, 6, 24, w), F32),
        pltpu.SemaphoreType.DMA((n,)),
        pltpu.SemaphoreType.DMA((n,)),
        pltpu.SemaphoreType.DMA((n,)),
        pltpu.SemaphoreType.DMA((12 * n,)),
        pltpu.SemaphoreType.DMA((12 * n,)),
    ]


def scatter_sources(refs, pieces):
    return [(refs[which], at * STEP, STEP) for which, at in pieces]


def norm_back(value, source, base, gain):
    source = source.astype(F32)
    r = lax.rsqrt(jnp.mean(source * source, axis=1, keepdims=True) + EPSILON)
    n = source * r
    e = value * gain
    inner = jnp.mean(e * n, axis=1, keepdims=True)
    return base.astype(F32) + r * (e - n * inner), jnp.sum(value * n, axis=0, keepdims=True)


def load(ref, scratch, sem):
    copy = pltpu.make_async_copy(ref, scratch, sem)
    copy.start()
    return copy


def middle_kernel(pieces, count, x_ref, source_ref, base_ref, gain_ref, w_ref, *refs):
    ins, refs = refs[:count], refs[count:]
    grad_ref, gg_ref, share_ref, sums_ref = refs[:4]
    source_s, base_s, w_s, opp, nbr, held, own_s, blocks, csem, *sem = refs[4:17]
    here, ring = Place(), YRing(x_ref.shape[0], 2, *sem[0:2])
    total = ScatterSum(here, scatter_sources(ins, pieces), *refs[17:])
    n = total.n
    far = (ring.dp, ring.far)
    meet(ring.neighbours() + [far] + here.peers())
    ring.start(x_ref, opp, nbr, 0)
    q, h = ring.quarter, ring.half
    ring.fetch(x_ref, held, own_s, csem)
    for k in range(n):
        total.exchange(k)
    loads = [
        load(rows_of(source_ref, ring.me * q, q), source_s, csem.at[3]),
        load(rows_of(base_ref, ring.me * q, q), base_s, csem.at[4]),
        load(w_ref, w_s, csem.at[5]),
    ]
    ring.relay(opp, nbr, held, 0)
    ring.start(x_ref, opp, nbr, 1)
    each(0, n, total.first)
    each(0, n - 2, total.first_relay)
    ring.relay(opp, nbr, held, 1)
    for copy in loads:
        copy.wait()
    sums, swaps, keeps = 0.0, [], []
    inner = gg_ref.shape[1]
    for wave in (0, 1):
        for part in (0, 1):
            at, value = ring.collect(own_s, nbr, part, wave)
            value, more = norm_back(value, source_s[at, :], base_s[at, :], gain_row(gain_ref))
            grad_ref[at, :] = value
            sums = sums + more
        tall = ring.tall
        low = jnp.concatenate(
            [grad_ref[part * h + wave * tall : part * h + wave * tall + tall, :] for part in (0, 1)], axis=0
        ).astype(jnp.bfloat16)
        for j, by in enumerate((2, 1, 3, 0)):
            to = lax.rem(ring.me + by, Y)
            blocks[wave, j] = mm_t(low, rows_of(w_s, to * inner, inner)[...])
            for part in (0, 1):
                src = blocks.at[wave, j, part * tall : part * tall + tall]
                into = rows_of(gg_ref, ring.me * q + part * h + wave * tall, tall)
                if by:
                    at = (wave * 3 + j) * 2 + part
                    swaps.append(push(src, into, *sem[2:4], at, (ring.dp, to)))
                else:
                    keeps.append(load(src, into, csem.at[6 + wave * 2 + part]))
        if wave == 0:
            each(n - 2, n, total.first_relay)
    sums_ref[...] = sums
    each(0, n, total.second)
    each(0, n, total.second_relay)
    each(0, n, lambda k: total.result(k, share_ref, k))
    for copy in swaps:
        copy.wait_recv()
    for copy in keeps:
        copy.wait()
    for copy in swaps:
        copy.wait_send()
    ring.finish()
    each(0, n, total.sent)


def reduce_middle(partial, source, base, gain, w_full, grads, pieces, call_id):
    n = len(pieces)
    hbm, vmem = pl.BlockSpec(memory_space=pl.ANY), pl.BlockSpec(memory_space=pltpu.VMEM)
    rows, columns = partial.shape
    quarter, inner = rows // Y, w_full.shape[0] // Y
    return pl.pallas_call(
        functools.partial(middle_kernel, pieces, len(grads)),
        out_shape=[
            jax.ShapeDtypeStruct((quarter, columns), F32),
            jax.ShapeDtypeStruct((rows, inner), F32),
            jax.ShapeDtypeStruct((48, n * STEP), F32),
            jax.ShapeDtypeStruct((1, columns), F32),
        ],
        in_specs=[hbm, hbm, hbm, vmem, hbm] + [hbm] * len(grads),
        out_specs=[vmem, hbm, vmem, vmem],
        scratch_shapes=[
            pltpu.VMEM((quarter, columns), source.dtype),
            pltpu.VMEM((quarter, columns), base.dtype),
            pltpu.VMEM(w_full.shape, w_full.dtype),
        ]
        + ring_scratch(quarter, columns)
        + [
            pltpu.VMEM((quarter, columns), F32),
            pltpu.VMEM((2, 4, quarter // 2, inner), F32),
            pltpu.SemaphoreType.DMA((10,)),
        ]
        + sems(12, 12)
        + scatter_scratch(n, STEP),
        compiler_params=pltpu.CompilerParams(
            collective_id=call_id, has_side_effects=True, vmem_limit_bytes=56 << 20
        ),
    )(partial, source, base, gain, w_full, *grads)


def input_kernel(
    pieces, count, x_ref, source_ref, base_ref, gain_ref, other_ref, fall_ref, square_ref, more_ref,
    bias_ref, length_ref, bucket_ref, *refs
):
    ins, refs = refs[:count], refs[count:]
    out_ref, out_share_ref, share_ref, sums_ref = refs[:4]
    source_s, opp, nbr, held, own_s, mine_s, wide_s, landed, csem, *sem = refs[4:17]
    bufs, arrived, asem, bsem = refs[17:21]
    here, ring = Place(), YRing(x_ref.shape[0], 1, *sem[0:2])
    total = ScatterSum(here, scatter_sources(ins, pieces), *refs[21:])
    tiny = SmallSum(here, bufs, arrived, asem, bsem)
    n, first = total.n, wide_s.shape[1] // STEP
    meet(ring.neighbours() + here.peers() + tiny.far)
    ring.start(x_ref, opp, nbr, 0)
    q, h = ring.quarter, ring.half
    ring.fetch(x_ref, held, own_s, csem)
    copy = load(rows_of(source_ref, ring.me * q, q), source_s, csem.at[3])
    for k in range(n):
        total.exchange(k)
    each(0, n // 2, total.first)
    ring.relay(opp, nbr, held, 0)
    each(n // 2, n, total.first)
    each(0, n - 2, total.first_relay)
    copy.wait()
    sums = 0.0
    for wave in (0,):
        for part in (0, 1):
            at, value = ring.collect(own_s, nbr, part, wave)
            value, more = norm_back(value, source_s[at, :], base_ref[at, :], gain_row(gain_ref))
            mine_s[at, :] = value
            ring.spread(part, wave, mine_s, out_ref)
            sums = sums + more
    kept = load(mine_s, rows_of(out_ref, ring.me * q, q), csem.at[4])
    bufs[0, 0:1, :] = sums
    bufs[0, 1:2, :] = other_ref[...]
    bufs[0, 8:16, :] = jnp.zeros_like(bufs[0, 8:16, :])
    bufs[0, 2:3, :] = jnp.zeros((1, sums_ref.shape[1]), F32)
    bufs[0, 3:9, :] = fall_ref[0:6, :]
    lane = lax.broadcasted_iota(jnp.int32, (1, PAIR), 1)
    both = jnp.sum(square_ref[...], axis=1, keepdims=True)
    in_bucket = lambda value: jnp.where(lane == bucket_ref[0], value, 0.0)
    bufs[0, 2:3, 0:PAIR] = in_bucket(jnp.sum(more_ref[...], axis=1, keepdims=True))
    for at, value in enumerate((both[0:1], both[1:2], length_ref[0].astype(F32))):
        bufs[0, 9:10, at * PAIR : at * PAIR + PAIR] = in_bucket(value)
    diagonal = lax.broadcasted_iota(jnp.int32, bias_ref.shape, 0) == lax.broadcasted_iota(
        jnp.int32, bias_ref.shape, 1
    )
    bufs[0, 10:11, 0:PAIR] = jnp.sum(jnp.where(diagonal, bias_ref[...], 0.0), axis=0, keepdims=True)
    tiny.send(0)
    each(n - 2, n, total.first_relay)
    each(0, n, total.second)
    ring.forward(0, out_ref)
    tiny.take(0)
    tiny.send(1)
    each(0, n, total.second_relay)
    tiny.take(1)
    tiny.send(2)
    each(0, first, lambda k: total.result(k, wide_s, k))
    inner = landed.shape[2]
    swaps = []
    for j, by in enumerate((2, 1, 3)):
        to = lax.rem(ring.me + by, Y)
        columns = pl.ds(pl.multiple_of(to * inner, 128), inner)
        swaps.append(push(wide_s.at[:, columns], landed.at[j], *sem[2:4], j, (ring.dp, to)))
    each(first, n, lambda k: total.result(k, share_ref, k - first))
    tiny.take(2)
    tiny.send(3)
    own = wide_s[:, pl.ds(pl.multiple_of(ring.me * inner, 128), inner)]
    for j, copy in enumerate(swaps):
        copy.wait_recv()
        own = own + landed[j]
    out_share_ref[...] = own
    tiny.take(3)
    rows = lax.broadcasted_iota(jnp.int32, sums_ref.shape, 0)
    sums_ref[...] = jnp.where(rows < 3, bufs[4], bufs[3])
    ring.arrive(0)
    kept.wait()
    for copy in swaps:
        copy.wait_send()
    tiny.finish()
    ring.finish()
    each(0, n, total.sent)


def reduce_input(partial, source, base, gain, small, grads, pieces, call_id):
    n = len(pieces)
    smem = pl.BlockSpec(memory_space=pltpu.SMEM)
    hbm, vmem = pl.BlockSpec(memory_space=pl.ANY), pl.BlockSpec(memory_space=pltpu.VMEM)
    rows, columns = partial.shape
    quarter, inner = rows // Y, grads[0].shape[1] // Y
    wide = grads[0].shape[1]
    shares = n * STEP - wide
    return pl.pallas_call(
        functools.partial(input_kernel, pieces, len(grads)),
        out_shape=[
            jax.ShapeDtypeStruct(partial.shape, F32),
            jax.ShapeDtypeStruct((48, inner), F32),
            jax.ShapeDtypeStruct((48, shares), F32),
            jax.ShapeDtypeStruct((16, columns), F32),
        ],
        in_specs=[hbm, hbm, vmem, vmem] + [vmem] * 5 + [smem] * 2 + [hbm] * len(grads),
        out_specs=[hbm] + [vmem] * 3,
        scratch_shapes=[pltpu.VMEM((quarter, columns), source.dtype)]
        + ring_scratch(quarter, columns)
        + [
            pltpu.VMEM((quarter, columns), F32),
            pltpu.VMEM((quarter, columns), F32),
            pltpu.VMEM((48, wide), F32),
            pltpu.VMEM((3, 48, inner), F32),
            pltpu.SemaphoreType.DMA((5,)),
        ]
        + sems(24, 3)
        + [pltpu.VMEM((5, 16, columns), F32), pltpu.VMEM((10, 16, columns), F32)]
        + sems(10)
        + scatter_scratch(n, STEP),
        compiler_params=pltpu.CompilerParams(
            collective_id=call_id, has_side_effects=True, vmem_limit_bytes=56 << 20
        ),
    )(partial, source, base, gain, *small, *grads)


HEAD = 64
PAIR = 128
NEG = -1e30


def rows_at(i, size):
    return pl.ds(pl.multiple_of(i * size, size), size)


def lane_is(shape, index):
    return lax.broadcasted_iota(jnp.int32, shape, len(shape) - 1) == index


def first_head(shape):
    return lax.broadcasted_iota(jnp.int32, shape, len(shape) - 1) < HEAD


def halves_mean(values):
    first = first_head(values.shape)
    low = jnp.sum(jnp.where(first, values, 0.0), axis=1, keepdims=True) * (1.0 / HEAD)
    high = jnp.sum(jnp.where(first, 0.0, values), axis=1, keepdims=True) * (1.0 / HEAD)
    return low, high


def one_row(ref, index):
    rows = ref[...]
    picked = lax.broadcasted_iota(jnp.int32, rows.shape, 0) == index
    return jnp.sum(jnp.where(picked, rows, 0.0), axis=0, keepdims=True)


def running_sum(values, backward=False):
    count = values.shape[1]
    at = lax.broadcasted_iota(jnp.int32, values.shape, 1)
    shift = 1
    while shift < count:
        if backward:
            moved = jnp.where(at < count - shift, pltpu.roll(values, count - shift, 1), 0.0)
        else:
            moved = jnp.where(at >= shift, pltpu.roll(values, shift, 1), 0.0)
        values = values + moved
        shift *= 2
    return values


def mm(left, right):
    return jnp.dot(left, right, preferred_element_type=F32)


def mm_t(left, right):
    return lax.dot_general(left, right, (((1,), (1,)), ((), ())), preferred_element_type=F32)


def t_mm(left, right):
    return lax.dot_general(left, right, (((0,), (0,)), ((), ())), preferred_element_type=F32)


def whole(shape):
    return pl.BlockSpec(shape, lambda *_: (0,) * len(shape), pipeline_mode=pl.Buffered(1))


def struct(*shape, t=F32):
    return jax.ShapeDtypeStruct(shape, t)


def local_call(kernel, grid, in_specs, out_specs, out_shape, scratch, limit, flops, moved, call_id=None):
    return pl.pallas_call(
        kernel,
        grid_spec=pltpu.PrefetchScalarGridSpec(
            num_scalar_prefetch=1,
            grid=(grid,),
            in_specs=in_specs,
            out_specs=out_specs,
            scratch_shapes=scratch,
        ),
        out_shape=out_shape,
        compiler_params=pltpu.CompilerParams(
            vmem_limit_bytes=limit << 20,
            collective_id=call_id,
            has_side_effects=call_id is not None,
        ),
        cost_estimate=pl.CostEstimate(
            flops=flops * 10**9, bytes_accessed=moved * 10**6, transcendentals=4 * 10**6
        ),
    )


def forward_kernel(
    length_ref, x_ref, gain_ref, wq_ref, wk_ref, wv_ref, wo_ref, wf_ref, bf_ref, w_ref,
    gain2_ref, cot_in, wg_in, wu_in, wd_in,
    low_out, qn_ref, kn_ref, v_ref, sig_ref, att_ref, stat_ref, decay_ref, gated_out, full_out,
    mid_out, normed_out, grad_out, gate_out, up_out, hid_out, mlp_out, sums_ref,
    top_s, row_s, q_s, k_s, w_s, pre_s, gs, ws, mine, wf_s, bf_s, low_ref, gated_ref, full_ref,
    wg_s, wu_s, wd_s, cot_s, mid_s, normed_s, grad_s, gate_s, up_s, hid_s, mlp_s, osem, *sem,
):
    step = pl.program_id(0)
    seq = x_ref.shape[0]
    length = length_ref[0]
    here = Place()
    me, right, left, far = (lax.rem(here.my + by, Y) for by in (0, 1, 3, 2))
    sibling, right1, left1, right2, left2 = here.peers()
    c, p1, p2, half, quarter = here.c, here.p1, here.p2, seq // 2, seq // Y
    cross_order = (p2, here.l2, here.r2, here.o2)

    def plane(j):
        return link(mine, ws.at[c, p2, p1, 2 - j], *sem[2:4], j, (here.dp, (right, far, left)[j]))

    def torus(stage, j):
        if stage == 0:
            at, spots, to = (lambda p: ws.at[c, p2, p]), (p1, here.l1, here.r1), (right1, left1)
        else:
            at, spots, to = (lambda p: ws.at[c, p]), (p2, here.l2, here.r2), (right2, left2)
        spot, part, side = ((0, 0, 0), (0, 1, 0), (0, 0, 1), (0, 1, 1), (1, 0, 0), (2, 1, 1))[j]
        cut = (slice(0, 2), slice(2, 4 if stage else 3))[part]
        piece = at(spots[spot]).at[cut]
        return link(piece, piece, *sem[4 + 2 * stage : 6 + 2 * stage], j, to[side])

    def cross(j):
        piece = ws.at[c, cross_order[j]]
        return link(piece, piece, *sem[8:10], j, sibling)

    def gate(pair, j):
        owner, part, to = (
            (me, 0, right), (me, 1, right), (me, 0, left), (me, 1, left), (left, 0, right), (right, 1, left)
        )[j]
        piece = gs.at[pair, owner, part * half : part * half + half]
        return link(piece, piece, *sem[0:2], pair * 6 + j, (here.dp, to))

    def hand_on(pair, come, go):
        gate(pair, come).wait_recv()
        gate(pair, go).start()

    def flush(j):
        src, dst = (
            (low_ref, low_out),
            (full_ref, full_out),
            (rows_of(gated_ref, me * quarter, quarter), gated_out),
            (wg_in, wg_s),
            (wu_in, wu_s),
            (wd_in, wd_s),
        )[j]
        return pltpu.make_async_copy(src, dst, osem.at[j])

    def leave(j, chunk):
        src, dst = (
            (mid_s, mid_out), (normed_s, normed_out), (grad_s, grad_out), (gate_s, gate_out),
            (up_s, up_out), (hid_s, hid_out), (mlp_s, mlp_out),
        )[j]
        return pltpu.make_async_copy(src, dst.at[rows_at(chunk, half)], osem.at[6 + j])

    def come(chunk):
        return pltpu.make_async_copy(cot_in.at[rows_at(chunk, half)], cot_s, osem.at[13])

    def pass_on(make):
        make(0).wait_recv()
        make(4).start()
        make(3).wait_recv()
        make(5).start()

    def arrived(make):
        for j in (1, 2, 4, 5):
            make(j).wait_recv()

    @pl.when(step == 0)
    def _():
        tall, wide = ws.shape[4], ws.shape[5]
        two = w_ref[
            pl.ds(pl.multiple_of(here.chip // 2 * (2 * tall), 16), 2 * tall),
            pl.ds(pl.multiple_of(c * wide, 128), wide),
        ].astype(F32)
        mine[...] = jnp.where(lax.rem(here.chip, 2) == 0, two[0:tall], two[tall:])
        meet([(here.dp, right), (here.dp, left), (here.dp, far)] + here.peers())
        for j in range(3):
            plane(j).start()

    @pl.when(step == 0)
    def _():
        def norm(i, carry):
            at = rows_at(i, 128)
            x = x_ref[at, :].astype(F32)
            r = lax.rsqrt(jnp.mean(x * x, axis=1, keepdims=True) + EPSILON)
            low_ref[at, :] = (x * r * gain_row(gain_ref)).astype(jnp.bfloat16)
            return carry

        lax.fori_loop(0, seq // 128, norm, 0)
        flush(0).start()
        heads = wf_ref.shape[0]
        wf_s[...] = jnp.zeros_like(wf_s)
        wf_s[0:heads, :] = wf_ref[...]
        bf_s[...] = jnp.zeros_like(bf_s)
        bf_s[:, 0:heads] = bf_ref[...].astype(F32)
        for j in range(3):
            plane(j).wait_recv()
        for j in range(4):
            torus(0, j).start()
        pre = mm_t(wf_s[...], low_ref[...])[0:8] + jnp.broadcast_to(bf_s[...], (PAIR, PAIR)).T[0:8, 0:1]
        fall = jnp.minimum(pre, 0.0) - jnp.log1p(jnp.exp(-jnp.abs(pre)))
        decay = running_sum(fall)
        column = lax.broadcasted_iota(jnp.int32, decay.shape, 1)
        decay_ref[0] = decay
        decay_ref[1] = jax.nn.sigmoid(-pre)
        row_s[...] = jnp.where(column < length, decay, -NEG)
        final = jnp.sum(jnp.where(column == length - 1, decay, 0.0), axis=1, keepdims=True)
        top = jnp.where(column < length, decay, final)
        top_s[...] = jnp.concatenate([top, jnp.zeros((PAIR - 8, seq), F32)], axis=0).T

    for j, ref in enumerate((wq_ref, wk_ref, wv_ref, wo_ref)):
        w_s[:, j * PAIR : j * PAIR + PAIR] = ref[...]
    pre_s[...] = mm(low_ref[...], w_s[...])

    def norms(i, carry):
        at = rows_at(i, 128)
        for j, n_ref, s, col in ((0, qn_ref, q_s, 0), (1, kn_ref, k_s, 2)):
            pre = pre_s[at, j * PAIR : j * PAIR + PAIR]
            a, b = halves_mean(pre * pre)
            a, b = lax.rsqrt(a + EPSILON), lax.rsqrt(b + EPSILON)
            n = pre * jnp.where(first_head(pre.shape), a, b)
            n_ref[at, :] = n
            s[at, :] = n.astype(jnp.bfloat16)
            here = jnp.where(lane_is(pre.shape, col), a, jnp.where(lane_is(pre.shape, col + 1), b, 0.0))
            stat_ref[at, :] = here if col == 0 else stat_ref[at, :] + here
        v_ref[at, :] = pre_s[at, 2 * PAIR : 3 * PAIR].astype(jnp.bfloat16)
        sig_ref[at, :] = jax.nn.sigmoid(pre_s[at, 3 * PAIR : 4 * PAIR])
        return carry

    lax.fori_loop(0, seq // 128, norms, 0)

    @pl.when(step == 1)
    def _():
        for j in (3, 4, 5):
            flush(j).start()
        come(0).start()

    lines = [one_row(row_s, 2 * step + head) for head in (0, 1)]
    first = first_head((128, PAIR))
    zero = jnp.zeros((128, PAIR), jnp.bfloat16)
    upper = lax.broadcasted_iota(jnp.int32, (128, 128), 1) > lax.broadcasted_iota(
        jnp.int32, (128, 128), 0
    )
    for i in range(seq // 128):
        at, n = slice(i * 128, i * 128 + 128), i * 128 + 128
        q = q_s[at, :]
        two = jnp.concatenate([jnp.where(first, q, zero), jnp.where(first, zero, q)], axis=0)
        raw = mm_t(two, k_s[0:n, :]) * (HEAD ** (-0.5))
        probs = []
        for head in (0, 1):
            column = jnp.sum(
                jnp.where(lane_is((128, PAIR), 2 * step + head), top_s[at, :], 0.0), axis=1, keepdims=True
            )
            s = raw[head * 128 : head * 128 + 128] + (column - lines[head][:, 0:n])
            diagonal = jnp.where(upper, NEG, s[:, n - 128 :])
            s = diagonal if i == 0 else jnp.concatenate([s[:, : n - 128], diagonal], axis=1)
            p = jnp.exp(s)
            probs.append((p * (1.0 / jnp.sum(p, axis=1, keepdims=True))).astype(jnp.bfloat16))
        both = mm(jnp.concatenate(probs, axis=0), v_ref[0:n, :])
        out = jnp.where(first, both[0:128], both[128:])
        att_ref[at, :] = out
        gs[step, me, at, :] = (out * sig_ref[at, :]).astype(jnp.bfloat16).astype(F32)
        if n == half:
            gate(step, 0).start()
            gate(step, 2).start()

            @pl.when(step > 0)
            def _():
                hand_on(step - 1, 0, 4)

            @pl.when(step == 0)
            def _():
                pass_on(lambda j: torus(0, j))


    gate(step, 3).start()

    @pl.when(step == 0)
    def _():
        gate(0, 1).start()
        arrived(lambda j: torus(0, j))
        for j in range(4):
            torus(1, j).start()
        cross(0).start()

    @pl.when(step > 0)
    def _():
        hand_on(step - 1, 3, 5)

    @pl.when(step == pl.num_programs(0) - 1)
    def _():
        pairs = gs.shape[0]
        pass_on(lambda j: torus(1, j))
        torus(1, 1).wait_recv()
        cross(1).start()
        torus(1, 2).wait_recv()
        cross(2).start()
        hand_on(step, 0, 4)
        for pair in range(1, pairs):
            gate(pair, 1).start()
        hand_on(step, 3, 5)
        torus(1, 4).wait_recv()
        torus(1, 5).wait_recv()
        cross(3).start()
        tall, wide, shard = ws.shape[4], ws.shape[5], w_ref.shape[0]
        rows_of(full_ref, me * shard, shard)[...] = w_ref[...]

        def turn(h):
            def piece(k, carry):
                on, m = k // 8, lax.rem(k, 8)
                x, z = m // 2, lax.rem(m, 2) * 2
                rows = rows_at(lax.rem(me + on + 1, Y) * (shard // (2 * tall)) + m, 2 * tall)
                parts = [ws[h, z + t, x, on] if h == 0 else ws[h, x, z + t, on] for t in (0, 1)]
                both = jnp.concatenate(parts, axis=0).astype(jnp.bfloat16)
                full_ref[rows, h * wide : h * wide + wide] = both
                return carry

            lax.fori_loop(0, 8 * (Y - 1), piece, 0)

        for h in (0, 1):
            pl.when(c == h)(functools.partial(turn, h))
        for j in (3, 4, 5):
            flush(j).wait()
        outer, inner = full_ref.shape[1] // 2, wg_s.shape[1] // 2
        columns = lambda k, size: pl.ds(pl.multiple_of(k * size, size), size)
        sums_ref[...] = jnp.zeros_like(sums_ref)

        def feed_forward(chunk):
            rows = rows_at(chunk, half)
            for part, names in enumerate(((2, 4), (1, 5))):

                @pl.when(chunk == part)
                def _():
                    for pair in range(pairs):
                        for j in names:
                            gate(pair, j).wait_recv()

            for pair in range(pairs):
                for y in range(Y):
                    lane = (y * pairs + pair) * PAIR
                    gated_ref[rows, lane : lane + PAIR] = gs[pair, y, rows, :].astype(jnp.bfloat16)

            @pl.when(chunk == 1)
            def _():
                flush(2).start()
                for j in range(7):
                    leave(j, 0).wait()
                come(1).start()

            kept = lax.broadcasted_iota(jnp.int32, (half, 1), 0) + chunk * half < length

            def project(k):
                @pl.when((k == 1) & (chunk == 0))
                def _():
                    for j in range(4):
                        cross(j).wait_recv()
                    for h in (0, 1):
                        pl.when(c != h)(functools.partial(turn, h))
                    flush(1).start()

                at = columns(lax.rem(k + c, 2), outer)
                branch = mm(gated_ref[rows, :], full_ref[:, at])
                x = x_ref[rows, at].astype(F32)
                mid_s[:, at] = x + branch
                for row, value in ((0, x), (1, branch)):
                    value = jnp.where(kept, value * value, 0.0)
                    sums_ref[row : row + 1, at] = sums_ref[row : row + 1, at] + jnp.sum(
                        value, axis=0, keepdims=True
                    )

            each(0, 2, project)
            leave(0, chunk).start()

            def norm(i, carry):
                at = rows_at(i, 128)
                mid = mid_s[at, :]
                r = lax.rsqrt(jnp.mean(mid * mid, axis=1, keepdims=True) + EPSILON)
                normed_s[at, :] = (mid * r * gain_row(gain2_ref)).astype(jnp.bfloat16)
                return carry

            lax.fori_loop(0, half // 128, norm, 0)
            leave(1, chunk).start()

            def hidden(k):
                at = columns(k, inner)
                gate_s[:, at] = mm(normed_s[...], wg_s[:, at])
                up_s[:, at] = mm(normed_s[...], wu_s[:, at])
                pre = gate_s[:, at]
                hid_s[:, at] = (pre * jax.nn.sigmoid(pre) * up_s[:, at]).astype(jnp.bfloat16)

            each(0, 2, hidden)
            for j in (3, 4, 5):
                leave(j, chunk).start()

            come(chunk).wait()
            grad_s[...] = jnp.where(kept, cot_s[...].astype(F32), 0.0).astype(jnp.bfloat16)
            leave(2, chunk).start()

            def project_out(k):
                at = columns(k, outer)
                mlp_s[:, at] = mm(hid_s[...], wd_s[:, at])

            each(0, 2, project_out)
            leave(6, chunk).start()

        each(0, 2, feed_forward)
        for j in range(7):
            leave(j, 1).wait()
        for j in range(3):
            flush(j).wait()
            plane(j).wait_send()
        for stage in (0, 1):
            for j in range(6):
                torus(stage, j).wait_send()
        for j in range(4):
            cross(j).wait_send()
        for pair in range(pairs):
            for j in range(6):
                gate(pair, j).wait_send()


def forward(
    tokens, cotangent, length, gain, wq, wk, wv, wo, wf, bf, w_out, gain2, wg, wu, wd, call_id
):
    seq, width = tokens.shape
    heads, hidden, half = wq.shape[1], wg.shape[1], seq // 2
    weights = pl.BlockSpec((width, PAIR), lambda i, _: (0, i))
    lanes = pl.BlockSpec((seq, PAIR), lambda i, _: (0, i))
    low = jnp.bfloat16
    half_rows = lambda w, t=F32: pltpu.VMEM((half, w), t)
    return local_call(
        forward_kernel,
        heads // PAIR,
        [whole((seq, width)), whole((width,))] + [weights] * 4
        + [whole(wf.shape), whole(bf.shape), whole(w_out.shape), whole((width,))] + [HBM] * 4,
        [HBM] + [lanes] * 6 + [whole((2, 8, seq))] + [HBM] * 9 + [whole((2, width))],
        [
            struct(seq, width, t=low), struct(seq, heads), struct(seq, heads), struct(seq, heads, t=low),
            struct(seq, heads), struct(seq, heads), struct(seq, heads),
            struct(2, 8, seq), struct(seq // Y, heads * Y, t=low), struct(heads * Y, width, t=low),
            struct(seq, width), struct(seq, width, t=low), struct(seq, width, t=low),
            struct(seq, hidden), struct(seq, hidden), struct(seq, hidden, t=low), struct(seq, width),
            struct(2, width),
        ],
        [
            pltpu.VMEM((seq, PAIR), F32),
            pltpu.VMEM((8, seq), F32),
            pltpu.VMEM((seq, PAIR), low),
            pltpu.VMEM((seq, PAIR), low),
            pltpu.VMEM((width, 4 * PAIR), low),
            pltpu.VMEM((seq, 4 * PAIR), F32),
            pltpu.VMEM((heads // PAIR, Y, seq, PAIR), F32),
            pltpu.VMEM((2, 4, 4, Y - 1, heads // 16, width // 2), F32),
            pltpu.VMEM((heads // 16, width // 2), F32),
            pltpu.VMEM((16, width), low),
            pltpu.VMEM((1, PAIR), F32),
            pltpu.VMEM((seq, width), low),
            pltpu.VMEM((seq, width), low),
            pltpu.VMEM((heads * Y, width), low),
            pltpu.VMEM((width, hidden), low),
            pltpu.VMEM((width, hidden), low),
            pltpu.VMEM((hidden, width), low),
            half_rows(width, low), half_rows(width), half_rows(width, low), half_rows(width, low),
            half_rows(hidden), half_rows(hidden), half_rows(hidden, low), half_rows(width),
            pltpu.SemaphoreType.DMA((14,)),
        ]
        + sems(6 * (heads // PAIR), 3, 6, 6, 4),
        63, 17, 60, call_id,
    )(length, tokens, gain, wq, wk, wv, wo, wf, bf, w_out, gain2, cotangent, wg, wu, wd)


def copier(sem):
    count = iter(range(sem.shape[0]))

    def copy(src, dst):
        return load(src, dst, sem.at[next(count)])

    return copy


def reduce_links(rows, x, opp, nbr, held, sem):
    dp, me = lax.axis_index("dp"), lax.axis_index("mp")
    right, left, far = lax.rem(me + 1, Y), lax.rem(me + 3, Y), lax.rem(me + 2, Y)
    q, h = rows // Y, rows // Y // 2

    def message(name):
        src, dst, to = {
            "oR": (lambda: rows_of(x, far * q, h), lambda: opp.at[0], right),
            "oL": (lambda: rows_of(x, far * q + h, h), lambda: opp.at[1], left),
            "iR": (lambda: rows_of(x, right * q + h, h), lambda: nbr.at[0, h:q], right),
            "iL": (lambda: rows_of(x, left * q, h), lambda: nbr.at[1, 0:h], left),
            "dR": (lambda: held.at[0], lambda: nbr.at[0, 0:h], right),
            "dL": (lambda: held.at[1], lambda: nbr.at[1, h:q], left),
        }[name]
        return link(src(), dst(), *sem, STEPS.index(name), (dp, to))

    return message, me, right, left, [(dp, right), (dp, left)]


def mlp_backward_kernel(
    length_ref, grad_in, low_in, gate_in, up_in, hid_in, wd_in, wg_in, wu_in, x_ref, mid_ref,
    back_out, gd_out, gg_out, gu_out, layer_ref, square_ref,
    grad_ref, low_ref, gate_ref, up_ref, hid_ref, wd_ref, wg_ref, wu_ref,
    dg_s, du_s, back_s, bufs, opp, nbr, held, own_s, mid_s, csem, *sem,
):
    seq, width = grad_ref.shape
    units = wd_ref.shape[0] // 2
    low16 = jnp.bfloat16
    message, me, right, left, peers = reduce_links(seq, x_ref, opp, nbr, held, sem)
    q, h = seq // Y, seq // Y // 2
    copy = copier(csem)
    need = [
        copy(grad_in, grad_ref),
        copy(wd_in.at[0:units], wd_ref.at[0:units]),
        copy(gate_in.at[:, 0:units], gate_ref.at[:, 0:units]),
        copy(up_in.at[:, 0:units], up_ref.at[:, 0:units]),
    ]
    meet(peers)
    for name in STEPS[:4]:
        message(name).start()
    for c in need[0:2]:
        c.wait()
    next_low, next_hid = copy(low_in, low_ref), copy(hid_in, hid_ref)
    more = [
        copy(wd_in.at[units:], wd_ref.at[units:]),
        copy(gate_in.at[:, units:], gate_ref.at[:, units:]),
        copy(up_in.at[:, units:], up_ref.at[:, units:]),
    ]
    weights = [copy(wg_in, wg_ref), copy(wu_in, wu_ref)]
    adds = [
        copy(rows_of(x_ref, right * q, h), held.at[0]),
        copy(rows_of(x_ref, left * q + h, h), held.at[1]),
        copy(rows_of(x_ref, me * q, q), own_s),
        copy(rows_of(mid_ref, me * q, q), mid_s),
    ]
    spots = (gd_out, gg_out, gu_out)
    columns = lambda j: pl.ds(pl.multiple_of(j * units, units), units)
    flush = lambda j, which: pltpu.make_async_copy(
        bufs.at[which, j], spots[which].at[:, columns(j)], csem.at[csem.shape[0] - 6 + which * 2 + j]
    )

    def write(which, left_of, right_of, j):
        slot, at = bufs.at[which, j], columns(j)

        def rows(i, carry):
            part = rows_at(i, 768)
            slot[part, :] = t_mm(left_of[:, part], right_of[:, at])
            return carry

        lax.fori_loop(0, width // 768, rows, 0)
        flush(j, which).start()

    def tile(j):
        at = columns(j)

        @pl.when(j == 1)
        def _():
            for c in more:
                c.wait()

        grad = mm_t(grad_ref[...], wd_ref[at, :])

        @pl.when(j == 0)
        def _():
            for c in need[2:4]:
                c.wait()

        gate = gate_ref[:, at]
        sig = jax.nn.sigmoid(gate)
        dg_s[:, at] = (grad * up_ref[:, at] * (sig * (1.0 + gate * (1.0 - sig)))).astype(low16)
        du_s[:, at] = (grad * (gate * sig)).astype(low16)

        @pl.when(j == 0)
        def _():
            next_low.wait()
            next_hid.wait()

        write(0, grad_ref, hid_ref, j)
        write(1, low_ref, dg_s, j)

        @pl.when(j == 1)
        def _():
            for part, (come, go) in enumerate((("oR", "dR"), ("oL", "dL"))):
                message(come).wait_recv()
                adds[part].wait()
                held[part] = held[part] + opp[part]
                message(go).start()

        write(2, low_ref, du_s, j)

    each(0, 2, tile)
    for c in weights:
        c.wait()

    def back(i, carry):
        rows = rows_at(i, 768)
        back_s[:, rows] = mm_t(dg_s[...], wg_ref[rows, :])
        back_s[:, rows] = back_s[:, rows] + mm_t(du_s[...], wu_ref[rows, :])
        return carry

    lax.fori_loop(0, width // 768, back, 0)
    last = copy(back_s, back_out)
    adds[2].wait()
    adds[3].wait()
    sums = 0.0
    for part, names in enumerate((("dR", "iL"), ("iR", "dL"))):
        for name in names:
            message(name).wait_recv()
        at = slice(part * h, part * h + h)
        branch = own_s[at, :] + nbr[0, at] + nbr[1, at]
        layer_ref[at, :] = (mid_s[at, :] + branch).astype(low16).astype(F32)
        row = lax.broadcasted_iota(jnp.int32, (h, 1), 0) + (me * q + part * h)
        kept = jnp.where(row < length_ref[0], branch * branch, 0.0)
        sums = sums + jnp.sum(kept, axis=0, keepdims=True)
    square_ref[...] = sums
    last.wait()
    for j in (0, 1):
        for which in range(3):
            flush(j, which).wait()
    for name in STEPS[:6]:
        message(name).wait_send()


def mlp_backward(length, grad, low, gate, up, hid, wg, wu, wd, branch, mid, call_id):
    seq, width = low.shape
    hidden = wg.shape[1]
    quarter = seq // Y
    low16 = jnp.bfloat16
    smem = pl.BlockSpec(memory_space=pltpu.SMEM)
    inputs = (grad, low, gate, up, hid, wd, wg, wu)
    return pl.pallas_call(
        mlp_backward_kernel,
        in_specs=[smem] + [HBM] * 10,
        out_specs=[HBM] * 4 + [VMEM] * 2,
        out_shape=[struct(seq, width)] + [struct(width, hidden)] * 3
        + [struct(quarter, width), struct(1, width)],
        scratch_shapes=[pltpu.VMEM(a.shape, a.dtype) for a in inputs]
        + [pltpu.VMEM((seq, hidden), low16)] * 2
        + [pltpu.VMEM((seq, width), F32), pltpu.VMEM((3, 2, width, hidden // 2), F32)]
        + ring_scratch(quarter, width)
        + [pltpu.VMEM((quarter, width), F32)] * 2
        + [pltpu.SemaphoreType.DMA((22,))]
        + sems(6),
        compiler_params=pltpu.CompilerParams(
            vmem_limit_bytes=62 << 20, collective_id=call_id, has_side_effects=True
        ),
    )(length, *inputs, branch, mid)


def backward_kernel(
    length_ref, gg_ref, low_in, qn_ref, kn_ref, v_ref, sig_ref, att_ref, stat_ref,
    decay_ref, wq_ref, wk_ref, wv_ref, wo_ref, wf_ref, own_ref, gated_ref, layer_ref,
    back_out, four_out, gout_out, gf_ref, bias_ref, out_ref,
    k_s, do_s, line_s, top_s, both_s, dq_s, dk_s, dv_s, all_s, fall_s, w_s, wf_s, lay_s, back_ref, wide_s, low_ref, osem,
    *sem,
):
    step = pl.program_id(0)
    seq, width = low_ref.shape
    length = length_ref[0]
    low16 = jnp.bfloat16
    wide = 4 * PAIR
    dp, me = lax.axis_index("dp"), lax.axis_index("mp")
    right, left = lax.rem(me + 1, Y), lax.rem(me + 3, Y)
    q, h = seq // Y, seq // Y // 2

    def spread(j):
        owner, part, to = (
            (me, 0, right), (me, 1, right), (me, 0, left), (me, 1, left), (left, 0, right), (right, 1, left)
        )[j]
        piece = rows_of(lay_s, owner * q + part * h, h)
        source = layer_ref.at[part * h : part * h + h] if j < 4 else piece
        return link(source, piece, *sem, j, (dp, to))

    def fetch(j):
        pair = ((layer_ref, rows_of(lay_s, me * q, q)), (low_in, low_ref))[j]
        return pltpu.make_async_copy(*pair, osem.at[5 + j])

    @pl.when(step == 0)
    def _():
        meet([(dp, right), (dp, left)])
        for j in range(4):
            spread(j).start()
        for j in (0, 1):
            fetch(j).start()

    @pl.when(step == 2)
    def _():
        spread(0).wait_recv()
        spread(4).start()
        spread(3).wait_recv()
        spread(5).start()

    @pl.when(step == 0)
    def _():
        heads = wf_ref.shape[0]
        wf_s[...] = jnp.zeros_like(wf_s)
        wf_s[0:heads, :] = wf_ref[...]
        decay = decay_ref[0]
        column = lax.broadcasted_iota(jnp.int32, decay.shape, 1)
        final = jnp.sum(jnp.where(column == length - 1, decay, 0.0), axis=1, keepdims=True)
        line_s[...] = jnp.where(column < length, decay, final)
        masked = jnp.where(column < length, decay, -NEG)
        top_s[...] = jnp.concatenate([masked, jnp.zeros((PAIR - 8, seq), F32)], axis=0).T
        fall_s[...] = jnp.zeros_like(fall_s)

    base = pl.multiple_of(step * wide, wide)
    part = lambda j: pl.ds(pl.multiple_of(base + j * PAIR, PAIR), PAIR)
    for j, w_ref in enumerate((wq_ref, wk_ref, wv_ref, wo_ref)):
        w_s[:, part(j)] = w_ref[...]
    first = first_head((seq, PAIR))
    gg, sig = gg_ref[...], sig_ref[...]
    do_s[...] = (gg * sig).astype(low16)
    all_s[:, part(3)] = (gg * att_ref[...] * sig * (1.0 - sig)).astype(low16)
    k_s[...] = kn_ref[...].astype(low16)
    dk_s[...] = jnp.zeros_like(dk_s)
    dv_s[...] = jnp.zeros_like(dv_s)
    columns, lines = [], [one_row(line_s, 2 * step + head) for head in (0, 1)]
    for head in (0, 1):
        column = jnp.sum(
            jnp.where(lane_is((seq, PAIR), 2 * step + head), top_s[...], 0.0), axis=1, keepdims=True
        )
        columns.append(column)
    both_s[...] = jnp.concatenate([jnp.broadcast_to(column, (seq, PAIR)) for column in columns], axis=1)
    ones = jnp.concatenate(
        [jnp.where(lane_is((128, PAIR), 2 * step + head), 1.0, 0.0) for head in (0, 1)], axis=0
    ).astype(low16)
    lanes = lax.broadcasted_iota(jnp.int32, (seq, PAIR), 1)
    marks = jnp.where(lanes // 2 == step, 1.0, 0.0).astype(low16)
    block = first_head((128, PAIR))
    zero = jnp.zeros((128, PAIR), low16)
    lower = lax.broadcasted_iota(jnp.int32, (128, 256), 0) > lax.rem(
        lax.broadcasted_iota(jnp.int32, (128, 256), 1), 128
    )
    for i in range(seq // 128):
        at, n = slice(i * 128, i * 128 + 128), i * 128 + 128
        query = qn_ref[at, :].astype(low16)
        do = do_s[at, :]
        two_q, two_do = (
            jnp.concatenate([jnp.where(block, t, zero), jnp.where(block, zero, t)], axis=0)
            for t in (query, do)
        )
        s = mm_t(k_s[0:n, :], two_q) * (HEAD ** (-0.5))
        s = s + (jnp.concatenate([line[:, at] for line in lines], axis=1) - both_s[0:n, :])
        diagonal = jnp.where(lower, NEG, s[n - 128 :, :])
        s = diagonal if i == 0 else jnp.concatenate([s[: n - 128, :], diagonal], axis=0)
        p = jnp.exp(s)
        p = p * (1.0 / jnp.sum(p, axis=0, keepdims=True))
        gp = mm_t(v_ref[0:n, :], two_do)
        ds = (p * (gp - jnp.sum(p * gp, axis=0, keepdims=True))).astype(low16)
        dv_s[0:n, :] = dv_s[0:n, :] + mm(p.astype(low16), two_do)
        dk_s[0:n, :] = dk_s[0:n, :] + mm(ds, jnp.concatenate([two_q, ones], axis=1))
        pieces = t_mm(ds, jnp.concatenate([k_s[0:n, :], marks[0:n]], axis=1))
        one, two = pieces[0:128], pieces[128:]
        dq_s[at, :] = jnp.where(block, one[:, 0:PAIR], two[:, 0:PAIR])
        fall_s[at, :] = fall_s[at, :] + (
            jnp.where(lane_is((128, PAIR), 2 * step), one[:, PAIR:], 0.0)
            + jnp.where(lane_is((128, PAIR), 2 * step + 1), two[:, PAIR:], 0.0)
        )
    fall_s[...] = fall_s[...] - dk_s[:, PAIR:]
    stat = stat_ref[...]
    for e, n_ref, col, to in ((dq_s, qn_ref, 0, 0), (dk_s, kn_ref, 2, 1)):
        e = e[:, 0:PAIR] * (HEAD ** (-0.5))
        n = n_ref[...]
        a, b = halves_mean(e * n)
        r = jnp.where(first, stat[:, col : col + 1], stat[:, col + 1 : col + 2])
        all_s[:, part(to)] = (r * (e - n * jnp.where(first, a, b))).astype(low16)
    all_s[:, part(2)] = dv_s[...].astype(low16)
    slot = lax.rem(step, 2)

    @pl.when(step == 0)
    def _():
        for j in (0, 1):
            fetch(j).wait()

    def flush(j, at, step):
        columns = pl.ds(pl.multiple_of(step * wide, wide), wide)
        out = (four_out, gout_out)[j].at[:, columns]
        return pltpu.make_async_copy(wide_s.at[at, j], out, osem.at[at * 2 + j])

    @pl.when(step == 2)
    def _():
        for j in (0, 1):
            flush(j, 0, 0).wait()

    def grads(k, carry):
        rows = rows_at(k, 768)
        wide_s[slot, 0, rows, :] = t_mm(low_ref[:, rows], all_s[:, pl.ds(base, wide)])
        wide_s[slot, 1, rows, :] = t_mm(own_ref[:, rows].astype(low16), gated_ref[...])
        return carry

    lax.fori_loop(0, width // 768, grads, 0)
    for j in (0, 1):
        flush(j, slot, step).start()

    @pl.when(step == pl.num_programs(0) - 1)
    def _():
        fall = running_sum(fall_s[...].T[0:8], backward=True) * decay_ref[1]
        fall = jnp.concatenate([fall, jnp.zeros_like(fall)], axis=0).astype(low16)
        bias = jnp.sum(fall.astype(F32), axis=1, keepdims=True)
        bias_ref[...] = jnp.broadcast_to(bias[0:8], (8, PAIR))
        gf_ref[...] = mm(fall, low_ref[...])[0:8]

        def tail(k, carry):
            rows = rows_at(k, 768)
            back_ref[:, rows] = mm_t(all_s[...], w_s[rows, :])
            back_ref[:, rows] = back_ref[:, rows] + t_mm(fall, wf_s[:, rows])
            return carry

        lax.fori_loop(0, width // 768, tail, 0)
        last = load(back_ref, back_out, osem.at[4])
        for names, owners in (((1, 2), (me, left, right)), ((4, 5), (lax.rem(me + 2, Y),))):
            for j in names:
                spread(j).wait_recv()
            for owner in owners:
                out_ref[rows_at(owner, q), :] = lay_s[rows_at(owner, q), :].astype(low16)
        for at, done in ((1, 1), (0, 2)):
            for j in (0, 1):
                flush(j, at, done).wait()
        last.wait()
        for j in range(6):
            spread(j).wait_send()


def backward_attention(place, gg, low, qn, kn, v, sig, att, stat, decay, wq, wk, wv, wo, wf, own, gated, layer, call_id):
    seq, width = low.shape
    heads = wq.shape[1]
    weights = pl.BlockSpec((width, PAIR), lambda i, _: (0, i))
    lanes = pl.BlockSpec((seq, PAIR), lambda i, _: (0, i))
    full = whole((seq, width))
    low16 = jnp.bfloat16
    return local_call(
        backward_kernel,
        heads // PAIR,
        [lanes, HBM] + [lanes] * 6 + [whole((2, 8, seq))] + [weights] * 4
        + [whole(wf.shape), whole(own.shape)]
        + [pl.BlockSpec((own.shape[0], 4 * PAIR), lambda i, _: (0, i)), HBM],
        [HBM, HBM, HBM, whole((8, width)), whole((8, PAIR)), full],
        [
            struct(seq, width), struct(width, 4 * heads), struct(width, width), struct(8, width),
            struct(8, PAIR), struct(seq, width, t=low16),
        ],
        [
            pltpu.VMEM((seq, PAIR), low16),
            pltpu.VMEM((seq, PAIR), low16),
            pltpu.VMEM((8, seq), F32),
            pltpu.VMEM((seq, PAIR), F32),
            pltpu.VMEM((seq, 2 * PAIR), F32),
            pltpu.VMEM((seq, PAIR), F32),
            pltpu.VMEM((seq, 2 * PAIR), F32),
            pltpu.VMEM((seq, PAIR), F32),
            pltpu.VMEM((seq, 4 * heads), low16),
            pltpu.VMEM((seq, PAIR), F32),
            pltpu.VMEM((width, 4 * heads), low16),
            pltpu.VMEM((16, width), low16),
            pltpu.VMEM((seq, width), F32),
            pltpu.VMEM((seq, width), F32),
            pltpu.VMEM((2, 2, width, 4 * PAIR), F32),
            pltpu.VMEM((seq, width), low16),
            pltpu.SemaphoreType.DMA((7,)),
        ]
        + sems(6),
        62, 14, 50, call_id,
    )(place, gg, low, qn, kn, v, sig, att, stat, decay, wq, wk, wv, wo, wf, own, gated, layer)


def finish_kernel(
    grad_in, layer_in, wout_hbm, four_hbm, mlp_hbm, sums_hbm,
    grad_ref, layer_ref, wout_ref, q_ref, k_ref, v_ref, o_ref, gate_ref, up_ref, down_ref,
    gain_ref, gain2_ref, fall_ref, rms_ref, bias_ref,
    grad_s, layer_s, four_in, mlp_in, sums_in, sem,
):
    copy = copier(sem)
    rows = grad_in.shape[0] // 4
    parts = [slice(j * rows, j * rows + rows) for j in range(4)]
    come = [(copy(grad_in.at[p], grad_s.at[p]), grad_s.at[p], grad_ref.at[p]) for p in parts]
    small = [copy(wout_hbm, wout_ref), copy(four_hbm, four_in), copy(mlp_hbm, mlp_in), copy(sums_hbm, sums_in)]
    come += [(copy(layer_in.at[p], layer_s.at[p]), layer_s.at[p], layer_ref.at[p]) for p in parts]
    copies = []

    def leave(some):
        for arrived, mid, dst in some:
            arrived.wait()
            copies.append(copy(mid, dst))

    leave(come[0:4])
    for c in small:
        c.wait()
    inner = q_ref.shape[1]
    for j, ref in enumerate((q_ref, k_ref, v_ref, o_ref)):
        for pair in range(inner // PAIR):
            lane = (pair * 4 + j) * PAIR
            ref[:, pair * PAIR : pair * PAIR + PAIR] = four_in[:, lane : lane + PAIR]
    units = gate_ref.shape[1]
    down_ref[...] = mlp_in[:, 0:units]
    gate_ref[...] = mlp_in[:, units : 2 * units]
    up_ref[...] = four_in[:, 4 * inner : 4 * inner + units]
    leave(come[4:8])
    share, width = gain_ref.shape[1], sums_in.shape[1]
    row = lax.broadcasted_iota(jnp.int32, (width, share), 0)
    lane = lax.broadcasted_iota(jnp.int32, (width, share), 1)
    pick = jnp.where(row == lane + lax.axis_index("dp") * share, 1.0, 0.0)
    own = jnp.dot(
        sums_in[...], pick, precision=lax.Precision.HIGHEST, preferred_element_type=F32
    )
    gain_ref[...] = own[0:1]
    gain2_ref[...] = own[1:2]
    fall_ref[...] = own[3 : 3 + fall_ref.shape[0]]
    square = lambda row, at: sums_in[row : row + 1, at * PAIR : at * PAIR + NBUCKET]
    squares = jnp.concatenate([square(9, 0), square(9, 1), square(2, 0)], axis=0)
    rms_ref[...] = jnp.sqrt(squares / (square(9, 2) * width))
    bias_ref[...] = sums_in[10:11, 0 : bias_ref.shape[1]]
    for c in copies:
        c.wait()


def finish(grad, layer, out_share, share, mlp_share, sums, heads):
    rows, inner = out_share.shape
    units = mlp_share.shape[1] // 2
    return pl.pallas_call(
        finish_kernel,
        out_shape=[
            struct(*grad.shape), struct(*layer.shape, t=layer.dtype), *[struct(rows, inner)] * 5,
            *[struct(rows, units)] * 3, struct(1, rows), struct(1, rows), struct(heads, rows),
            struct(3, NBUCKET), struct(1, heads),
        ],
        in_specs=[HBM] * 6,
        out_specs=[HBM, HBM] + [VMEM] * 13,
        scratch_shapes=[pltpu.VMEM(a.shape, a.dtype) for a in (grad, layer, share, mlp_share, sums)]
        + [pltpu.SemaphoreType.DMA((20,))],
        compiler_params=pltpu.CompilerParams(vmem_limit_bytes=60 << 20),
    )(grad, layer, out_share, share, mlp_share, sums)


def per_device(
    tokens, lengths, buckets, out_cotangent, gain_attn, w_query, w_key, w_value, w_outgate,
    w_forget, b_forget, w_out, gain_mlp, w_gate, w_up, w_down,
):
    x, cotangent = tokens[0], out_cotangent[0]
    heads = w_forget.shape[1]
    gain_in, gain_mid = gain_attn, gain_mlp
    weights = (w_query, w_key, w_value, w_outgate, w_forget.T)
    (
        low, qn, kn, value, sig, attended, stat, decay, gated, w_full,
        middle, mid_low, grad_rows, gate, up, hidden, mlp_local, squares,
    ) = forward(
        x, cotangent, lengths, gain_in, *weights, b_forget[None], w_out, gain_mid, w_gate, w_up, w_down, 0
    )
    mid_local, g_down, g_gate, g_up, layer_own, mlp_square = mlp_backward(
        lengths, grad_rows, mid_low, gate, up, hidden, w_gate, w_up, w_down, mlp_local, middle, 1
    )
    grad_own, gg, mlp_share, mlp_gain = reduce_middle(
        mid_local, middle, grad_rows, gain_mid, w_full, [g_down, g_gate],
        ((0, 0), (0, 1), (1, 0), (1, 1)), 2,
    )
    in_local, g_four, g_out, g_fall, bias, layer_out = backward_attention(
        lengths, gg, low, qn, kn, value, sig, attended, stat, decay, *weights, grad_own, gated,
        layer_own, 3,
    )
    small = (mlp_gain, g_fall, squares, mlp_square, bias, lengths, buckets)
    input_grad, out_share, share, sums = reduce_input(
        in_local, x, grad_own, gain_in, small, [g_out, g_four, g_up],
        ((0, 0), (0, 1), (0, 2), (1, 0), (1, 1), (1, 2), (2, 0), (2, 1)), 4,
    )
    (
        input_grad, layer_out, g_out, g_query, g_key, g_value, g_outgate, g_gate, g_up, g_down,
        g_gain, g_gain_mid, g_fall, rms, bias,
    ) = finish(input_grad, layer_out, out_share, share, mlp_share, sums, heads)
    return (
        layer_out[None],
        input_grad[None],
        g_gain[0],
        g_query,
        g_key,
        g_value,
        g_outgate,
        g_fall.T,
        bias[0],
        g_out.T,
        g_gain_mid[0],
        g_gate,
        g_up,
        g_down.T,
        rms,
    )


def solution(mesh):
    placed = (
        P("dp", None, None),
        P("dp"),
        P("dp"),
        P("dp", None, None),
        P(),
        P(None, "mp"),
        P(None, "mp"),
        P(None, "mp"),
        P(None, "mp"),
        P(None, "mp"),
        P("mp"),
        P("mp", None),
        P(),
        P(None, "mp"),
        P(None, "mp"),
        P("mp", None),
    )
    return jax.shard_map(
        per_device,
        mesh=mesh,
        in_specs=placed,
        out_specs=(
            P("dp", None, None),
            P("dp", None, None),
            P("dp"),
            P("dp", "mp"),
            P("dp", "mp"),
            P("dp", "mp"),
            P("dp", "mp"),
            P("dp", "mp"),
            P("mp"),
            P("mp", "dp"),
            P("dp"),
            P("dp", "mp"),
            P("dp", "mp"),
            P("mp", "dp"),
            P(),
        ),
        check_vma=False,
    )
```
